32 devices in a mesh: sp: 4 (over x, core), fsdp: 8 (over z, y).
Axes of the slice: x: 2, y: 2, z: 4, core: 2. Of those that a mesh axis runs over, the one named last changes fastest.
Arguments:
- tokens: bfloat16 [8, 4096, 512], P('fsdp', 'sp'), may hold values from -6 to 6
- starts: int32 [8, 4096], P('fsdp', 'sp'), may hold values from 0 to 4095, as said below
- norm1_gain: bfloat16 [512], P('fsdp'), may hold values from 0.25 to 1.75
- norm1_bias: bfloat16 [512], P('fsdp'), may hold values from -3 to 3
- w_qkv: bfloat16 [512, 1536], P('fsdp'), may hold values from -0.25 to 0.25
- q_bias: bfloat16 [512], P('fsdp'), may hold values from -3 to 3
- v_bias: bfloat16 [512], P('fsdp'), may hold values from -3 to 3
- w_out: bfloat16 [512, 512], P('fsdp'), may hold values from -2 to 2
- out_bias: bfloat16 [512], P('fsdp'), may hold values from -3 to 3
- norm2_gain: bfloat16 [512], P('fsdp'), may hold values from 0.25 to 1.75
- norm2_bias: bfloat16 [512], P('fsdp'), may hold values from -3 to 3
- w_fc: bfloat16 [512, 2048], P('fsdp'), may hold values from -0.25 to 0.25
- fc_bias: bfloat16 [2048], P('fsdp'), may hold values from -4 to 4
- w_proj: bfloat16 [2048, 512], P('fsdp'), may hold values from -0.125 to 0.125
- proj_bias: bfloat16 [512], P('fsdp'), may hold values from -3 to 3
- cotangent: bfloat16 [8, 4096, 512], P('fsdp', 'sp'), may hold values from -6 to 6
Outputs:
- block_out: bfloat16 [8, 4096, 512], P('fsdp', 'sp')
- grad_tokens: bfloat16 [8, 4096, 512], P('fsdp', 'sp')
- grad_norm1_gain: float32 [512], P('fsdp')
- grad_norm1_bias: float32 [512], P('fsdp')
- grad_w_qkv: float32 [512, 1536], P('fsdp')
- grad_q_bias: float32 [512], P('fsdp')
- grad_v_bias: float32 [512], P('fsdp')
- grad_w_out: float32 [512, 512], P('fsdp')
- grad_out_bias: float32 [512], P('fsdp')
- grad_norm2_gain: float32 [512], P('fsdp')
- grad_norm2_bias: float32 [512], P('fsdp')
- grad_w_fc: float32 [512, 2048], P('fsdp')
- grad_fc_bias: float32 [2048], P('fsdp')
- grad_w_proj: float32 [2048, 512], P('fsdp')
- grad_proj_bias: float32 [512], P('fsdp')
The draws below stay inside these ranges and needn't reach their ends.
Inputs may be any that keep to these rules, and one draw needn't show every extreme that they name: starts[s, i] is the first position of the document that holds position i of stream s: it never falls along a stream, starts[s, i] <= i, and starts[s, i] = i where a document begins. Documents never cross streams and may cross devices; in every draw one stream is a single document of 4096 positions and one stream ends with a document of one position.
All inputs are finite; a program needn't handle non-finite values.
Results may differ from the reference program's by a relative error of at most 0.011.
Values may be sent and summed in bfloat16 or wider, within the bound.
A program may use at most 192 MiB of HBM per device.

```python
import jax
import jax.numpy as jnp
from jax import lax

D = 512
HEADS = 8
HEAD_DIM = 64
FF = 2048
SEQ_LEN = 4096
STREAMS = 8


def draw_starts(key, part):
    cut_key, whole_key = jax.random.split(key)
    positions = jnp.arange(SEQ_LEN, dtype=jnp.int32)[None, :]
    streams = jnp.arange(STREAMS, dtype=jnp.int32)[:, None]
    cuts = jax.random.randint(cut_key, (STREAMS, SEQ_LEN), 0, max(SEQ_LEN // 4, 2)) == 0
    single = jax.random.randint(whole_key, (), 0, STREAMS)
    ending = (single + 1) % STREAMS
    cuts = cuts & (streams != single)
    cuts = cuts | (positions == 0) | (streams == ending) & (positions == SEQ_LEN - 1)
    marks = jnp.where(cuts, positions, 0).astype(jnp.int32)
    return lax.cummax(marks, axis=1)


def block_scale(rng, shape, shards, least, high):
    level = 1.0
    for axis_at, parts in shards:
        draws = jax.random.uniform(jax.random.fold_in(jax.random.fold_in(rng, 6), axis_at), (parts,), jnp.float32, least / len(shards), high / len(shards))
        level = level * jnp.repeat(jnp.exp(draws), shape[axis_at] // parts).reshape((-1,) + (1,) * (len(shape) - 1 - axis_at))
    return level


def noise(stream_key, extent, scale, reach, cuts=(), kind=jnp.bfloat16):
    values = scale * jax.random.normal(stream_key, extent, jnp.float32)
    if cuts:
        values = values * block_scale(stream_key, extent, cuts, -0.22, 0.18)
    return jnp.clip(values, -reach, reach).astype(kind)


def setup_inputs(seed: int = 0) -> dict:
    key_list = jax.random.split(jax.random.key(seed), 17)
    tokens = noise(key_list[0], (STREAMS, SEQ_LEN, D), 1.0, 6.0, ((0, 8), (1, 4)))
    starts = draw_starts(jax.random.fold_in(key_list[16], 71), 0)
    norm1_gain = jnp.clip(1.0 + 0.15 * jax.random.normal(key_list[2], (D,), jnp.float32), 0.25, 1.75).astype(jnp.bfloat16)
    norm1_bias = noise(key_list[3], (D,), 0.3, 3.0, ((0, 8),))
    w_qkv = noise(key_list[4], (D, 3 * D), D ** -0.5, 0.25, ((0, 8),))
    q_bias = noise(key_list[5], (D,), 0.3, 3.0, ((0, 8),))
    v_bias = noise(key_list[6], (D,), 0.3, 3.0, ((0, 8),))
    w_out = noise(key_list[7], (D, D), (D // 64) ** -0.5, 2.0, ((0, 8),))
    out_bias = noise(key_list[8], (D,), 0.3, 3.0, ((0, 8),))
    norm2_gain = jnp.clip(1.0 + 0.15 * jax.random.normal(key_list[9], (D,), jnp.float32), 0.25, 1.75).astype(jnp.bfloat16)
    norm2_bias = noise(key_list[10], (D,), 0.3, 3.0, ((0, 8),))
    w_fc = noise(key_list[11], (D, FF), D ** -0.5, 0.25, ((0, 8),))
    fc_bias = noise(key_list[12], (FF,), 0.5, 4.0, ((0, 8),))
    w_proj = noise(key_list[13], (FF, D), FF ** -0.5, 0.125, ((0, 8),))
    proj_bias = noise(key_list[14], (D,), 0.3, 3.0, ((0, 8),))
    cotangent = noise(key_list[15], (STREAMS, SEQ_LEN, D), 1.0, 6.0, ((0, 8), (1, 4)))
    return dict(tokens=tokens, starts=starts, norm1_gain=norm1_gain, norm1_bias=norm1_bias, w_qkv=w_qkv, q_bias=q_bias, v_bias=v_bias, w_out=w_out, out_bias=out_bias, norm2_gain=norm2_gain, norm2_bias=norm2_bias, w_fc=w_fc, fc_bias=fc_bias, w_proj=w_proj, proj_bias=proj_bias, cotangent=cotangent)


EPSILON = 1e-05
HIGHEST = lax.Precision.HIGHEST

@jax.custom_vjp
def low(v):
    return lax.optimization_barrier(v.astype(jnp.bfloat16)).astype(jnp.float32)

@jax.custom_vjp
def low_back(v):
    return v

def low_keep(v):
    return (low(v), None)

def low_pass(kept, grad):
    return (grad,)

def back_keep(v):
    return (v, None)

def back_low(kept, grad):
    return (low(grad),)
low.defvjp(low_keep, low_pass)
low_back.defvjp(back_keep, back_low)

def normalize(values, norm_gain, norm_bias):
    centered = values - lax.optimization_barrier(jnp.mean(values, -1, keepdims=True))
    inverse = lax.rsqrt(lax.optimization_barrier(jnp.mean(centered * centered, -1, keepdims=True)) + EPSILON)
    return centered * inverse * norm_gain + norm_bias

def attend_block(queries, keys_all, values_all, doc_first, positions):
    raw_scores = jnp.einsum('qhd,khd->hqk', queries, keys_all, precision=HIGHEST)
    scores = low_back(raw_scores) * HEAD_DIM ** (-0.5)
    columns = jnp.arange(keys_all.shape[0], dtype=jnp.int32)
    allowed = (columns[None, :] >= doc_first[:, None]) & (columns[None, :] <= positions[:, None])
    scores = jnp.where(allowed[None], scores, -1e+30)
    largest = lax.optimization_barrier(jnp.max(scores, axis=-1, keepdims=True))
    weights = jnp.exp(scores - largest)
    softmax_w = weights / lax.optimization_barrier(jnp.sum(weights, axis=-1, keepdims=True))
    return jnp.einsum('hqk,khd->qhd', low(softmax_w), values_all, precision=HIGHEST)

def layer_forward(stream, doc_first, parameters):
    norm1_gain, norm1_bias, w_qkv, q_bias, v_bias, w_out, out_bias, norm2_gain, norm2_bias, w_fc, fc_bias, w_proj, proj_bias = parameters
    length = stream.shape[0]
    normed_one = low(normalize(stream, norm1_gain, norm1_bias))
    qkv_shift = jnp.concatenate([q_bias, jnp.zeros_like(q_bias), v_bias])
    projected = low(low_back(jnp.dot(normed_one, w_qkv, precision=HIGHEST) + qkv_shift))
    split_heads = projected.reshape(length, 3, HEADS, HEAD_DIM)
    block_rows = min(512, length)
    block_count = length // block_rows
    queries = split_heads[:, 0].reshape(block_count, block_rows, HEADS, HEAD_DIM)
    keys_all = split_heads[:, 1]
    values_all = split_heads[:, 2]
    positions = jnp.arange(length, dtype=jnp.int32).reshape(block_count, block_rows)
    attend = jax.checkpoint(attend_block)
    mixed_heads = lax.map(lambda pieces: attend(pieces[0], keys_all, values_all, pieces[1], pieces[2]), (queries, doc_first.reshape(block_count, block_rows), positions))
    attended = low(low_back(mixed_heads.reshape(length, HEADS * HEAD_DIM)))
    resid = stream + low_back(jnp.dot(attended, w_out, precision=HIGHEST)) + out_bias
    normed_two = low(normalize(resid, norm2_gain, norm2_bias))
    hidden = low_back(jnp.dot(normed_two, w_fc, precision=HIGHEST)) + fc_bias
    gelu_low = low(hidden * jax.nn.sigmoid(1.702 * hidden))
    return resid + low_back(jnp.dot(gelu_low, w_proj, precision=HIGHEST)) + proj_bias

def reference(tokens, starts, norm1_gain, norm1_bias, w_qkv, q_bias, v_bias, w_out, out_bias, norm2_gain, norm2_bias, w_fc, fc_bias, w_proj, proj_bias, cotangent):
    parameters = tuple((weight_arr.astype(jnp.float32) for weight_arr in (norm1_gain, norm1_bias, w_qkv, q_bias, v_bias, w_out, out_bias, norm2_gain, norm2_bias, w_fc, fc_bias, w_proj, proj_bias)))

    def one_stream(running, stream_items):
        stream, doc_first, seed_grad = stream_items
        result, pullback = jax.vjp(lambda inputs, weights_all: layer_forward(inputs, doc_first, weights_all), stream.astype(jnp.float32), parameters)
        input_grad, weight_grads = pullback(seed_grad.astype(jnp.float32))
        running = tuple((acc_grad + new_grad for acc_grad, new_grad in zip(running, weight_grads)))
        return (running, (result.astype(jnp.bfloat16), input_grad.astype(jnp.bfloat16)))
    zero_grads = tuple((jnp.zeros_like(weight_arr) for weight_arr in parameters))
    running, (outputs, input_grads) = lax.scan(one_stream, zero_grads, (tokens, starts, cotangent))
    return (outputs, input_grads, running[0], running[1], running[2], running[3], running[4], running[5], running[6], running[7], running[8], running[9], running[10], running[11], running[12])
```

```python
import functools

import jax
import jax.numpy as jnp
from jax import lax
from jax.experimental import pallas as pl
from jax.experimental.pallas import tpu as pltpu
from jax.sharding import PartitionSpec as P

HEAD_DIM = 64
EPSILON = 1e-05
NEG = -1e30
F32 = jnp.float32
BF16 = jnp.bfloat16
NN = (((1,), (0,)), ((), ()))
NT = (((1,), (1,)), ((), ()))
TN = (((0,), (0,)), ((), ()))
VMEM_LIMIT = 60 << 20
PAD = 16


def dot(left, right, dims=NN):
    return lax.dot_general(left, right, dims, preferred_element_type=F32)


def normalize(values):
    centered = values - jnp.mean(values, -1, keepdims=True)
    inverse = lax.rsqrt(jnp.mean(centered * centered, -1, keepdims=True) + EPSILON)
    return centered * inverse, inverse


def normalize_back(incoming, normed, inverse):
    return inverse * (
        incoming
        - jnp.mean(incoming, -1, keepdims=True)
        - normed * jnp.mean(incoming * normed, -1, keepdims=True)
    )


def whole(shape):
    return pl.BlockSpec(shape, lambda *_: (0,) * len(shape))


def params():
    return pltpu.CompilerParams(vmem_limit_bytes=VMEM_LIMIT)


def cost(flops, size, exps=0):
    return pl.CostEstimate(flops=flops, bytes_accessed=size, transcendentals=exps)


def weight_rows(w_ref, rows):
    parts = w_ref.shape[0]
    return w_ref[:, 0:rows, :].reshape(parts * rows, w_ref.shape[2])


GAIN_ONE, BIAS_ONE, Q_BIAS, V_BIAS, OUT_BIAS, GAIN_TWO, BIAS_TWO, PROJ_BIAS = range(8)


def qkv_kernel(rows, groups, x_ref, st_ref, w_ref, small_ref, o_ref):
    width = x_ref.shape[-1] // groups
    model = x_ref.shape[-1]
    normed, _ = normalize(x_ref[...].astype(F32))
    small = small_ref[...]
    act = (normed * small[GAIN_ONE : GAIN_ONE + 1] + small[BIAS_ONE : BIAS_ONE + 1]).astype(BF16)
    weight = weight_rows(w_ref, rows)
    for part, row in ((0, Q_BIAS), (1, None), (2, V_BIAS)):
        out = dot(act, weight[:, part * model : (part + 1) * model])
        if row is not None:
            out = out + small[row : row + 1]
        out = out.astype(BF16)
        for g in range(groups):
            o_ref[g, part] = out[:, g * width : (g + 1) * width]


def project_qkv(x, starts, weight, rows, small, groups, tile=256):
    length, model = x.shape
    width = model // groups
    return pl.pallas_call(
        functools.partial(qkv_kernel, rows, groups),
        out_shape=jax.ShapeDtypeStruct((groups, 3, length, width), BF16),
        grid=(length // tile,),
        in_specs=[
            pl.BlockSpec((tile, model), lambda i: (i, 0)),
            whole(starts.shape),
            whole(weight.shape),
            whole(small.shape),
        ],
        out_specs=pl.BlockSpec((groups, 3, tile, width), lambda i: (0, 0, i, 0)),
        compiler_params=params(),
        cost_estimate=cost(6 * length * model * model, 10 * length * model),
        name="project_qkv",
    )(x, starts, weight, small)


def lane_mask(h, x):
    lane = lax.broadcasted_iota(jnp.int32, x.shape, 1)
    return jnp.where(lane // HEAD_DIM == h, x, jnp.zeros_like(x))


def sweep(block, first, i, bq, bk):
    diag = (i * bq) // bk
    low = jnp.min(first) // bk
    full = jnp.minimum((jnp.max(first) + bk - 1) // bk, diag)
    pl.loop(low, full)(lambda j: block(j, True))
    pl.loop(jnp.maximum(full, low), diag)(lambda j: block(j, False))
    pl.loop(jnp.maximum(diag, low), diag + max(bq // bk, 1))(lambda j: block(j, True))


def place(base, per):
    return base // per, pl.multiple_of(base % per, 128)


def block_mask(first, i, bq, bk, base):
    pos = i * bq + lax.broadcasted_iota(jnp.int32, (1, bq), 1)
    rows = lax.broadcasted_iota(jnp.int32, (bk, bq), 0)
    return (rows >= first - base) & (rows <= pos - base)


def attend_kernel(bq, bk, heads, qkv_ref, st_ref, o_ref, lse_ref, m_sc, l_sc, acc_sc):
    i = pl.program_id(0)
    per = qkv_ref.shape[2]
    m_sc[...] = jnp.full_like(m_sc, NEG)
    l_sc[...] = jnp.zeros_like(l_sc)
    acc_sc[...] = jnp.zeros_like(acc_sc)
    src, off = place(i * bq, per)
    q = (qkv_ref[src, 0, pl.ds(off, bq), :] * HEAD_DIM ** (-0.5)).astype(BF16)
    qs = [lane_mask(h, q) for h in range(heads)]
    first = st_ref[...]

    def block(j, masked):
        base = j * bk
        ksrc, koff = place(base, per)
        k = qkv_ref[ksrc, 1, pl.ds(koff, bk), :]
        v = qkv_ref[ksrc, 2, pl.ds(koff, bk), :]
        if masked:
            ok = block_mask(first, i, bq, bk, base)
        for h in range(heads):
            sl = slice(h * HEAD_DIM, (h + 1) * HEAD_DIM)
            s = dot(k, qs[h], NT)
            if masked:
                s = jnp.where(ok, s, NEG)
            m_old = m_sc[h : h + 1, :]
            m_new = jnp.maximum(m_old, jnp.max(s, 0, keepdims=True))
            p = jnp.exp(s - m_new)
            alpha = jnp.exp(m_old - m_new)
            l_sc[h : h + 1, :] = l_sc[h : h + 1, :] * alpha + jnp.sum(p, 0, keepdims=True)
            m_sc[h : h + 1, :] = m_new
            acc_sc[sl, :] = acc_sc[sl, :] * alpha + dot(v[:, sl], p.astype(BF16), TN)

    sweep(block, first, i, bq, bk)
    for h in range(heads):
        sl = slice(h * HEAD_DIM, (h + 1) * HEAD_DIM)
        acc_sc[sl, :] = acc_sc[sl, :] * (1.0 / l_sc[h : h + 1, :])
        lse_ref[h : h + 1, :] = m_sc[h : h + 1, :] + jnp.log(l_sc[h : h + 1, :])
    o_ref[0] = acc_sc[...].T.astype(BF16)


def attention_forward(qkv, starts, bq=512, bk=512):
    groups, _, per, width = qkv.shape
    length = groups * per
    split = per // bq
    heads = width // HEAD_DIM
    return pl.pallas_call(
        functools.partial(attend_kernel, bq, bk, heads),
        out_shape=(
            jax.ShapeDtypeStruct((groups, per, width), BF16),
            jax.ShapeDtypeStruct((8, length), F32),
        ),
        grid=(length // bq,),
        in_specs=[whole(qkv.shape), pl.BlockSpec((1, bq), lambda i: (0, i))],
        out_specs=[
            pl.BlockSpec((1, bq, width), lambda i: (i // split, i % split, 0)),
            pl.BlockSpec((8, bq), lambda i: (0, i)),
        ],
        scratch_shapes=[pltpu.VMEM((8, bq), F32)] * 2 + [pltpu.VMEM((width, bq), F32)],
        compiler_params=params(),
        cost_estimate=cost(8 * length * length * width, 8 * length * width, length * length),
        name="attention_forward",
    )(qkv, starts)


def attend_back_kernel(
    bq, bk, heads, qkv_ref, do_ref, o_ref, lse_ref, st_ref, out_ref, dqt_sc, dk_sc, dv_sc
):
    i = pl.program_id(0)
    per = qkv_ref.shape[2]
    scale = HEAD_DIM ** (-0.5)

    @pl.when(i == 0)
    def _():
        dk_sc[...] = jnp.zeros_like(dk_sc)
        dv_sc[...] = jnp.zeros_like(dv_sc)

    dqt_sc[...] = jnp.zeros_like(dqt_sc)
    src, off = place(i * bq, per)
    q = (qkv_ref[src, 0, pl.ds(off, bq), :] * scale).astype(BF16)
    do = do_ref[0]
    qs = [lane_mask(h, q) for h in range(heads)]
    dos = [lane_mask(h, do) for h in range(heads)]
    prod = (do.astype(F32) * o_ref[0].astype(F32)).T
    delta = [
        jnp.sum(prod[h * HEAD_DIM : (h + 1) * HEAD_DIM], 0, keepdims=True) for h in range(heads)
    ]
    lse = [lse_ref[h : h + 1, :] for h in range(heads)]
    first = st_ref[...]

    def block(j, masked):
        base = j * bk
        ksrc, koff = place(base, per)
        krows = pl.ds(pl.multiple_of(base, bk), bk)
        k = qkv_ref[ksrc, 1, pl.ds(koff, bk), :]
        v = qkv_ref[ksrc, 2, pl.ds(koff, bk), :]
        if masked:
            ok = block_mask(first, i, bq, bk, base)
        dv = dk = None
        for h in range(heads):
            sl = slice(h * HEAD_DIM, (h + 1) * HEAD_DIM)
            s = dot(k, qs[h], NT)
            if masked:
                s = jnp.where(ok, s, NEG)
            p = jnp.exp(s - lse[h])
            ds = (p * (dot(v, dos[h], NT) - delta[h])).astype(BF16)
            dvh = dot(p.astype(BF16), dos[h])
            dkh = dot(ds, qs[h])
            dv = dvh if dv is None else dv + dvh
            dk = dkh if dk is None else dk + dkh
            dqt_sc[sl, :] += dot(k[:, sl], ds, TN)
        dv_sc[krows, :] += dv
        dk_sc[krows, :] += dk

    sweep(block, first, i, bq, bk)
    out_ref[src, 0, pl.ds(off, bq), :] = (dqt_sc[...] * scale).T.astype(BF16)

    @pl.when(i == pl.num_programs(0) - 1)
    def _():
        for g in range(qkv_ref.shape[0]):
            out_ref[g, 1] = dk_sc[g * per : (g + 1) * per, :].astype(BF16)
            out_ref[g, 2] = dv_sc[g * per : (g + 1) * per, :].astype(BF16)


def attention_backward(qkv, grad, out, lse, starts, bq=512, bk=512):
    groups, _, per, width = qkv.shape
    length = groups * per
    split = per // bq
    heads = width // HEAD_DIM
    rows = pl.BlockSpec((1, bq, width), lambda i: (i // split, i % split, 0))
    return pl.pallas_call(
        functools.partial(attend_back_kernel, bq, bk, heads),
        out_shape=jax.ShapeDtypeStruct(qkv.shape, BF16),
        grid=(length // bq,),
        in_specs=[
            whole(qkv.shape),
            rows,
            rows,
            pl.BlockSpec((8, bq), lambda i: (0, i)),
            pl.BlockSpec((1, bq), lambda i: (0, i)),
        ],
        out_specs=whole(qkv.shape),
        scratch_shapes=[pltpu.VMEM((width, bq), F32)] + [pltpu.VMEM((length, width), F32)] * 2,
        compiler_params=params(),
        cost_estimate=cost(20 * length * length * width, 16 * length * width, length * length),
        name="attention_backward",
    )(qkv, grad, out, lse, starts)


def put(ref, first, value):
    @pl.when(first)
    def _():
        ref[...] = value

    @pl.when(jnp.logical_not(first))
    def _():
        ref[...] += value


def column_sum(x):
    return jnp.sum(x, 0, keepdims=True)


def middle_kernel(
    groups, x_ref, attn_ref, wa_ref, wp_ref, small_ref, fcb_ref, cot_ref,
    out_ref, resid_ref, ga_ref, gwo_ref, gwf_ref, gwp_ref, gs_ref,
):
    first = pl.program_id(0) == 0
    model = x_ref.shape[-1]
    width = model // groups
    small = small_ref[...]
    w_out = wa_ref[:, 0:model]
    w_fc = wa_ref[:, model:]
    w_proj = wp_ref[...]
    attn = jnp.concatenate([attn_ref[g] for g in range(groups)], 1)
    resid = x_ref[...].astype(F32) + dot(attn, w_out) + small[OUT_BIAS : OUT_BIAS + 1]
    normed, inverse = normalize(resid)
    gain = small[GAIN_TWO : GAIN_TWO + 1]
    act = (normed * gain + small[BIAS_TWO : BIAS_TWO + 1]).astype(BF16)
    hidden = dot(act, w_fc) + fcb_ref[...]
    sig = 1.0 / (1.0 + jnp.exp(-1.702 * hidden))
    gelu = hidden * sig
    slope = sig + 1.702 * gelu * (1.0 - sig)
    gelu = gelu.astype(BF16)
    out_ref[...] = (resid + dot(gelu, w_proj) + small[PROJ_BIAS : PROJ_BIAS + 1]).astype(BF16)
    up = cot_ref[...]
    put(gwp_ref, first, dot(gelu, up, TN))
    grad_hidden = dot(up, w_proj, NT) * slope
    low = grad_hidden.astype(BF16)
    put(gwf_ref, first, dot(act, low, TN))
    grad_act = dot(low, w_fc, NT)
    up = up.astype(F32)
    grad_resid = up + normalize_back(grad_act * gain, normed, inverse)
    resid_ref[...] = grad_resid
    resid_low = grad_resid.astype(BF16)
    put(gwo_ref, first, dot(attn, resid_low, TN))
    grad_attn = dot(resid_low, w_out, NT).astype(BF16)
    for g in range(groups):
        ga_ref[g] = grad_attn[:, g * width : (g + 1) * width]
    put(gs_ref.at[0:1, :], first, column_sum(grad_hidden))
    put(gs_ref.at[1:2, 0:model], first, column_sum(grad_resid))
    put(gs_ref.at[2:3, 0:model], first, column_sum(grad_act * normed))
    put(gs_ref.at[3:4, 0:model], first, column_sum(grad_act))
    put(gs_ref.at[4:5, 0:model], first, column_sum(up))


def middle(x, attn, w_a, w_proj, small, fc_bias, cotangent, tile=256):
    length, model = x.shape
    groups = attn.shape[0]
    hid = w_proj.shape[0]
    rows = pl.BlockSpec((tile, model), lambda i: (i, 0))
    slabs = pl.BlockSpec((groups, tile, model // groups), lambda i: (0, i, 0))
    return pl.pallas_call(
        functools.partial(middle_kernel, groups),
        out_shape=(
            jax.ShapeDtypeStruct((length, model), BF16),
            jax.ShapeDtypeStruct((length, model), F32),
            jax.ShapeDtypeStruct(attn.shape, BF16),
            jax.ShapeDtypeStruct((model, model), F32),
            jax.ShapeDtypeStruct((model, hid), F32),
            jax.ShapeDtypeStruct((hid, model), F32),
            jax.ShapeDtypeStruct((8, hid), F32),
        ),
        grid=(length // tile,),
        in_specs=[rows, slabs, whole(w_a.shape), whole(w_proj.shape), whole(small.shape),
                  whole(fc_bias.shape), rows],
        out_specs=[rows, rows, slabs, whole((model, model)), whole((model, hid)),
                   whole((hid, model)), whole((8, hid))],
        compiler_params=params(),
        cost_estimate=cost(12 * length * model * hid + 6 * length * model * model,
                           16 * model * hid, length * hid),
        name="middle",
    )(x, attn, w_a, w_proj, small, fc_bias, cotangent)


def last_kernel(rows, x_ref, g_ref, resid_ref, w_ref, small_ref, gt_ref, gw_ref, gs_ref):
    first = pl.program_id(0) == 0
    groups = g_ref.shape[0]
    small = small_ref[...]
    normed, inverse = normalize(x_ref[...].astype(F32))
    gain = small[GAIN_ONE : GAIN_ONE + 1]
    act = (normed * gain + small[BIAS_ONE : BIAS_ONE + 1]).astype(BF16)
    grad = jnp.concatenate([g_ref[g, part] for part in range(3) for g in range(groups)], 1)
    model = x_ref.shape[-1]
    put(gw_ref, first, dot(act, grad, TN))
    grad_act = dot(grad, weight_rows(w_ref, rows), NT)
    gt_ref[...] = (
        resid_ref[...] + normalize_back(grad_act * gain, normed, inverse)
    ).astype(BF16)
    put(gs_ref.at[0:1], first, column_sum(grad_act * normed))
    put(gs_ref.at[1:2], first, column_sum(grad_act))
    put(gs_ref.at[2:3], first, column_sum(grad[:, 0:model].astype(F32)))
    put(gs_ref.at[3:4], first, column_sum(grad[:, 2 * model :].astype(F32)))


def last(x, grad, resid, weight, rows, small, tile=256):
    length, model = x.shape
    groups, _, _, width = grad.shape
    block = pl.BlockSpec((tile, model), lambda i: (i, 0))
    return pl.pallas_call(
        functools.partial(last_kernel, rows),
        out_shape=(
            jax.ShapeDtypeStruct((length, model), BF16),
            jax.ShapeDtypeStruct((model, 3 * model), F32),
            jax.ShapeDtypeStruct((8, model), F32),
        ),
        grid=(length // tile,),
        in_specs=[
            block,
            pl.BlockSpec((groups, 3, tile, width), lambda i: (0, 0, i, 0)),
            block,
            whole(weight.shape),
            whole(small.shape),
        ],
        out_specs=[block, whole((model, 3 * model)), whole((8, model))],
        compiler_params=params(),
        cost_estimate=cost(12 * length * model * model, 20 * length * model),
        name="last",
    )(x, grad, resid, weight, small)


def per_device(
    tokens, starts, norm1_gain, norm1_bias, w_qkv, q_bias, v_bias, w_out, out_bias, norm2_gain,
    norm2_bias, w_fc, fc_bias, w_proj, proj_bias, cotangent,
):
    groups = lax.axis_size("sp")
    parts = lax.axis_size("fsdp")
    rows, triple = w_qkv.shape
    piece = norm1_gain.shape[0]
    x = tokens[0]
    gather = functools.partial(lax.all_gather, axis_name="fsdp", axis=0, tiled=True)

    vectors = jnp.concatenate(
        [norm1_gain, norm1_bias, q_bias, v_bias, out_bias, norm2_gain, norm2_bias, proj_bias, fc_bias]
    )
    vectors = jnp.pad(vectors.reshape(1, -1), ((0, PAD - 1), (0, triple - vectors.shape[0])))
    packed = gather(jnp.concatenate([w_qkv, vectors], 0)).reshape(parts, rows + PAD, triple)
    vectors = packed[:, rows, :].astype(F32)
    small = vectors[:, : 8 * piece].reshape(parts, 8, piece).swapaxes(0, 1).reshape(8, parts * piece)
    fcb = vectors[:, 8 * piece : 8 * piece + fc_bias.shape[0]].reshape(1, -1)
    if rows % 16 == 0:
        weight, weight_count = packed, rows
    else:
        weight, weight_count = packed[:, :rows].reshape(1, parts * rows, triple), parts * rows
    doc_first = lax.all_gather(starts, "sp", axis=1, tiled=True)
    w_a = gather(jnp.concatenate([w_out, w_fc], 1))
    w_p = gather(w_proj)

    exchange = functools.partial(
        lax.all_to_all, axis_name="sp", split_axis=0, concat_axis=0, tiled=True
    )
    qkv = exchange(project_qkv(x, starts, weight, weight_count, small, groups))
    out, lse = attention_forward(qkv, doc_first)
    attn = exchange(out)
    block_out, grad_resid, grad_attn, g_out, g_fc, g_proj, g_small = middle(
        x, attn, w_a, w_p, small, fcb, cotangent[0]
    )
    model = x.shape[1]
    g_a = jnp.concatenate([g_out, g_fc], 1)
    g_a = lax.psum(lax.psum_scatter(g_a, "fsdp", scatter_dimension=0, tiled=True), "sp")
    g_p = lax.psum(lax.psum_scatter(g_proj, "fsdp", scatter_dimension=0, tiled=True), "sp")
    grad = exchange(attention_backward(qkv, exchange(grad_attn), out, lse, doc_first))
    grad_tokens, g_qkv, g_last = last(x, grad, grad_resid, weight, weight_count, small)

    bits = jnp.concatenate([g_last[:4], g_small[1:5, :model]], 0)
    bits = bits.reshape(8, parts, piece).swapaxes(0, 1).reshape(parts, 8 * piece)
    bits = jnp.concatenate([bits, g_small[0].reshape(parts, -1)], 1)
    bits = jnp.pad(bits[:, None, :], ((0, 0), (0, 7), (0, triple - bits.shape[1])))
    g_q = jnp.concatenate([g_qkv.reshape(parts, rows, triple), bits], 1).reshape(-1, triple)
    g_q = lax.psum(lax.psum_scatter(g_q, "fsdp", scatter_dimension=0, tiled=True), "sp")
    vec = [g_q[rows, k * piece : (k + 1) * piece] for k in range(8)]
    g_fcb = g_q[rows, 8 * piece : 8 * piece + fc_bias.shape[0]]
    return (
        block_out[None], grad_tokens[None], vec[0], vec[1], g_q[:rows], vec[2], vec[3],
        g_a[:, :model], vec[4], vec[5], vec[6], g_a[:, model:], g_fcb, g_p, vec[7],
    )


def solution(mesh):
    row, mat = P("fsdp"), P("fsdp", None)
    stream = P("fsdp", "sp", None)
    return jax.shard_map(
        per_device,
        mesh=mesh,
        in_specs=(stream, P("fsdp", "sp"), row, row, mat, row, row, mat, row, row, row, mat, row,
                  mat, row, stream),
        out_specs=(stream, stream, row, row, mat, row, row, mat, row, row, row, mat, row, mat, row),
        check_vma=False,
    )
```

```python
import functools

import jax
import jax.numpy as jnp
from jax import lax
from jax.experimental import pallas as pl
from jax.experimental.pallas import tpu as pltpu
from jax.sharding import PartitionSpec as P

HEAD_DIM = 64
EPSILON = 1e-05
NEG = -1e30
F32 = jnp.float32
BF16 = jnp.bfloat16
NN = (((1,), (0,)), ((), ()))
NT = (((1,), (1,)), ((), ()))
TN = (((0,), (0,)), ((), ()))
VMEM_LIMIT = 60 << 20


def dot(left, right, dims=NN):
    return lax.dot_general(left, right, dims, preferred_element_type=F32)


def normalize(values):
    centered = values - jnp.mean(values, -1, keepdims=True)
    inverse = lax.rsqrt(jnp.mean(centered * centered, -1, keepdims=True) + EPSILON)
    return centered * inverse, inverse


def normalize_back(incoming, normed, inverse):
    return inverse * (
        incoming
        - jnp.mean(incoming, -1, keepdims=True)
        - normed * jnp.mean(incoming * normed, -1, keepdims=True)
    )


def whole(shape):
    return pl.BlockSpec(shape, lambda *_: (0,) * len(shape))


def params():
    return pltpu.CompilerParams(vmem_limit_bytes=VMEM_LIMIT)


def cost(flops, size, exps=0):
    return pl.CostEstimate(flops=flops, bytes_accessed=size, transcendentals=exps)


def weight_rows(w_ref, rows):
    parts = w_ref.shape[0]
    return w_ref[:, 0:rows, :].reshape(parts * rows, w_ref.shape[2])


def peer(sp, fsdp):
    return {"sp": sp, "fsdp": fsdp}


def remote(src, dst, send, recv, where):
    return pltpu.make_async_remote_copy(
        src_ref=src, dst_ref=dst, send_sem=send, recv_sem=recv,
        device_id=where, device_id_type=pl.DeviceIdType.MESH,
    )


def others(me, count):
    return [lax.rem(me + k, count) for k in range(1, count)]


def greet(groups, parts):
    p, f = lax.axis_index("sp"), lax.axis_index("fsdp")
    barrier = pltpu.get_barrier_semaphore()
    for q in others(p, groups):
        pl.semaphore_signal(barrier, inc=1, device_id=peer(q, f), device_id_type=pl.DeviceIdType.MESH)
    for g in others(f, parts):
        pl.semaphore_signal(barrier, inc=1, device_id=peer(p, g), device_id_type=pl.DeviceIdType.MESH)


def greeted(groups, parts):
    pl.semaphore_wait(pltpu.get_barrier_semaphore(), groups + parts - 2)


def gather_kernel(groups, parts, *refs):
    w_ref, st_ref = refs[:2]
    vec_refs = refs[2:11]
    (wg_ref, sg_ref, small_ref, fcb_ref, own, vg,
     v_send, v_recv, s_send, s_recv, w_send, w_recv) = refs[11:]
    p, f = lax.axis_index("sp"), lax.axis_index("fsdp")
    core = lax.rem(p, 2)
    mate = p + 1 - 2 * core
    major = parts // 2
    a, b = f // 2, lax.rem(f, 2)
    twin = a * 2 + 1 - b
    half = w_ref.shape[1] // 2
    lanes = pl.ds(pl.multiple_of(core * half, 128), half)
    mate_lanes = pl.ds(pl.multiple_of((1 - core) * half, 128), half)

    greet(groups, parts)
    piece = vec_refs[0].shape[1]
    bits = min(128, vec_refs[8].shape[1])
    runs = vec_refs[8].shape[1] // bits
    own[...] = jnp.zeros_like(own)
    for k in range(8):
        own[k : k + 1, 0:piece] = vec_refs[k][...].astype(F32)
    for k in range(runs):
        own[8 + k : 9 + k, 0:bits] = vec_refs[8][:, k * bits : (k + 1) * bits].astype(F32)
    vg[f] = own[...]
    wg_ref[f] = w_ref[...]
    sg_ref[p] = st_ref[...]
    greeted(groups, parts)

    copies = []

    def go(copy):
        copy.start()
        copies.append(copy)

    def block(g, lane):
        return wg_ref.at[g, :, lane]

    steps = [lax.rem(a + k, major) for k in range(1, major)]
    for k, c in enumerate(steps):
        go(remote(w_ref.at[:, lanes], block(f, lanes), w_send.at[0, k], w_recv.at[0, f], peer(p, c * 2 + b)))
    go(remote(w_ref.at[:, lanes], block(f, lanes), w_send.at[0, major], w_recv.at[0, f], peer(p, twin)))
    for k, q in enumerate(others(p, groups)):
        go(remote(st_ref, sg_ref.at[p], s_send.at[k], s_recv.at[p], peer(q, f)))
    for k, g in enumerate(others(f, parts)):
        go(remote(own, vg.at[f], v_send.at[k], v_recv.at[f], peer(p, g)))

    def arrived(g, lane, row):
        remote(block(g, lane), block(g, lane), w_send.at[0, 0], w_recv.at[row, g], peer(mate, f)).wait_recv()

    back = [lax.rem(a + major - k, major) for k in range(1, major)]
    slot = 0
    for c in back:
        g = c * 2 + b
        arrived(g, lanes, 0)
        go(remote(block(g, lanes), block(g, lanes), w_send.at[1, slot], w_recv.at[0, g], peer(p, twin)))
        go(remote(block(g, lanes), block(g, lanes), w_send.at[2, slot], w_recv.at[1, g], peer(mate, f)))
        slot += 1
    for c in [a] + back:
        g = c * 2 + 1 - b
        arrived(g, lanes, 0)
        go(remote(block(g, lanes), block(g, lanes), w_send.at[2, slot], w_recv.at[1, g], peer(mate, f)))
        slot += 1
    for g in others(f, parts):
        remote(own, vg.at[g], v_send.at[0], v_recv.at[g], peer(p, g)).wait_recv()
    for g in range(parts):
        small_ref[:, g * piece : (g + 1) * piece] = vg[g, 0:8, 0:piece]
        for k in range(runs):
            at = (g * runs + k) * bits
            fcb_ref[:, at : at + bits] = vg[g, 8 + k : 9 + k, 0:bits]
    for q in others(p, groups):
        remote(st_ref, sg_ref.at[q], s_send.at[0], s_recv.at[q], peer(q, f)).wait_recv()
    for g in others(f, parts):
        arrived(g, mate_lanes, 1)
    for copy in copies:
        copy.wait_send()


def gather_front(w_qkv, starts, vectors, groups, parts):
    rows, triple = w_qkv.shape
    starts = starts.reshape(-1, 128)
    vectors = [v.reshape(1, -1) for v in vectors]
    dma = pltpu.SemaphoreType.DMA
    vmem = pl.BlockSpec(memory_space=pltpu.VMEM)
    return pl.pallas_call(
        functools.partial(gather_kernel, groups, parts),
        out_shape=(
            jax.ShapeDtypeStruct((parts, rows, triple), BF16),
            jax.ShapeDtypeStruct((groups,) + starts.shape, jnp.int32),
            jax.ShapeDtypeStruct((8, parts * vectors[0].shape[1]), F32),
            jax.ShapeDtypeStruct((1, parts * vectors[8].shape[1]), F32),
        ),
        in_specs=[vmem] * 11,
        out_specs=[vmem] * 4,
        scratch_shapes=[
            pltpu.VMEM((16, 128), F32), pltpu.VMEM((parts, 16, 128), F32),
            dma((parts,)), dma((parts,)), dma((groups,)), dma((groups,)),
            dma((3, parts)), dma((2, parts)),
        ],
        compiler_params=pltpu.CompilerParams(
            vmem_limit_bytes=VMEM_LIMIT, collective_id=0, has_side_effects=True
        ),
        name="gather_front",
    )(w_qkv, starts, *vectors)


GAIN_ONE, BIAS_ONE, Q_BIAS, V_BIAS, OUT_BIAS, GAIN_TWO, BIAS_TWO, PROJ_BIAS = range(8)


def qkv_kernel(rows, groups, x_ref, w_ref, small_ref, o_ref):
    width = x_ref.shape[-1] // groups
    model = x_ref.shape[-1]
    normed, _ = normalize(x_ref[...].astype(F32))
    small = small_ref[...]
    act = (normed * small[GAIN_ONE : GAIN_ONE + 1] + small[BIAS_ONE : BIAS_ONE + 1]).astype(BF16)
    weight = weight_rows(w_ref, rows)
    for part, row in ((0, Q_BIAS), (1, None), (2, V_BIAS)):
        out = dot(act, weight[:, part * model : (part + 1) * model])
        if row is not None:
            out = out + small[row : row + 1]
        out = out.astype(BF16)
        for g in range(groups):
            o_ref[g, part] = out[:, g * width : (g + 1) * width]


def project_qkv(x, weight, rows, small, groups, tile=256):
    length, model = x.shape
    width = model // groups
    return pl.pallas_call(
        functools.partial(qkv_kernel, rows, groups),
        out_shape=jax.ShapeDtypeStruct((groups, 3, length, width), BF16),
        grid=(length // tile,),
        in_specs=[
            pl.BlockSpec((tile, model), lambda i: (i, 0)),
            whole(weight.shape),
            whole(small.shape),
        ],
        out_specs=pl.BlockSpec((groups, 3, tile, width), lambda i: (0, 0, i, 0)),
        compiler_params=params(),
        cost_estimate=cost(6 * length * model * model, 10 * length * model),
        name="project_qkv",
    )(x, weight, small)


def lane_mask(h, x):
    lane = lax.broadcasted_iota(jnp.int32, x.shape, 1)
    return jnp.where(lane // HEAD_DIM == h, x, jnp.zeros_like(x))


def sweep(block, first, i, bq, bk):
    diag = (i * bq) // bk
    low = jnp.min(first) // bk
    full = jnp.minimum((jnp.max(first) + bk - 1) // bk, diag)
    pl.loop(low, full)(lambda j: block(j, True))
    pl.loop(jnp.maximum(full, low), diag)(lambda j: block(j, False))
    pl.loop(jnp.maximum(diag, low), diag + max(bq // bk, 1))(lambda j: block(j, True))


def place(base, per):
    return base // per, pl.multiple_of(base % per, 128)


def block_mask(first, i, bq, bk, base):
    pos = i * bq + lax.broadcasted_iota(jnp.int32, (1, bq), 1)
    rows = lax.broadcasted_iota(jnp.int32, (bk, bq), 0)
    return (rows >= first - base) & (rows <= pos - base)


def attend_kernel(bq, bk, heads, qkv_ref, st_ref, o_ref, lse_ref, m_sc, l_sc, acc_sc):
    i = pl.program_id(0)
    per = qkv_ref.shape[2]
    m_sc[...] = jnp.full_like(m_sc, NEG)
    l_sc[...] = jnp.zeros_like(l_sc)
    acc_sc[...] = jnp.zeros_like(acc_sc)
    src, off = place(i * bq, per)
    q = (qkv_ref[src, 0, pl.ds(off, bq), :] * HEAD_DIM ** (-0.5)).astype(BF16)
    qs = [lane_mask(h, q) for h in range(heads)]
    first = st_ref[...]

    def block(j, masked):
        base = j * bk
        ksrc, koff = place(base, per)
        k = qkv_ref[ksrc, 1, pl.ds(koff, bk), :]
        v = qkv_ref[ksrc, 2, pl.ds(koff, bk), :]
        if masked:
            ok = block_mask(first, i, bq, bk, base)
        for h in range(heads):
            sl = slice(h * HEAD_DIM, (h + 1) * HEAD_DIM)
            s = dot(k, qs[h], NT)
            if masked:
                s = jnp.where(ok, s, NEG)
            m_old = m_sc[h : h + 1, :]
            m_new = jnp.maximum(m_old, jnp.max(s, 0, keepdims=True))
            p = jnp.exp(s - m_new)
            alpha = jnp.exp(m_old - m_new)
            l_sc[h : h + 1, :] = l_sc[h : h + 1, :] * alpha + jnp.sum(p, 0, keepdims=True)
            m_sc[h : h + 1, :] = m_new
            acc_sc[sl, :] = acc_sc[sl, :] * alpha + dot(v[:, sl], p.astype(BF16), TN)

    sweep(block, first, i, bq, bk)
    for h in range(heads):
        sl = slice(h * HEAD_DIM, (h + 1) * HEAD_DIM)
        acc_sc[sl, :] = acc_sc[sl, :] * (1.0 / l_sc[h : h + 1, :])
        lse_ref[h : h + 1, :] = m_sc[h : h + 1, :] + jnp.log(l_sc[h : h + 1, :])
    o_ref[0] = acc_sc[...].T.astype(BF16)


def attention_forward(qkv, starts, bq=512, bk=512):
    groups, _, per, width = qkv.shape
    length = groups * per
    split = per // bq
    heads = width // HEAD_DIM
    return pl.pallas_call(
        functools.partial(attend_kernel, bq, bk, heads),
        out_shape=(
            jax.ShapeDtypeStruct((groups, per, width), BF16),
            jax.ShapeDtypeStruct((8, length), F32),
        ),
        grid=(length // bq,),
        in_specs=[whole(qkv.shape), pl.BlockSpec((1, bq), lambda i: (0, i))],
        out_specs=[
            pl.BlockSpec((1, bq, width), lambda i: (i // split, i % split, 0)),
            pl.BlockSpec((8, bq), lambda i: (0, i)),
        ],
        scratch_shapes=[pltpu.VMEM((8, bq), F32)] * 2 + [pltpu.VMEM((width, bq), F32)],
        compiler_params=params(),
        cost_estimate=cost(8 * length * length * width, 8 * length * width, length * length),
        name="attention_forward",
    )(qkv, starts)


def attend_back_kernel(
    bq, bk, heads, qkv_ref, do_ref, o_ref, lse_ref, st_ref, out_ref, dqt_sc, dk_sc, dv_sc
):
    i = pl.program_id(0)
    per = qkv_ref.shape[2]
    scale = HEAD_DIM ** (-0.5)

    @pl.when(i == 0)
    def _():
        dk_sc[...] = jnp.zeros_like(dk_sc)
        dv_sc[...] = jnp.zeros_like(dv_sc)

    dqt_sc[...] = jnp.zeros_like(dqt_sc)
    src, off = place(i * bq, per)
    q = (qkv_ref[src, 0, pl.ds(off, bq), :] * scale).astype(BF16)
    do = do_ref[0]
    qs = [lane_mask(h, q) for h in range(heads)]
    dos = [lane_mask(h, do) for h in range(heads)]
    prod = (do.astype(F32) * o_ref[0].astype(F32)).T
    delta = [
        jnp.sum(prod[h * HEAD_DIM : (h + 1) * HEAD_DIM], 0, keepdims=True) for h in range(heads)
    ]
    lse = [lse_ref[h : h + 1, :] for h in range(heads)]
    first = st_ref[...]

    def block(j, masked):
        base = j * bk
        ksrc, koff = place(base, per)
        krows = pl.ds(pl.multiple_of(base, bk), bk)
        k = qkv_ref[ksrc, 1, pl.ds(koff, bk), :]
        v = qkv_ref[ksrc, 2, pl.ds(koff, bk), :]
        if masked:
            ok = block_mask(first, i, bq, bk, base)
        dv = dk = None
        for h in range(heads):
            sl = slice(h * HEAD_DIM, (h + 1) * HEAD_DIM)
            s = dot(k, qs[h], NT)
            if masked:
                s = jnp.where(ok, s, NEG)
            p = jnp.exp(s - lse[h])
            ds = (p * (dot(v, dos[h], NT) - delta[h])).astype(BF16)
            dvh = dot(p.astype(BF16), dos[h])
            dkh = dot(ds, qs[h])
            dv = dvh if dv is None else dv + dvh
            dk = dkh if dk is None else dk + dkh
            dqt_sc[sl, :] += dot(k[:, sl], ds, TN)
        dv_sc[krows, :] += dv
        dk_sc[krows, :] += dk

    sweep(block, first, i, bq, bk)
    out_ref[src, 0, pl.ds(off, bq), :] = (dqt_sc[...] * scale).T.astype(BF16)

    @pl.when(i == pl.num_programs(0) - 1)
    def _():
        for g in range(qkv_ref.shape[0]):
            out_ref[g, 1] = dk_sc[g * per : (g + 1) * per, :].astype(BF16)
            out_ref[g, 2] = dv_sc[g * per : (g + 1) * per, :].astype(BF16)


def attention_backward(qkv, grad, out, lse, starts, bq=512, bk=512):
    groups, _, per, width = qkv.shape
    length = groups * per
    split = per // bq
    heads = width // HEAD_DIM
    rows = pl.BlockSpec((1, bq, width), lambda i: (i // split, i % split, 0))
    return pl.pallas_call(
        functools.partial(attend_back_kernel, bq, bk, heads),
        out_shape=jax.ShapeDtypeStruct(qkv.shape, BF16),
        grid=(length // bq,),
        in_specs=[
            whole(qkv.shape),
            rows,
            rows,
            pl.BlockSpec((8, bq), lambda i: (0, i)),
            pl.BlockSpec((1, bq), lambda i: (0, i)),
        ],
        out_specs=whole(qkv.shape),
        scratch_shapes=[pltpu.VMEM((width, bq), F32)] + [pltpu.VMEM((length, width), F32)] * 2,
        compiler_params=params(),
        cost_estimate=cost(20 * length * length * width, 16 * length * width, length * length),
        name="attention_backward",
    )(qkv, grad, out, lse, starts)


def put(ref, first, value):
    @pl.when(first)
    def _():
        ref[...] = value

    @pl.when(jnp.logical_not(first))
    def _():
        ref[...] += value


def column_sum(x):
    return jnp.sum(x, 0, keepdims=True)


def middle_kernel(
    groups, x_ref, attn_ref, wa_ref, wp_ref, small_ref, fcb_ref, cot_ref,
    out_ref, resid_ref, ga_ref, gwa_ref, gwp_ref, gs_ref, gwa_sc, gwp_sc,
):
    first = pl.program_id(0) == 0
    model = x_ref.shape[-1]
    width = model // groups
    small = small_ref[...]
    w_out = wa_ref[:, 0:model]
    w_fc = wa_ref[:, model:]
    w_proj = wp_ref[...]
    attn = jnp.concatenate([attn_ref[g] for g in range(groups)], 1)
    resid = x_ref[...].astype(F32) + dot(attn, w_out) + small[OUT_BIAS : OUT_BIAS + 1]
    normed, inverse = normalize(resid)
    gain = small[GAIN_TWO : GAIN_TWO + 1]
    act = (normed * gain + small[BIAS_TWO : BIAS_TWO + 1]).astype(BF16)
    hidden = dot(act, w_fc) + fcb_ref[...]
    sig = 1.0 / (1.0 + jnp.exp(-1.702 * hidden))
    gelu = hidden * sig
    slope = sig + 1.702 * gelu * (1.0 - sig)
    gelu = gelu.astype(BF16)
    out_ref[...] = (resid + dot(gelu, w_proj) + small[PROJ_BIAS : PROJ_BIAS + 1]).astype(BF16)
    up = cot_ref[...]
    put(gwp_sc, first, dot(gelu, up, TN))
    grad_hidden = dot(up, w_proj, NT) * slope
    low = grad_hidden.astype(BF16)
    put(gwa_sc.at[:, model:], first, dot(act, low, TN))
    grad_act = dot(low, w_fc, NT)
    up = up.astype(F32)
    grad_resid = up + normalize_back(grad_act * gain, normed, inverse)
    resid_ref[...] = grad_resid
    resid_low = grad_resid.astype(BF16)
    put(gwa_sc.at[:, 0:model], first, dot(attn, resid_low, TN))
    grad_attn = dot(resid_low, w_out, NT).astype(BF16)
    for g in range(groups):
        ga_ref[g] = grad_attn[:, g * width : (g + 1) * width]
    put(gs_ref.at[0:1, :], first, column_sum(grad_hidden))
    put(gs_ref.at[1:2, 0:model], first, column_sum(grad_resid))
    put(gs_ref.at[2:3, 0:model], first, column_sum(grad_act * normed))
    put(gs_ref.at[3:4, 0:model], first, column_sum(grad_act))
    put(gs_ref.at[4:5, 0:model], first, column_sum(up))

    @pl.when(pl.program_id(0) == pl.num_programs(0) - 1)
    def _():
        gwa_ref[...] = gwa_sc[...].astype(BF16)
        gwp_ref[...] = gwp_sc[...].astype(BF16)


def middle(x, attn, w_a, w_proj, small, fc_bias, cotangent, tile=256):
    length, model = x.shape
    groups = attn.shape[0]
    hid = w_proj.shape[0]
    rows = pl.BlockSpec((tile, model), lambda i: (i, 0))
    slabs = pl.BlockSpec((groups, tile, model // groups), lambda i: (0, i, 0))
    return pl.pallas_call(
        functools.partial(middle_kernel, groups),
        out_shape=(
            jax.ShapeDtypeStruct((length, model), BF16),
            jax.ShapeDtypeStruct((length, model), F32),
            jax.ShapeDtypeStruct(attn.shape, BF16),
            jax.ShapeDtypeStruct((model, model + hid), BF16),
            jax.ShapeDtypeStruct((hid, model), BF16),
            jax.ShapeDtypeStruct((8, hid), F32),
        ),
        grid=(length // tile,),
        in_specs=[rows, slabs, whole(w_a.shape), whole(w_proj.shape), whole(small.shape),
                  whole(fc_bias.shape), rows],
        out_specs=[rows, rows, slabs, whole((model, model + hid)),
                   whole((hid, model)), whole((8, hid))],
        scratch_shapes=[pltpu.VMEM((model, model + hid), F32), pltpu.VMEM((hid, model), F32)],
        compiler_params=params(),
        cost_estimate=cost(12 * length * model * hid + 6 * length * model * model,
                           16 * model * hid, length * hid),
        name="middle",
    )(x, attn, w_a, w_proj, small, fc_bias, cotangent)


def last_kernel(
    rows, parts, chunk, x_ref, g_ref, resid_ref, w_ref, small_ref, gs_in,
    gt_ref, gw_ref, gv_ref,
    acc, out, vec, mine, vsend, vpart, low, r1, s2, r2, keep, s3, r3,
    v1s, v1r, v2s, v2r, c1s, c1r, c2s, c2r, c3s, c3r, c4s, c4r,
):
    step = pl.program_id(0)
    first = step == 0
    groups = g_ref.shape[0]
    model = x_ref.shape[-1]
    p, f = lax.axis_index("sp"), lax.axis_index("fsdp")

    @pl.when(first)
    def _():
        greet(groups, parts)

    small = small_ref[...]
    normed, inverse = normalize(x_ref[...].astype(F32))
    gain = small[GAIN_ONE : GAIN_ONE + 1]
    act = (normed * gain + small[BIAS_ONE : BIAS_ONE + 1]).astype(BF16)
    grad = jnp.concatenate([g_ref[g, part] for part in range(3) for g in range(groups)], 1)
    put(acc, first, dot(act, grad, TN))
    grad_act = dot(grad, weight_rows(w_ref, rows), NT)
    gt_ref[...] = (
        resid_ref[...] + normalize_back(grad_act * gain, normed, inverse)
    ).astype(BF16)
    put(vec.at[0:1], first, column_sum(grad_act * normed))
    put(vec.at[1:2], first, column_sum(grad_act))
    put(vec.at[2:3], first, column_sum(grad[:, 0:model].astype(F32)))
    put(vec.at[3:4], first, column_sum(grad[:, 2 * model :].astype(F32)))

    @pl.when(step == pl.num_programs(0) - 1)
    def _():
        shard = acc.shape[0] // parts
        core = lax.rem(p, 2)
        side = p // 2
        mate = p + 1 - 2 * core
        across = p + groups // 2 - side * groups
        half = acc.shape[1] // 2
        quarter = half // 2
        count = quarter // chunk

        def lane(c, s, k):
            return pl.ds(pl.multiple_of(c * half + s * quarter + k * chunk, 128), chunk)

        copies = []

        def go(copy):
            copy.start()
            copies.append(copy)

        low[...] = acc[...].astype(BF16)
        vec[4:8, :] = gs_in[1:5, 0:model]
        piece = model // parts
        fc = gs_in.shape[1] // parts
        bits = min(128, fc)
        vsend[...] = jnp.zeros_like(vsend)
        for g in range(parts):
            vsend[g, 0:8, 0:piece] = vec[:, g * piece : (g + 1) * piece]
            for k in range(fc // bits):
                at = g * fc + k * bits
                vsend[g, 8 + k : 9 + k, 0:bits] = gs_in[0:1, at : at + bits]
        greeted(groups, parts)

        for k in range(count):
            for s in range(2):
                go(remote(low.at[:, lane(1 - core, s, k)], r1.at[k, s], c1s.at[k, s], c1r.at[k, s],
                          peer(mate, f)))
        for n, g in enumerate(others(f, parts)):
            go(remote(vsend.at[g], vpart.at[f], v1s.at[n], v1r.at[f], peer(p, g)))
        for k in range(count):
            for s in range(2):
                remote(r1.at[k, s], r1.at[k, s], c1s.at[k, s], c1r.at[k, s], peer(mate, f)).wait_recv()
            s2[k] = (acc[:, lane(core, 1 - side, k)] + r1[k, 1 - side].astype(F32)).astype(BF16)
            go(remote(s2.at[k], r2.at[k], c2s.at[k], c2r.at[k], peer(across, f)))
        for k in range(count):
            remote(s2.at[k], r2.at[k], c2s.at[k], c2r.at[k], peer(across, f)).wait_recv()
            total = acc[:, lane(core, side, k)] + r1[k, side].astype(F32) + r2[k].astype(F32)
            keep[k] = total
            s3[k] = total.astype(BF16)
            for n, g in enumerate(others(f, parts)):
                rows_of = pl.ds(pl.multiple_of(g * shard, shard), shard)
                go(remote(s3.at[k, rows_of], r3.at[k, f], c3s.at[k, n], c3r.at[k, f], peer(p, g)))
        for g in others(f, parts):
            remote(vsend.at[g], vpart.at[g], v1s.at[0], v1r.at[g], peer(p, g)).wait_recv()
        total = vsend[f]
        for g in others(f, parts):
            total = total + vpart[g]
        mine[p] = total
        for n, q in enumerate(others(p, groups)):
            go(remote(mine.at[p], mine.at[p], v2s.at[n], v2r.at[p], peer(q, f)))
        for k in range(count):
            for g in others(f, parts):
                remote(r3.at[k, g], r3.at[k, g], c3s.at[k, 0], c3r.at[k, g], peer(p, g)).wait_recv()
            total = keep[k, pl.ds(pl.multiple_of(f * shard, shard), shard)]
            for g in others(f, parts):
                total = total + r3[k, g].astype(F32)
            out[:, lane(core, side, k)] = total
            for n, q in enumerate(others(p, groups)):
                there = out.at[:, lane(core, side, k)]
                go(remote(there, there, c4s.at[k, n], c4r.at[k, p], peer(q, f)))
        for q in others(p, groups):
            remote(mine.at[q], mine.at[q], v2s.at[0], v2r.at[q], peer(q, f)).wait_recv()
        total = mine[0]
        for q in range(1, groups):
            total = total + mine[q]
        gv_ref[...] = total
        for k in range(count):
            for q in others(p, groups):
                there = out.at[:, lane(lax.rem(q, 2), q // 2, k)]
                remote(there, there, c4s.at[k, 0], c4r.at[k, q], peer(q, f)).wait_recv()
        gw_ref[...] = out[...]
        for copy in copies:
            copy.wait_send()


def last(x, grad, resid, weight, rows, small, sums, parts, tile=256, chunk=128):
    length, model = x.shape
    groups, _, _, width = grad.shape
    block = pl.BlockSpec((tile, model), lambda i: (i, 0))
    triple = 3 * model
    shard = model // parts
    count = triple // 4 // chunk
    dma = pltpu.SemaphoreType.DMA
    vmem = pltpu.VMEM
    return pl.pallas_call(
        functools.partial(last_kernel, rows, parts, chunk),
        out_shape=(
            jax.ShapeDtypeStruct((length, model), BF16),
            jax.ShapeDtypeStruct((shard, triple), F32),
            jax.ShapeDtypeStruct((16, 128), F32),
        ),
        grid=(length // tile,),
        in_specs=[
            block,
            pl.BlockSpec((groups, 3, tile, width), lambda i: (0, 0, i, 0)),
            block,
            whole(weight.shape),
            whole(small.shape),
            whole(sums.shape),
        ],
        out_specs=[block, whole((shard, triple)), whole((16, 128))],
        scratch_shapes=[
            vmem((model, triple), F32), vmem((shard, triple), F32), vmem((8, model), F32),
            vmem((groups, 16, 128), F32),
            vmem((parts, 16, 128), F32), vmem((parts, 16, 128), F32),
            vmem((model, triple), BF16), vmem((count, 2, model, chunk), BF16),
            vmem((count, model, chunk), BF16), vmem((count, model, chunk), BF16),
            vmem((count, model, chunk), F32), vmem((count, model, chunk), BF16),
            vmem((count, parts, shard, chunk), BF16),
            dma((parts,)), dma((parts,)), dma((groups,)), dma((groups,)),
            dma((count, 2)), dma((count, 2)), dma((count,)), dma((count,)),
            dma((count, parts)), dma((count, parts)), dma((count, groups)), dma((count, groups)),
        ],
        compiler_params=pltpu.CompilerParams(
            vmem_limit_bytes=VMEM_LIMIT, collective_id=1, has_side_effects=True
        ),
        cost_estimate=cost(12 * length * model * model, 20 * length * model),
        name="last",
    )(x, grad, resid, weight, small, sums)


def per_device(
    tokens, starts, norm1_gain, norm1_bias, w_qkv, q_bias, v_bias, w_out, out_bias, norm2_gain,
    norm2_bias, w_fc, fc_bias, w_proj, proj_bias, cotangent,
):
    groups = lax.axis_size("sp")
    parts = lax.axis_size("fsdp")
    rows, triple = w_qkv.shape
    piece = norm1_gain.shape[0]
    x = tokens[0]
    gather = functools.partial(lax.all_gather, axis_name="fsdp", axis=0, tiled=True)
    vectors = [
        norm1_gain, norm1_bias, q_bias, v_bias, out_bias, norm2_gain, norm2_bias, proj_bias, fc_bias
    ]
    packed, doc_first, small, fcb = gather_front(w_qkv, starts, vectors, groups, parts)
    doc_first = doc_first.reshape(1, -1)
    if rows % 16 == 0:
        weight, weight_count = packed, rows
    else:
        weight, weight_count = packed.reshape(1, parts * rows, triple), parts * rows
    w_a = gather(jnp.concatenate([w_out, w_fc], 1))
    w_p = gather(w_proj)

    exchange = functools.partial(
        lax.all_to_all, axis_name="sp", split_axis=0, concat_axis=0, tiled=True
    )
    qkv = exchange(project_qkv(x, weight, weight_count, small, groups))
    out, lse = attention_forward(qkv, doc_first)
    attn = exchange(out)
    block_out, grad_resid, grad_attn, g_a, g_p, sums = middle(
        x, attn, w_a, w_p, small, fcb, cotangent[0]
    )
    model = x.shape[1]
    g_a = lax.psum_scatter(g_a, "fsdp", scatter_dimension=0, tiled=True)
    g_p = lax.psum_scatter(g_p, "fsdp", scatter_dimension=0, tiled=True)
    g_a, g_p = lax.psum((g_a.astype(F32), g_p.astype(F32)), "sp")
    grad = exchange(attention_backward(qkv, exchange(grad_attn), out, lse, doc_first))
    grad_tokens, g_q, g_v = last(x, grad, grad_resid, weight, weight_count, small, sums, parts)
    vec = [g_v[k, :piece] for k in range(8)]
    fc = fc_bias.shape[0]
    g_fcb = g_v[8 : 8 + max(fc // 128, 1), : min(fc, 128)].reshape(fc)
    return (
        block_out[None], grad_tokens[None], vec[0], vec[1], g_q, vec[2], vec[3],
        g_a[:, :model], vec[4], vec[5], vec[6], g_a[:, model:], g_fcb, g_p, vec[7],
    )


def solution(mesh):
    row, mat = P("fsdp"), P("fsdp", None)
    stream = P("fsdp", "sp", None)
    return jax.shard_map(
        per_device,
        mesh=mesh,
        in_specs=(stream, P("fsdp", "sp"), row, row, mat, row, row, mat, row, row, row, mat, row,
                  mat, row, stream),
        out_specs=(stream, stream, row, row, mat, row, row, mat, row, row, row, mat, row, mat, row),
        check_vma=False,
    )
```

```python
import functools

import jax
import jax.numpy as jnp
from jax import lax
from jax.experimental import pallas as pl
from jax.experimental.pallas import tpu as pltpu
from jax.sharding import PartitionSpec as P

HEAD_DIM = 64
EPSILON = 1e-05
NEG = -1e30
F32 = jnp.float32
BF16 = jnp.bfloat16
NN = (((1,), (0,)), ((), ()))
NT = (((1,), (1,)), ((), ()))
TN = (((0,), (0,)), ((), ()))
VMEM_LIMIT = 60 << 20


def dot(left, right, dims=NN):
    return lax.dot_general(left, right, dims, preferred_element_type=F32)


def normalize(values):
    centered = values - jnp.mean(values, -1, keepdims=True)
    inverse = lax.rsqrt(jnp.mean(centered * centered, -1, keepdims=True) + EPSILON)
    return centered * inverse, inverse


def normalize_back(incoming, normed, inverse):
    return inverse * (
        incoming
        - jnp.mean(incoming, -1, keepdims=True)
        - normed * jnp.mean(incoming * normed, -1, keepdims=True)
    )


def whole(shape):
    return pl.BlockSpec(shape, lambda *_: (0,) * len(shape))


def params():
    return pltpu.CompilerParams(vmem_limit_bytes=VMEM_LIMIT)


def cost(flops, size, exps=0):
    return pl.CostEstimate(flops=flops, bytes_accessed=size, transcendentals=exps)


def weight_rows(w_ref, rows):
    parts = w_ref.shape[0]
    return w_ref[:, 0:rows, :].reshape(parts * rows, w_ref.shape[2])


def peer(sp, fsdp):
    return {"sp": sp, "fsdp": fsdp}


def remote(src, dst, send, recv, where):
    return pltpu.make_async_remote_copy(
        src_ref=src, dst_ref=dst, send_sem=send, recv_sem=recv,
        device_id=where, device_id_type=pl.DeviceIdType.MESH,
    )


def others(me, count):
    return [lax.rem(me + k, count) for k in range(1, count)]


def greet(groups, parts):
    p, f = lax.axis_index("sp"), lax.axis_index("fsdp")
    barrier = pltpu.get_barrier_semaphore()
    for q in others(p, groups):
        pl.semaphore_signal(barrier, inc=1, device_id=peer(q, f), device_id_type=pl.DeviceIdType.MESH)
    for g in others(f, parts):
        pl.semaphore_signal(barrier, inc=1, device_id=peer(p, g), device_id_type=pl.DeviceIdType.MESH)


def greeted(groups, parts):
    pl.semaphore_wait(pltpu.get_barrier_semaphore(), groups + parts - 2)


def gather_kernel(groups, parts, *refs):
    w_ref, st_ref = refs[:2]
    vec_refs = refs[2:11]
    (wg_ref, sg_ref, small_ref, fcb_ref, own, vg,
     v_send, v_recv, s_send, s_recv, w_send, w_recv) = refs[11:]
    p, f = lax.axis_index("sp"), lax.axis_index("fsdp")
    core = lax.rem(p, 2)
    mate = p + 1 - 2 * core
    major = parts // 2
    a, b = f // 2, lax.rem(f, 2)
    twin = a * 2 + 1 - b
    half = w_ref.shape[1] // 2
    lanes = pl.ds(pl.multiple_of(core * half, 128), half)
    mate_lanes = pl.ds(pl.multiple_of((1 - core) * half, 128), half)

    greet(groups, parts)
    piece = vec_refs[0].shape[1]
    bits = min(128, vec_refs[8].shape[1])
    runs = vec_refs[8].shape[1] // bits
    own[...] = jnp.zeros_like(own)
    for k in range(8):
        own[k : k + 1, 0:piece] = vec_refs[k][...].astype(F32)
    for k in range(runs):
        own[8 + k : 9 + k, 0:bits] = vec_refs[8][:, k * bits : (k + 1) * bits].astype(F32)
    vg[f] = own[...]
    wg_ref[f] = w_ref[...]
    sg_ref[p] = st_ref[...]
    greeted(groups, parts)

    copies = []

    def go(copy):
        copy.start()
        copies.append(copy)

    def block(g, lane):
        return wg_ref.at[g, :, lane]

    steps = [lax.rem(a + k, major) for k in range(1, major)]
    for k, c in enumerate(steps):
        go(remote(w_ref.at[:, lanes], block(f, lanes), w_send.at[0, k], w_recv.at[0, f], peer(p, c * 2 + b)))
    go(remote(w_ref.at[:, lanes], block(f, lanes), w_send.at[0, major], w_recv.at[0, f], peer(p, twin)))
    for k, q in enumerate(others(p, groups)):
        go(remote(st_ref, sg_ref.at[p], s_send.at[k], s_recv.at[p], peer(q, f)))
    for k, g in enumerate(others(f, parts)):
        go(remote(own, vg.at[f], v_send.at[k], v_recv.at[f], peer(p, g)))

    def arrived(g, lane, row):
        remote(block(g, lane), block(g, lane), w_send.at[0, 0], w_recv.at[row, g], peer(mate, f)).wait_recv()

    back = [lax.rem(a + major - k, major) for k in range(1, major)]
    slot = 0
    for c in back:
        g = c * 2 + b
        arrived(g, lanes, 0)
        go(remote(block(g, lanes), block(g, lanes), w_send.at[1, slot], w_recv.at[0, g], peer(p, twin)))
        go(remote(block(g, lanes), block(g, lanes), w_send.at[2, slot], w_recv.at[1, g], peer(mate, f)))
        slot += 1
    for c in [a] + back:
        g = c * 2 + 1 - b
        arrived(g, lanes, 0)
        go(remote(block(g, lanes), block(g, lanes), w_send.at[2, slot], w_recv.at[1, g], peer(mate, f)))
        slot += 1
    for g in others(f, parts):
        remote(own, vg.at[g], v_send.at[0], v_recv.at[g], peer(p, g)).wait_recv()
    for g in range(parts):
        small_ref[:, g * piece : (g + 1) * piece] = vg[g, 0:8, 0:piece]
        for k in range(runs):
            at = (g * runs + k) * bits
            fcb_ref[:, at : at + bits] = vg[g, 8 + k : 9 + k, 0:bits]
    for q in others(p, groups):
        remote(st_ref, sg_ref.at[q], s_send.at[0], s_recv.at[q], peer(q, f)).wait_recv()
    for g in others(f, parts):
        arrived(g, mate_lanes, 1)
    for copy in copies:
        copy.wait_send()


def gather_front(w_qkv, starts, vectors, groups, parts):
    rows, triple = w_qkv.shape
    starts = starts.reshape(-1, 128)
    vectors = [v.reshape(1, -1) for v in vectors]
    dma = pltpu.SemaphoreType.DMA
    vmem = pl.BlockSpec(memory_space=pltpu.VMEM)
    return pl.pallas_call(
        functools.partial(gather_kernel, groups, parts),
        out_shape=(
            jax.ShapeDtypeStruct((parts, rows, triple), BF16),
            jax.ShapeDtypeStruct((groups,) + starts.shape, jnp.int32),
            jax.ShapeDtypeStruct((8, parts * vectors[0].shape[1]), F32),
            jax.ShapeDtypeStruct((1, parts * vectors[8].shape[1]), F32),
        ),
        in_specs=[vmem] * 11,
        out_specs=[vmem] * 4,
        scratch_shapes=[
            pltpu.VMEM((16, 128), F32), pltpu.VMEM((parts, 16, 128), F32),
            dma((parts,)), dma((parts,)), dma((groups,)), dma((groups,)),
            dma((3, parts)), dma((2, parts)),
        ],
        compiler_params=pltpu.CompilerParams(
            vmem_limit_bytes=VMEM_LIMIT, collective_id=0, has_side_effects=True
        ),
        name="gather_front",
    )(w_qkv, starts, *vectors)


GAIN_ONE, BIAS_ONE, Q_BIAS, V_BIAS, OUT_BIAS, GAIN_TWO, BIAS_TWO, PROJ_BIAS = range(8)


def qkv_kernel(rows, groups, x_ref, w_ref, small_ref, o_ref):
    width = x_ref.shape[-1] // groups
    model = x_ref.shape[-1]
    normed, _ = normalize(x_ref[...].astype(F32))
    small = small_ref[...]
    act = (normed * small[GAIN_ONE : GAIN_ONE + 1] + small[BIAS_ONE : BIAS_ONE + 1]).astype(BF16)
    weight = weight_rows(w_ref, rows)
    for part, row in ((0, Q_BIAS), (1, None), (2, V_BIAS)):
        out = dot(act, weight[:, part * model : (part + 1) * model])
        if row is not None:
            out = out + small[row : row + 1]
        out = out.astype(BF16)
        for g in range(groups):
            o_ref[g, part] = out[:, g * width : (g + 1) * width]


def project_qkv(x, weight, rows, small, groups, tile=256):
    length, model = x.shape
    width = model // groups
    return pl.pallas_call(
        functools.partial(qkv_kernel, rows, groups),
        out_shape=jax.ShapeDtypeStruct((groups, 3, length, width), BF16),
        grid=(length // tile,),
        in_specs=[
            pl.BlockSpec((tile, model), lambda i: (i, 0)),
            whole(weight.shape),
            whole(small.shape),
        ],
        out_specs=pl.BlockSpec((groups, 3, tile, width), lambda i: (0, 0, i, 0)),
        compiler_params=params(),
        cost_estimate=cost(6 * length * model * model, 10 * length * model),
        name="project_qkv",
    )(x, weight, small)


def lane_mask(h, x):
    lane = lax.broadcasted_iota(jnp.int32, x.shape, 1)
    return jnp.where(lane // HEAD_DIM == h, x, jnp.zeros_like(x))


def triangle(index, size):
    row = sum((index >= m * (m + 1) // 2).astype(jnp.int32) for m in range(1, size))
    return row, index - row * (row + 1) // 2


def triangle_by_column(index, size):
    starts = [c * (2 * size + 1 - c) // 2 for c in range(size)]
    col = sum((index >= at).astype(jnp.int32) for at in starts[1:])
    return col + index - col * (2 * size + 1 - col) // 2, col


def pick(cond, this, other):
    return jnp.where(cond, this, other)


class Place:
    def __init__(self, groups, count):
        self.p, self.f = lax.axis_index("sp"), lax.axis_index("fsdp")
        self.side = self.p // 2
        self.core = lax.rem(self.p, 2)
        self.mate = self.p + 1 - 2 * self.core
        far = (1 - self.side) * 2
        self.far = (far + self.core, far + 1 - self.core)
        self.groups = groups
        self.count = count
        self.half = 2 * count
        self.near_block = self.side * self.half
        self.far_block = (1 - self.side) * self.half

    def peer(self, q):
        return peer(q, self.f)

    def others(self):
        return others(self.p, self.groups)

    def meet(self):
        barrier = pltpu.get_barrier_semaphore()
        for q in self.others():
            pl.semaphore_signal(
                barrier, inc=1, device_id=self.peer(q), device_id_type=pl.DeviceIdType.MESH
            )
        pl.semaphore_wait(barrier, self.groups - 1)


def rows_of(block, count, size):
    return block // count, pl.ds(pl.multiple_of(lax.rem(block, count) * size, size), size)


def mask_of(first, q, k, size, diagonal):
    rows = lax.broadcasted_iota(jnp.int32, (size, size), 0)
    ok = rows >= first - k * size
    if diagonal:
        ok = ok & (rows <= lax.broadcasted_iota(jnp.int32, (1, size), 1))
    return ok


def attend_kernel(
    size, heads, own_ref, st_ref, qkv_ref, o_ref, lse_ref, attn_ref,
    m_sc, l_sc, acc_sc, near_s, near_r, far_s, far_r, out_s, out_r,
):
    groups, _, per, _ = own_ref.shape
    count = per // size
    at = Place(groups, count)
    p, side, half = at.p, at.side, at.half
    m_sc[...] = jnp.full_like(m_sc, NEG)
    l_sc[...] = jnp.zeros_like(l_sc)
    acc_sc[...] = jnp.zeros_like(acc_sc)
    qkv_ref[p] = own_ref[p]
    at.meet()

    near = remote(own_ref.at[at.mate], qkv_ref.at[p], near_s, near_r, at.peer(at.mate))
    near.start()

    def part_of(n):
        n = lax.rem(n + pick(side == 1, 0, count), 3 * count)
        return pick(n < count, 0, 1 + lax.rem(n - count, 2)), pick(n < count, n, (n - count) // 2)

    def far_copy(n, d):
        t, b = part_of(n)
        rows = pl.ds(pl.multiple_of(b * size, size), size)
        return remote(
            own_ref.at[at.far[d], t, rows], qkv_ref.at[p, t, rows], far_s.at[d, n],
            far_r.at[p, t, b], at.peer(at.far[d]),
        )

    for n in range(3 * count):
        for d in range(2):
            far_copy(n, d).start()

    def far_wait(t, block):
        src, rows = rows_of(block, count, size)
        there = qkv_ref.at[src, t, rows]
        remote(there, there, far_s.at[0, 0], far_r.at[src, t, lax.rem(block, count)], at.peer(src)).wait_recv()

    def block(q, k, diagonal):
        src, rows = rows_of(q, count, size)
        cols = pl.ds(pl.multiple_of(q * size, size), size)
        ksrc, krows = rows_of(k, count, size)
        query = (qkv_ref[src, 0, rows, :] * HEAD_DIM ** (-0.5)).astype(BF16)
        key = qkv_ref[ksrc, 1, krows, :]
        value = qkv_ref[ksrc, 2, krows, :]
        ok = mask_of(st_ref[:, cols], q, k, size, diagonal)
        for h in range(heads):
            sl = slice(h * HEAD_DIM, (h + 1) * HEAD_DIM)
            s = jnp.where(ok, dot(key, lane_mask(h, query), NT), NEG)
            m_old = m_sc[h : h + 1, cols]
            m_new = jnp.maximum(m_old, jnp.max(s, 0, keepdims=True))
            e = jnp.exp(s - m_new)
            alpha = jnp.exp(m_old - m_new)
            l_sc[h : h + 1, cols] = l_sc[h : h + 1, cols] * alpha + jnp.sum(e, 0, keepdims=True)
            m_sc[h : h + 1, cols] = m_new
            acc_sc[sl, cols] = acc_sc[sl, cols] * alpha + dot(value[:, sl], e.astype(BF16), TN)

    def out_copy(q):
        src, rows = rows_of(q, count, size)
        return remote(
            o_ref.at[src, rows], attn_ref.at[p, rows], out_s.at[q], out_r.at[p, lax.rem(q, count)],
            at.peer(src),
        )

    def finish(q):
        src, rows = rows_of(q, count, size)
        cols = pl.ds(pl.multiple_of(q * size, size), size)
        parts = []
        for h in range(heads):
            sl = slice(h * HEAD_DIM, (h + 1) * HEAD_DIM)
            total = l_sc[h : h + 1, cols]
            parts.append(acc_sc[sl, cols] * (1.0 / total))
            lse_ref[h : h + 1, cols] = m_sc[h : h + 1, cols] + jnp.log(total)
        out = jnp.concatenate(parts, 0).T.astype(BF16)
        o_ref[src, rows] = out

        @pl.when(src == p)
        def _():
            attn_ref[p, rows] = out

        @pl.when(src != p)
        def _():
            out_copy(q).start()

    small = count * (count + 1) // 2
    cross = 2 * small + count * count
    bulk = cross + half * half
    end = bulk + half * (half + 1) // 2

    @pl.loop(0, end)
    def _(step):
        second = step >= small
        row, col = triangle(step - pick(second, small, 0), count)
        base = pick(second, at.mate, p) * count
        q, k = base + row, base + col
        c = step - 2 * small
        in_cross = (step >= 2 * small) & (step < cross)
        q = pick(in_cross, at.near_block + count + c // count, q)
        k = pick(in_cross, at.near_block + lax.rem(c, count), k)
        c = step - cross
        in_bulk = (step >= cross) & (step < bulk)
        outer, inner = c // half, lax.rem(c, half)
        outer = lax.rem(outer, 2) * count + outer // 2
        q = pick(in_bulk, half + pick(side == 0, outer, inner), q)
        k = pick(in_bulk, pick(side == 0, inner, outer), k)
        in_last = step >= bulk
        row, col = triangle(step - bulk, half)
        q = pick(in_last, at.far_block + row, q)
        k = pick(in_last, at.far_block + col, k)

        @pl.when(step == small)
        def _():
            near.wait_recv()

        starts_outer = in_bulk & (inner == 0)
        starts_row = in_last & (col == 0)

        @pl.when((starts_outer & (side == 0)) | (starts_row & (side == 1)))
        def _():
            far_wait(0, q)

        @pl.when((starts_outer & (side == 1)) | (starts_row & (side == 0)))
        def _():
            far_block = pick(in_bulk, k, q)
            far_wait(1, far_block)
            far_wait(2, far_block)

        @pl.when(q == k)
        def _():
            block(q, k, True)

        @pl.when(q != k)
        def _():
            block(q, k, False)

        near_done = step == pick(side == 0, cross, bulk) - 1
        low = pick(near_done, at.near_block, q)
        high = pick(near_done, at.near_block + half, pick(in_last & (q == k), q + 1, q))
        pl.loop(low, high)(finish)

    for q in at.others():
        for b in range(count):
            rows = pl.ds(b * size, size)
            there = attn_ref.at[q, rows]
            remote(there, there, out_s.at[0], out_r.at[q, b], at.peer(q)).wait_recv()
            out_copy(q * count + b).wait_send()
    near.wait_send()
    for n in range(3 * count):
        for d in range(2):
            far_copy(n, d).wait_send()


def attention_forward(own, starts, size=512):
    groups, _, per, width = own.shape
    length = groups * per
    heads = width // HEAD_DIM
    count = per // size
    dma = pltpu.SemaphoreType.DMA
    vmem = pl.BlockSpec(memory_space=pltpu.VMEM)
    return pl.pallas_call(
        functools.partial(attend_kernel, size, heads),
        out_shape=(
            jax.ShapeDtypeStruct(own.shape, BF16),
            jax.ShapeDtypeStruct((groups, per, width), BF16),
            jax.ShapeDtypeStruct((8, length), F32),
            jax.ShapeDtypeStruct((groups, per, width), BF16),
        ),
        in_specs=[vmem] * 2,
        out_specs=[vmem] * 4,
        scratch_shapes=[pltpu.VMEM((8, length), F32)] * 2 + [
            pltpu.VMEM((width, length), F32), dma(()), dma(()), dma((2, 3 * count)),
            dma((groups, 3, count)), dma((groups * count,)), dma((groups, count)),
        ],
        compiler_params=pltpu.CompilerParams(
            vmem_limit_bytes=VMEM_LIMIT, collective_id=2, has_side_effects=True
        ),
        cost_estimate=cost(4 * length * length * width, 16 * length * width, length * length),
        name="attention_forward",
    )(own, starts)


def attend_back_kernel(
    size, heads, qkv_ref, own_ref, o_ref, lse_ref, st_ref, out_ref,
    do_sc, delta_sc, dqt_sc, dk_sc, dv_sc, stage, near_s, near_r, far_s, far_r, out_s, out_r,
):
    groups, _, per, _ = qkv_ref.shape
    count = per // size
    at = Place(groups, count)
    p, side, half = at.p, at.side, at.half
    scale = HEAD_DIM ** (-0.5)
    dqt_sc[...] = jnp.zeros_like(dqt_sc)
    dk_sc[...] = jnp.zeros_like(dk_sc)
    dv_sc[...] = jnp.zeros_like(dv_sc)
    do_sc[p] = own_ref[p]
    at.meet()

    near = remote(own_ref.at[at.mate], do_sc.at[p], near_s, near_r, at.peer(at.mate))
    near.start()

    def far_copy(b, d):
        rows = pl.ds(b * size, size)
        return remote(
            own_ref.at[at.far[d], rows], do_sc.at[p, rows], far_s.at[d, b], far_r.at[p, b],
            at.peer(at.far[d]),
        )

    for b in range(count):
        for d in range(2):
            far_copy(b, d).start()

    def columns(block):
        return pl.ds(pl.multiple_of(block * size, size), size)

    def prepare(q):
        src, rows = rows_of(q, count, size)
        prod = (do_sc[src, rows].astype(F32) * o_ref[src, rows].astype(F32)).T
        for h in range(heads):
            sl = slice(h * HEAD_DIM, (h + 1) * HEAD_DIM)
            delta_sc[h : h + 1, columns(q)] = jnp.sum(prod[sl], 0, keepdims=True)

    def block(q, k, diagonal):
        src, rows = rows_of(q, count, size)
        cols = columns(q)
        ksrc, krows = rows_of(k, count, size)
        query = (qkv_ref[src, 0, rows, :] * scale).astype(BF16)
        grad = do_sc[src, rows]
        key = qkv_ref[ksrc, 1, krows, :]
        value = qkv_ref[ksrc, 2, krows, :]
        ok = mask_of(st_ref[:, cols], q, k, size, diagonal)
        dv = dk = None
        for h in range(heads):
            sl = slice(h * HEAD_DIM, (h + 1) * HEAD_DIM)
            query_h, grad_h = lane_mask(h, query), lane_mask(h, grad)
            s = jnp.where(ok, dot(key, query_h, NT), NEG)
            e = jnp.exp(s - lse_ref[h : h + 1, cols])
            ds = (e * (dot(value, grad_h, NT) - delta_sc[h : h + 1, cols])).astype(BF16)
            dvh = dot(e.astype(BF16), grad_h)
            dkh = dot(ds, query_h)
            dv = dvh if dv is None else dv + dvh
            dk = dkh if dk is None else dk + dkh
            dqt_sc[sl, cols] += dot(key[:, sl], ds, TN)
        dv_sc[cols_of(k), :] += dv
        dk_sc[cols_of(k), :] += dk

    cols_of = columns

    def out_copy(block, part):
        src, rows = rows_of(block, count, size)
        return remote(
            stage.at[src, part, rows], out_ref.at[p, part, rows], out_s.at[block, part],
            out_r.at[p, part, lax.rem(block, count)], at.peer(src),
        )

    def give(block, part, value):
        src, rows = rows_of(block, count, size)

        @pl.when(src == p)
        def _():
            out_ref[p, part, rows] = value

        @pl.when(src != p)
        def _():
            stage[src, part, rows] = value
            out_copy(block, part).start()

    def finish_query(q):
        give(q, 0, (dqt_sc[:, columns(q)] * scale).T.astype(BF16))

    def finish_key(k):
        give(k, 1, dk_sc[columns(k), :].astype(BF16))
        give(k, 2, dv_sc[columns(k), :].astype(BF16))

    small = count * (count + 1) // 2
    far = 2 * small
    bulk = far + half * (half + 1) // 2
    cross = bulk + half * half
    end = cross + count * count

    @pl.loop(0, end)
    def _(step):
        second = step >= small
        row, col = triangle(step - pick(second, small, 0), count)
        base = pick(second, at.mate, p) * count
        q, k = base + row, base + col
        in_far = (step >= far) & (step < bulk)
        row, column = triangle_by_column(step - far, half)
        q = pick(in_far, at.far_block + row, q)
        k = pick(in_far, at.far_block + column, k)
        c = step - bulk
        in_bulk = (step >= bulk) & (step < cross)
        outer, inner = c // half, lax.rem(c, half)
        q = pick(in_bulk, half + pick(side == 0, outer, inner), q)
        k = pick(in_bulk, pick(side == 0, inner, outer), k)
        c = step - cross
        in_cross = step >= cross
        q = pick(in_cross, at.near_block + count + c // count, q)
        k = pick(in_cross, at.near_block + lax.rem(c, count), k)

        @pl.when(step == small)
        def _():
            near.wait_recv()

        @pl.when(in_far & (column == 0))
        def _():
            src, rows = rows_of(q, count, size)
            there = do_sc.at[src, rows]
            remote(there, there, far_s.at[0, 0], far_r.at[src, lax.rem(q, count)], at.peer(src)).wait_recv()

        @pl.when(((step < far) & (col == 0)) | (in_far & (column == 0)))
        def _():
            prepare(q)

        @pl.when(q == k)
        def _():
            block(q, k, True)

        @pl.when(q != k)
        def _():
            block(q, k, False)

        column_done = in_far & (row == half - 1)
        outer_done = in_bulk & (inner == half - 1)
        done = step == end - 1
        near_low, near_high = at.near_block, at.near_block + half
        query = (column_done & (side == 1)) | (outer_done & (side == 0))
        block_id = at.far_block + pick(in_far, column, outer)
        pl.loop(
            pick(done, near_low, block_id),
            pick(done, near_high, pick(query, block_id + 1, block_id)),
        )(finish_query)
        key = (column_done & (side == 0)) | (outer_done & (side == 1))
        pl.loop(
            pick(done, near_low, block_id),
            pick(done, near_high, pick(key, block_id + 1, block_id)),
        )(finish_key)

    for q in at.others():
        for b in range(count):
            for part in range(3):
                there = out_ref.at[q, part, pl.ds(b * size, size)]
                remote(there, there, out_s.at[0, 0], out_r.at[q, part, b], at.peer(q)).wait_recv()
                out_copy(q * count + b, part).wait_send()
    near.wait_send()
    for b in range(count):
        for d in range(2):
            far_copy(b, d).wait_send()


def attention_backward(qkv, grad, out, lse, starts, size=512):
    groups, _, per, width = qkv.shape
    length = groups * per
    heads = width // HEAD_DIM
    count = per // size
    dma = pltpu.SemaphoreType.DMA
    vmem = pl.BlockSpec(memory_space=pltpu.VMEM)
    return pl.pallas_call(
        functools.partial(attend_back_kernel, size, heads),
        out_shape=jax.ShapeDtypeStruct(qkv.shape, BF16),
        in_specs=[vmem] * 5,
        out_specs=vmem,
        scratch_shapes=[
            pltpu.VMEM((groups, per, width), BF16), pltpu.VMEM((8, length), F32),
            pltpu.VMEM((width, length), F32), pltpu.VMEM((length, width), F32),
            pltpu.VMEM((length, width), F32), pltpu.VMEM(qkv.shape, BF16),
            dma(()), dma(()), dma((2, count)), dma((groups, count)),
            dma((groups * count, 3)), dma((groups, 3, count)),
        ],
        compiler_params=pltpu.CompilerParams(
            vmem_limit_bytes=VMEM_LIMIT, collective_id=3, has_side_effects=True
        ),
        cost_estimate=cost(10 * length * length * width, 24 * length * width, length * length),
        name="attention_backward",
    )(qkv, grad, out, lse, starts)


def put(ref, first, value):
    @pl.when(first)
    def _():
        ref[...] = value

    @pl.when(jnp.logical_not(first))
    def _():
        ref[...] += value


def column_sum(x):
    return jnp.sum(x, 0, keepdims=True)


def middle_kernel(
    groups, x_ref, attn_ref, wa_ref, wp_ref, small_ref, fcb_ref, cot_ref,
    out_ref, resid_ref, ga_ref, gwa_ref, gwp_ref, gs_ref, gwa_sc, gwp_sc,
):
    first = pl.program_id(0) == 0
    model = x_ref.shape[-1]
    width = model // groups
    small = small_ref[...]
    w_out = wa_ref[:, 0:model]
    w_fc = wa_ref[:, model:]
    w_proj = wp_ref[...]
    attn = jnp.concatenate([attn_ref[g] for g in range(groups)], 1)
    resid = x_ref[...].astype(F32) + dot(attn, w_out) + small[OUT_BIAS : OUT_BIAS + 1]
    normed, inverse = normalize(resid)
    gain = small[GAIN_TWO : GAIN_TWO + 1]
    act = (normed * gain + small[BIAS_TWO : BIAS_TWO + 1]).astype(BF16)
    hidden = dot(act, w_fc) + fcb_ref[...]
    sig = 1.0 / (1.0 + jnp.exp(-1.702 * hidden))
    gelu = hidden * sig
    slope = sig + 1.702 * gelu * (1.0 - sig)
    gelu = gelu.astype(BF16)
    out_ref[...] = (resid + dot(gelu, w_proj) + small[PROJ_BIAS : PROJ_BIAS + 1]).astype(BF16)
    up = cot_ref[...]
    put(gwp_sc, first, dot(gelu, up, TN))
    grad_hidden = dot(up, w_proj, NT) * slope
    low = grad_hidden.astype(BF16)
    put(gwa_sc.at[:, model:], first, dot(act, low, TN))
    grad_act = dot(low, w_fc, NT)
    up = up.astype(F32)
    grad_resid = up + normalize_back(grad_act * gain, normed, inverse)
    resid_ref[...] = grad_resid
    resid_low = grad_resid.astype(BF16)
    put(gwa_sc.at[:, 0:model], first, dot(attn, resid_low, TN))
    grad_attn = dot(resid_low, w_out, NT).astype(BF16)
    for g in range(groups):
        ga_ref[g] = grad_attn[:, g * width : (g + 1) * width]
    put(gs_ref.at[0:1, :], first, column_sum(grad_hidden))
    put(gs_ref.at[1:2, 0:model], first, column_sum(grad_resid))
    put(gs_ref.at[2:3, 0:model], first, column_sum(grad_act * normed))
    put(gs_ref.at[3:4, 0:model], first, column_sum(grad_act))
    put(gs_ref.at[4:5, 0:model], first, column_sum(up))

    @pl.when(pl.program_id(0) == pl.num_programs(0) - 1)
    def _():
        gwa_ref[...] = gwa_sc[...].astype(BF16)
        gwp_ref[...] = gwp_sc[...].astype(BF16)


def middle(x, attn, w_a, w_proj, small, fc_bias, cotangent, tile=256):
    length, model = x.shape
    groups = attn.shape[0]
    hid = w_proj.shape[0]
    rows = pl.BlockSpec((tile, model), lambda i: (i, 0))
    slabs = pl.BlockSpec((groups, tile, model // groups), lambda i: (0, i, 0))
    return pl.pallas_call(
        functools.partial(middle_kernel, groups),
        out_shape=(
            jax.ShapeDtypeStruct((length, model), BF16),
            jax.ShapeDtypeStruct((length, model), F32),
            jax.ShapeDtypeStruct(attn.shape, BF16),
            jax.ShapeDtypeStruct((model, model + hid), BF16),
            jax.ShapeDtypeStruct((hid, model), BF16),
            jax.ShapeDtypeStruct((8, hid), F32),
        ),
        grid=(length // tile,),
        in_specs=[rows, slabs, whole(w_a.shape), whole(w_proj.shape), whole(small.shape),
                  whole(fc_bias.shape), rows],
        out_specs=[rows, rows, slabs, whole((model, model + hid)),
                   whole((hid, model)), whole((8, hid))],
        scratch_shapes=[pltpu.VMEM((model, model + hid), F32), pltpu.VMEM((hid, model), F32)],
        compiler_params=params(),
        cost_estimate=cost(12 * length * model * hid + 6 * length * model * model,
                           16 * model * hid, length * hid),
        name="middle",
    )(x, attn, w_a, w_proj, small, fc_bias, cotangent)


def last_kernel(
    rows, parts, chunk, x_ref, g_ref, resid_ref, w_ref, small_ref, gs_in,
    gt_ref, gw_ref, gv_ref,
    acc, out, vec, mine, vsend, vpart, low, r1, s2, r2, keep, s3, r3,
    v1s, v1r, v2s, v2r, c1s, c1r, c2s, c2r, c3s, c3r, c4s, c4r,
):
    step = pl.program_id(0)
    first = step == 0
    groups = g_ref.shape[0]
    model = x_ref.shape[-1]
    p, f = lax.axis_index("sp"), lax.axis_index("fsdp")

    @pl.when(first)
    def _():
        greet(groups, parts)

    small = small_ref[...]
    normed, inverse = normalize(x_ref[...].astype(F32))
    gain = small[GAIN_ONE : GAIN_ONE + 1]
    act = (normed * gain + small[BIAS_ONE : BIAS_ONE + 1]).astype(BF16)
    grad = jnp.concatenate([g_ref[g, part] for part in range(3) for g in range(groups)], 1)
    put(acc, first, dot(act, grad, TN))
    grad_act = dot(grad, weight_rows(w_ref, rows), NT)
    gt_ref[...] = (
        resid_ref[...] + normalize_back(grad_act * gain, normed, inverse)
    ).astype(BF16)
    put(vec.at[0:1], first, column_sum(grad_act * normed))
    put(vec.at[1:2], first, column_sum(grad_act))
    put(vec.at[2:3], first, column_sum(grad[:, 0:model].astype(F32)))
    put(vec.at[3:4], first, column_sum(grad[:, 2 * model :].astype(F32)))

    @pl.when(step == pl.num_programs(0) - 1)
    def _():
        shard = acc.shape[0] // parts
        core = lax.rem(p, 2)
        side = p // 2
        mate = p + 1 - 2 * core
        across = p + groups // 2 - side * groups
        half = acc.shape[1] // 2
        quarter = half // 2
        count = quarter // chunk

        def lane(c, s, k):
            return pl.ds(pl.multiple_of(c * half + s * quarter + k * chunk, 128), chunk)

        copies = []

        def go(copy):
            copy.start()
            copies.append(copy)

        low[...] = acc[...].astype(BF16)
        vec[4:8, :] = gs_in[1:5, 0:model]
        piece = model // parts
        fc = gs_in.shape[1] // parts
        bits = min(128, fc)
        vsend[...] = jnp.zeros_like(vsend)
        for g in range(parts):
            vsend[g, 0:8, 0:piece] = vec[:, g * piece : (g + 1) * piece]
            for k in range(fc // bits):
                at = g * fc + k * bits
                vsend[g, 8 + k : 9 + k, 0:bits] = gs_in[0:1, at : at + bits]
        greeted(groups, parts)

        for k in range(count):
            for s in range(2):
                go(remote(low.at[:, lane(1 - core, s, k)], r1.at[k, s], c1s.at[k, s], c1r.at[k, s],
                          peer(mate, f)))
        for n, g in enumerate(others(f, parts)):
            go(remote(vsend.at[g], vpart.at[f], v1s.at[n], v1r.at[f], peer(p, g)))
        for k in range(count):
            for s in range(2):
                remote(r1.at[k, s], r1.at[k, s], c1s.at[k, s], c1r.at[k, s], peer(mate, f)).wait_recv()
            s2[k] = (acc[:, lane(core, 1 - side, k)] + r1[k, 1 - side].astype(F32)).astype(BF16)
            go(remote(s2.at[k], r2.at[k], c2s.at[k], c2r.at[k], peer(across, f)))
        for k in range(count):
            remote(s2.at[k], r2.at[k], c2s.at[k], c2r.at[k], peer(across, f)).wait_recv()
            total = acc[:, lane(core, side, k)] + r1[k, side].astype(F32) + r2[k].astype(F32)
            keep[k] = total
            s3[k] = total.astype(BF16)
            for n, g in enumerate(others(f, parts)):
                rows_of = pl.ds(pl.multiple_of(g * shard, shard), shard)
                go(remote(s3.at[k, rows_of], r3.at[k, f], c3s.at[k, n], c3r.at[k, f], peer(p, g)))
        for g in others(f, parts):
            remote(vsend.at[g], vpart.at[g], v1s.at[0], v1r.at[g], peer(p, g)).wait_recv()
        total = vsend[f]
        for g in others(f, parts):
            total = total + vpart[g]
        mine[p] = total
        for n, q in enumerate(others(p, groups)):
            go(remote(mine.at[p], mine.at[p], v2s.at[n], v2r.at[p], peer(q, f)))
        for k in range(count):
            for g in others(f, parts):
                remote(r3.at[k, g], r3.at[k, g], c3s.at[k, 0], c3r.at[k, g], peer(p, g)).wait_recv()
            total = keep[k, pl.ds(pl.multiple_of(f * shard, shard), shard)]
            for g in others(f, parts):
                total = total + r3[k, g].astype(F32)
            out[:, lane(core, side, k)] = total
            for n, q in enumerate(others(p, groups)):
                there = out.at[:, lane(core, side, k)]
                go(remote(there, there, c4s.at[k, n], c4r.at[k, p], peer(q, f)))
        for q in others(p, groups):
            remote(mine.at[q], mine.at[q], v2s.at[0], v2r.at[q], peer(q, f)).wait_recv()
        total = mine[0]
        for q in range(1, groups):
            total = total + mine[q]
        gv_ref[...] = total
        for k in range(count):
            for q in others(p, groups):
                there = out.at[:, lane(lax.rem(q, 2), q // 2, k)]
                remote(there, there, c4s.at[k, 0], c4r.at[k, q], peer(q, f)).wait_recv()
        gw_ref[...] = out[...]
        for copy in copies:
            copy.wait_send()


def last(x, grad, resid, weight, rows, small, sums, parts, tile=256, chunk=128):
    length, model = x.shape
    groups, _, _, width = grad.shape
    block = pl.BlockSpec((tile, model), lambda i: (i, 0))
    triple = 3 * model
    shard = model // parts
    count = triple // 4 // chunk
    dma = pltpu.SemaphoreType.DMA
    vmem = pltpu.VMEM
    return pl.pallas_call(
        functools.partial(last_kernel, rows, parts, chunk),
        out_shape=(
            jax.ShapeDtypeStruct((length, model), BF16),
            jax.ShapeDtypeStruct((shard, triple), F32),
            jax.ShapeDtypeStruct((16, 128), F32),
        ),
        grid=(length // tile,),
        in_specs=[
            block,
            pl.BlockSpec((groups, 3, tile, width), lambda i: (0, 0, i, 0)),
            block,
            whole(weight.shape),
            whole(small.shape),
            whole(sums.shape),
        ],
        out_specs=[block, whole((shard, triple)), whole((16, 128))],
        scratch_shapes=[
            vmem((model, triple), F32), vmem((shard, triple), F32), vmem((8, model), F32),
            vmem((groups, 16, 128), F32),
            vmem((parts, 16, 128), F32), vmem((parts, 16, 128), F32),
            vmem((model, triple), BF16), vmem((count, 2, model, chunk), BF16),
            vmem((count, model, chunk), BF16), vmem((count, model, chunk), BF16),
            vmem((count, model, chunk), F32), vmem((count, model, chunk), BF16),
            vmem((count, parts, shard, chunk), BF16),
            dma((parts,)), dma((parts,)), dma((groups,)), dma((groups,)),
            dma((count, 2)), dma((count, 2)), dma((count,)), dma((count,)),
            dma((count, parts)), dma((count, parts)), dma((count, groups)), dma((count, groups)),
        ],
        compiler_params=pltpu.CompilerParams(
            vmem_limit_bytes=VMEM_LIMIT, collective_id=1, has_side_effects=True
        ),
        cost_estimate=cost(12 * length * model * model, 20 * length * model),
        name="last",
    )(x, grad, resid, weight, small, sums)


def per_device(
    tokens, starts, norm1_gain, norm1_bias, w_qkv, q_bias, v_bias, w_out, out_bias, norm2_gain,
    norm2_bias, w_fc, fc_bias, w_proj, proj_bias, cotangent,
):
    groups = lax.axis_size("sp")
    parts = lax.axis_size("fsdp")
    rows, triple = w_qkv.shape
    piece = norm1_gain.shape[0]
    x = tokens[0]
    gather = functools.partial(lax.all_gather, axis_name="fsdp", axis=0, tiled=True)
    vectors = [
        norm1_gain, norm1_bias, q_bias, v_bias, out_bias, norm2_gain, norm2_bias, proj_bias, fc_bias
    ]
    packed, doc_first, small, fcb = gather_front(w_qkv, starts, vectors, groups, parts)
    doc_first = doc_first.reshape(1, -1)
    if rows % 16 == 0:
        weight, weight_count = packed, rows
    else:
        weight, weight_count = packed.reshape(1, parts * rows, triple), parts * rows
    w_a = gather(jnp.concatenate([w_out, w_fc], 1))
    w_p = gather(w_proj)

    slabs = project_qkv(x, weight, weight_count, small, groups)
    qkv, out, lse, attn = attention_forward(slabs, doc_first)
    block_out, grad_resid, grad_attn, g_a, g_p, sums = middle(
        x, attn, w_a, w_p, small, fcb, cotangent[0]
    )
    model = x.shape[1]
    g_a = lax.psum_scatter(g_a, "fsdp", scatter_dimension=0, tiled=True)
    g_p = lax.psum_scatter(g_p, "fsdp", scatter_dimension=0, tiled=True)
    g_a, g_p = lax.psum((g_a.astype(F32), g_p.astype(F32)), "sp")
    grad = attention_backward(qkv, grad_attn, out, lse, doc_first)
    grad_tokens, g_q, g_v = last(x, grad, grad_resid, weight, weight_count, small, sums, parts)
    vec = [g_v[k, :piece] for k in range(8)]
    fc = fc_bias.shape[0]
    g_fcb = g_v[8 : 8 + max(fc // 128, 1), : min(fc, 128)].reshape(fc)
    return (
        block_out[None], grad_tokens[None], vec[0], vec[1], g_q, vec[2], vec[3],
        g_a[:, :model], vec[4], vec[5], vec[6], g_a[:, model:], g_fcb, g_p, vec[7],
    )


def solution(mesh):
    row, mat = P("fsdp"), P("fsdp", None)
    stream = P("fsdp", "sp", None)
    return jax.shard_map(
        per_device,
        mesh=mesh,
        in_specs=(stream, P("fsdp", "sp"), row, row, mat, row, row, mat, row, row, row, mat, row,
                  mat, row, stream),
        out_specs=(stream, stream, row, row, mat, row, row, mat, row, row, row, mat, row, mat, row),
        check_vma=False,
    )
```

```python
import functools

import jax
import jax.numpy as jnp
from jax import lax
from jax.experimental import pallas as pl
from jax.experimental.pallas import tpu as pltpu
from jax.sharding import PartitionSpec as P

HEAD_DIM = 64
EPSILON = 1e-05
NEG = -1e30
F32 = jnp.float32
BF16 = jnp.bfloat16
NN = (((1,), (0,)), ((), ()))
NT = (((1,), (1,)), ((), ()))
TN = (((0,), (0,)), ((), ()))
VMEM_LIMIT = 60 << 20


def dot(left, right, dims=NN):
    return lax.dot_general(left, right, dims, preferred_element_type=F32)


def normalize(values):
    centered = values - jnp.mean(values, -1, keepdims=True)
    inverse = lax.rsqrt(jnp.mean(centered * centered, -1, keepdims=True) + EPSILON)
    return centered * inverse, inverse


def normalize_back(incoming, normed, inverse):
    return inverse * (
        incoming
        - jnp.mean(incoming, -1, keepdims=True)
        - normed * jnp.mean(incoming * normed, -1, keepdims=True)
    )


def whole(shape):
    return pl.BlockSpec(shape, lambda *_: (0,) * len(shape))


def params():
    return pltpu.CompilerParams(vmem_limit_bytes=VMEM_LIMIT)


def cost(flops, size, exps=0):
    return pl.CostEstimate(flops=flops, bytes_accessed=size, transcendentals=exps)


def weight_rows(w_ref, rows):
    parts = w_ref.shape[0]
    return w_ref[:, 0:rows, :].reshape(parts * rows, w_ref.shape[2])


def peer(sp, fsdp):
    return {"sp": sp, "fsdp": fsdp}


def remote(src, dst, send, recv, where):
    return pltpu.make_async_remote_copy(
        src_ref=src, dst_ref=dst, send_sem=send, recv_sem=recv,
        device_id=where, device_id_type=pl.DeviceIdType.MESH,
    )


def others(me, count):
    return [lax.rem(me + k, count) for k in range(1, count)]


def greet(groups, parts):
    p, f = lax.axis_index("sp"), lax.axis_index("fsdp")
    barrier = pltpu.get_barrier_semaphore()
    for q in others(p, groups):
        pl.semaphore_signal(barrier, inc=1, device_id=peer(q, f), device_id_type=pl.DeviceIdType.MESH)
    for g in others(f, parts):
        pl.semaphore_signal(barrier, inc=1, device_id=peer(p, g), device_id_type=pl.DeviceIdType.MESH)


def greeted(groups, parts):
    pl.semaphore_wait(pltpu.get_barrier_semaphore(), groups + parts - 2)


class Spread:
    def __init__(self, src, dst, parts, send, recv, own):
        self.src, self.dst, self.send, self.recv, self.own = src, dst, send, recv, own
        self.p, self.f = lax.axis_index("sp"), lax.axis_index("fsdp")
        core = lax.rem(self.p, 2)
        self.mate = self.p + 1 - 2 * core
        self.parts, self.major = parts, parts // 2
        self.a, self.b = self.f // 2, lax.rem(self.f, 2)
        self.twin = self.a * 2 + 1 - self.b
        half = src.shape[1] // 2
        self.lanes = pl.ds(pl.multiple_of(core * half, 128), half)
        self.mate_lanes = pl.ds(pl.multiple_of((1 - core) * half, 128), half)

    def back(self, k):
        return lax.rem(self.a + self.major - k, self.major)

    def block(self, g, lanes=None):
        return self.dst.at[g, :, self.lanes if lanes is None else lanes]

    def first(self, k):
        where = lax.rem(self.a + k, self.major) * 2 + self.b
        where = self.twin if k == 0 else where
        return remote(
            self.src.at[:, self.lanes], self.block(self.f), self.send.at[0, k],
            self.recv.at[0, self.f], peer(self.p, where),
        )

    def to_twin(self, k):
        g = self.back(k) * 2 + self.b
        return remote(
            self.block(g), self.block(g), self.send.at[1, k], self.recv.at[0, g],
            peer(self.p, self.twin),
        )

    def to_mate(self, k, b):
        g = self.back(k) * 2 + b
        slot = k if b is self.b else self.major + k
        return remote(
            self.block(g), self.block(g), self.send.at[2, slot], self.recv.at[1, g],
            peer(self.mate, self.f),
        )

    def keep(self):
        return pltpu.make_async_copy(self.src, self.dst.at[self.f], self.own)

    def start(self):
        self.keep().start()
        for k in list(range(1, self.major)) + [0]:
            self.first(k).start()

    def relay(self, k):
        self.to_twin(k).wait_recv()
        self.to_twin(k).start()
        self.to_mate(k, self.b).start()

    def relay_twin(self, k):
        other = 1 - self.b
        copy = self.to_mate(k, other)
        g = self.back(k) * 2 + other
        remote(
            self.block(g), self.block(g), self.send.at[1, 0], self.recv.at[0, g],
            peer(self.p, self.twin),
        ).wait_recv()
        copy.start()

    def finish(self):
        for g in others(self.f, self.parts):
            there = self.block(g, self.mate_lanes)
            remote(
                there, there, self.send.at[1, 0], self.recv.at[1, g], peer(self.mate, self.f)
            ).wait_recv()
        for k in range(self.major):
            self.first(k).wait_send()
            self.to_mate(k, 1 - self.b).wait_send()
        for k in range(1, self.major):
            self.to_twin(k).wait_send()
            self.to_mate(k, self.b).wait_send()
        self.keep().wait()

    @staticmethod
    def semaphores(parts):
        dma = pltpu.SemaphoreType.DMA
        return [dma((3, parts)), dma((2, parts)), dma(())]


class Fold:
    def __init__(self, src, out, parts, mine, r1, r2, s2, r3, own, send1, recv1, send2, recv2, send3, recv3):
        self.__dict__.update(
            src=src, out=out, mine=mine, r1=r1, r2=r2, s2=s2, r3=r3, own=own, send1=send1,
            recv1=recv1, send2=send2, recv2=recv2, send3=send3, recv3=recv3,
        )
        self.p, self.f = lax.axis_index("sp"), lax.axis_index("fsdp")
        core = lax.rem(self.p, 2)
        self.mate = self.p + 1 - 2 * core
        self.major = parts // 2
        self.a, self.b = self.f // 2, lax.rem(self.f, 2)
        self.twin = self.a * 2 + 1 - self.b
        half = src.shape[2] // 2
        self.lanes = pl.ds(pl.multiple_of(core * half, 128), half)
        self.mate_lanes = pl.ds(pl.multiple_of((1 - core) * half, 128), half)

    def keep(self):
        return pltpu.make_async_copy(self.src.at[:, :, self.lanes], self.mine, self.own)

    def to_mate(self):
        return remote(
            self.src.at[:, :, self.mate_lanes], self.r1, self.send1, self.recv1,
            peer(self.mate, self.f),
        )

    def to_twin(self, c):
        return remote(
            self.mine.at[c * 2 + 1 - self.b], self.r2.at[c], self.send2.at[c], self.recv2.at[c],
            peer(self.p, self.twin),
        )

    def along(self, k):
        c = lax.rem(self.a + k, self.major)
        return remote(
            self.s2.at[c], self.r3.at[self.a], self.send3.at[c], self.recv3.at[self.a],
            peer(self.p, c * 2 + self.b),
        )

    def start(self):
        self.to_mate().start()
        self.keep().start()

    def pairs(self):
        self.keep().wait()
        self.to_mate().wait()
        self.mine[...] = (self.mine[...].astype(F32) + self.r1[...].astype(F32)).astype(BF16)
        for c in range(self.major):
            self.to_twin(c).start()

    def planes(self):
        for c in range(self.major):
            self.to_twin(c).wait()
            self.s2[c] = (
                self.mine[c * 2 + self.b].astype(F32) + self.r2[c].astype(F32)
            ).astype(BF16)
        for k in range(1, self.major):
            self.along(k).start()

    def lines(self):
        total = self.mine[self.f].astype(F32) + self.r2[self.a].astype(F32)
        for k in range(1, self.major):
            c = lax.rem(self.a + k, self.major)
            remote(
                self.r3.at[c], self.r3.at[c], self.send3.at[0], self.recv3.at[c],
                peer(self.p, self.twin),
            ).wait_recv()
            total = total + self.r3[c].astype(F32)
        self.out[...] = total.astype(BF16)
        for k in range(1, self.major):
            self.along(k).wait_send()

    @staticmethod
    def scratch(parts, rows, lanes):
        dma = pltpu.SemaphoreType.DMA
        major, half = parts // 2, lanes // 2
        return [
            pltpu.VMEM((parts, rows, half), BF16), pltpu.VMEM((parts, rows, half), BF16),
            pltpu.VMEM((major, rows, half), BF16), pltpu.VMEM((major, rows, half), BF16),
            pltpu.VMEM((major, rows, half), BF16), dma(()), dma(()), dma(()),
            dma((major,)), dma((major,)), dma((major,)), dma((major,)),
        ]


def gather_kernel(groups, parts, *refs):
    w_ref, st_ref = refs[:2]
    vec_refs = refs[2:11]
    (wg_ref, sg_ref, small_ref, fcb_ref, own, vg,
     v_send, v_recv, s_send, s_recv, w_send, w_recv, w_own) = refs[11:]
    p, f = lax.axis_index("sp"), lax.axis_index("fsdp")
    spread = Spread(w_ref, wg_ref, parts, w_send, w_recv, w_own)

    greet(groups, parts)
    piece = vec_refs[0].shape[1]
    runs, bits = vec_refs[8].shape
    own[...] = jnp.zeros_like(own)
    for k in range(8):
        own[k : k + 1, 0:piece] = vec_refs[k][...].astype(F32)
    own[8 : 8 + runs, 0:bits] = vec_refs[8][...].astype(F32)
    vg[f] = own[...]
    sg_ref[p] = st_ref[...]
    greeted(groups, parts)

    copies = []

    def go(copy):
        copy.start()
        copies.append(copy)

    spread.start()
    for k, q in enumerate(others(p, groups)):
        go(remote(st_ref, sg_ref.at[p], s_send.at[k], s_recv.at[p], peer(q, f)))
    for k, g in enumerate(others(f, parts)):
        go(remote(own, vg.at[f], v_send.at[k], v_recv.at[f], peer(p, g)))
    for k in range(1, parts // 2):
        spread.relay(k)
    for k in range(parts // 2):
        spread.relay_twin(k)
    for g in others(f, parts):
        remote(own, vg.at[g], v_send.at[0], v_recv.at[g], peer(p, g)).wait_recv()
    for g in range(parts):
        small_ref[:, g * piece : (g + 1) * piece] = vg[g, 0:8, 0:piece]
        for k in range(runs):
            at = (g * runs + k) * bits
            fcb_ref[:, at : at + bits] = vg[g, 8 + k : 9 + k, 0:bits]
    for q in others(p, groups):
        remote(st_ref, sg_ref.at[q], s_send.at[0], s_recv.at[q], peer(q, f)).wait_recv()
    spread.finish()
    for copy in copies:
        copy.wait_send()


def gather_front(w_qkv, starts, vectors, groups, parts):
    rows, triple = w_qkv.shape
    starts = starts.reshape(-1, 128)
    fc = vectors[8].shape[0]
    vectors = [v.reshape(1, -1) for v in vectors[:8]] + [vectors[8].reshape(-1, min(fc, 128))]
    dma = pltpu.SemaphoreType.DMA
    vmem = pl.BlockSpec(memory_space=pltpu.VMEM)
    return pl.pallas_call(
        functools.partial(gather_kernel, groups, parts),
        out_shape=(
            jax.ShapeDtypeStruct((parts, rows, triple), BF16),
            jax.ShapeDtypeStruct((groups,) + starts.shape, jnp.int32),
            jax.ShapeDtypeStruct((8, parts * vectors[0].shape[1]), F32),
            jax.ShapeDtypeStruct((1, parts * fc), F32),
        ),
        in_specs=[vmem] * 11,
        out_specs=[vmem] * 4,
        scratch_shapes=[
            pltpu.VMEM((16, 128), F32), pltpu.VMEM((parts, 16, 128), F32),
            dma((parts,)), dma((parts,)), dma((groups,)), dma((groups,)),
            *Spread.semaphores(parts),
        ],
        compiler_params=pltpu.CompilerParams(
            vmem_limit_bytes=VMEM_LIMIT, collective_id=0, has_side_effects=True
        ),
        name="gather_front",
    )(w_qkv, starts, *vectors)


GAIN_ONE, BIAS_ONE, Q_BIAS, V_BIAS, OUT_BIAS, GAIN_TWO, BIAS_TWO, PROJ_BIAS = range(8)


def qkv_kernel(rows, groups, x_ref, w_ref, small_ref, o_ref):
    width = x_ref.shape[-1] // groups
    model = x_ref.shape[-1]
    normed, _ = normalize(x_ref[...].astype(F32))
    small = small_ref[...]
    act = (normed * small[GAIN_ONE : GAIN_ONE + 1] + small[BIAS_ONE : BIAS_ONE + 1]).astype(BF16)
    weight = weight_rows(w_ref, rows)
    for part, row in ((0, Q_BIAS), (1, None), (2, V_BIAS)):
        out = dot(act, weight[:, part * model : (part + 1) * model])
        if row is not None:
            out = out + small[row : row + 1]
        out = out.astype(BF16)
        for g in range(groups):
            o_ref[g, part] = out[:, g * width : (g + 1) * width]


def project_qkv(x, weight, rows, small, groups, tile=256):
    length, model = x.shape
    width = model // groups
    return pl.pallas_call(
        functools.partial(qkv_kernel, rows, groups),
        out_shape=jax.ShapeDtypeStruct((groups, 3, length, width), BF16),
        grid=(length // tile,),
        in_specs=[
            pl.BlockSpec((tile, model), lambda i: (i, 0)),
            whole(weight.shape),
            whole(small.shape),
        ],
        out_specs=pl.BlockSpec((groups, 3, tile, width), lambda i: (0, 0, i, 0)),
        compiler_params=params(),
        cost_estimate=cost(6 * length * model * model, 10 * length * model),
        name="project_qkv",
    )(x, weight, small)


def lane_mask(h, x):
    lane = lax.broadcasted_iota(jnp.int32, x.shape, 1)
    return jnp.where(lane // HEAD_DIM == h, x, jnp.zeros_like(x))


def triangle(index, size):
    row = sum((index >= m * (m + 1) // 2).astype(jnp.int32) for m in range(1, size))
    return row, index - row * (row + 1) // 2


def triangle_by_column(index, size):
    starts = [c * (2 * size + 1 - c) // 2 for c in range(size)]
    col = sum((index >= at).astype(jnp.int32) for at in starts[1:])
    return col + index - col * (2 * size + 1 - col) // 2, col


def pick(cond, this, other):
    return jnp.where(cond, this, other)


class Place:
    def __init__(self, groups, count):
        self.p, self.f = lax.axis_index("sp"), lax.axis_index("fsdp")
        self.side = self.p // 2
        self.core = lax.rem(self.p, 2)
        self.mate = self.p + 1 - 2 * self.core
        far = (1 - self.side) * 2
        self.far = (far + self.core, far + 1 - self.core)
        self.groups = groups
        self.count = count
        self.half = 2 * count
        self.near_block = self.side * self.half
        self.far_block = (1 - self.side) * self.half

    def peer(self, q):
        return peer(q, self.f)

    def others(self):
        return others(self.p, self.groups)

    def meet(self):
        barrier = pltpu.get_barrier_semaphore()
        for q in self.others():
            pl.semaphore_signal(
                barrier, inc=1, device_id=self.peer(q), device_id_type=pl.DeviceIdType.MESH
            )
        pl.semaphore_wait(barrier, self.groups - 1)


def rows_of(block, count, size):
    return block // count, pl.ds(pl.multiple_of(lax.rem(block, count) * size, size), size)


def mask_of(first, q, k, size, diagonal):
    rows = lax.broadcasted_iota(jnp.int32, (size, size), 0)
    ok = rows >= first - k * size
    if diagonal:
        ok = ok & (rows <= lax.broadcasted_iota(jnp.int32, (1, size), 1))
    return ok


def attend_kernel(
    size, heads, parts, own_ref, st_ref, *refs
):
    shards, refs = refs[:3], refs[3:]
    (qkv_ref, o_ref, lse_ref, attn_ref), wide, refs = refs[:4], refs[4:7], refs[7:]
    m_sc, l_sc, acc_sc, near_s, near_r, far_s, far_r, out_s, out_r = refs[:9]
    spreads = [
        Spread(shards[n], wide[n], parts, *refs[9 + 3 * n : 12 + 3 * n]) for n in range(3)
    ]
    groups, _, per, _ = own_ref.shape
    count = per // size
    at = Place(groups, count)
    p, side, half = at.p, at.side, at.half
    m_sc[...] = jnp.full_like(m_sc, NEG)
    l_sc[...] = jnp.zeros_like(l_sc)
    acc_sc[...] = jnp.zeros_like(acc_sc)
    greet(groups, parts)
    qkv_ref[p] = own_ref[p]
    greeted(groups, parts)

    near = remote(own_ref.at[at.mate], qkv_ref.at[p], near_s, near_r, at.peer(at.mate))
    near.start()

    def part_of(n):
        n = lax.rem(n + pick(side == 1, 0, count), 3 * count)
        return pick(n < count, 0, 1 + lax.rem(n - count, 2)), pick(n < count, n, (n - count) // 2)

    def far_copy(n, d):
        t, b = part_of(n)
        rows = pl.ds(pl.multiple_of(b * size, size), size)
        return remote(
            own_ref.at[at.far[d], t, rows], qkv_ref.at[p, t, rows], far_s.at[d, n],
            far_r.at[p, t, b], at.peer(at.far[d]),
        )

    for n in range(3 * count):
        for d in range(2):
            far_copy(n, d).start()
    for spread in spreads:
        spread.start()

    def far_wait(t, block):
        src, rows = rows_of(block, count, size)
        there = qkv_ref.at[src, t, rows]
        remote(there, there, far_s.at[0, 0], far_r.at[src, t, lax.rem(block, count)], at.peer(src)).wait_recv()

    def block(q, k, diagonal):
        src, rows = rows_of(q, count, size)
        cols = pl.ds(pl.multiple_of(q * size, size), size)
        ksrc, krows = rows_of(k, count, size)
        query = (qkv_ref[src, 0, rows, :] * HEAD_DIM ** (-0.5)).astype(BF16)
        key = qkv_ref[ksrc, 1, krows, :]
        value = qkv_ref[ksrc, 2, krows, :]
        ok = mask_of(st_ref[:, cols], q, k, size, diagonal)
        for h in range(heads):
            sl = slice(h * HEAD_DIM, (h + 1) * HEAD_DIM)
            s = jnp.where(ok, dot(key, lane_mask(h, query), NT), NEG)
            m_old = m_sc[h : h + 1, cols]
            m_new = jnp.maximum(m_old, jnp.max(s, 0, keepdims=True))
            e = jnp.exp(s - m_new)
            alpha = jnp.exp(m_old - m_new)
            l_sc[h : h + 1, cols] = l_sc[h : h + 1, cols] * alpha + jnp.sum(e, 0, keepdims=True)
            m_sc[h : h + 1, cols] = m_new
            acc_sc[sl, cols] = acc_sc[sl, cols] * alpha + dot(value[:, sl], e.astype(BF16), TN)

    def out_copy(q):
        src, rows = rows_of(q, count, size)
        return remote(
            o_ref.at[src, rows], attn_ref.at[p, rows], out_s.at[q], out_r.at[p, lax.rem(q, count)],
            at.peer(src),
        )

    def finish(q):
        src, rows = rows_of(q, count, size)
        cols = pl.ds(pl.multiple_of(q * size, size), size)
        parts = []
        for h in range(heads):
            sl = slice(h * HEAD_DIM, (h + 1) * HEAD_DIM)
            total = l_sc[h : h + 1, cols]
            parts.append(acc_sc[sl, cols] * (1.0 / total))
            lse_ref[h : h + 1, cols] = m_sc[h : h + 1, cols] + jnp.log(total)
        out = jnp.concatenate(parts, 0).T.astype(BF16)
        o_ref[src, rows] = out

        @pl.when(src == p)
        def _():
            attn_ref[p, rows] = out

        @pl.when(src != p)
        def _():
            out_copy(q).start()

    small = count * (count + 1) // 2
    cross = 2 * small + count * count
    bulk = cross + half * half
    end = bulk + half * (half + 1) // 2

    @pl.loop(0, end)
    def _(step):
        second = step >= small
        row, col = triangle(step - pick(second, small, 0), count)
        base = pick(second, at.mate, p) * count
        q, k = base + row, base + col
        c = step - 2 * small
        in_cross = (step >= 2 * small) & (step < cross)
        q = pick(in_cross, at.near_block + count + c // count, q)
        k = pick(in_cross, at.near_block + lax.rem(c, count), k)
        c = step - cross
        in_bulk = (step >= cross) & (step < bulk)
        outer, inner = c // half, lax.rem(c, half)
        outer = lax.rem(outer, 2) * count + outer // 2
        q = pick(in_bulk, half + pick(side == 0, outer, inner), q)
        k = pick(in_bulk, pick(side == 0, inner, outer), k)
        in_last = step >= bulk
        row, col = triangle(step - bulk, half)
        q = pick(in_last, at.far_block + row, q)
        k = pick(in_last, at.far_block + col, k)

        @pl.when(step == small)
        def _():
            near.wait_recv()

        starts_outer = in_bulk & (inner == 0)
        starts_row = in_last & (col == 0)

        @pl.when((starts_outer & (side == 0)) | (starts_row & (side == 1)))
        def _():
            far_wait(0, q)

        @pl.when((starts_outer & (side == 1)) | (starts_row & (side == 0)))
        def _():
            far_block = pick(in_bulk, k, q)
            far_wait(1, far_block)
            far_wait(2, far_block)

        @pl.when(q == k)
        def _():
            block(q, k, True)

        @pl.when(q != k)
        def _():
            block(q, k, False)

        major = parts // 2
        for n in range(1, major):
            @pl.when(step == end // 4 + (n - 1) * (end // 4) // (major - 1))
            def _(n=n):
                for spread in spreads:
                    spread.relay(n)
        for n in range(major):
            @pl.when(step == end // 2 + 1 + n * (end // 2 - 2) // major)
            def _(n=n):
                for spread in spreads:
                    spread.relay_twin(n)

        near_done = step == pick(side == 0, cross, bulk) - 1
        low = pick(near_done, at.near_block, q)
        high = pick(near_done, at.near_block + half, pick(in_last & (q == k), q + 1, q))
        pl.loop(low, high)(finish)

    for q in at.others():
        for b in range(count):
            rows = pl.ds(b * size, size)
            there = attn_ref.at[q, rows]
            remote(there, there, out_s.at[0], out_r.at[q, b], at.peer(q)).wait_recv()
            out_copy(q * count + b).wait_send()
    near.wait_send()
    for n in range(3 * count):
        for d in range(2):
            far_copy(n, d).wait_send()
    for spread in spreads:
        spread.finish()


def attention_forward(own, starts, shards, parts, size=512):
    groups, _, per, width = own.shape
    length = groups * per
    heads = width // HEAD_DIM
    count = per // size
    dma = pltpu.SemaphoreType.DMA
    vmem = pl.BlockSpec(memory_space=pltpu.VMEM)
    return pl.pallas_call(
        functools.partial(attend_kernel, size, heads, parts),
        out_shape=(
            jax.ShapeDtypeStruct(own.shape, BF16),
            jax.ShapeDtypeStruct((groups, per, width), BF16),
            jax.ShapeDtypeStruct((8, length), F32),
            jax.ShapeDtypeStruct((groups, per, width), BF16),
            *[jax.ShapeDtypeStruct((parts,) + shard.shape, BF16) for shard in shards],
        ),
        in_specs=[vmem] * 5,
        out_specs=[vmem] * 4 + [pl.BlockSpec(memory_space=pl.ANY)] * 3,
        scratch_shapes=[pltpu.VMEM((8, length), F32)] * 2 + [
            pltpu.VMEM((width, length), F32), dma(()), dma(()), dma((2, 3 * count)),
            dma((groups, 3, count)), dma((groups * count,)), dma((groups, count)),
        ] + Spread.semaphores(parts) * 3,
        compiler_params=pltpu.CompilerParams(
            vmem_limit_bytes=VMEM_LIMIT, collective_id=2, has_side_effects=True
        ),
        cost_estimate=cost(4 * length * length * width, 16 * length * width, length * length),
        name="attention_forward",
    )(own, starts, *shards)


def attend_back_kernel(
    size, heads, parts, qkv_ref, own_ref, o_ref, lse_ref, st_ref, ga_ref, gp_ref,
    out_ref, fa_ref, fp_ref,
    do_sc, delta_sc, dqt_sc, dk_sc, dv_sc, stage, near_s, near_r, far_s, far_r, out_s, out_r, *refs
):
    folds = [Fold(ga_ref, fa_ref, parts, *refs[:12]), Fold(gp_ref, fp_ref, parts, *refs[12:])]
    groups, _, per, _ = qkv_ref.shape
    count = per // size
    at = Place(groups, count)
    p, side, half = at.p, at.side, at.half
    scale = HEAD_DIM ** (-0.5)
    dqt_sc[...] = jnp.zeros_like(dqt_sc)
    dk_sc[...] = jnp.zeros_like(dk_sc)
    dv_sc[...] = jnp.zeros_like(dv_sc)
    greet(groups, parts)
    do_sc[p] = own_ref[p]
    greeted(groups, parts)

    near = remote(own_ref.at[at.mate], do_sc.at[p], near_s, near_r, at.peer(at.mate))
    near.start()

    def far_copy(b, d):
        rows = pl.ds(b * size, size)
        return remote(
            own_ref.at[at.far[d], rows], do_sc.at[p, rows], far_s.at[d, b], far_r.at[p, b],
            at.peer(at.far[d]),
        )

    for b in range(count):
        for d in range(2):
            far_copy(b, d).start()
    for fold in folds:
        fold.start()

    def columns(block):
        return pl.ds(pl.multiple_of(block * size, size), size)

    def prepare(q):
        src, rows = rows_of(q, count, size)
        prod = (do_sc[src, rows].astype(F32) * o_ref[src, rows].astype(F32)).T
        for h in range(heads):
            sl = slice(h * HEAD_DIM, (h + 1) * HEAD_DIM)
            delta_sc[h : h + 1, columns(q)] = jnp.sum(prod[sl], 0, keepdims=True)

    def block(q, k, diagonal):
        src, rows = rows_of(q, count, size)
        cols = columns(q)
        ksrc, krows = rows_of(k, count, size)
        query = (qkv_ref[src, 0, rows, :] * scale).astype(BF16)
        grad = do_sc[src, rows]
        key = qkv_ref[ksrc, 1, krows, :]
        value = qkv_ref[ksrc, 2, krows, :]
        ok = mask_of(st_ref[:, cols], q, k, size, diagonal)
        dv = dk = None
        for h in range(heads):
            sl = slice(h * HEAD_DIM, (h + 1) * HEAD_DIM)
            query_h, grad_h = lane_mask(h, query), lane_mask(h, grad)
            s = jnp.where(ok, dot(key, query_h, NT), NEG)
            e = jnp.exp(s - lse_ref[h : h + 1, cols])
            ds = (e * (dot(value, grad_h, NT) - delta_sc[h : h + 1, cols])).astype(BF16)
            dvh = dot(e.astype(BF16), grad_h)
            dkh = dot(ds, query_h)
            dv = dvh if dv is None else dv + dvh
            dk = dkh if dk is None else dk + dkh
            dqt_sc[sl, cols] += dot(key[:, sl], ds, TN)
        dv_sc[cols_of(k), :] += dv
        dk_sc[cols_of(k), :] += dk

    cols_of = columns

    def out_copy(block, part):
        src, rows = rows_of(block, count, size)
        return remote(
            stage.at[src, part, rows], out_ref.at[p, part, rows], out_s.at[block, part],
            out_r.at[p, part, lax.rem(block, count)], at.peer(src),
        )

    def give(block, part, value):
        src, rows = rows_of(block, count, size)

        @pl.when(src == p)
        def _():
            out_ref[p, part, rows] = value

        @pl.when(src != p)
        def _():
            stage[src, part, rows] = value
            out_copy(block, part).start()

    def finish_query(q):
        give(q, 0, (dqt_sc[:, columns(q)] * scale).T.astype(BF16))

    def finish_key(k):
        give(k, 1, dk_sc[columns(k), :].astype(BF16))
        give(k, 2, dv_sc[columns(k), :].astype(BF16))

    small = count * (count + 1) // 2
    far = 2 * small
    bulk = far + half * (half + 1) // 2
    cross = bulk + half * half
    end = cross + count * count

    @pl.loop(0, end)
    def _(step):
        second = step >= small
        row, col = triangle(step - pick(second, small, 0), count)
        base = pick(second, at.mate, p) * count
        q, k = base + row, base + col
        in_far = (step >= far) & (step < bulk)
        row, column = triangle_by_column(step - far, half)
        q = pick(in_far, at.far_block + row, q)
        k = pick(in_far, at.far_block + column, k)
        c = step - bulk
        in_bulk = (step >= bulk) & (step < cross)
        outer, inner = c // half, lax.rem(c, half)
        q = pick(in_bulk, half + pick(side == 0, outer, inner), q)
        k = pick(in_bulk, pick(side == 0, inner, outer), k)
        c = step - cross
        in_cross = step >= cross
        q = pick(in_cross, at.near_block + count + c // count, q)
        k = pick(in_cross, at.near_block + lax.rem(c, count), k)

        @pl.when(step == small)
        def _():
            near.wait_recv()

        @pl.when(in_far & (column == 0))
        def _():
            src, rows = rows_of(q, count, size)
            there = do_sc.at[src, rows]
            remote(there, there, far_s.at[0, 0], far_r.at[src, lax.rem(q, count)], at.peer(src)).wait_recv()

        @pl.when(((step < far) & (col == 0)) | (in_far & (column == 0)))
        def _():
            prepare(q)

        @pl.when(q == k)
        def _():
            block(q, k, True)

        @pl.when(q != k)
        def _():
            block(q, k, False)

        for n, fold in enumerate(folds):
            pl.when(step == end // 8 + n)(fold.pairs)
            pl.when(step == end * 3 // 8 + n * (end // 6))(fold.planes)
            pl.when(step == end * 5 // 8 + n * (end // 4))(fold.lines)

        column_done = in_far & (row == half - 1)
        outer_done = in_bulk & (inner == half - 1)
        done = step == end - 1
        near_low, near_high = at.near_block, at.near_block + half
        query = (column_done & (side == 1)) | (outer_done & (side == 0))
        block_id = at.far_block + pick(in_far, column, outer)
        pl.loop(
            pick(done, near_low, block_id),
            pick(done, near_high, pick(query, block_id + 1, block_id)),
        )(finish_query)
        key = (column_done & (side == 0)) | (outer_done & (side == 1))
        pl.loop(
            pick(done, near_low, block_id),
            pick(done, near_high, pick(key, block_id + 1, block_id)),
        )(finish_key)

    for q in at.others():
        for b in range(count):
            for part in range(3):
                there = out_ref.at[q, part, pl.ds(b * size, size)]
                remote(there, there, out_s.at[0, 0], out_r.at[q, part, b], at.peer(q)).wait_recv()
                out_copy(q * count + b, part).wait_send()
    near.wait_send()
    for b in range(count):
        for d in range(2):
            far_copy(b, d).wait_send()


def attention_backward(qkv, grad, out, lse, starts, g_a, g_p, size=512):
    groups, _, per, width = qkv.shape
    length = groups * per
    heads = width // HEAD_DIM
    count = per // size
    parts = g_a.shape[0]
    dma = pltpu.SemaphoreType.DMA
    vmem = pl.BlockSpec(memory_space=pltpu.VMEM)
    return pl.pallas_call(
        functools.partial(attend_back_kernel, size, heads, parts),
        out_shape=(
            jax.ShapeDtypeStruct(qkv.shape, BF16),
            jax.ShapeDtypeStruct((g_a.shape[1], g_a.shape[2] // 2), BF16),
            jax.ShapeDtypeStruct((g_p.shape[1], g_p.shape[2] // 2), BF16),
        ),
        in_specs=[vmem] * 5 + [pl.BlockSpec(memory_space=pl.ANY)] * 2,
        out_specs=[vmem] * 3,
        scratch_shapes=[
            pltpu.VMEM((groups, per, width), BF16), pltpu.VMEM((8, length), F32),
            pltpu.VMEM((width, length), F32), pltpu.VMEM((length, width), F32),
            pltpu.VMEM((length, width), F32), pltpu.VMEM(qkv.shape, BF16),
            dma(()), dma(()), dma((2, count)), dma((groups, count)),
            dma((groups * count, 3)), dma((groups, 3, count)),
            *Fold.scratch(*g_a.shape), *Fold.scratch(*g_p.shape),
        ],
        compiler_params=pltpu.CompilerParams(
            vmem_limit_bytes=VMEM_LIMIT, collective_id=3, has_side_effects=True
        ),
        cost_estimate=cost(10 * length * length * width, 24 * length * width, length * length),
        name="attention_backward",
    )(qkv, grad, out, lse, starts, g_a, g_p)


def put(ref, first, value):
    @pl.when(first)
    def _():
        ref[...] = value

    @pl.when(jnp.logical_not(first))
    def _():
        ref[...] += value


def column_sum(x):
    return jnp.sum(x, 0, keepdims=True)


def middle_kernel(
    groups, x_ref, attn_ref, wo_ref, wf_ref, wp_ref, small_ref, fcb_ref, cot_ref,
    out_ref, resid_ref, ga_ref, gwa_ref, gwp_ref, gs_ref, gwa_sc, gwp_sc,
):
    first = pl.program_id(0) == 0
    model = x_ref.shape[-1]
    width = model // groups
    small = small_ref[...]
    w_out = weight_rows(wo_ref, wo_ref.shape[1])
    w_fc = weight_rows(wf_ref, wf_ref.shape[1])
    w_proj = weight_rows(wp_ref, wp_ref.shape[1])
    attn = jnp.concatenate([attn_ref[g] for g in range(groups)], 1)
    resid = x_ref[...].astype(F32) + dot(attn, w_out) + small[OUT_BIAS : OUT_BIAS + 1]
    normed, inverse = normalize(resid)
    gain = small[GAIN_TWO : GAIN_TWO + 1]
    act = (normed * gain + small[BIAS_TWO : BIAS_TWO + 1]).astype(BF16)
    hidden = dot(act, w_fc) + fcb_ref[...]
    sig = 1.0 / (1.0 + jnp.exp(-1.702 * hidden))
    gelu = hidden * sig
    slope = sig + 1.702 * gelu * (1.0 - sig)
    gelu = gelu.astype(BF16)
    out_ref[...] = (resid + dot(gelu, w_proj) + small[PROJ_BIAS : PROJ_BIAS + 1]).astype(BF16)
    up = cot_ref[...]
    put(gwp_sc, first, dot(gelu, up, TN))
    grad_hidden = dot(up, w_proj, NT) * slope
    low = grad_hidden.astype(BF16)
    put(gwa_sc.at[:, model:], first, dot(act, low, TN))
    grad_act = dot(low, w_fc, NT)
    up = up.astype(F32)
    grad_resid = up + normalize_back(grad_act * gain, normed, inverse)
    resid_ref[...] = grad_resid
    resid_low = grad_resid.astype(BF16)
    put(gwa_sc.at[:, 0:model], first, dot(attn, resid_low, TN))
    grad_attn = dot(resid_low, w_out, NT).astype(BF16)
    for g in range(groups):
        ga_ref[g] = grad_attn[:, g * width : (g + 1) * width]
    put(gs_ref.at[0:1, :], first, column_sum(grad_hidden))
    put(gs_ref.at[1:2, 0:model], first, column_sum(grad_resid))
    put(gs_ref.at[2:3, 0:model], first, column_sum(grad_act * normed))
    put(gs_ref.at[3:4, 0:model], first, column_sum(grad_act))
    put(gs_ref.at[4:5, 0:model], first, column_sum(up))

    @pl.when(pl.program_id(0) == pl.num_programs(0) - 1)
    def _():
        gwa_ref[...] = gwa_sc[...].astype(BF16)
        gwp_ref[...] = gwp_sc[...].astype(BF16)


def middle(x, attn, w_out, w_fc, w_proj, small, fc_bias, cotangent, tile=256):
    length, model = x.shape
    groups = attn.shape[0]
    hid = w_fc.shape[2]
    rows = pl.BlockSpec((tile, model), lambda i: (i, 0))
    slabs = pl.BlockSpec((groups, tile, model // groups), lambda i: (0, i, 0))
    return pl.pallas_call(
        functools.partial(middle_kernel, groups),
        out_shape=(
            jax.ShapeDtypeStruct((length, model), BF16),
            jax.ShapeDtypeStruct((length, model), F32),
            jax.ShapeDtypeStruct(attn.shape, BF16),
            jax.ShapeDtypeStruct((model, model + hid), BF16),
            jax.ShapeDtypeStruct((hid, model), BF16),
            jax.ShapeDtypeStruct((8, hid), F32),
        ),
        grid=(length // tile,),
        in_specs=[rows, slabs, whole(w_out.shape), whole(w_fc.shape), whole(w_proj.shape), whole(small.shape),
                  whole(fc_bias.shape), rows],
        out_specs=[rows, rows, slabs, whole((model, model + hid)),
                   whole((hid, model)), whole((8, hid))],
        scratch_shapes=[pltpu.VMEM((model, model + hid), F32), pltpu.VMEM((hid, model), F32)],
        compiler_params=params(),
        cost_estimate=cost(12 * length * model * hid + 6 * length * model * model,
                           16 * model * hid, length * hid),
        name="middle",
    )(x, attn, w_out, w_fc, w_proj, small, fc_bias, cotangent)


def last_kernel(
    rows, parts, chunk, x_ref, g_ref, resid_ref, w_ref, small_ref, gs_in, fa_ref, fp_ref,
    gt_ref, gw_ref, gv_ref, go_ref, gf_ref, gp_ref,
    xa, xp, fulla, fullp, xs, xr, ys, yr, acc, out, vec, mine, vsend, vpart, low, r1, s2, r2, keep, s3, r3,
    v1s, v1r, v2s, v2r, c1s, c1r, c2s, c2r, c3s, c3r, c4s, c4r,
):
    step = pl.program_id(0)
    first = step == 0
    groups = g_ref.shape[0]
    model = x_ref.shape[-1]
    p, f = lax.axis_index("sp"), lax.axis_index("fsdp")

    @pl.when(first)
    def _():
        greet(groups, parts)

    core = lax.rem(p, 2)
    side = p // 2
    mate = p + 1 - 2 * core
    across = p + groups // 2 - side * groups
    cross = [
        remote(src, dst, xs.at[n], xr.at[n], peer(across, f))
        for n, (src, dst) in enumerate(((fa_ref, xa), (fp_ref, xp)))
    ]

    @pl.when(step == 1)
    def _():
        greeted(groups, parts)
        for copy in cross:
            copy.start()

    small = small_ref[...]
    normed, inverse = normalize(x_ref[...].astype(F32))
    gain = small[GAIN_ONE : GAIN_ONE + 1]
    act = (normed * gain + small[BIAS_ONE : BIAS_ONE + 1]).astype(BF16)
    grad = jnp.concatenate([g_ref[g, part] for part in range(3) for g in range(groups)], 1)
    put(acc, first, dot(act, grad, TN))
    grad_act = dot(grad, weight_rows(w_ref, rows), NT)
    gt_ref[...] = (
        resid_ref[...] + normalize_back(grad_act * gain, normed, inverse)
    ).astype(BF16)
    put(vec.at[0:1], first, column_sum(grad_act * normed))
    put(vec.at[1:2], first, column_sum(grad_act))
    put(vec.at[2:3], first, column_sum(grad[:, 0:model].astype(F32)))
    put(vec.at[3:4], first, column_sum(grad[:, 2 * model :].astype(F32)))

    @pl.when(step == pl.num_programs(0) - 1)
    def _():
        shard = acc.shape[0] // parts
        half = acc.shape[1] // 2
        quarter = half // 2
        count = quarter // chunk

        def lane(c, s, k):
            return pl.ds(pl.multiple_of(c * half + s * quarter + k * chunk, 128), chunk)

        copies = []

        def go(copy):
            copy.start()
            copies.append(copy)

        low[...] = acc[...].astype(BF16)
        vec[4:8, :] = gs_in[1:5, 0:model]
        piece = model // parts
        fc = gs_in.shape[1] // parts
        bits = min(128, fc)
        vsend[...] = jnp.zeros_like(vsend)
        for g in range(parts):
            vsend[g, 0:8, 0:piece] = vec[:, g * piece : (g + 1) * piece]
            for k in range(fc // bits):
                at = g * fc + k * bits
                vsend[g, 8 + k : 9 + k, 0:bits] = gs_in[0:1, at : at + bits]

        for k in range(count):
            for s in range(2):
                go(remote(low.at[:, lane(1 - core, s, k)], r1.at[k, s], c1s.at[k, s], c1r.at[k, s],
                          peer(mate, f)))
        for n, g in enumerate(others(f, parts)):
            go(remote(vsend.at[g], vpart.at[f], v1s.at[n], v1r.at[f], peer(p, g)))
        for k in range(count):
            for s in range(2):
                remote(r1.at[k, s], r1.at[k, s], c1s.at[k, s], c1r.at[k, s], peer(mate, f)).wait_recv()
            s2[k] = (acc[:, lane(core, 1 - side, k)] + r1[k, 1 - side].astype(F32)).astype(BF16)
            go(remote(s2.at[k], r2.at[k], c2s.at[k], c2r.at[k], peer(across, f)))
        folded = []
        for n, (mine_ref, theirs, full) in enumerate(((fa_ref, xa, fulla), (fp_ref, xp, fullp))):
            cross[n].wait()
            wide = mine_ref.shape[1]
            here = full.at[:, pl.ds(pl.multiple_of(core * wide, 128), wide)]
            there = full.at[:, pl.ds(pl.multiple_of((1 - core) * wide, 128), wide)]
            here[...] = mine_ref[...].astype(F32) + theirs[...].astype(F32)
            go(remote(here, here, ys.at[n], yr.at[n], peer(mate, f)))
            folded.append(remote(there, there, ys.at[n], yr.at[n], peer(mate, f)))
        for k in range(count):
            remote(s2.at[k], r2.at[k], c2s.at[k], c2r.at[k], peer(across, f)).wait_recv()
            total = acc[:, lane(core, side, k)] + r1[k, side].astype(F32) + r2[k].astype(F32)
            keep[k] = total
            s3[k] = total.astype(BF16)
            for n, g in enumerate(others(f, parts)):
                rows_of = pl.ds(pl.multiple_of(g * shard, shard), shard)
                go(remote(s3.at[k, rows_of], r3.at[k, f], c3s.at[k, n], c3r.at[k, f], peer(p, g)))
        for g in others(f, parts):
            remote(vsend.at[g], vpart.at[g], v1s.at[0], v1r.at[g], peer(p, g)).wait_recv()
        total = vsend[f]
        for g in others(f, parts):
            total = total + vpart[g]
        mine[p] = total
        for n, q in enumerate(others(p, groups)):
            go(remote(mine.at[p], mine.at[p], v2s.at[n], v2r.at[p], peer(q, f)))
        for k in range(count):
            for g in others(f, parts):
                remote(r3.at[k, g], r3.at[k, g], c3s.at[k, 0], c3r.at[k, g], peer(p, g)).wait_recv()
            total = keep[k, pl.ds(pl.multiple_of(f * shard, shard), shard)]
            for g in others(f, parts):
                total = total + r3[k, g].astype(F32)
            out[:, lane(core, side, k)] = total
            for n, q in enumerate(others(p, groups)):
                there = out.at[:, lane(core, side, k)]
                go(remote(there, there, c4s.at[k, n], c4r.at[k, p], peer(q, f)))
        for q in others(p, groups):
            remote(mine.at[q], mine.at[q], v2s.at[0], v2r.at[q], peer(q, f)).wait_recv()
        total = mine[0]
        for q in range(1, groups):
            total = total + mine[q]
        gv_ref[...] = total
        for k in range(count):
            for q in others(p, groups):
                there = out.at[:, lane(lax.rem(q, 2), q // 2, k)]
                remote(there, there, c4s.at[k, 0], c4r.at[k, q], peer(q, f)).wait_recv()
        gw_ref[...] = out[...]
        for copy in folded:
            copy.wait_recv()
        go_ref[...] = fulla[:, 0:model]
        gf_ref[...] = fulla[:, model:]
        gp_ref[...] = fullp[...]
        for copy in copies:
            copy.wait_send()


def last(x, grad, resid, weight, rows, small, sums, f_a, f_p, parts, tile=256, chunk=128):
    length, model = x.shape
    groups, _, _, width = grad.shape
    block = pl.BlockSpec((tile, model), lambda i: (i, 0))
    triple = 3 * model
    shard = model // parts
    count = triple // 4 // chunk
    dma = pltpu.SemaphoreType.DMA
    vmem = pltpu.VMEM
    return pl.pallas_call(
        functools.partial(last_kernel, rows, parts, chunk),
        out_shape=(
            jax.ShapeDtypeStruct((length, model), BF16),
            jax.ShapeDtypeStruct((shard, triple), F32),
            jax.ShapeDtypeStruct((16, 128), F32),
            jax.ShapeDtypeStruct((f_a.shape[0], model), F32),
            jax.ShapeDtypeStruct((f_a.shape[0], 2 * f_a.shape[1] - model), F32),
            jax.ShapeDtypeStruct((f_p.shape[0], 2 * f_p.shape[1]), F32),
        ),
        grid=(length // tile,),
        in_specs=[
            block,
            pl.BlockSpec((groups, 3, tile, width), lambda i: (0, 0, i, 0)),
            block,
            whole(weight.shape),
            whole(small.shape),
            whole(sums.shape),
            whole(f_a.shape),
            whole(f_p.shape),
        ],
        out_specs=[
            block, whole((shard, triple)), whole((16, 128)), whole((f_a.shape[0], model)),
            whole((f_a.shape[0], 2 * f_a.shape[1] - model)),
            whole((f_p.shape[0], 2 * f_p.shape[1])),
        ],
        scratch_shapes=[
            vmem(f_a.shape, BF16), vmem(f_p.shape, BF16),
            vmem((f_a.shape[0], 2 * f_a.shape[1]), F32),
            vmem((f_p.shape[0], 2 * f_p.shape[1]), F32),
            dma((2,)), dma((2,)), dma((2,)), dma((2,)),
            vmem((model, triple), F32), vmem((shard, triple), F32), vmem((8, model), F32),
            vmem((groups, 16, 128), F32),
            vmem((parts, 16, 128), F32), vmem((parts, 16, 128), F32),
            vmem((model, triple), BF16), vmem((count, 2, model, chunk), BF16),
            vmem((count, model, chunk), BF16), vmem((count, model, chunk), BF16),
            vmem((count, model, chunk), F32), vmem((count, model, chunk), BF16),
            vmem((count, parts, shard, chunk), BF16),
            dma((parts,)), dma((parts,)), dma((groups,)), dma((groups,)),
            dma((count, 2)), dma((count, 2)), dma((count,)), dma((count,)),
            dma((count, parts)), dma((count, parts)), dma((count, groups)), dma((count, groups)),
        ],
        compiler_params=pltpu.CompilerParams(
            vmem_limit_bytes=VMEM_LIMIT, collective_id=1, has_side_effects=True
        ),
        cost_estimate=cost(12 * length * model * model, 20 * length * model),
        name="last",
    )(x, grad, resid, weight, small, sums, f_a, f_p)


def per_device(
    tokens, starts, norm1_gain, norm1_bias, w_qkv, q_bias, v_bias, w_out, out_bias, norm2_gain,
    norm2_bias, w_fc, fc_bias, w_proj, proj_bias, cotangent,
):
    groups = lax.axis_size("sp")
    parts = lax.axis_size("fsdp")
    rows, triple = w_qkv.shape
    piece = norm1_gain.shape[0]
    x = tokens[0]
    vectors = [
        norm1_gain, norm1_bias, q_bias, v_bias, out_bias, norm2_gain, norm2_bias, proj_bias, fc_bias
    ]
    packed, doc_first, small, fcb = gather_front(w_qkv, starts, vectors, groups, parts)
    doc_first = doc_first.reshape(1, -1)
    if rows % 16 == 0:
        weight, weight_count = packed, rows
    else:
        weight, weight_count = packed.reshape(1, parts * rows, triple), parts * rows
    slabs = project_qkv(x, weight, weight_count, small, groups)
    qkv, out, lse, attn, *wide = attention_forward(
        slabs, doc_first, (w_out, w_fc, w_proj), parts
    )
    wide = [w if w.shape[1] % 16 == 0 else w.reshape(1, -1, w.shape[2]) for w in wide]
    block_out, grad_resid, grad_attn, g_a, g_p, sums = middle(
        x, attn, *wide, small, fcb, cotangent[0]
    )
    grad, f_a, f_p = attention_backward(
        qkv, grad_attn, out, lse, doc_first,
        g_a.reshape(parts, -1, g_a.shape[1]), g_p.reshape(parts, -1, g_p.shape[1]),
    )
    grad_tokens, g_q, g_v, g_out, g_fc, g_p = last(
        x, grad, grad_resid, weight, weight_count, small, sums, f_a, f_p, parts
    )
    vec = [g_v[k, :piece] for k in range(8)]
    fc = fc_bias.shape[0]
    g_fcb = g_v[8 : 8 + max(fc // 128, 1), : min(fc, 128)].reshape(fc)
    return (
        block_out[None], grad_tokens[None], vec[0], vec[1], g_q, vec[2], vec[3],
        g_out, vec[4], vec[5], vec[6], g_fc, g_fcb, g_p, vec[7],
    )


def solution(mesh):
    row, mat = P("fsdp"), P("fsdp", None)
    stream = P("fsdp", "sp", None)
    return jax.shard_map(
        per_device,
        mesh=mesh,
        in_specs=(stream, P("fsdp", "sp"), row, row, mat, row, row, mat, row, row, row, mat, row,
                  mat, row, stream),
        out_specs=(stream, stream, row, row, mat, row, row, mat, row, row, row, mat, row, mat, row),
        check_vma=False,
    )
```

```python
import functools

import jax
import jax.numpy as jnp
from jax import lax
from jax.experimental import pallas as pl
from jax.experimental.pallas import tpu as pltpu
from jax.sharding import PartitionSpec as P

HEAD_DIM = 64
EPSILON = 1e-05
NEG = -1e30
F32 = jnp.float32
BF16 = jnp.bfloat16
RELAY_AT, RELAY_GAP, TWIN_AT = 12, 3, 20
NN = (((1,), (0,)), ((), ()))
NT = (((1,), (1,)), ((), ()))
TN = (((0,), (0,)), ((), ()))
VMEM_LIMIT = 60 << 20


def dot(left, right, dims=NN):
    return lax.dot_general(left, right, dims, preferred_element_type=F32)


def normalize(values):
    centered = values - jnp.mean(values, -1, keepdims=True)
    inverse = lax.rsqrt(jnp.mean(centered * centered, -1, keepdims=True) + EPSILON)
    return centered * inverse, inverse


def normalize_back(incoming, normed, inverse):
    return inverse * (
        incoming
        - jnp.mean(incoming, -1, keepdims=True)
        - normed * jnp.mean(incoming * normed, -1, keepdims=True)
    )


def whole(shape):
    return pl.BlockSpec(shape, lambda *_: (0,) * len(shape))


def params():
    return pltpu.CompilerParams(vmem_limit_bytes=VMEM_LIMIT)


def cost(flops, size, exps=0):
    return pl.CostEstimate(flops=flops, bytes_accessed=size, transcendentals=exps)


def weight_rows(w_ref, rows):
    parts = w_ref.shape[0]
    return w_ref[:, 0:rows, :].reshape(parts * rows, w_ref.shape[2])


def peer(sp, fsdp):
    return {"sp": sp, "fsdp": fsdp}


def remote(src, dst, send, recv, where):
    return pltpu.make_async_remote_copy(
        src_ref=src, dst_ref=dst, send_sem=send, recv_sem=recv,
        device_id=where, device_id_type=pl.DeviceIdType.MESH,
    )


def others(me, count):
    return [lax.rem(me + k, count) for k in range(1, count)]


def greet(groups, parts):
    p, f = lax.axis_index("sp"), lax.axis_index("fsdp")
    barrier = pltpu.get_barrier_semaphore()
    for q in others(p, groups):
        pl.semaphore_signal(barrier, inc=1, device_id=peer(q, f), device_id_type=pl.DeviceIdType.MESH)
    for g in others(f, parts):
        pl.semaphore_signal(barrier, inc=1, device_id=peer(p, g), device_id_type=pl.DeviceIdType.MESH)


def greeted(groups, parts):
    pl.semaphore_wait(pltpu.get_barrier_semaphore(), groups + parts - 2)


class Spread:
    def __init__(self, src, dst, parts, send, recv, own):
        self.src, self.dst, self.send, self.recv, self.own = src, dst, send, recv, own
        self.p, self.f = lax.axis_index("sp"), lax.axis_index("fsdp")
        core = lax.rem(self.p, 2)
        self.mate = self.p + 1 - 2 * core
        self.parts, self.major = parts, parts // 2
        self.a, self.b = self.f // 2, lax.rem(self.f, 2)
        self.twin = self.a * 2 + 1 - self.b
        half = src.shape[1] // 2
        self.lanes = pl.ds(pl.multiple_of(core * half, 128), half)
        self.mate_lanes = pl.ds(pl.multiple_of((1 - core) * half, 128), half)

    def back(self, k):
        return lax.rem(self.a + self.major - k, self.major)

    def block(self, g, lanes=None):
        return self.dst.at[g, :, self.lanes if lanes is None else lanes]

    def first(self, k):
        where = lax.rem(self.a + k, self.major) * 2 + self.b
        where = self.twin if k == 0 else where
        return remote(
            self.src.at[:, self.lanes], self.block(self.f), self.send.at[0, k],
            self.recv.at[0, self.f], peer(self.p, where),
        )

    def to_twin(self, k):
        g = self.back(k) * 2 + self.b
        return remote(
            self.block(g), self.block(g), self.send.at[1, k], self.recv.at[0, g],
            peer(self.p, self.twin),
        )

    def to_mate(self, k, b):
        g = self.back(k) * 2 + b
        slot = k if b is self.b else self.major + k
        return remote(
            self.block(g), self.block(g), self.send.at[2, slot], self.recv.at[1, g],
            peer(self.mate, self.f),
        )

    def keep(self):
        return pltpu.make_async_copy(self.src, self.dst.at[self.f], self.own)

    def start_lines(self):
        self.keep().start()
        for k in range(1, self.major):
            self.first(k).start()

    def start_twin(self):
        self.first(0).start()

    def start(self):
        self.start_lines()
        self.start_twin()

    def relay(self, k):
        self.to_twin(k).wait_recv()
        self.to_twin(k).start()
        self.to_mate(k, self.b).start()

    def relay_twin(self, k):
        other = 1 - self.b
        copy = self.to_mate(k, other)
        g = self.back(k) * 2 + other
        remote(
            self.block(g), self.block(g), self.send.at[1, 0], self.recv.at[0, g],
            peer(self.p, self.twin),
        ).wait_recv()
        copy.start()

    def finish(self):
        for g in others(self.f, self.parts):
            there = self.block(g, self.mate_lanes)
            remote(
                there, there, self.send.at[1, 0], self.recv.at[1, g], peer(self.mate, self.f)
            ).wait_recv()
        for k in range(self.major):
            self.first(k).wait_send()
            self.to_mate(k, 1 - self.b).wait_send()
        for k in range(1, self.major):
            self.to_twin(k).wait_send()
            self.to_mate(k, self.b).wait_send()
        self.keep().wait()

    @staticmethod
    def semaphores(parts):
        dma = pltpu.SemaphoreType.DMA
        return [dma((3, parts)), dma((2, parts)), dma(())]


class Fold:
    def __init__(self, src, out, parts, mine, r1, r2, s2, r3, own, send1, recv1, send2, recv2, send3, recv3):
        self.__dict__.update(
            src=src, out=out, mine=mine, r1=r1, r2=r2, s2=s2, r3=r3, own=own, send1=send1,
            recv1=recv1, send2=send2, recv2=recv2, send3=send3, recv3=recv3,
        )
        self.p, self.f = lax.axis_index("sp"), lax.axis_index("fsdp")
        core = lax.rem(self.p, 2)
        self.mate = self.p + 1 - 2 * core
        self.major = parts // 2
        self.a, self.b = self.f // 2, lax.rem(self.f, 2)
        self.twin = self.a * 2 + 1 - self.b
        half = src.shape[2] // 2
        self.lanes = pl.ds(pl.multiple_of(core * half, 128), half)
        self.mate_lanes = pl.ds(pl.multiple_of((1 - core) * half, 128), half)

    def keep(self):
        return pltpu.make_async_copy(self.src.at[:, :, self.lanes], self.mine, self.own)

    def to_mate(self):
        return remote(
            self.src.at[:, :, self.mate_lanes], self.r1, self.send1, self.recv1,
            peer(self.mate, self.f),
        )

    def to_twin(self, c):
        return remote(
            self.mine.at[c * 2 + 1 - self.b], self.r2.at[c], self.send2.at[c], self.recv2.at[c],
            peer(self.p, self.twin),
        )

    def along(self, k):
        c = lax.rem(self.a + k, self.major)
        return remote(
            self.s2.at[c], self.r3.at[self.a], self.send3.at[c], self.recv3.at[self.a],
            peer(self.p, c * 2 + self.b),
        )

    def start(self):
        self.to_mate().start()
        self.keep().start()

    def pairs(self):
        self.keep().wait()
        self.to_mate().wait()
        self.mine[...] = (self.mine[...].astype(F32) + self.r1[...].astype(F32)).astype(BF16)
        for c in range(self.major):
            self.to_twin(c).start()

    def planes(self):
        for c in range(self.major):
            self.to_twin(c).wait()
            self.s2[c] = (
                self.mine[c * 2 + self.b].astype(F32) + self.r2[c].astype(F32)
            ).astype(BF16)
        for k in range(1, self.major):
            self.along(k).start()

    def lines(self):
        total = self.mine[self.f].astype(F32) + self.r2[self.a].astype(F32)
        for k in range(1, self.major):
            c = lax.rem(self.a + k, self.major)
            remote(
                self.r3.at[c], self.r3.at[c], self.send3.at[0], self.recv3.at[c],
                peer(self.p, self.twin),
            ).wait_recv()
            total = total + self.r3[c].astype(F32)
        self.out[...] = total.astype(BF16)
        for k in range(1, self.major):
            self.along(k).wait_send()

    @staticmethod
    def scratch(parts, rows, lanes):
        dma = pltpu.SemaphoreType.DMA
        major, half = parts // 2, lanes // 2
        return [
            pltpu.VMEM((parts, rows, half), BF16), pltpu.VMEM((parts, rows, half), BF16),
            pltpu.VMEM((major, rows, half), BF16), pltpu.VMEM((major, rows, half), BF16),
            pltpu.VMEM((major, rows, half), BF16), dma(()), dma(()), dma(()),
            dma((major,)), dma((major,)), dma((major,)), dma((major,)),
        ]


GAIN_ONE, BIAS_ONE, Q_BIAS, V_BIAS, OUT_BIAS, GAIN_TWO, BIAS_TWO, PROJ_BIAS = range(8)


def lane_mask(h, x):
    lane = lax.broadcasted_iota(jnp.int32, x.shape, 1)
    return jnp.where(lane // HEAD_DIM == h, x, jnp.zeros_like(x))


def triangle(index, size):
    row = sum((index >= m * (m + 1) // 2).astype(jnp.int32) for m in range(1, size))
    return row, index - row * (row + 1) // 2


def triangle_by_column(index, size):
    starts = [c * (2 * size + 1 - c) // 2 for c in range(size)]
    col = sum((index >= at).astype(jnp.int32) for at in starts[1:])
    return col + index - col * (2 * size + 1 - col) // 2, col


def pick(cond, this, other):
    return jnp.where(cond, this, other)


class Place:
    def __init__(self, groups, count):
        self.p, self.f = lax.axis_index("sp"), lax.axis_index("fsdp")
        self.side = self.p // 2
        self.core = lax.rem(self.p, 2)
        self.mate = self.p + 1 - 2 * self.core
        far = (1 - self.side) * 2
        self.far = (far + self.core, far + 1 - self.core)
        self.groups = groups
        self.count = count
        self.half = 2 * count
        self.near_block = self.side * self.half
        self.far_block = (1 - self.side) * self.half

    def peer(self, q):
        return peer(q, self.f)

    def others(self):
        return others(self.p, self.groups)

    def meet(self):
        barrier = pltpu.get_barrier_semaphore()
        for q in self.others():
            pl.semaphore_signal(
                barrier, inc=1, device_id=self.peer(q), device_id_type=pl.DeviceIdType.MESH
            )
        pl.semaphore_wait(barrier, self.groups - 1)


def rows_of(block, count, size):
    return block // count, pl.ds(pl.multiple_of(lax.rem(block, count) * size, size), size)


def mask_of(first, q, k, size, diagonal):
    rows = lax.broadcasted_iota(jnp.int32, (size, size), 0)
    ok = rows >= first - k * size
    if diagonal:
        ok = ok & (rows <= lax.broadcasted_iota(jnp.int32, (1, size), 1))
    return ok


def front_kernel(size, heads, groups, parts, tile, x_ref, wq_ref, st_in, *refs):
    vec_refs, shards, refs = refs[:9], refs[9:12], refs[12:]
    qkv_ref, o_ref, lse_ref, attn_ref, st_ref, small_ref, fcb_ref, wq_all = refs[:8]
    wide, refs = refs[8:11], refs[11:]
    own_ref, sg, own_vec, vg, m_sc, l_sc, acc_sc = refs[:7]
    v_send, v_recv, s_send, s_recv, near_s, near_r, far_s, far_r, out_s, out_r = refs[7:17]
    first_spread, *spreads = [
        Spread(src, dst, parts, *refs[17 + 3 * n : 20 + 3 * n])
        for n, (src, dst) in enumerate(zip((wq_ref,) + shards, (wq_all,) + wide))
    ]
    per, model = x_ref.shape
    width = model // groups
    count = per // size
    major = parts // 2
    at = Place(groups, count)
    p, f, side, half = at.p, at.f, at.side, at.half

    greet(groups, parts)
    piece = vec_refs[0].shape[1]
    runs, bits = vec_refs[8].shape
    own_vec[...] = jnp.zeros_like(own_vec)
    for k in range(8):
        own_vec[k : k + 1, 0:piece] = vec_refs[k][...].astype(F32)
    own_vec[8 : 8 + runs, 0:bits] = vec_refs[8][...].astype(F32)
    vg[f] = own_vec[...]
    sg[p] = st_in[...]
    m_sc[...] = jnp.full_like(m_sc, NEG)
    l_sc[...] = jnp.zeros_like(l_sc)
    acc_sc[...] = jnp.zeros_like(acc_sc)
    greeted(groups, parts)

    copies = []

    def go(copy):
        copy.start()
        copies.append(copy)

    first_spread.start()
    for k, q in enumerate(at.others()):
        go(remote(st_in, sg.at[p], s_send.at[k], s_recv.at[p], at.peer(q)))
    for k, g in enumerate(others(f, parts)):
        go(remote(own_vec, vg.at[f], v_send.at[k], v_recv.at[f], peer(p, g)))
    for k in range(1, major):
        first_spread.relay(k)
    for k in range(major):
        first_spread.relay_twin(k)
    for g in others(f, parts):
        remote(own_vec, vg.at[g], v_send.at[0], v_recv.at[g], peer(p, g)).wait_recv()
    for g in range(parts):
        small_ref[:, g * piece : (g + 1) * piece] = vg[g, 0:8, 0:piece]
        for k in range(runs):
            lane = (g * runs + k) * bits
            fcb_ref[:, lane : lane + bits] = vg[g, 8 + k : 9 + k, 0:bits]
    for q in at.others():
        remote(st_in, sg.at[q], s_send.at[0], s_recv.at[q], at.peer(q)).wait_recv()
    for q in range(groups):
        for k in range(per // 128):
            lane = q * per + k * 128
            st_ref[:, lane : lane + 128] = sg[q, k : k + 1]
    first_spread.finish()
    for spread in spreads:
        spread.start_lines()

    def far_copy(b, t, d):
        rows = pl.ds(pl.multiple_of(b * size, size), size)
        return remote(
            own_ref.at[at.far[d], t, rows], qkv_ref.at[p, t, rows], far_s.at[d, b, t],
            far_r.at[p, t, b], at.peer(at.far[d]),
        )

    near = remote(own_ref.at[at.mate], qkv_ref.at[p], near_s, near_r, at.peer(at.mate))

    @pl.loop(0, per // tile)
    def _(i):
        rows = pl.ds(pl.multiple_of(i * tile, tile), tile)
        normed, _ = normalize(x_ref[rows].astype(F32))
        small = small_ref[...]
        act = (normed * small[GAIN_ONE : GAIN_ONE + 1] + small[BIAS_ONE : BIAS_ONE + 1]).astype(BF16)
        weight = weight_rows(wq_all, wq_all.shape[1])
        for part, row in ((0, Q_BIAS), (1, None), (2, V_BIAS)):
            out = dot(act, weight[:, part * model : (part + 1) * model])
            if row is not None:
                out = out + small[row : row + 1]
            out = out.astype(BF16)
            for g in range(groups):
                own_ref[g, part, rows] = out[:, g * width : (g + 1) * width]

        @pl.when(lax.rem(i + 1, size // tile) == 0)
        def _():
            for n in range(3):
                for d in range(2):
                    far_copy((i + 1) // (size // tile) - 1, lax.rem(n + pick(side == 1, 0, 1), 3), d).start()

    near.start()
    for spread in spreads:
        spread.start_twin()
    qkv_ref[p] = own_ref[p]

    def far_wait(t, block):
        src, rows = rows_of(block, count, size)
        there = qkv_ref.at[src, t, rows]
        remote(there, there, far_s.at[0, 0, 0], far_r.at[src, t, lax.rem(block, count)], at.peer(src)).wait_recv()

    def block(q, k, diagonal):
        src, rows = rows_of(q, count, size)
        cols = pl.ds(pl.multiple_of(q * size, size), size)
        ksrc, krows = rows_of(k, count, size)
        query = (qkv_ref[src, 0, rows, :] * HEAD_DIM ** (-0.5)).astype(BF16)
        key = qkv_ref[ksrc, 1, krows, :]
        value = qkv_ref[ksrc, 2, krows, :]
        ok = mask_of(st_ref[:, cols], q, k, size, diagonal)
        for h in range(heads):
            sl = slice(h * HEAD_DIM, (h + 1) * HEAD_DIM)
            s = jnp.where(ok, dot(key, lane_mask(h, query), NT), NEG)
            m_old = m_sc[h : h + 1, cols]
            m_new = jnp.maximum(m_old, jnp.max(s, 0, keepdims=True))
            e = jnp.exp(s - m_new)
            alpha = jnp.exp(m_old - m_new)
            l_sc[h : h + 1, cols] = l_sc[h : h + 1, cols] * alpha + jnp.sum(e, 0, keepdims=True)
            m_sc[h : h + 1, cols] = m_new
            acc_sc[sl, cols] = acc_sc[sl, cols] * alpha + dot(value[:, sl], e.astype(BF16), TN)

    def out_copy(q):
        src, rows = rows_of(q, count, size)
        return remote(
            o_ref.at[src, rows], attn_ref.at[p, rows], out_s.at[q], out_r.at[p, lax.rem(q, count)],
            at.peer(src),
        )

    def finish(q):
        src, rows = rows_of(q, count, size)
        cols = pl.ds(pl.multiple_of(q * size, size), size)
        parts = []
        for h in range(heads):
            sl = slice(h * HEAD_DIM, (h + 1) * HEAD_DIM)
            total = l_sc[h : h + 1, cols]
            parts.append(acc_sc[sl, cols] * (1.0 / total))
            lse_ref[h : h + 1, cols] = m_sc[h : h + 1, cols] + jnp.log(total)
        out = jnp.concatenate(parts, 0).T.astype(BF16)
        o_ref[src, rows] = out

        @pl.when(src == p)
        def _():
            attn_ref[p, rows] = out

        @pl.when(src != p)
        def _():
            out_copy(q).start()

    small = count * (count + 1) // 2
    cross = 2 * small + count * count
    bulk = cross + half * half
    end = bulk + half * (half + 1) // 2

    @pl.loop(0, end)
    def _(step):
        second = step >= small
        row, col = triangle(step - pick(second, small, 0), count)
        base = pick(second, at.mate, p) * count
        q, k = base + row, base + col
        c = step - 2 * small
        in_cross = (step >= 2 * small) & (step < cross)
        q = pick(in_cross, at.near_block + count + c // count, q)
        k = pick(in_cross, at.near_block + lax.rem(c, count), k)
        c = step - cross
        in_bulk = (step >= cross) & (step < bulk)
        outer, inner = c // half, lax.rem(c, half)
        outer = lax.rem(outer, 2) * count + outer // 2
        q = pick(in_bulk, half + pick(side == 0, outer, inner), q)
        k = pick(in_bulk, pick(side == 0, inner, outer), k)
        in_last = step >= bulk
        row, col = triangle(step - bulk, half)
        q = pick(in_last, at.far_block + row, q)
        k = pick(in_last, at.far_block + col, k)

        @pl.when(step == small)
        def _():
            near.wait_recv()

        starts_outer = in_bulk & (inner == 0)
        starts_row = in_last & (col == 0)

        @pl.when((starts_outer & (side == 0)) | (starts_row & (side == 1)))
        def _():
            far_wait(0, q)

        @pl.when((starts_outer & (side == 1)) | (starts_row & (side == 0)))
        def _():
            far_block = pick(in_bulk, k, q)
            far_wait(1, far_block)
            far_wait(2, far_block)

        @pl.when(q == k)
        def _():
            block(q, k, True)

        @pl.when(q != k)
        def _():
            block(q, k, False)

        for n in range(1, major):
            @pl.when(step == RELAY_AT + (n - 1) * RELAY_GAP * 2 // (major - 1))
            def _(n=n):
                for spread in spreads:
                    spread.relay(n)
        for n in range(major):
            @pl.when(step == TWIN_AT + n * (end - 1 - TWIN_AT) // (major - 1))
            def _(n=n):
                for spread in spreads:
                    spread.relay_twin(n)

        near_done = step == pick(side == 0, cross, bulk) - 1
        low = pick(near_done, at.near_block, q)
        high = pick(near_done, at.near_block + half, pick(in_last & (q == k), q + 1, q))
        pl.loop(low, high)(finish)

    for q in at.others():
        for b in range(count):
            rows = pl.ds(b * size, size)
            there = attn_ref.at[q, rows]
            remote(there, there, out_s.at[0], out_r.at[q, b], at.peer(q)).wait_recv()
            out_copy(q * count + b).wait_send()
    near.wait_send()
    for b in range(count):
        for t in range(3):
            for d in range(2):
                far_copy(b, t, d).wait_send()
    for copy in copies:
        copy.wait_send()
    for spread in spreads:
        spread.finish()


def front(x, w_qkv, starts, vectors, shards, groups, parts, size=512, tile=256):
    per, model = x.shape
    length = groups * per
    width = model // groups
    heads = width // HEAD_DIM
    count = per // size
    starts = starts.reshape(-1, 128)
    fc = vectors[8].shape[0]
    piece = vectors[0].shape[0]
    vectors = [v.reshape(1, -1) for v in vectors[:8]] + [vectors[8].reshape(-1, min(fc, 128))]
    dma = pltpu.SemaphoreType.DMA
    vmem = pl.BlockSpec(memory_space=pltpu.VMEM)
    slabs = (groups, 3, per, width)
    return pl.pallas_call(
        functools.partial(front_kernel, size, heads, groups, parts, tile),
        out_shape=(
            jax.ShapeDtypeStruct(slabs, BF16),
            jax.ShapeDtypeStruct((groups, per, width), BF16),
            jax.ShapeDtypeStruct((8, length), F32),
            jax.ShapeDtypeStruct((groups, per, width), BF16),
            jax.ShapeDtypeStruct((1, length), jnp.int32),
            jax.ShapeDtypeStruct((8, parts * piece), F32),
            jax.ShapeDtypeStruct((1, parts * fc), F32),
            jax.ShapeDtypeStruct((parts,) + w_qkv.shape, BF16),
            *[jax.ShapeDtypeStruct((parts,) + shard.shape, BF16) for shard in shards],
        ),
        in_specs=[vmem] * 15,
        out_specs=[vmem] * 8 + [pl.BlockSpec(memory_space=pl.ANY)] * 3,
        scratch_shapes=[
            pltpu.VMEM(slabs, BF16), pltpu.VMEM((groups,) + starts.shape, jnp.int32),
            pltpu.VMEM((16, 128), F32), pltpu.VMEM((parts, 16, 128), F32),
            pltpu.VMEM((8, length), F32), pltpu.VMEM((8, length), F32),
            pltpu.VMEM((width, length), F32),
            dma((parts,)), dma((parts,)), dma((groups,)), dma((groups,)), dma(()), dma(()),
            dma((2, count, 3)), dma((groups, 3, count)), dma((groups * count,)), dma((groups, count)),
        ] + Spread.semaphores(parts) * 4,
        compiler_params=pltpu.CompilerParams(
            vmem_limit_bytes=VMEM_LIMIT, collective_id=2, has_side_effects=True
        ),
        cost_estimate=cost(4 * length * length * width, 16 * length * width, length * length),
        name="front",
    )(x, w_qkv, starts, *vectors, *shards)


def attend_back_kernel(
    size, heads, parts, qkv_ref, own_ref, o_ref, lse_ref, st_ref, ga_ref, gp_ref,
    out_ref, fa_ref, fp_ref,
    do_sc, delta_sc, dqt_sc, dk_sc, dv_sc, stage, near_s, near_r, far_s, far_r, out_s, out_r, *refs
):
    folds = [Fold(ga_ref, fa_ref, parts, *refs[:12]), Fold(gp_ref, fp_ref, parts, *refs[12:])]
    groups, _, per, _ = qkv_ref.shape
    count = per // size
    at = Place(groups, count)
    p, side, half = at.p, at.side, at.half
    scale = HEAD_DIM ** (-0.5)
    dqt_sc[...] = jnp.zeros_like(dqt_sc)
    dk_sc[...] = jnp.zeros_like(dk_sc)
    dv_sc[...] = jnp.zeros_like(dv_sc)
    greet(groups, parts)
    do_sc[p] = own_ref[p]
    greeted(groups, parts)

    near = remote(own_ref.at[at.mate], do_sc.at[p], near_s, near_r, at.peer(at.mate))
    near.start()

    def far_copy(b, d):
        rows = pl.ds(b * size, size)
        return remote(
            own_ref.at[at.far[d], rows], do_sc.at[p, rows], far_s.at[d, b], far_r.at[p, b],
            at.peer(at.far[d]),
        )

    for b in range(count):
        for d in range(2):
            far_copy(b, d).start()
    for fold in folds:
        fold.start()

    def columns(block):
        return pl.ds(pl.multiple_of(block * size, size), size)

    def prepare(q):
        src, rows = rows_of(q, count, size)
        prod = (do_sc[src, rows].astype(F32) * o_ref[src, rows].astype(F32)).T
        for h in range(heads):
            sl = slice(h * HEAD_DIM, (h + 1) * HEAD_DIM)
            delta_sc[h : h + 1, columns(q)] = jnp.sum(prod[sl], 0, keepdims=True)

    def block(q, k, diagonal):
        src, rows = rows_of(q, count, size)
        cols = columns(q)
        ksrc, krows = rows_of(k, count, size)
        query = (qkv_ref[src, 0, rows, :] * scale).astype(BF16)
        grad = do_sc[src, rows]
        key = qkv_ref[ksrc, 1, krows, :]
        value = qkv_ref[ksrc, 2, krows, :]
        ok = mask_of(st_ref[:, cols], q, k, size, diagonal)
        dv = dk = None
        for h in range(heads):
            sl = slice(h * HEAD_DIM, (h + 1) * HEAD_DIM)
            query_h, grad_h = lane_mask(h, query), lane_mask(h, grad)
            s = jnp.where(ok, dot(key, query_h, NT), NEG)
            e = jnp.exp(s - lse_ref[h : h + 1, cols])
            ds = (e * (dot(value, grad_h, NT) - delta_sc[h : h + 1, cols])).astype(BF16)
            dvh = dot(e.astype(BF16), grad_h)
            dkh = dot(ds, query_h)
            dv = dvh if dv is None else dv + dvh
            dk = dkh if dk is None else dk + dkh
            dqt_sc[sl, cols] += dot(key[:, sl], ds, TN)
        dv_sc[cols_of(k), :] += dv
        dk_sc[cols_of(k), :] += dk

    cols_of = columns

    def out_copy(block, part):
        src, rows = rows_of(block, count, size)
        return remote(
            stage.at[src, part, rows], out_ref.at[p, part, rows], out_s.at[block, part],
            out_r.at[p, part, lax.rem(block, count)], at.peer(src),
        )

    def give(block, part, value):
        src, rows = rows_of(block, count, size)

        @pl.when(src == p)
        def _():
            out_ref[p, part, rows] = value

        @pl.when(src != p)
        def _():
            stage[src, part, rows] = value
            out_copy(block, part).start()

    def finish_query(q):
        give(q, 0, (dqt_sc[:, columns(q)] * scale).T.astype(BF16))

    def finish_key(k):
        give(k, 1, dk_sc[columns(k), :].astype(BF16))
        give(k, 2, dv_sc[columns(k), :].astype(BF16))

    small = count * (count + 1) // 2
    far = 2 * small
    bulk = far + half * (half + 1) // 2
    cross = bulk + half * half
    end = cross + count * count

    @pl.loop(0, end)
    def _(step):
        second = step >= small
        row, col = triangle(step - pick(second, small, 0), count)
        base = pick(second, at.mate, p) * count
        q, k = base + row, base + col
        in_far = (step >= far) & (step < bulk)
        row, column = triangle_by_column(step - far, half)
        q = pick(in_far, at.far_block + row, q)
        k = pick(in_far, at.far_block + column, k)
        c = step - bulk
        in_bulk = (step >= bulk) & (step < cross)
        outer, inner = c // half, lax.rem(c, half)
        q = pick(in_bulk, half + pick(side == 0, outer, inner), q)
        k = pick(in_bulk, pick(side == 0, inner, outer), k)
        c = step - cross
        in_cross = step >= cross
        q = pick(in_cross, at.near_block + count + c // count, q)
        k = pick(in_cross, at.near_block + lax.rem(c, count), k)

        @pl.when(step == small)
        def _():
            near.wait_recv()

        @pl.when(in_far & (column == 0))
        def _():
            src, rows = rows_of(q, count, size)
            there = do_sc.at[src, rows]
            remote(there, there, far_s.at[0, 0], far_r.at[src, lax.rem(q, count)], at.peer(src)).wait_recv()

        @pl.when(((step < far) & (col == 0)) | (in_far & (column == 0)))
        def _():
            prepare(q)

        @pl.when(q == k)
        def _():
            block(q, k, True)

        @pl.when(q != k)
        def _():
            block(q, k, False)

        for n, fold in enumerate(folds):
            pl.when(step == end // 6 + n)(fold.pairs)
            pl.when(step == end // 2 + 1 + 3 * n)(fold.planes)
            pl.when(step == end - 2 + n)(fold.lines)

        column_done = in_far & (row == half - 1)
        outer_done = in_bulk & (inner == half - 1)
        done = step == end - 1
        near_low, near_high = at.near_block, at.near_block + half
        query = (column_done & (side == 1)) | (outer_done & (side == 0))
        block_id = at.far_block + pick(in_far, column, outer)
        pl.loop(
            pick(done, near_low, block_id),
            pick(done, near_high, pick(query, block_id + 1, block_id)),
        )(finish_query)
        key = (column_done & (side == 0)) | (outer_done & (side == 1))
        pl.loop(
            pick(done, near_low, block_id),
            pick(done, near_high, pick(key, block_id + 1, block_id)),
        )(finish_key)

    for q in at.others():
        for b in range(count):
            for part in range(3):
                there = out_ref.at[q, part, pl.ds(b * size, size)]
                remote(there, there, out_s.at[0, 0], out_r.at[q, part, b], at.peer(q)).wait_recv()
                out_copy(q * count + b, part).wait_send()
    near.wait_send()
    for b in range(count):
        for d in range(2):
            far_copy(b, d).wait_send()


def attention_backward(qkv, grad, out, lse, starts, g_a, g_p, size=512):
    groups, _, per, width = qkv.shape
    length = groups * per
    heads = width // HEAD_DIM
    count = per // size
    parts = g_a.shape[0]
    dma = pltpu.SemaphoreType.DMA
    vmem = pl.BlockSpec(memory_space=pltpu.VMEM)
    return pl.pallas_call(
        functools.partial(attend_back_kernel, size, heads, parts),
        out_shape=(
            jax.ShapeDtypeStruct(qkv.shape, BF16),
            jax.ShapeDtypeStruct((g_a.shape[1], g_a.shape[2] // 2), BF16),
            jax.ShapeDtypeStruct((g_p.shape[1], g_p.shape[2] // 2), BF16),
        ),
        in_specs=[vmem] * 5 + [pl.BlockSpec(memory_space=pl.ANY)] * 2,
        out_specs=[vmem] * 3,
        scratch_shapes=[
            pltpu.VMEM((groups, per, width), BF16), pltpu.VMEM((8, length), F32),
            pltpu.VMEM((width, length), F32), pltpu.VMEM((length, width), F32),
            pltpu.VMEM((length, width), F32), pltpu.VMEM(qkv.shape, BF16),
            dma(()), dma(()), dma((2, count)), dma((groups, count)),
            dma((groups * count, 3)), dma((groups, 3, count)),
            *Fold.scratch(*g_a.shape), *Fold.scratch(*g_p.shape),
        ],
        compiler_params=pltpu.CompilerParams(
            vmem_limit_bytes=VMEM_LIMIT, collective_id=3, has_side_effects=True
        ),
        cost_estimate=cost(10 * length * length * width, 24 * length * width, length * length),
        name="attention_backward",
    )(qkv, grad, out, lse, starts, g_a, g_p)


def put(ref, first, value):
    @pl.when(first)
    def _():
        ref[...] = value

    @pl.when(jnp.logical_not(first))
    def _():
        ref[...] += value


def column_sum(x):
    return jnp.sum(x, 0, keepdims=True)


def middle_kernel(
    groups, x_ref, attn_ref, wo_ref, wf_ref, wp_ref, small_ref, fcb_ref, cot_ref,
    out_ref, resid_ref, ga_ref, gwa_ref, gwp_ref, gs_ref, gwa_sc, gwp_sc,
):
    first = pl.program_id(0) == 0
    model = x_ref.shape[-1]
    width = model // groups
    small = small_ref[...]
    w_out = weight_rows(wo_ref, wo_ref.shape[1])
    w_fc = weight_rows(wf_ref, wf_ref.shape[1])
    w_proj = weight_rows(wp_ref, wp_ref.shape[1])
    attn = jnp.concatenate([attn_ref[g] for g in range(groups)], 1)
    resid = x_ref[...].astype(F32) + dot(attn, w_out) + small[OUT_BIAS : OUT_BIAS + 1]
    normed, inverse = normalize(resid)
    gain = small[GAIN_TWO : GAIN_TWO + 1]
    act = (normed * gain + small[BIAS_TWO : BIAS_TWO + 1]).astype(BF16)
    hidden = dot(act, w_fc) + fcb_ref[...]
    sig = 1.0 / (1.0 + jnp.exp(-1.702 * hidden))
    gelu = hidden * sig
    slope = sig + 1.702 * gelu * (1.0 - sig)
    gelu = gelu.astype(BF16)
    out_ref[...] = (resid + dot(gelu, w_proj) + small[PROJ_BIAS : PROJ_BIAS + 1]).astype(BF16)
    up = cot_ref[...]
    put(gwp_sc, first, dot(gelu, up, TN))
    grad_hidden = dot(up, w_proj, NT) * slope
    low = grad_hidden.astype(BF16)
    put(gwa_sc.at[:, model:], first, dot(act, low, TN))
    grad_act = dot(low, w_fc, NT)
    up = up.astype(F32)
    grad_resid = up + normalize_back(grad_act * gain, normed, inverse)
    resid_ref[...] = grad_resid
    resid_low = grad_resid.astype(BF16)
    put(gwa_sc.at[:, 0:model], first, dot(attn, resid_low, TN))
    grad_attn = dot(resid_low, w_out, NT).astype(BF16)
    for g in range(groups):
        ga_ref[g] = grad_attn[:, g * width : (g + 1) * width]
    put(gs_ref.at[0:1, :], first, column_sum(grad_hidden))
    put(gs_ref.at[1:2, 0:model], first, column_sum(grad_resid))
    put(gs_ref.at[2:3, 0:model], first, column_sum(grad_act * normed))
    put(gs_ref.at[3:4, 0:model], first, column_sum(grad_act))
    put(gs_ref.at[4:5, 0:model], first, column_sum(up))

    @pl.when(pl.program_id(0) == pl.num_programs(0) - 1)
    def _():
        gwa_ref[...] = gwa_sc[...].astype(BF16)
        gwp_ref[...] = gwp_sc[...].astype(BF16)


def middle(x, attn, w_out, w_fc, w_proj, small, fc_bias, cotangent, tile=256):
    length, model = x.shape
    groups = attn.shape[0]
    hid = w_fc.shape[2]
    rows = pl.BlockSpec((tile, model), lambda i: (i, 0))
    slabs = pl.BlockSpec((groups, tile, model // groups), lambda i: (0, i, 0))
    return pl.pallas_call(
        functools.partial(middle_kernel, groups),
        out_shape=(
            jax.ShapeDtypeStruct((length, model), BF16),
            jax.ShapeDtypeStruct((length, model), F32),
            jax.ShapeDtypeStruct(attn.shape, BF16),
            jax.ShapeDtypeStruct((model, model + hid), BF16),
            jax.ShapeDtypeStruct((hid, model), BF16),
            jax.ShapeDtypeStruct((8, hid), F32),
        ),
        grid=(length // tile,),
        in_specs=[rows, slabs, whole(w_out.shape), whole(w_fc.shape), whole(w_proj.shape), whole(small.shape),
                  whole(fc_bias.shape), rows],
        out_specs=[rows, rows, slabs, whole((model, model + hid)),
                   whole((hid, model)), whole((8, hid))],
        scratch_shapes=[pltpu.VMEM((model, model + hid), F32), pltpu.VMEM((hid, model), F32)],
        compiler_params=params(),
        cost_estimate=cost(12 * length * model * hid + 6 * length * model * model,
                           16 * model * hid, length * hid),
        name="middle",
    )(x, attn, w_out, w_fc, w_proj, small, fc_bias, cotangent)


def last_kernel(
    rows, parts, chunk, x_ref, g_ref, resid_ref, w_ref, small_ref, gs_in, fa_ref, fp_ref,
    gt_ref, gw_ref, gv_ref, go_ref, gf_ref, gp_ref,
    xa, xp, fulla, fullp, xs, xr, ys, yr, acc, out, vec, mine, vsend, vpart, low, r1, s2, r2, keep, s3, r3,
    v1s, v1r, v2s, v2r, c1s, c1r, c2s, c2r, c3s, c3r, c4s, c4r,
):
    step = pl.program_id(0)
    first = step == 0
    groups = g_ref.shape[0]
    model = x_ref.shape[-1]
    p, f = lax.axis_index("sp"), lax.axis_index("fsdp")

    @pl.when(first)
    def _():
        greet(groups, parts)

    core = lax.rem(p, 2)
    side = p // 2
    mate = p + 1 - 2 * core
    across = p + groups // 2 - side * groups
    cross = [
        remote(src, dst, xs.at[n], xr.at[n], peer(across, f))
        for n, (src, dst) in enumerate(((fa_ref, xa), (fp_ref, xp)))
    ]

    @pl.when(step == 1)
    def _():
        greeted(groups, parts)
        for copy in cross:
            copy.start()

    small = small_ref[...]
    normed, inverse = normalize(x_ref[...].astype(F32))
    gain = small[GAIN_ONE : GAIN_ONE + 1]
    act = (normed * gain + small[BIAS_ONE : BIAS_ONE + 1]).astype(BF16)
    grad = jnp.concatenate([g_ref[g, part] for part in range(3) for g in range(groups)], 1)
    put(acc, first, dot(act, grad, TN))
    grad_act = dot(grad, weight_rows(w_ref, rows), NT)
    gt_ref[...] = (
        resid_ref[...] + normalize_back(grad_act * gain, normed, inverse)
    ).astype(BF16)
    put(vec.at[0:1], first, column_sum(grad_act * normed))
    put(vec.at[1:2], first, column_sum(grad_act))
    put(vec.at[2:3], first, column_sum(grad[:, 0:model].astype(F32)))
    put(vec.at[3:4], first, column_sum(grad[:, 2 * model :].astype(F32)))

    @pl.when(step == pl.num_programs(0) - 1)
    def _():
        shard = acc.shape[0] // parts
        half = acc.shape[1] // 2
        quarter = half // 2
        count = quarter // chunk

        def lane(c, s, k):
            return pl.ds(pl.multiple_of(c * half + s * quarter + k * chunk, 128), chunk)

        copies = []

        def go(copy):
            copy.start()
            copies.append(copy)

        low[...] = acc[...].astype(BF16)
        vec[4:8, :] = gs_in[1:5, 0:model]
        piece = model // parts
        fc = gs_in.shape[1] // parts
        bits = min(128, fc)
        vsend[...] = jnp.zeros_like(vsend)
        for g in range(parts):
            vsend[g, 0:8, 0:piece] = vec[:, g * piece : (g + 1) * piece]
            for k in range(fc // bits):
                at = g * fc + k * bits
                vsend[g, 8 + k : 9 + k, 0:bits] = gs_in[0:1, at : at + bits]

        for k in range(count):
            for s in range(2):
                go(remote(low.at[:, lane(1 - core, s, k)], r1.at[k, s], c1s.at[k, s], c1r.at[k, s],
                          peer(mate, f)))
        for n, g in enumerate(others(f, parts)):
            go(remote(vsend.at[g], vpart.at[f], v1s.at[n], v1r.at[f], peer(p, g)))
        for k in range(count):
            for s in range(2):
                remote(r1.at[k, s], r1.at[k, s], c1s.at[k, s], c1r.at[k, s], peer(mate, f)).wait_recv()
            s2[k] = (acc[:, lane(core, 1 - side, k)] + r1[k, 1 - side].astype(F32)).astype(BF16)
            go(remote(s2.at[k], r2.at[k], c2s.at[k], c2r.at[k], peer(across, f)))
        folded = []
        for n, (mine_ref, theirs, full) in enumerate(((fa_ref, xa, fulla), (fp_ref, xp, fullp))):
            cross[n].wait()
            wide = mine_ref.shape[1]
            here = full.at[:, pl.ds(pl.multiple_of(core * wide, 128), wide)]
            there = full.at[:, pl.ds(pl.multiple_of((1 - core) * wide, 128), wide)]
            here[...] = mine_ref[...].astype(F32) + theirs[...].astype(F32)
            go(remote(here, here, ys.at[n], yr.at[n], peer(mate, f)))
            folded.append(remote(there, there, ys.at[n], yr.at[n], peer(mate, f)))
        for k in range(count):
            remote(s2.at[k], r2.at[k], c2s.at[k], c2r.at[k], peer(across, f)).wait_recv()
            total = acc[:, lane(core, side, k)] + r1[k, side].astype(F32) + r2[k].astype(F32)
            keep[k] = total
            s3[k] = total.astype(BF16)
            for n, g in enumerate(others(f, parts)):
                rows_of = pl.ds(pl.multiple_of(g * shard, shard), shard)
                go(remote(s3.at[k, rows_of], r3.at[k, f], c3s.at[k, n], c3r.at[k, f], peer(p, g)))
        for g in others(f, parts):
            remote(vsend.at[g], vpart.at[g], v1s.at[0], v1r.at[g], peer(p, g)).wait_recv()
        total = vsend[f]
        for g in others(f, parts):
            total = total + vpart[g]
        mine[p] = total
        for n, q in enumerate(others(p, groups)):
            go(remote(mine.at[p], mine.at[p], v2s.at[n], v2r.at[p], peer(q, f)))
        for k in range(count):
            for g in others(f, parts):
                remote(r3.at[k, g], r3.at[k, g], c3s.at[k, 0], c3r.at[k, g], peer(p, g)).wait_recv()
            total = keep[k, pl.ds(pl.multiple_of(f * shard, shard), shard)]
            for g in others(f, parts):
                total = total + r3[k, g].astype(F32)
            out[:, lane(core, side, k)] = total
            for n, q in enumerate(others(p, groups)):
                there = out.at[:, lane(core, side, k)]
                go(remote(there, there, c4s.at[k, n], c4r.at[k, p], peer(q, f)))
        for q in others(p, groups):
            remote(mine.at[q], mine.at[q], v2s.at[0], v2r.at[q], peer(q, f)).wait_recv()
        total = mine[0]
        for q in range(1, groups):
            total = total + mine[q]
        gv_ref[...] = total
        for k in range(count):
            for q in others(p, groups):
                there = out.at[:, lane(lax.rem(q, 2), q // 2, k)]
                remote(there, there, c4s.at[k, 0], c4r.at[k, q], peer(q, f)).wait_recv()
        gw_ref[...] = out[...]
        for copy in folded:
            copy.wait_recv()
        go_ref[...] = fulla[:, 0:model]
        gf_ref[...] = fulla[:, model:]
        gp_ref[...] = fullp[...]
        for copy in copies:
            copy.wait_send()


def last(x, grad, resid, weight, rows, small, sums, f_a, f_p, parts, tile=256, chunk=128):
    length, model = x.shape
    groups, _, _, width = grad.shape
    block = pl.BlockSpec((tile, model), lambda i: (i, 0))
    triple = 3 * model
    shard = model // parts
    count = triple // 4 // chunk
    dma = pltpu.SemaphoreType.DMA
    vmem = pltpu.VMEM
    return pl.pallas_call(
        functools.partial(last_kernel, rows, parts, chunk),
        out_shape=(
            jax.ShapeDtypeStruct((length, model), BF16),
            jax.ShapeDtypeStruct((shard, triple), F32),
            jax.ShapeDtypeStruct((16, 128), F32),
            jax.ShapeDtypeStruct((f_a.shape[0], model), F32),
            jax.ShapeDtypeStruct((f_a.shape[0], 2 * f_a.shape[1] - model), F32),
            jax.ShapeDtypeStruct((f_p.shape[0], 2 * f_p.shape[1]), F32),
        ),
        grid=(length // tile,),
        in_specs=[
            block,
            pl.BlockSpec((groups, 3, tile, width), lambda i: (0, 0, i, 0)),
            block,
            whole(weight.shape),
            whole(small.shape),
            whole(sums.shape),
            whole(f_a.shape),
            whole(f_p.shape),
        ],
        out_specs=[
            block, whole((shard, triple)), whole((16, 128)), whole((f_a.shape[0], model)),
            whole((f_a.shape[0], 2 * f_a.shape[1] - model)),
            whole((f_p.shape[0], 2 * f_p.shape[1])),
        ],
        scratch_shapes=[
            vmem(f_a.shape, BF16), vmem(f_p.shape, BF16),
            vmem((f_a.shape[0], 2 * f_a.shape[1]), F32),
            vmem((f_p.shape[0], 2 * f_p.shape[1]), F32),
            dma((2,)), dma((2,)), dma((2,)), dma((2,)),
            vmem((model, triple), F32), vmem((shard, triple), F32), vmem((8, model), F32),
            vmem((groups, 16, 128), F32),
            vmem((parts, 16, 128), F32), vmem((parts, 16, 128), F32),
            vmem((model, triple), BF16), vmem((count, 2, model, chunk), BF16),
            vmem((count, model, chunk), BF16), vmem((count, model, chunk), BF16),
            vmem((count, model, chunk), F32), vmem((count, model, chunk), BF16),
            vmem((count, parts, shard, chunk), BF16),
            dma((parts,)), dma((parts,)), dma((groups,)), dma((groups,)),
            dma((count, 2)), dma((count, 2)), dma((count,)), dma((count,)),
            dma((count, parts)), dma((count, parts)), dma((count, groups)), dma((count, groups)),
        ],
        compiler_params=pltpu.CompilerParams(
            vmem_limit_bytes=VMEM_LIMIT, collective_id=1, has_side_effects=True
        ),
        cost_estimate=cost(12 * length * model * model, 20 * length * model),
        name="last",
    )(x, grad, resid, weight, small, sums, f_a, f_p)


def per_device(
    tokens, starts, norm1_gain, norm1_bias, w_qkv, q_bias, v_bias, w_out, out_bias, norm2_gain,
    norm2_bias, w_fc, fc_bias, w_proj, proj_bias, cotangent,
):
    groups = lax.axis_size("sp")
    parts = lax.axis_size("fsdp")
    rows, triple = w_qkv.shape
    piece = norm1_gain.shape[0]
    x = tokens[0]
    vectors = [
        norm1_gain, norm1_bias, q_bias, v_bias, out_bias, norm2_gain, norm2_bias, proj_bias, fc_bias
    ]
    qkv, out, lse, attn, doc_first, small, fcb, packed, *wide = front(
        x, w_qkv, starts, vectors, (w_out, w_fc, w_proj), groups, parts
    )
    if rows % 16 == 0:
        weight, weight_count = packed, rows
    else:
        weight, weight_count = packed.reshape(1, parts * rows, triple), parts * rows
    wide = [w if w.shape[1] % 16 == 0 else w.reshape(1, -1, w.shape[2]) for w in wide]
    block_out, grad_resid, grad_attn, g_a, g_p, sums = middle(
        x, attn, *wide, small, fcb, cotangent[0]
    )
    grad, f_a, f_p = attention_backward(
        qkv, grad_attn, out, lse, doc_first,
        g_a.reshape(parts, -1, g_a.shape[1]), g_p.reshape(parts, -1, g_p.shape[1]),
    )
    grad_tokens, g_q, g_v, g_out, g_fc, g_p = last(
        x, grad, grad_resid, weight, weight_count, small, sums, f_a, f_p, parts
    )
    vec = [g_v[k, :piece] for k in range(8)]
    fc = fc_bias.shape[0]
    g_fcb = g_v[8 : 8 + max(fc // 128, 1), : min(fc, 128)].reshape(fc)
    return (
        block_out[None], grad_tokens[None], vec[0], vec[1], g_q, vec[2], vec[3],
        g_out, vec[4], vec[5], vec[6], g_fc, g_fcb, g_p, vec[7],
    )


def solution(mesh):
    row, mat = P("fsdp"), P("fsdp", None)
    stream = P("fsdp", "sp", None)
    return jax.shard_map(
        per_device,
        mesh=mesh,
        in_specs=(stream, P("fsdp", "sp"), row, row, mat, row, row, mat, row, row, row, mat, row,
                  mat, row, stream),
        out_specs=(stream, stream, row, row, mat, row, row, mat, row, row, row, mat, row, mat, row),
        check_vma=False,
    )
```

```python
import functools

import jax
import jax.numpy as jnp
from jax import lax
from jax.experimental import pallas as pl
from jax.experimental.pallas import tpu as pltpu
from jax.sharding import PartitionSpec as P

HEAD_DIM = 64
EPSILON = 1e-05
NEG = -1e30
F32 = jnp.float32
BF16 = jnp.bfloat16
RELAY_AT, RELAY_GAP, TWIN_AT = 12, 3, 20
NN = (((1,), (0,)), ((), ()))
NT = (((1,), (1,)), ((), ()))
TN = (((0,), (0,)), ((), ()))
VMEM_LIMIT = 60 << 20


def dot(left, right, dims=NN):
    return lax.dot_general(left, right, dims, preferred_element_type=F32)


def normalize(values):
    centered = values - jnp.mean(values, -1, keepdims=True)
    inverse = lax.rsqrt(jnp.mean(centered * centered, -1, keepdims=True) + EPSILON)
    return centered * inverse, inverse


def normalize_back(incoming, normed, inverse):
    return inverse * (
        incoming
        - jnp.mean(incoming, -1, keepdims=True)
        - normed * jnp.mean(incoming * normed, -1, keepdims=True)
    )


def whole(shape):
    return pl.BlockSpec(shape, lambda *_: (0,) * len(shape))


def params():
    return pltpu.CompilerParams(vmem_limit_bytes=VMEM_LIMIT)


def cost(flops, size, exps=0):
    return pl.CostEstimate(flops=flops, bytes_accessed=size, transcendentals=exps)


def weight_rows(w_ref, rows):
    parts = w_ref.shape[0]
    return w_ref[:, 0:rows, :].reshape(parts * rows, w_ref.shape[2])


def peer(sp, fsdp):
    return {"sp": sp, "fsdp": fsdp}


def remote(src, dst, send, recv, where):
    return pltpu.make_async_remote_copy(
        src_ref=src, dst_ref=dst, send_sem=send, recv_sem=recv,
        device_id=where, device_id_type=pl.DeviceIdType.MESH,
    )


def others(me, count):
    return [lax.rem(me + k, count) for k in range(1, count)]


def greet(groups, parts):
    p, f = lax.axis_index("sp"), lax.axis_index("fsdp")
    barrier = pltpu.get_barrier_semaphore()
    for q in others(p, groups):
        pl.semaphore_signal(barrier, inc=1, device_id=peer(q, f), device_id_type=pl.DeviceIdType.MESH)
    for g in others(f, parts):
        pl.semaphore_signal(barrier, inc=1, device_id=peer(p, g), device_id_type=pl.DeviceIdType.MESH)


def greeted(groups, parts):
    pl.semaphore_wait(pltpu.get_barrier_semaphore(), groups + parts - 2)


class Spread:
    def __init__(self, src, dst, parts, send, recv, own):
        self.src, self.dst, self.send, self.recv, self.own = src, dst, send, recv, own
        self.p, self.f = lax.axis_index("sp"), lax.axis_index("fsdp")
        core = lax.rem(self.p, 2)
        self.mate = self.p + 1 - 2 * core
        self.parts, self.major = parts, parts // 2
        self.a, self.b = self.f // 2, lax.rem(self.f, 2)
        self.twin = self.a * 2 + 1 - self.b
        half = src.shape[1] // 2
        self.lanes = pl.ds(pl.multiple_of(core * half, 128), half)
        self.mate_lanes = pl.ds(pl.multiple_of((1 - core) * half, 128), half)

    def back(self, k):
        return lax.rem(self.a + self.major - k, self.major)

    def block(self, g, lanes=None):
        return self.dst.at[g, :, self.lanes if lanes is None else lanes]

    def first(self, k):
        where = lax.rem(self.a + k, self.major) * 2 + self.b
        where = self.twin if k == 0 else where
        return remote(
            self.src.at[:, self.lanes], self.block(self.f), self.send.at[0, k],
            self.recv.at[0, self.f], peer(self.p, where),
        )

    def to_twin(self, k):
        g = self.back(k) * 2 + self.b
        return remote(
            self.block(g), self.block(g), self.send.at[1, k], self.recv.at[0, g],
            peer(self.p, self.twin),
        )

    def to_mate(self, k, b):
        g = self.back(k) * 2 + b
        slot = k if b is self.b else self.major + k
        return remote(
            self.block(g), self.block(g), self.send.at[2, slot], self.recv.at[1, g],
            peer(self.mate, self.f),
        )

    def keep(self):
        return pltpu.make_async_copy(self.src, self.dst.at[self.f], self.own)

    def start_lines(self):
        self.keep().start()
        for k in range(1, self.major):
            self.first(k).start()

    def start_twin(self):
        self.first(0).start()

    def start(self):
        self.start_lines()
        self.start_twin()

    def relay(self, k):
        self.to_twin(k).wait_recv()
        self.to_twin(k).start()
        self.to_mate(k, self.b).start()

    def relay_twin(self, k):
        other = 1 - self.b
        copy = self.to_mate(k, other)
        g = self.back(k) * 2 + other
        remote(
            self.block(g), self.block(g), self.send.at[1, 0], self.recv.at[0, g],
            peer(self.p, self.twin),
        ).wait_recv()
        copy.start()

    def finish(self):
        for g in others(self.f, self.parts):
            there = self.block(g, self.mate_lanes)
            remote(
                there, there, self.send.at[1, 0], self.recv.at[1, g], peer(self.mate, self.f)
            ).wait_recv()
        for k in range(self.major):
            self.first(k).wait_send()
            self.to_mate(k, 1 - self.b).wait_send()
        for k in range(1, self.major):
            self.to_twin(k).wait_send()
            self.to_mate(k, self.b).wait_send()
        self.keep().wait()

    @staticmethod
    def semaphores(parts):
        dma = pltpu.SemaphoreType.DMA
        return [dma((3, parts)), dma((2, parts)), dma(())]


class Fold:
    def __init__(self, src, out, parts, mine, r1, r2, s2, r3, own, send1, recv1, send2, recv2, send3, recv3):
        self.__dict__.update(
            src=src, out=out, mine=mine, r1=r1, r2=r2, s2=s2, r3=r3, own=own, send1=send1,
            recv1=recv1, send2=send2, recv2=recv2, send3=send3, recv3=recv3,
        )
        self.p, self.f = lax.axis_index("sp"), lax.axis_index("fsdp")
        core = lax.rem(self.p, 2)
        self.mate = self.p + 1 - 2 * core
        self.major = parts // 2
        self.a, self.b = self.f // 2, lax.rem(self.f, 2)
        self.twin = self.a * 2 + 1 - self.b
        half = src.shape[2] // 2
        self.lanes = pl.ds(pl.multiple_of(core * half, 128), half)
        self.mate_lanes = pl.ds(pl.multiple_of((1 - core) * half, 128), half)

    def keep(self):
        return pltpu.make_async_copy(self.src.at[:, :, self.lanes], self.mine, self.own)

    def to_mate(self):
        return remote(
            self.src.at[:, :, self.mate_lanes], self.r1, self.send1, self.recv1,
            peer(self.mate, self.f),
        )

    def to_twin(self, c):
        return remote(
            self.mine.at[c * 2 + 1 - self.b], self.r2.at[c], self.send2.at[c], self.recv2.at[c],
            peer(self.p, self.twin),
        )

    def along(self, k):
        c = lax.rem(self.a + k, self.major)
        return remote(
            self.s2.at[c], self.r3.at[self.a], self.send3.at[c], self.recv3.at[self.a],
            peer(self.p, c * 2 + self.b),
        )

    def start(self):
        self.to_mate().start()
        self.keep().start()

    def pairs(self):
        self.keep().wait()
        self.to_mate().wait()
        self.mine[...] = (self.mine[...].astype(F32) + self.r1[...].astype(F32)).astype(BF16)
        for c in range(self.major):
            self.to_twin(c).start()

    def planes(self):
        for c in range(self.major):
            self.to_twin(c).wait()
            self.s2[c] = (
                self.mine[c * 2 + self.b].astype(F32) + self.r2[c].astype(F32)
            ).astype(BF16)
        for k in range(1, self.major):
            self.along(k).start()

    def lines(self):
        total = self.mine[self.f].astype(F32) + self.r2[self.a].astype(F32)
        for k in range(1, self.major):
            c = lax.rem(self.a + k, self.major)
            remote(
                self.r3.at[c], self.r3.at[c], self.send3.at[0], self.recv3.at[c],
                peer(self.p, self.twin),
            ).wait_recv()
            total = total + self.r3[c].astype(F32)
        self.out[...] = total.astype(BF16)
        for k in range(1, self.major):
            self.along(k).wait_send()

    @staticmethod
    def scratch(parts, rows, lanes):
        dma = pltpu.SemaphoreType.DMA
        major, half = parts // 2, lanes // 2
        return [
            pltpu.VMEM((parts, rows, half), BF16), pltpu.VMEM((parts, rows, half), BF16),
            pltpu.VMEM((major, rows, half), BF16), pltpu.VMEM((major, rows, half), BF16),
            pltpu.VMEM((major, rows, half), BF16), dma(()), dma(()), dma(()),
            dma((major,)), dma((major,)), dma((major,)), dma((major,)),
        ]


def column_sum(x):
    return jnp.sum(x, 0, keepdims=True)


GAIN_ONE, BIAS_ONE, Q_BIAS, V_BIAS, OUT_BIAS, GAIN_TWO, BIAS_TWO, PROJ_BIAS = range(8)


def lane_mask(h, x):
    lane = lax.broadcasted_iota(jnp.int32, x.shape, 1)
    return jnp.where(lane // HEAD_DIM == h, x, jnp.zeros_like(x))


def triangle(index, size):
    row = sum((index >= m * (m + 1) // 2).astype(jnp.int32) for m in range(1, size))
    return row, index - row * (row + 1) // 2


def triangle_by_column(index, size):
    starts = [c * (2 * size + 1 - c) // 2 for c in range(size)]
    col = sum((index >= at).astype(jnp.int32) for at in starts[1:])
    return col + index - col * (2 * size + 1 - col) // 2, col


def pick(cond, this, other):
    return jnp.where(cond, this, other)


class Place:
    def __init__(self, groups, count):
        self.p, self.f = lax.axis_index("sp"), lax.axis_index("fsdp")
        self.side = self.p // 2
        self.core = lax.rem(self.p, 2)
        self.mate = self.p + 1 - 2 * self.core
        far = (1 - self.side) * 2
        self.far = (far + self.core, far + 1 - self.core)
        self.groups = groups
        self.count = count
        self.half = 2 * count
        self.near_block = self.side * self.half
        self.far_block = (1 - self.side) * self.half

    def peer(self, q):
        return peer(q, self.f)

    def others(self):
        return others(self.p, self.groups)

    def meet(self):
        barrier = pltpu.get_barrier_semaphore()
        for q in self.others():
            pl.semaphore_signal(
                barrier, inc=1, device_id=self.peer(q), device_id_type=pl.DeviceIdType.MESH
            )
        pl.semaphore_wait(barrier, self.groups - 1)


def rows_of(block, count, size):
    return block // count, pl.ds(pl.multiple_of(lax.rem(block, count) * size, size), size)


def mask_of(first, q, k, size, diagonal):
    rows = lax.broadcasted_iota(jnp.int32, (size, size), 0)
    ok = rows >= first - k * size
    if diagonal:
        ok = ok & (rows <= lax.broadcasted_iota(jnp.int32, (1, size), 1))
    return ok


def front_kernel(size, heads, groups, parts, tile, x_ref, wq_ref, st_in, *refs):
    vec_refs, shards, refs = refs[:9], refs[9:12], refs[12:]
    qkv_ref, o_ref, lse_ref, attn_ref, st_ref, small_ref, fcb_ref, wq_all = refs[:8]
    wide, refs = refs[8:11], refs[11:]
    own_ref, sg, own_vec, vg, m_sc, l_sc, acc_sc = refs[:7]
    v_send, v_recv, s_send, s_recv, near_s, near_r, far_s, far_r, out_s, out_r = refs[7:17]
    first_spread, *spreads = [
        Spread(src, dst, parts, *refs[17 + 3 * n : 20 + 3 * n])
        for n, (src, dst) in enumerate(zip((wq_ref,) + shards, (wq_all,) + wide))
    ]
    per, model = x_ref.shape
    width = model // groups
    count = per // size
    major = parts // 2
    at = Place(groups, count)
    p, f, side, half = at.p, at.f, at.side, at.half

    greet(groups, parts)
    piece = vec_refs[0].shape[1]
    runs, bits = vec_refs[8].shape
    own_vec[...] = jnp.zeros_like(own_vec)
    for k in range(8):
        own_vec[k : k + 1, 0:piece] = vec_refs[k][...].astype(F32)
    own_vec[8 : 8 + runs, 0:bits] = vec_refs[8][...].astype(F32)
    vg[f] = own_vec[...]
    sg[p] = st_in[...]
    m_sc[...] = jnp.full_like(m_sc, NEG)
    l_sc[...] = jnp.zeros_like(l_sc)
    acc_sc[...] = jnp.zeros_like(acc_sc)
    greeted(groups, parts)

    copies = []

    def go(copy):
        copy.start()
        copies.append(copy)

    first_spread.start()
    for k, q in enumerate(at.others()):
        go(remote(st_in, sg.at[p], s_send.at[k], s_recv.at[p], at.peer(q)))
    for k, g in enumerate(others(f, parts)):
        go(remote(own_vec, vg.at[f], v_send.at[k], v_recv.at[f], peer(p, g)))
    for k in range(1, major):
        first_spread.relay(k)
    for k in range(major):
        first_spread.relay_twin(k)
    for g in others(f, parts):
        remote(own_vec, vg.at[g], v_send.at[0], v_recv.at[g], peer(p, g)).wait_recv()
    for g in range(parts):
        small_ref[:, g * piece : (g + 1) * piece] = vg[g, 0:8, 0:piece]
        for k in range(runs):
            lane = (g * runs + k) * bits
            fcb_ref[:, lane : lane + bits] = vg[g, 8 + k : 9 + k, 0:bits]
    for q in at.others():
        remote(st_in, sg.at[q], s_send.at[0], s_recv.at[q], at.peer(q)).wait_recv()
    for q in range(groups):
        for k in range(per // 128):
            lane = q * per + k * 128
            st_ref[:, lane : lane + 128] = sg[q, k : k + 1]
    first_spread.finish()
    for spread in spreads:
        spread.start_lines()

    def far_copy(b, t, d):
        rows = pl.ds(pl.multiple_of(b * size, size), size)
        return remote(
            own_ref.at[at.far[d], t, rows], qkv_ref.at[p, t, rows], far_s.at[d, b, t],
            far_r.at[p, t, b], at.peer(at.far[d]),
        )

    near = remote(own_ref.at[at.mate], qkv_ref.at[p], near_s, near_r, at.peer(at.mate))

    @pl.loop(0, per // tile)
    def _(i):
        rows = pl.ds(pl.multiple_of(i * tile, tile), tile)
        normed, _ = normalize(x_ref[rows].astype(F32))
        small = small_ref[...]
        act = (normed * small[GAIN_ONE : GAIN_ONE + 1] + small[BIAS_ONE : BIAS_ONE + 1]).astype(BF16)
        weight = weight_rows(wq_all, wq_all.shape[1])
        for part, row in ((0, Q_BIAS), (1, None), (2, V_BIAS)):
            out = dot(act, weight[:, part * model : (part + 1) * model])
            if row is not None:
                out = out + small[row : row + 1]
            out = out.astype(BF16)
            for g in range(groups):
                own_ref[g, part, rows] = out[:, g * width : (g + 1) * width]

        @pl.when(lax.rem(i + 1, size // tile) == 0)
        def _():
            for n in range(3):
                for d in range(2):
                    far_copy((i + 1) // (size // tile) - 1, lax.rem(n + pick(side == 1, 0, 1), 3), d).start()

    near.start()
    for spread in spreads:
        spread.start_twin()
    qkv_ref[p] = own_ref[p]

    def far_wait(t, block):
        src, rows = rows_of(block, count, size)
        there = qkv_ref.at[src, t, rows]
        remote(there, there, far_s.at[0, 0, 0], far_r.at[src, t, lax.rem(block, count)], at.peer(src)).wait_recv()

    def block(q, k, diagonal):
        src, rows = rows_of(q, count, size)
        cols = pl.ds(pl.multiple_of(q * size, size), size)
        ksrc, krows = rows_of(k, count, size)
        query = (qkv_ref[src, 0, rows, :] * HEAD_DIM ** (-0.5)).astype(BF16)
        key = qkv_ref[ksrc, 1, krows, :]
        value = qkv_ref[ksrc, 2, krows, :]
        ok = mask_of(st_ref[:, cols], q, k, size, diagonal)
        for h in range(heads):
            sl = slice(h * HEAD_DIM, (h + 1) * HEAD_DIM)
            s = jnp.where(ok, dot(key, lane_mask(h, query), NT), NEG)
            m_old = m_sc[h : h + 1, cols]
            m_new = jnp.maximum(m_old, jnp.max(s, 0, keepdims=True))
            e = jnp.exp(s - m_new)
            alpha = jnp.exp(m_old - m_new)
            l_sc[h : h + 1, cols] = l_sc[h : h + 1, cols] * alpha + jnp.sum(e, 0, keepdims=True)
            m_sc[h : h + 1, cols] = m_new
            acc_sc[sl, cols] = acc_sc[sl, cols] * alpha + dot(value[:, sl], e.astype(BF16), TN)

    def out_copy(q):
        src, rows = rows_of(q, count, size)
        return remote(
            o_ref.at[src, rows], attn_ref.at[p, rows], out_s.at[q], out_r.at[p, lax.rem(q, count)],
            at.peer(src),
        )

    def finish(q):
        src, rows = rows_of(q, count, size)
        cols = pl.ds(pl.multiple_of(q * size, size), size)
        parts = []
        for h in range(heads):
            sl = slice(h * HEAD_DIM, (h + 1) * HEAD_DIM)
            total = l_sc[h : h + 1, cols]
            parts.append(acc_sc[sl, cols] * (1.0 / total))
            lse_ref[h : h + 1, cols] = m_sc[h : h + 1, cols] + jnp.log(total)
        out = jnp.concatenate(parts, 0).T.astype(BF16)
        o_ref[src, rows] = out

        @pl.when(src == p)
        def _():
            attn_ref[p, rows] = out

        @pl.when(src != p)
        def _():
            out_copy(q).start()

    small = count * (count + 1) // 2
    cross = 2 * small + count * count
    bulk = cross + half * half
    end = bulk + half * (half + 1) // 2

    @pl.loop(0, end)
    def _(step):
        second = step >= small
        row, col = triangle(step - pick(second, small, 0), count)
        base = pick(second, at.mate, p) * count
        q, k = base + row, base + col
        c = step - 2 * small
        in_cross = (step >= 2 * small) & (step < cross)
        q = pick(in_cross, at.near_block + count + c // count, q)
        k = pick(in_cross, at.near_block + lax.rem(c, count), k)
        c = step - cross
        in_bulk = (step >= cross) & (step < bulk)
        outer, inner = c // half, lax.rem(c, half)
        outer = lax.rem(outer, 2) * count + outer // 2
        q = pick(in_bulk, half + pick(side == 0, outer, inner), q)
        k = pick(in_bulk, pick(side == 0, inner, outer), k)
        in_last = step >= bulk
        row, col = triangle(step - bulk, half)
        q = pick(in_last, at.far_block + row, q)
        k = pick(in_last, at.far_block + col, k)

        @pl.when(step == small)
        def _():
            near.wait_recv()

        starts_outer = in_bulk & (inner == 0)
        starts_row = in_last & (col == 0)

        @pl.when((starts_outer & (side == 0)) | (starts_row & (side == 1)))
        def _():
            far_wait(0, q)

        @pl.when((starts_outer & (side == 1)) | (starts_row & (side == 0)))
        def _():
            far_block = pick(in_bulk, k, q)
            far_wait(1, far_block)
            far_wait(2, far_block)

        @pl.when(q == k)
        def _():
            block(q, k, True)

        @pl.when(q != k)
        def _():
            block(q, k, False)

        for n in range(1, major):
            @pl.when(step == RELAY_AT + (n - 1) * RELAY_GAP * 2 // (major - 1))
            def _(n=n):
                for spread in spreads:
                    spread.relay(n)
        for n in range(major):
            @pl.when(step == TWIN_AT + n * (end - 1 - TWIN_AT) // (major - 1))
            def _(n=n):
                for spread in spreads:
                    spread.relay_twin(n)

        near_done = step == pick(side == 0, cross, bulk) - 1
        low = pick(near_done, at.near_block, q)
        high = pick(near_done, at.near_block + half, pick(in_last & (q == k), q + 1, q))
        pl.loop(low, high)(finish)

    for q in at.others():
        for b in range(count):
            rows = pl.ds(b * size, size)
            there = attn_ref.at[q, rows]
            remote(there, there, out_s.at[0], out_r.at[q, b], at.peer(q)).wait_recv()
            out_copy(q * count + b).wait_send()
    near.wait_send()
    for b in range(count):
        for t in range(3):
            for d in range(2):
                far_copy(b, t, d).wait_send()
    for copy in copies:
        copy.wait_send()
    for spread in spreads:
        spread.finish()


def front(x, w_qkv, starts, vectors, shards, groups, parts, size=512, tile=256):
    per, model = x.shape
    length = groups * per
    width = model // groups
    heads = width // HEAD_DIM
    count = per // size
    starts = starts.reshape(-1, 128)
    fc = vectors[8].shape[0]
    piece = vectors[0].shape[0]
    vectors = [v.reshape(1, -1) for v in vectors[:8]] + [vectors[8].reshape(-1, min(fc, 128))]
    dma = pltpu.SemaphoreType.DMA
    vmem = pl.BlockSpec(memory_space=pltpu.VMEM)
    slabs = (groups, 3, per, width)
    return pl.pallas_call(
        functools.partial(front_kernel, size, heads, groups, parts, tile),
        out_shape=(
            jax.ShapeDtypeStruct(slabs, BF16),
            jax.ShapeDtypeStruct((groups, per, width), BF16),
            jax.ShapeDtypeStruct((8, length), F32),
            jax.ShapeDtypeStruct((groups, per, width), BF16),
            jax.ShapeDtypeStruct((1, length), jnp.int32),
            jax.ShapeDtypeStruct((8, parts * piece), F32),
            jax.ShapeDtypeStruct((1, parts * fc), F32),
            jax.ShapeDtypeStruct((parts,) + w_qkv.shape, BF16),
            *[jax.ShapeDtypeStruct((parts,) + shard.shape, BF16) for shard in shards],
        ),
        in_specs=[vmem] * 15,
        out_specs=[vmem] * 8 + [pl.BlockSpec(memory_space=pl.ANY)] * 3,
        scratch_shapes=[
            pltpu.VMEM(slabs, BF16), pltpu.VMEM((groups,) + starts.shape, jnp.int32),
            pltpu.VMEM((16, 128), F32), pltpu.VMEM((parts, 16, 128), F32),
            pltpu.VMEM((8, length), F32), pltpu.VMEM((8, length), F32),
            pltpu.VMEM((width, length), F32),
            dma((parts,)), dma((parts,)), dma((groups,)), dma((groups,)), dma(()), dma(()),
            dma((2, count, 3)), dma((groups, 3, count)), dma((groups * count,)), dma((groups, count)),
        ] + Spread.semaphores(parts) * 4,
        compiler_params=pltpu.CompilerParams(
            vmem_limit_bytes=VMEM_LIMIT, collective_id=2, has_side_effects=True
        ),
        cost_estimate=cost(4 * length * length * width, 16 * length * width, length * length),
        name="front",
    )(x, w_qkv, starts, *vectors, *shards)


def back_kernel(
    size, heads, parts, tile, qkv_ref, own_ref, o_ref, lse_ref, st_ref, ga_ref, gp_ref,
    x_any, resid_any, w_any, small_ref, sums_ref,
    gt_ref, gw_ref, gv_ref, go_ref, gf_ref, gpo_ref, *refs
):
    (do_sc, delta_sc, dqt_sc, dk_sc, dv_sc, stage, grad_sc,
     near_s, near_r, far_s, far_r, out_s, out_r) = refs[:13]
    fa_sc, fp_sc, x_sc, resid_sc, w_sc, act_sc, load = refs[13:20]
    (xa, xp, fulla, fullp, xs, xr, ys, yr) = refs[20:28]
    (acc, out, vec, mine, vsend, vpart, low, r1, s2, r2, keep, s3, r3) = refs[28:41]
    (v1s, v1r, v2s, v2r, c1s, c1r, c2s, c2r, c3s, c3r, c4s, c4r) = refs[41:53]
    folds = [Fold(ga_ref, fa_sc, parts, *refs[53:65]), Fold(gp_ref, fp_sc, parts, *refs[65:])]
    groups, _, per, width = qkv_ref.shape
    model = x_sc.shape[1]
    count = per // size
    at = Place(groups, count)
    p, f, side, core, half = at.p, at.f, at.side, at.core, at.half
    scale = HEAD_DIM ** (-0.5)
    loads = [
        pltpu.make_async_copy(src, dst, load.at[n])
        for n, (src, dst) in enumerate(((x_any, x_sc), (w_any, w_sc), (resid_any, resid_sc)))
    ]
    for copy in loads:
        copy.start()
    greet(groups, parts)
    dqt_sc[...] = jnp.zeros_like(dqt_sc)
    dk_sc[...] = jnp.zeros_like(dk_sc)
    dv_sc[...] = jnp.zeros_like(dv_sc)
    do_sc[p] = own_ref[p]
    greeted(groups, parts)

    near = remote(own_ref.at[at.mate], do_sc.at[p], near_s, near_r, at.peer(at.mate))
    near.start()

    def far_copy(b, d):
        rows = pl.ds(b * size, size)
        return remote(
            own_ref.at[at.far[d], rows], do_sc.at[p, rows], far_s.at[d, b], far_r.at[p, b],
            at.peer(at.far[d]),
        )

    for b in range(count):
        for d in range(2):
            far_copy(b, d).start()
    for fold in folds:
        fold.start()

    small = small_ref[...]
    gain = small[GAIN_ONE : GAIN_ONE + 1]
    bias = small[BIAS_ONE : BIAS_ONE + 1]
    loads[0].wait()

    @pl.loop(0, per // tile)
    def _(i):
        rows = pl.ds(pl.multiple_of(i * tile, tile), tile)
        normed, _ = normalize(x_sc[rows].astype(F32))
        act_sc[rows] = (normed * gain + bias).astype(BF16)

    def columns(block):
        return pl.ds(pl.multiple_of(block * size, size), size)

    def prepare(q):
        src, rows = rows_of(q, count, size)
        prod = (do_sc[src, rows].astype(F32) * o_ref[src, rows].astype(F32)).T
        for h in range(heads):
            sl = slice(h * HEAD_DIM, (h + 1) * HEAD_DIM)
            delta_sc[h : h + 1, columns(q)] = jnp.sum(prod[sl], 0, keepdims=True)

    def block(q, k, diagonal):
        src, rows = rows_of(q, count, size)
        cols = columns(q)
        ksrc, krows = rows_of(k, count, size)
        query = (qkv_ref[src, 0, rows, :] * scale).astype(BF16)
        grad = do_sc[src, rows]
        key = qkv_ref[ksrc, 1, krows, :]
        value = qkv_ref[ksrc, 2, krows, :]
        ok = mask_of(st_ref[:, cols], q, k, size, diagonal)
        dv = dk = None
        for h in range(heads):
            sl = slice(h * HEAD_DIM, (h + 1) * HEAD_DIM)
            query_h, grad_h = lane_mask(h, query), lane_mask(h, grad)
            s = jnp.where(ok, dot(key, query_h, NT), NEG)
            e = jnp.exp(s - lse_ref[h : h + 1, cols])
            ds = (e * (dot(value, grad_h, NT) - delta_sc[h : h + 1, cols])).astype(BF16)
            dvh = dot(e.astype(BF16), grad_h)
            dkh = dot(ds, query_h)
            dv = dvh if dv is None else dv + dvh
            dk = dkh if dk is None else dk + dkh
            dqt_sc[sl, cols] += dot(key[:, sl], ds, TN)
        dv_sc[cols_of(k), :] += dv
        dk_sc[cols_of(k), :] += dk

    cols_of = columns

    def out_copy(block, part):
        src, rows = rows_of(block, count, size)
        return remote(
            stage.at[src, part, rows], grad_sc.at[p, part, rows], out_s.at[block, part],
            out_r.at[p, part, lax.rem(block, count)], at.peer(src),
        )

    def give(block, part, value):
        src, rows = rows_of(block, count, size)

        @pl.when(src == p)
        def _():
            grad_sc[p, part, rows] = value

        @pl.when(src != p)
        def _():
            stage[src, part, rows] = value
            out_copy(block, part).start()

    def finish_query(q):
        give(q, 0, (dqt_sc[:, columns(q)] * scale).T.astype(BF16))

    def finish_key(k):
        give(k, 1, dk_sc[columns(k), :].astype(BF16))
        give(k, 2, dv_sc[columns(k), :].astype(BF16))

    small = count * (count + 1) // 2
    far = 2 * small
    bulk = far + half * (half + 1) // 2
    cross = bulk + half * half
    end = cross + count * count

    @pl.loop(0, end)
    def _(step):
        second = step >= small
        row, col = triangle(step - pick(second, small, 0), count)
        base = pick(second, at.mate, p) * count
        q, k = base + row, base + col
        in_far = (step >= far) & (step < bulk)
        row, column = triangle_by_column(step - far, half)
        q = pick(in_far, at.far_block + row, q)
        k = pick(in_far, at.far_block + column, k)
        c = step - bulk
        in_bulk = (step >= bulk) & (step < cross)
        outer, inner = c // half, lax.rem(c, half)
        q = pick(in_bulk, half + pick(side == 0, outer, inner), q)
        k = pick(in_bulk, pick(side == 0, inner, outer), k)
        c = step - cross
        in_cross = step >= cross
        q = pick(in_cross, at.near_block + count + c // count, q)
        k = pick(in_cross, at.near_block + lax.rem(c, count), k)

        @pl.when(step == small)
        def _():
            near.wait_recv()

        @pl.when(in_far & (column == 0))
        def _():
            src, rows = rows_of(q, count, size)
            there = do_sc.at[src, rows]
            remote(there, there, far_s.at[0, 0], far_r.at[src, lax.rem(q, count)], at.peer(src)).wait_recv()

        @pl.when(((step < far) & (col == 0)) | (in_far & (column == 0)))
        def _():
            prepare(q)

        @pl.when(q == k)
        def _():
            block(q, k, True)

        @pl.when(q != k)
        def _():
            block(q, k, False)

        for n, fold in enumerate(folds):
            pl.when(step == end // 6 + n)(fold.pairs)
            pl.when(step == end // 2 + 1 + 3 * n)(fold.planes)
            pl.when(step == end - 2 + n)(fold.lines)

        column_done = in_far & (row == half - 1)
        outer_done = in_bulk & (inner == half - 1)
        done = step == end - 1
        near_low, near_high = at.near_block, at.near_block + half
        query = (column_done & (side == 1)) | (outer_done & (side == 0))
        block_id = at.far_block + pick(in_far, column, outer)
        pl.loop(
            pick(done, near_low, block_id),
            pick(done, near_high, pick(query, block_id + 1, block_id)),
        )(finish_query)
        key = (column_done & (side == 0)) | (outer_done & (side == 1))
        pl.loop(
            pick(done, near_low, block_id),
            pick(done, near_high, pick(key, block_id + 1, block_id)),
        )(finish_key)

    across = p + groups // 2 - side * groups
    cross = [
        remote(src, dst, xs.at[n], xr.at[n], at.peer(across))
        for n, (src, dst) in enumerate(((fa_sc, xa), (fp_sc, xp)))
    ]
    for copy in cross:
        copy.start()
    for q in at.others():
        for b in range(count):
            for part in range(3):
                there = grad_sc.at[q, part, pl.ds(b * size, size)]
                remote(there, there, out_s.at[0, 0], out_r.at[q, part, b], at.peer(q)).wait_recv()

    copies = []

    def go(copy):
        copy.start()
        copies.append(copy)

    shard = model // parts
    chunks, chunk = acc.shape[0], acc.shape[2] // 2

    def number(c, s, k):
        return (c * 2 + s) * chunks + k

    def lane(c, s, k):
        return pl.ds(pl.multiple_of(number(c, s, k) * chunk, 128), chunk)

    def product(c, k):
        pair = []
        for s in range(2):
            n = number(c, s, k)
            pair.append(grad_sc[lax.rem(n, groups), n // groups])
        return dot(act_sc[...], jnp.concatenate(pair, 1), TN)

    mate = at.peer(at.mate)
    for k in range(chunks):
        low[k] = product(1 - core, k).astype(BF16)
        if k:
            go(remote(low.at[k - 1], r1.at[k - 1], c1s.at[k - 1], c1r.at[k - 1], mate))
    acc[0] = product(core, 0)
    go(remote(low.at[chunks - 1], r1.at[chunks - 1], c1s.at[chunks - 1], c1r.at[chunks - 1], mate))
    for k in range(1, chunks):
        acc[k] = product(core, k)
    for g in range(groups):
        lanes = slice(g * width, (g + 1) * width)
        vec[2:3, lanes] = column_sum(grad_sc[g, 0].astype(F32))
        vec[3:4, lanes] = column_sum(grad_sc[g, 2].astype(F32))
    this = pl.ds(pl.multiple_of(side * chunk, 128), chunk)
    that = pl.ds(pl.multiple_of((1 - side) * chunk, 128), chunk)
    for k in range(chunks):
        remote(r1.at[k], r1.at[k], c1s.at[k], c1r.at[k], mate).wait_recv()
        s2[k] = (acc[k, :, that] + r1[k, :, that].astype(F32)).astype(BF16)
        go(remote(s2.at[k], r2.at[k], c2s.at[k], c2r.at[k], at.peer(across)))

    loads[1].wait()
    loads[2].wait()
    vec[0:2, :] = jnp.zeros_like(vec[0:2, :])
    weight = weight_rows(w_sc, w_sc.shape[1])

    def token_rows(i):
        rows = pl.ds(pl.multiple_of(i * tile, tile), tile)
        normed, inverse = normalize(x_sc[rows].astype(F32))
        grad = jnp.concatenate([grad_sc[g, part, rows] for part in range(3) for g in range(groups)], 1)
        grad_act = dot(grad, weight, NT)
        gt_ref[rows] = (
            resid_sc[rows] + normalize_back(grad_act * gain, normed, inverse)
        ).astype(BF16)
        vec[0:1, :] += column_sum(grad_act * normed)
        vec[1:2, :] += column_sum(grad_act)

    pl.loop(0, per // tile)(token_rows)

    vec[4:8, :] = sums_ref[1:5, 0:model]
    piece = model // parts
    fc = sums_ref.shape[1] // parts
    bits = min(128, fc)
    vsend[...] = jnp.zeros_like(vsend)
    for g in range(parts):
        vsend[g, 0:8, 0:piece] = vec[:, g * piece : (g + 1) * piece]
        for k in range(fc // bits):
            first = g * fc + k * bits
            vsend[g, 8 + k : 9 + k, 0:bits] = sums_ref[0:1, first : first + bits]

    for k in range(chunks):
        remote(s2.at[k], r2.at[k], c2s.at[k], c2r.at[k], at.peer(across)).wait_recv()
        total = acc[k, :, this] + r1[k, :, this].astype(F32) + r2[k].astype(F32)
        keep[k] = total
        s3[k] = total.astype(BF16)
        for n, g in enumerate(others(f, parts)):
            rows = pl.ds(pl.multiple_of(g * shard, shard), shard)
            go(remote(s3.at[k, rows], r3.at[k, f], c3s.at[k, n], c3r.at[k, f], peer(p, g)))
    for n, g in enumerate(others(f, parts)):
        go(remote(vsend.at[g], vpart.at[f], v1s.at[n], v1r.at[f], peer(p, g)))
    folded = []
    for n, (mine_ref, theirs, full) in enumerate(((fa_sc, xa, fulla), (fp_sc, xp, fullp))):
        cross[n].wait()
        wide = mine_ref.shape[1]
        here = full.at[:, pl.ds(pl.multiple_of(core * wide, 128), wide)]
        there = full.at[:, pl.ds(pl.multiple_of((1 - core) * wide, 128), wide)]
        here[...] = mine_ref[...].astype(F32) + theirs[...].astype(F32)
        go(remote(here, here, ys.at[n], yr.at[n], mate))
        folded.append(remote(there, there, ys.at[n], yr.at[n], mate))
    for g in others(f, parts):
        remote(vsend.at[g], vpart.at[g], v1s.at[0], v1r.at[g], peer(p, g)).wait_recv()
    total = vsend[f]
    for g in others(f, parts):
        total = total + vpart[g]
    mine[p] = total
    for k in range(chunks):
        for g in others(f, parts):
            remote(r3.at[k, g], r3.at[k, g], c3s.at[k, 0], c3r.at[k, g], peer(p, g)).wait_recv()
        total = keep[k, pl.ds(pl.multiple_of(f * shard, shard), shard)]
        for g in others(f, parts):
            total = total + r3[k, g].astype(F32)
        there = out.at[:, lane(core, side, k)]
        there[...] = total.astype(BF16)
        for n, q in enumerate(at.others()):
            go(remote(there, there, c4s.at[k, n], c4r.at[k, p], at.peer(q)))
        if k == 0:
            for n, q in enumerate(at.others()):
                go(remote(mine.at[p], mine.at[p], v2s.at[n], v2r.at[p], at.peer(q)))
    for copy in folded:
        copy.wait_recv()
    go_ref[...] = fulla[:, 0:model]
    gf_ref[...] = fulla[:, model:]
    gpo_ref[...] = fullp[...]
    for q in at.others():
        remote(mine.at[q], mine.at[q], v2s.at[0], v2r.at[q], at.peer(q)).wait_recv()
    total = mine[0]
    for q in range(1, groups):
        total = total + mine[q]
    gv_ref[...] = total
    for k in range(chunks):
        for q in at.others():
            there = out.at[:, lane(lax.rem(q, 2), q // 2, k)]
            remote(there, there, c4s.at[k, 0], c4r.at[k, q], at.peer(q)).wait_recv()
    gw_ref[...] = out[...].astype(F32)
    for copy in copies:
        copy.wait_send()
    for q in at.others():
        for b in range(count):
            for part in range(3):
                out_copy(q * count + b, part).wait_send()
    near.wait_send()
    for b in range(count):
        for d in range(2):
            far_copy(b, d).wait_send()


def back(qkv, grad, out, lse, starts, g_a, g_p, x, resid, weight, small, sums, size=512, tile=256):
    groups, _, per, width = qkv.shape
    length = groups * per
    heads = width // HEAD_DIM
    count = per // size
    parts = g_a.shape[0]
    model = x.shape[1]
    triple = 3 * model
    shard = model // parts
    chunk = 128
    chunks = triple // 4 // chunk
    dma = pltpu.SemaphoreType.DMA
    vm = pltpu.VMEM
    vmem = pl.BlockSpec(memory_space=pltpu.VMEM)
    far = pl.BlockSpec(memory_space=pl.ANY)
    f_a = (g_a.shape[1], g_a.shape[2] // 2)
    f_p = (g_p.shape[1], g_p.shape[2] // 2)
    return pl.pallas_call(
        functools.partial(back_kernel, size, heads, parts, tile),
        out_shape=(
            jax.ShapeDtypeStruct((per, model), BF16),
            jax.ShapeDtypeStruct((shard, triple), F32),
            jax.ShapeDtypeStruct((16, 128), F32),
            jax.ShapeDtypeStruct((f_a[0], model), F32),
            jax.ShapeDtypeStruct((f_a[0], 2 * f_a[1] - model), F32),
            jax.ShapeDtypeStruct((f_p[0], 2 * f_p[1]), F32),
        ),
        in_specs=[vmem] * 5 + [far] * 5 + [vmem] * 2,
        out_specs=[vmem] * 6,
        scratch_shapes=[
            vm((groups, per, width), BF16), vm((8, length), F32),
            vm((width, length), F32), vm((length, width), F32),
            vm((length, width), F32), vm(qkv.shape, BF16), vm(qkv.shape, BF16),
            dma(()), dma(()), dma((2, count)), dma((groups, count)),
            dma((groups * count, 3)), dma((groups, 3, count)),
            vm(f_a, BF16), vm(f_p, BF16), vm(x.shape, BF16), vm(resid.shape, F32),
            vm(weight.shape, BF16), vm(x.shape, BF16), dma((3,)),
            vm(f_a, BF16), vm(f_p, BF16), vm((f_a[0], 2 * f_a[1]), F32),
            vm((f_p[0], 2 * f_p[1]), F32), dma((2,)), dma((2,)), dma((2,)), dma((2,)),
            vm((chunks, model, 2 * chunk), F32), vm((shard, triple), BF16), vm((8, model), F32),
            vm((groups, 16, 128), F32), vm((parts, 16, 128), F32), vm((parts, 16, 128), F32),
            vm((chunks, model, 2 * chunk), BF16), vm((chunks, model, 2 * chunk), BF16),
            vm((chunks, model, chunk), BF16), vm((chunks, model, chunk), BF16),
            vm((chunks, model, chunk), F32), vm((chunks, model, chunk), BF16),
            vm((chunks, parts, shard, chunk), BF16),
            dma((parts,)), dma((parts,)), dma((groups,)), dma((groups,)),
            dma((chunks,)), dma((chunks,)), dma((chunks,)), dma((chunks,)),
            dma((chunks, parts)), dma((chunks, parts)), dma((chunks, groups)), dma((chunks, groups)),
            *Fold.scratch(*g_a.shape), *Fold.scratch(*g_p.shape),
        ],
        compiler_params=pltpu.CompilerParams(
            vmem_limit_bytes=VMEM_LIMIT, collective_id=3, has_side_effects=True
        ),
        cost_estimate=cost(10 * length * length * width, 24 * length * width, length * length),
        name="back",
    )(qkv, grad, out, lse, starts, g_a, g_p, x, resid, weight, small, sums)


def hand_out_kernel(piece, fc, *refs):
    ins, outs = refs[:6], refs[6:]
    for src, dst in zip(ins[:5], outs[:5]):
        dst[...] = src[...]
    vec = ins[5]
    for k in range(8):
        outs[5 + k][...] = vec[k : k + 1, 0:piece]
    bits = min(fc, 128)
    for k in range(fc // bits):
        outs[13][:, k * bits : (k + 1) * bits] = vec[8 + k : 9 + k, 0:bits]


def hand_out(arrays, vec, piece, fc):
    vmem = pl.BlockSpec(memory_space=pltpu.VMEM)
    return pl.pallas_call(
        functools.partial(hand_out_kernel, piece, fc),
        out_shape=tuple(
            [jax.ShapeDtypeStruct(v.shape, v.dtype) for v in arrays]
            + [jax.ShapeDtypeStruct((1, piece), F32)] * 8
            + [jax.ShapeDtypeStruct((1, fc), F32)]
        ),
        in_specs=[vmem] * 6,
        out_specs=tuple([vmem] * 14),
        compiler_params=params(),
        name="hand_out",
    )(*arrays, vec)


def middle_kernel(
    groups, x_ref, attn_ref, wo_ref, wf_ref, wp_ref, small_ref, fcb_ref, cot_ref,
    out_ref, resid_ref, ga_ref, gwa_ref, gwp_ref, gs_ref,
):
    model = x_ref.shape[-1]
    width = model // groups
    small = small_ref[...]
    w_out = weight_rows(wo_ref, wo_ref.shape[1])
    w_fc = weight_rows(wf_ref, wf_ref.shape[1])
    w_proj = weight_rows(wp_ref, wp_ref.shape[1])
    attn = jnp.concatenate([attn_ref[g] for g in range(groups)], 1)
    resid = x_ref[...].astype(F32) + dot(attn, w_out) + small[OUT_BIAS : OUT_BIAS + 1]
    normed, inverse = normalize(resid)
    gain = small[GAIN_TWO : GAIN_TWO + 1]
    act = (normed * gain + small[BIAS_TWO : BIAS_TWO + 1]).astype(BF16)
    hidden = dot(act, w_fc) + fcb_ref[...]
    sig = 1.0 / (1.0 + jnp.exp(-1.702 * hidden))
    gelu = hidden * sig
    slope = sig + 1.702 * gelu * (1.0 - sig)
    gelu = gelu.astype(BF16)
    out_ref[...] = (resid + dot(gelu, w_proj) + small[PROJ_BIAS : PROJ_BIAS + 1]).astype(BF16)
    up = cot_ref[...]
    gwp_ref[...] = dot(gelu, up, TN).astype(BF16)
    grad_hidden = dot(up, w_proj, NT) * slope
    low = grad_hidden.astype(BF16)
    gwa_ref[:, model:] = dot(act, low, TN).astype(BF16)
    grad_act = dot(low, w_fc, NT)
    up = up.astype(F32)
    grad_resid = up + normalize_back(grad_act * gain, normed, inverse)
    resid_ref[...] = grad_resid
    resid_low = grad_resid.astype(BF16)
    gwa_ref[:, 0:model] = dot(attn, resid_low, TN).astype(BF16)
    grad_attn = dot(resid_low, w_out, NT).astype(BF16)
    for g in range(groups):
        ga_ref[g] = grad_attn[:, g * width : (g + 1) * width]
    gs_ref[0:1, :] = column_sum(grad_hidden)
    gs_ref[1:2, 0:model] = column_sum(grad_resid)
    gs_ref[2:3, 0:model] = column_sum(grad_act * normed)
    gs_ref[3:4, 0:model] = column_sum(grad_act)
    gs_ref[4:5, 0:model] = column_sum(up)


def middle(x, attn, w_out, w_fc, w_proj, small, fc_bias, cotangent):
    length, model = x.shape
    tile = length
    groups = attn.shape[0]
    hid = w_fc.shape[2]
    rows = pl.BlockSpec((tile, model), lambda i: (i, 0))
    slabs = pl.BlockSpec((groups, tile, model // groups), lambda i: (0, i, 0))
    return pl.pallas_call(
        functools.partial(middle_kernel, groups),
        out_shape=(
            jax.ShapeDtypeStruct((length, model), BF16),
            jax.ShapeDtypeStruct((length, model), F32),
            jax.ShapeDtypeStruct(attn.shape, BF16),
            jax.ShapeDtypeStruct((model, model + hid), BF16),
            jax.ShapeDtypeStruct((hid, model), BF16),
            jax.ShapeDtypeStruct((8, hid), F32),
        ),
        grid=(length // tile,),
        in_specs=[rows, slabs, whole(w_out.shape), whole(w_fc.shape), whole(w_proj.shape), whole(small.shape),
                  whole(fc_bias.shape), rows],
        out_specs=[rows, rows, slabs, whole((model, model + hid)),
                   whole((hid, model)), whole((8, hid))],
        compiler_params=params(),
        cost_estimate=cost(12 * length * model * hid + 6 * length * model * model,
                           16 * model * hid, length * hid),
        name="middle",
    )(x, attn, w_out, w_fc, w_proj, small, fc_bias, cotangent)


def per_device(
    tokens, starts, norm1_gain, norm1_bias, w_qkv, q_bias, v_bias, w_out, out_bias, norm2_gain,
    norm2_bias, w_fc, fc_bias, w_proj, proj_bias, cotangent,
):
    groups = lax.axis_size("sp")
    parts = lax.axis_size("fsdp")
    rows, triple = w_qkv.shape
    piece = norm1_gain.shape[0]
    x = tokens[0]
    vectors = [
        norm1_gain, norm1_bias, q_bias, v_bias, out_bias, norm2_gain, norm2_bias, proj_bias, fc_bias
    ]
    qkv, out, lse, attn, doc_first, small, fcb, packed, *wide = front(
        x, w_qkv, starts, vectors, (w_out, w_fc, w_proj), groups, parts
    )
    if rows % 16 == 0:
        weight, weight_count = packed, rows
    else:
        weight, weight_count = packed.reshape(1, parts * rows, triple), parts * rows
    wide = [w if w.shape[1] % 16 == 0 else w.reshape(1, -1, w.shape[2]) for w in wide]
    block_out, grad_resid, grad_attn, g_a, g_p, sums = middle(
        x, attn, *wide, small, fcb, cotangent[0]
    )
    grad_tokens, g_q, g_v, g_out, g_fc, g_p = back(
        qkv, grad_attn, out, lse, doc_first,
        g_a.reshape(parts, -1, g_a.shape[1]), g_p.reshape(parts, -1, g_p.shape[1]),
        x, grad_resid, weight, small, sums,
    )
    grad_tokens, g_q, g_out, g_fc, g_p, *vec, g_fcb = hand_out(
        (grad_tokens, g_q, g_out, g_fc, g_p), g_v, piece, fc_bias.shape[0]
    )
    vec = [v.reshape(-1) for v in vec]
    return (
        block_out[None], grad_tokens[None], vec[0], vec[1], g_q, vec[2], vec[3],
        g_out, vec[4], vec[5], vec[6], g_fc, g_fcb.reshape(-1), g_p, vec[7],
    )


def solution(mesh):
    row, mat = P("fsdp"), P("fsdp", None)
    stream = P("fsdp", "sp", None)
    return jax.shard_map(
        per_device,
        mesh=mesh,
        in_specs=(stream, P("fsdp", "sp"), row, row, mat, row, row, mat, row, row, row, mat, row,
                  mat, row, stream),
        out_specs=(stream, stream, row, row, mat, row, row, mat, row, row, row, mat, row, mat, row),
        check_vma=False,
    )
```

```python
import functools

import jax
import jax.numpy as jnp
from jax import lax
from jax.experimental import pallas as pl
from jax.experimental.pallas import tpu as pltpu
from jax.sharding import PartitionSpec as P

HEAD_DIM = 64
EPSILON = 1e-05
NEG = -1e30
F32 = jnp.float32
BF16 = jnp.bfloat16
LOG2E = 1.4426950408889634
FAR = 2.0**60
SPARE = 60
RELAY_AT, RELAY_GAP, TWIN_AT = 12, 3, 20
NN = (((1,), (0,)), ((), ()))
NT = (((1,), (1,)), ((), ()))
TN = (((0,), (0,)), ((), ()))
VMEM_LIMIT = 60 << 20


def dot(left, right, dims=NN):
    return lax.dot_general(left, right, dims, preferred_element_type=F32)


def normalize(values):
    centered = values - jnp.mean(values, -1, keepdims=True)
    inverse = lax.rsqrt(jnp.mean(centered * centered, -1, keepdims=True) + EPSILON)
    return centered * inverse, inverse


def normalize_back(incoming, normed, inverse):
    return inverse * (
        incoming
        - jnp.mean(incoming, -1, keepdims=True)
        - normed * jnp.mean(incoming * normed, -1, keepdims=True)
    )


def whole(shape):
    return pl.BlockSpec(shape, lambda *_: (0,) * len(shape))


def params():
    return pltpu.CompilerParams(vmem_limit_bytes=VMEM_LIMIT)


def cost(flops, size, exps=0):
    return pl.CostEstimate(flops=flops, bytes_accessed=size, transcendentals=exps)


def weight_rows(w_ref, rows):
    parts = w_ref.shape[0]
    return w_ref[:, 0:rows, :].reshape(parts * rows, w_ref.shape[2])


def peer(sp, fsdp):
    return {"sp": sp, "fsdp": fsdp}


def remote(src, dst, send, recv, where):
    return pltpu.make_async_remote_copy(
        src_ref=src, dst_ref=dst, send_sem=send, recv_sem=recv,
        device_id=where, device_id_type=pl.DeviceIdType.MESH,
    )


def others(me, count):
    return [lax.rem(me + k, count) for k in range(1, count)]


def greet(groups, parts):
    p, f = lax.axis_index("sp"), lax.axis_index("fsdp")
    barrier = pltpu.get_barrier_semaphore()
    for q in others(p, groups):
        pl.semaphore_signal(barrier, inc=1, device_id=peer(q, f), device_id_type=pl.DeviceIdType.MESH)
    for g in others(f, parts):
        pl.semaphore_signal(barrier, inc=1, device_id=peer(p, g), device_id_type=pl.DeviceIdType.MESH)


def greeted(groups, parts):
    pl.semaphore_wait(pltpu.get_barrier_semaphore(), groups + parts - 2)


class Spread:
    def __init__(self, src, dst, parts, send, recv, own):
        self.src, self.dst, self.send, self.recv, self.own = src, dst, send, recv, own
        self.p, self.f = lax.axis_index("sp"), lax.axis_index("fsdp")
        core = lax.rem(self.p, 2)
        self.mate = self.p + 1 - 2 * core
        self.parts, self.major = parts, parts // 2
        self.a, self.b = self.f // 2, lax.rem(self.f, 2)
        self.twin = self.a * 2 + 1 - self.b
        half = src.shape[1] // 2
        self.lanes = pl.ds(pl.multiple_of(core * half, 128), half)
        self.mate_lanes = pl.ds(pl.multiple_of((1 - core) * half, 128), half)

    def back(self, k):
        return lax.rem(self.a + self.major - k, self.major)

    def block(self, g, lanes=None):
        return self.dst.at[g, :, self.lanes if lanes is None else lanes]

    def first(self, k):
        where = lax.rem(self.a + k, self.major) * 2 + self.b
        where = self.twin if k == 0 else where
        return remote(
            self.src.at[:, self.lanes], self.block(self.f), self.send.at[0, k],
            self.recv.at[0, self.f], peer(self.p, where),
        )

    def to_twin(self, k):
        g = self.back(k) * 2 + self.b
        return remote(
            self.block(g), self.block(g), self.send.at[1, k], self.recv.at[0, g],
            peer(self.p, self.twin),
        )

    def to_mate(self, k, b):
        g = self.back(k) * 2 + b
        slot = k if b is self.b else self.major + k
        return remote(
            self.block(g), self.block(g), self.send.at[2, slot], self.recv.at[1, g],
            peer(self.mate, self.f),
        )

    def keep(self):
        return pltpu.make_async_copy(self.src, self.dst.at[self.f], self.own)

    def start_lines(self):
        self.keep().start()
        for k in range(1, self.major):
            self.first(k).start()

    def start_twin(self):
        self.first(0).start()

    def start(self):
        self.start_lines()
        self.start_twin()

    def relay(self, k):
        self.to_twin(k).wait_recv()
        self.to_twin(k).start()
        self.to_mate(k, self.b).start()

    def relay_twin(self, k):
        other = 1 - self.b
        copy = self.to_mate(k, other)
        g = self.back(k) * 2 + other
        remote(
            self.block(g), self.block(g), self.send.at[1, 0], self.recv.at[0, g],
            peer(self.p, self.twin),
        ).wait_recv()
        copy.start()

    def finish(self):
        for g in others(self.f, self.parts):
            there = self.block(g, self.mate_lanes)
            remote(
                there, there, self.send.at[1, 0], self.recv.at[1, g], peer(self.mate, self.f)
            ).wait_recv()
        for k in range(self.major):
            self.first(k).wait_send()
            self.to_mate(k, 1 - self.b).wait_send()
        for k in range(1, self.major):
            self.to_twin(k).wait_send()
            self.to_mate(k, self.b).wait_send()
        self.keep().wait()

    @staticmethod
    def semaphores(parts):
        dma = pltpu.SemaphoreType.DMA
        return [dma((3, parts)), dma((2, parts)), dma(())]


class Fold:
    def __init__(self, src, out, parts, mine, r1, r2, s2, r3, own, send1, recv1, send2, recv2, send3, recv3):
        self.__dict__.update(
            src=src, out=out, mine=mine, r1=r1, r2=r2, s2=s2, r3=r3, own=own, send1=send1,
            recv1=recv1, send2=send2, recv2=recv2, send3=send3, recv3=recv3,
        )
        self.p, self.f = lax.axis_index("sp"), lax.axis_index("fsdp")
        core = lax.rem(self.p, 2)
        self.mate = self.p + 1 - 2 * core
        self.major = parts // 2
        self.a, self.b = self.f // 2, lax.rem(self.f, 2)
        self.twin = self.a * 2 + 1 - self.b
        half = src.shape[2] // 2
        self.lanes = pl.ds(pl.multiple_of(core * half, 128), half)
        self.mate_lanes = pl.ds(pl.multiple_of((1 - core) * half, 128), half)

    def keep(self):
        return pltpu.make_async_copy(self.src.at[:, :, self.lanes], self.mine, self.own)

    def to_mate(self):
        return remote(
            self.src.at[:, :, self.mate_lanes], self.r1, self.send1, self.recv1,
            peer(self.mate, self.f),
        )

    def to_twin(self, c):
        return remote(
            self.mine.at[c * 2 + 1 - self.b], self.r2.at[c], self.send2.at[c], self.recv2.at[c],
            peer(self.p, self.twin),
        )

    def along(self, k):
        c = lax.rem(self.a + k, self.major)
        return remote(
            self.s2.at[c], self.r3.at[self.a], self.send3.at[c], self.recv3.at[self.a],
            peer(self.p, c * 2 + self.b),
        )

    def start(self):
        self.to_mate().start()
        self.keep().start()

    def pairs(self):
        self.keep().wait()
        self.to_mate().wait()
        self.mine[...] = (self.mine[...].astype(F32) + self.r1[...].astype(F32)).astype(BF16)
        for c in range(self.major):
            self.to_twin(c).start()

    def planes(self):
        for c in range(self.major):
            self.to_twin(c).wait()
            self.s2[c] = (
                self.mine[c * 2 + self.b].astype(F32) + self.r2[c].astype(F32)
            ).astype(BF16)
        for k in range(1, self.major):
            self.along(k).start()

    def lines(self):
        total = self.mine[self.f].astype(F32) + self.r2[self.a].astype(F32)
        for k in range(1, self.major):
            c = lax.rem(self.a + k, self.major)
            remote(
                self.r3.at[c], self.r3.at[c], self.send3.at[0], self.recv3.at[c],
                peer(self.p, self.twin),
            ).wait_recv()
            total = total + self.r3[c].astype(F32)
        self.out[...] = total.astype(BF16)
        for k in range(1, self.major):
            self.along(k).wait_send()

    @staticmethod
    def scratch(parts, rows, lanes):
        dma = pltpu.SemaphoreType.DMA
        major, half = parts // 2, lanes // 2
        return [
            pltpu.VMEM((parts, rows, half), BF16), pltpu.VMEM((parts, rows, half), BF16),
            pltpu.VMEM((major, rows, half), BF16), pltpu.VMEM((major, rows, half), BF16),
            pltpu.VMEM((major, rows, half), BF16), dma(()), dma(()), dma(()),
            dma((major,)), dma((major,)), dma((major,)), dma((major,)),
        ]


def column_sum(x):
    return jnp.sum(x, 0, keepdims=True)


GAIN_ONE, BIAS_ONE, Q_BIAS, V_BIAS, OUT_BIAS, GAIN_TWO, BIAS_TWO, PROJ_BIAS = range(8)


def triangle(index, size):
    row = sum((index >= m * (m + 1) // 2).astype(jnp.int32) for m in range(1, size))
    return row, index - row * (row + 1) // 2


def triangle_by_column(index, size):
    starts = [c * (2 * size + 1 - c) // 2 for c in range(size)]
    col = sum((index >= at).astype(jnp.int32) for at in starts[1:])
    return col + index - col * (2 * size + 1 - col) // 2, col


def pick(cond, this, other):
    return jnp.where(cond, this, other)


class Place:
    def __init__(self, groups, count):
        self.p, self.f = lax.axis_index("sp"), lax.axis_index("fsdp")
        self.side = self.p // 2
        self.core = lax.rem(self.p, 2)
        self.mate = self.p + 1 - 2 * self.core
        far = (1 - self.side) * 2
        self.far = (far + self.core, far + 1 - self.core)
        self.groups = groups
        self.count = count
        self.half = 2 * count
        self.near_block = self.side * self.half
        self.far_block = (1 - self.side) * self.half

    def peer(self, q):
        return peer(q, self.f)

    def others(self):
        return others(self.p, self.groups)

    def meet(self):
        barrier = pltpu.get_barrier_semaphore()
        for q in self.others():
            pl.semaphore_signal(
                barrier, inc=1, device_id=self.peer(q), device_id_type=pl.DeviceIdType.MESH
            )
        pl.semaphore_wait(barrier, self.groups - 1)


def rows_of(block, count, size):
    return block // count, pl.ds(pl.multiple_of(lax.rem(block, count) * size, size), size)


def head_lanes(h, x, rest):
    lane = lax.broadcasted_iota(jnp.int32, x.shape, 1)
    return jnp.where(lane // HEAD_DIM == h, x, rest)


def causal(size):
    rows = lax.broadcasted_iota(jnp.int32, (size, size), 0)
    return rows <= lax.broadcasted_iota(jnp.int32, (size, size), 1)


def document_codes(starts, length):
    shape = (2 * HEAD_DIM, starts.shape[1])
    row = lax.rem(lax.broadcasted_iota(jnp.int32, shape, 0), HEAD_DIM)
    bits = max(1, (length - 1).bit_length())
    bit = lax.shift_right_logical(jnp.broadcast_to(starts, shape), row // 2) & 1
    code = jnp.where(lax.rem(row, 2) == 0, bit, 1 - bit).astype(F32)
    used = row < 2 * bits
    query = jnp.where(used, code, 0.0)
    key = jnp.where(used, (code - 1.0) * FAR, 1.0)
    return query.T.astype(BF16), key.T.astype(BF16)


def value_lanes(values, size):
    shape = (2 * HEAD_DIM, size)
    row = lax.broadcasted_iota(jnp.int32, shape, 0)
    out = jnp.zeros(shape, F32)
    for h, value in enumerate(values):
        rest = -value
        for n in range(3):
            piece = rest.astype(BF16).astype(F32)
            rest = rest - piece
            out = jnp.where(row == (1 - h) * HEAD_DIM + SPARE + n, piece, out)
    return out.T.astype(BF16)


def front_kernel(size, heads, groups, parts, tile, x_ref, wq_ref, st_in, *refs):
    vec_refs, shards, refs = refs[:9], refs[9:12], refs[12:]
    qkv_ref, o_ref, lse_ref, attn_ref, eq_ref, ek_ref, small_ref, fcb_ref, wq_all = refs[:9]
    wide, refs = refs[9:12], refs[12:]
    own_ref, sg, own_vec, vg, m_sc, l_sc, acc_sc = refs[:7]
    v_send, v_recv, s_send, s_recv, near_s, near_r, far_s, far_r, out_s, out_r = refs[7:17]
    first_spread, *spreads = [
        Spread(src, dst, parts, *refs[17 + 3 * n : 20 + 3 * n])
        for n, (src, dst) in enumerate(zip((wq_ref,) + shards, (wq_all,) + wide))
    ]
    per, model = x_ref.shape
    width = model // groups
    count = per // size
    major = parts // 2
    at = Place(groups, count)
    p, f, side, half = at.p, at.f, at.side, at.half

    greet(groups, parts)
    piece = vec_refs[0].shape[1]
    runs, bits = vec_refs[8].shape
    own_vec[...] = jnp.zeros_like(own_vec)
    for k in range(8):
        own_vec[k : k + 1, 0:piece] = vec_refs[k][...].astype(F32)
    own_vec[8 : 8 + runs, 0:bits] = vec_refs[8][...].astype(F32)
    vg[f] = own_vec[...]
    sg[p] = st_in[...]
    m_sc[...] = jnp.full_like(m_sc, NEG)
    l_sc[...] = jnp.zeros_like(l_sc)
    acc_sc[...] = jnp.zeros_like(acc_sc)
    greeted(groups, parts)

    copies = []

    def go(copy):
        copy.start()
        copies.append(copy)

    first_spread.start()
    for k, q in enumerate(at.others()):
        go(remote(st_in, sg.at[p], s_send.at[k], s_recv.at[p], at.peer(q)))
    for k, g in enumerate(others(f, parts)):
        go(remote(own_vec, vg.at[f], v_send.at[k], v_recv.at[f], peer(p, g)))
    for q in at.others():
        remote(st_in, sg.at[q], s_send.at[0], s_recv.at[q], at.peer(q)).wait_recv()

    @pl.loop(0, groups)
    def _(q):
        starts = jnp.concatenate([sg[q, k : k + 1] for k in range(per // 128)], 1)
        rows = pl.ds(pl.multiple_of(q * per, per), per)
        eq_ref[rows], ek_ref[rows] = document_codes(starts, groups * per)

    for k in range(1, major):
        first_spread.relay(k)
    for k in range(major):
        first_spread.relay_twin(k)
    for g in others(f, parts):
        remote(own_vec, vg.at[g], v_send.at[0], v_recv.at[g], peer(p, g)).wait_recv()
    for g in range(parts):
        small_ref[:, g * piece : (g + 1) * piece] = vg[g, 0:8, 0:piece]
        for k in range(runs):
            lane = (g * runs + k) * bits
            fcb_ref[:, lane : lane + bits] = vg[g, 8 + k : 9 + k, 0:bits]
    first_spread.finish()
    for spread in spreads:
        spread.start_lines()

    def far_copy(b, t, d):
        rows = pl.ds(pl.multiple_of(b * size, size), size)
        return remote(
            own_ref.at[at.far[d], t, rows], qkv_ref.at[p, t, rows], far_s.at[d, b, t],
            far_r.at[p, t, b], at.peer(at.far[d]),
        )

    near = remote(own_ref.at[at.mate], qkv_ref.at[p], near_s, near_r, at.peer(at.mate))

    @pl.loop(0, per // tile)
    def _(i):
        rows = pl.ds(pl.multiple_of(i * tile, tile), tile)
        normed, _ = normalize(x_ref[rows].astype(F32))
        small = small_ref[...]
        act = (normed * small[GAIN_ONE : GAIN_ONE + 1] + small[BIAS_ONE : BIAS_ONE + 1]).astype(BF16)
        weight = weight_rows(wq_all, wq_all.shape[1])
        for part, row in ((0, Q_BIAS), (1, None), (2, V_BIAS)):
            out = dot(act, weight[:, part * model : (part + 1) * model])
            if row is not None:
                out = out + small[row : row + 1]
            out = out.astype(BF16)
            if part == 0:
                out = (out.astype(F32) * (HEAD_DIM ** (-0.5) * LOG2E)).astype(BF16)
            for g in range(groups):
                own_ref[g, part, rows] = out[:, g * width : (g + 1) * width]

        @pl.when(lax.rem(i + 1, size // tile) == 0)
        def _():
            for n in range(3):
                for d in range(2):
                    far_copy((i + 1) // (size // tile) - 1, lax.rem(n + pick(side == 1, 0, 1), 3), d).start()

    near.start()
    for spread in spreads:
        spread.start_twin()
    qkv_ref[p] = own_ref[p]

    def far_wait(t, block):
        src, rows = rows_of(block, count, size)
        there = qkv_ref.at[src, t, rows]
        remote(there, there, far_s.at[0, 0, 0], far_r.at[src, t, lax.rem(block, count)], at.peer(src)).wait_recv()

    def block(q, k, diagonal):
        src, rows = rows_of(q, count, size)
        cols = pl.ds(pl.multiple_of(q * size, size), size)
        ksrc, krows = rows_of(k, count, size)
        query = qkv_ref[src, 0, rows, :]
        key = qkv_ref[ksrc, 1, krows, :]
        value = qkv_ref[ksrc, 2, krows, :]
        code_q = eq_ref[cols, :]
        code_k = ek_ref[pl.ds(pl.multiple_of(k * size, size), size), :]
        old = [(m_sc[h : h + 1, cols], l_sc[h : h + 1, cols]) for h in range(heads)]
        acc = acc_sc[:, cols]
        scores = [
            dot(head_lanes(h, key, code_k), head_lanes(h, query, code_q), NT) for h in range(heads)
        ]
        new, parts = [], []
        for h in range(heads):
            s = scores[h]
            if diagonal:
                s = jnp.where(causal(size), s, NEG)
            m_old, l_old = old[h]
            m_new = jnp.maximum(m_old, jnp.max(s, 0, keepdims=True))
            e = jnp.exp2(s - m_new).astype(BF16)
            alpha = jnp.exp2(m_old - m_new)
            mixed = dot(head_lanes(h, value, jnp.ones_like(value)), e, TN)
            low, other = h * HEAD_DIM, (1 - h) * HEAD_DIM
            new.append((m_new, l_old * alpha + mixed[other : other + 1]))
            parts.append(acc[low : low + HEAD_DIM] * alpha + mixed[low : low + HEAD_DIM])
        acc_sc[:, cols] = jnp.concatenate(parts, 0)
        for h in range(heads):
            m_sc[h : h + 1, cols], l_sc[h : h + 1, cols] = new[h]

    def out_copy(q):
        src, rows = rows_of(q, count, size)
        return remote(
            o_ref.at[src, rows], attn_ref.at[p, rows], out_s.at[q], out_r.at[p, lax.rem(q, count)],
            at.peer(src),
        )

    def finish(q):
        src, rows = rows_of(q, count, size)
        cols = pl.ds(pl.multiple_of(q * size, size), size)
        parts = []
        for h in range(heads):
            sl = slice(h * HEAD_DIM, (h + 1) * HEAD_DIM)
            total = l_sc[h : h + 1, cols]
            parts.append(acc_sc[sl, cols] * (1.0 / total))
            lse_ref[h : h + 1, cols] = m_sc[h : h + 1, cols] + jnp.log2(total)
        out = jnp.concatenate(parts, 0).T.astype(BF16)
        o_ref[src, rows] = out

        @pl.when(src == p)
        def _():
            attn_ref[p, rows] = out

        @pl.when(src != p)
        def _():
            out_copy(q).start()

    small = count * (count + 1) // 2
    cross = 2 * small + count * count
    bulk = cross + half * half
    end = bulk + half * (half + 1) // 2

    @pl.loop(0, end)
    def _(step):
        second = step >= small
        row, col = triangle(step - pick(second, small, 0), count)
        base = pick(second, at.mate, p) * count
        q, k = base + row, base + col
        c = step - 2 * small
        in_cross = (step >= 2 * small) & (step < cross)
        q = pick(in_cross, at.near_block + count + c // count, q)
        k = pick(in_cross, at.near_block + lax.rem(c, count), k)
        c = step - cross
        in_bulk = (step >= cross) & (step < bulk)
        outer, inner = c // half, lax.rem(c, half)
        outer = lax.rem(outer, 2) * count + outer // 2
        q = pick(in_bulk, half + pick(side == 0, outer, inner), q)
        k = pick(in_bulk, pick(side == 0, inner, outer), k)
        in_last = step >= bulk
        row, col = triangle(step - bulk, half)
        q = pick(in_last, at.far_block + row, q)
        k = pick(in_last, at.far_block + col, k)

        @pl.when(step == small)
        def _():
            near.wait_recv()

        starts_outer = in_bulk & (inner == 0)
        starts_row = in_last & (col == 0)

        @pl.when((starts_outer & (side == 0)) | (starts_row & (side == 1)))
        def _():
            far_wait(0, q)

        @pl.when((starts_outer & (side == 1)) | (starts_row & (side == 0)))
        def _():
            far_block = pick(in_bulk, k, q)
            far_wait(1, far_block)
            far_wait(2, far_block)

        @pl.when(q == k)
        def _():
            block(q, k, True)

        @pl.when(q != k)
        def _():
            block(q, k, False)

        for n in range(1, major):
            @pl.when(step == RELAY_AT + (n - 1) * RELAY_GAP * 2 // (major - 1))
            def _(n=n):
                for spread in spreads:
                    spread.relay(n)
        for n in range(major):
            @pl.when(step == TWIN_AT + n * (end - 1 - TWIN_AT) // (major - 1))
            def _(n=n):
                for spread in spreads:
                    spread.relay_twin(n)

        near_done = step == pick(side == 0, cross, bulk) - 1
        low = pick(near_done, at.near_block, q)
        high = pick(near_done, at.near_block + half, pick(in_last & (q == k), q + 1, q))
        pl.loop(low, high)(finish)

    for q in at.others():
        for b in range(count):
            rows = pl.ds(b * size, size)
            there = attn_ref.at[q, rows]
            remote(there, there, out_s.at[0], out_r.at[q, b], at.peer(q)).wait_recv()
            out_copy(q * count + b).wait_send()
    near.wait_send()
    for b in range(count):
        for t in range(3):
            for d in range(2):
                far_copy(b, t, d).wait_send()
    for copy in copies:
        copy.wait_send()
    for spread in spreads:
        spread.finish()


def front(x, w_qkv, starts, vectors, shards, groups, parts, size=512, tile=256):
    per, model = x.shape
    length = groups * per
    width = model // groups
    heads = width // HEAD_DIM
    count = per // size
    starts = starts.reshape(-1, 128)
    fc = vectors[8].shape[0]
    piece = vectors[0].shape[0]
    vectors = [v.reshape(1, -1) for v in vectors[:8]] + [vectors[8].reshape(-1, min(fc, 128))]
    dma = pltpu.SemaphoreType.DMA
    vmem = pl.BlockSpec(memory_space=pltpu.VMEM)
    slabs = (groups, 3, per, width)
    return pl.pallas_call(
        functools.partial(front_kernel, size, heads, groups, parts, tile),
        out_shape=(
            jax.ShapeDtypeStruct(slabs, BF16),
            jax.ShapeDtypeStruct((groups, per, width), BF16),
            jax.ShapeDtypeStruct((8, length), F32),
            jax.ShapeDtypeStruct((groups, per, width), BF16),
            jax.ShapeDtypeStruct((length, width), BF16),
            jax.ShapeDtypeStruct((length, width), BF16),
            jax.ShapeDtypeStruct((8, parts * piece), F32),
            jax.ShapeDtypeStruct((1, parts * fc), F32),
            jax.ShapeDtypeStruct((parts,) + w_qkv.shape, BF16),
            *[jax.ShapeDtypeStruct((parts,) + shard.shape, BF16) for shard in shards],
        ),
        in_specs=[vmem] * 15,
        out_specs=[vmem] * 9 + [pl.BlockSpec(memory_space=pl.ANY)] * 3,
        scratch_shapes=[
            pltpu.VMEM(slabs, BF16), pltpu.VMEM((groups,) + starts.shape, jnp.int32),
            pltpu.VMEM((16, 128), F32), pltpu.VMEM((parts, 16, 128), F32),
            pltpu.VMEM((8, length), F32), pltpu.VMEM((8, length), F32),
            pltpu.VMEM((width, length), F32),
            dma((parts,)), dma((parts,)), dma((groups,)), dma((groups,)), dma(()), dma(()),
            dma((2, count, 3)), dma((groups, 3, count)), dma((groups * count,)), dma((groups, count)),
        ] + Spread.semaphores(parts) * 4,
        compiler_params=pltpu.CompilerParams(
            vmem_limit_bytes=VMEM_LIMIT, collective_id=2, has_side_effects=True
        ),
        cost_estimate=cost(4 * length * length * width, 16 * length * width, length * length),
        name="front",
    )(x, w_qkv, starts, *vectors, *shards)


def back_kernel(
    size, heads, parts, tile, qkv_ref, own_ref, o_ref, lse_ref, eq_ref, ek_ref, ga_ref, gp_ref,
    x_any, resid_any, w_any, small_ref, sums_ref,
    gt_ref, gw_ref, gv_ref, go_ref, gf_ref, gpo_ref, *refs
):
    (do_sc, qa_sc, da_sc, dqt_sc, dk_sc, dv_sc, stage, grad_sc,
     near_s, near_r, far_s, far_r, out_s, out_r) = refs[:14]
    fa_sc, fp_sc, x_sc, resid_sc, w_sc, act_sc, load = refs[14:21]
    (xa, xp, fulla, fullp, xs, xr, ys, yr) = refs[21:29]
    (acc, out, vec, mine, vsend, vpart, low, r1, s2, r2, keep, s3, r3) = refs[29:42]
    (v1s, v1r, v2s, v2r, c1s, c1r, c2s, c2r, c3s, c3r, c4s, c4r) = refs[42:54]
    folds = [Fold(ga_ref, fa_sc, parts, *refs[54:66]), Fold(gp_ref, fp_sc, parts, *refs[66:])]
    groups, _, per, width = qkv_ref.shape
    model = x_sc.shape[1]
    count = per // size
    at = Place(groups, count)
    p, f, side, core, half = at.p, at.f, at.side, at.core, at.half
    scale = HEAD_DIM ** (-0.5)
    loads = [
        pltpu.make_async_copy(src, dst, load.at[n])
        for n, (src, dst) in enumerate(((x_any, x_sc), (w_any, w_sc), (resid_any, resid_sc)))
    ]
    for copy in loads:
        copy.start()
    greet(groups, parts)
    dqt_sc[...] = jnp.zeros_like(dqt_sc)
    dk_sc[...] = jnp.zeros_like(dk_sc)
    dv_sc[...] = jnp.zeros_like(dv_sc)
    do_sc[p] = own_ref[p]
    greeted(groups, parts)

    near = remote(own_ref.at[at.mate], do_sc.at[p], near_s, near_r, at.peer(at.mate))
    near.start()

    def far_copy(b, d):
        rows = pl.ds(b * size, size)
        return remote(
            own_ref.at[at.far[d], rows], do_sc.at[p, rows], far_s.at[d, b], far_r.at[p, b],
            at.peer(at.far[d]),
        )

    for b in range(count):
        for d in range(2):
            far_copy(b, d).start()
    for fold in folds:
        fold.start()

    small = small_ref[...]
    gain = small[GAIN_ONE : GAIN_ONE + 1]
    bias = small[BIAS_ONE : BIAS_ONE + 1]
    loads[0].wait()

    @pl.loop(0, per // tile)
    def _(i):
        rows = pl.ds(pl.multiple_of(i * tile, tile), tile)
        normed, _ = normalize(x_sc[rows].astype(F32))
        act_sc[rows] = (normed * gain + bias).astype(BF16)

    def columns(block):
        return pl.ds(pl.multiple_of(block * size, size), size)

    def prepare(q):
        src, rows = rows_of(q, count, size)
        cols = columns(q)
        prod = (do_sc[src, rows].astype(F32) * o_ref[src, rows].astype(F32)).T
        delta = [
            jnp.sum(prod[h * HEAD_DIM : (h + 1) * HEAD_DIM], 0, keepdims=True) for h in range(heads)
        ]
        da_sc[cols, :] = value_lanes(delta, size)
        lse = [lse_ref[h : h + 1, cols] for h in range(heads)]
        qa_sc[cols, :] = eq_ref[cols, :] + value_lanes(lse, size)

    def block(q, k, diagonal):
        src, rows = rows_of(q, count, size)
        cols, kcols = columns(q), columns(k)
        ksrc, krows = rows_of(k, count, size)
        query, query_rest = qkv_ref[src, 0, rows, :], qa_sc[cols, :]
        grad, grad_rest = do_sc[src, rows], da_sc[cols, :]
        key, key_rest = qkv_ref[ksrc, 1, krows, :], ek_ref[kcols, :]
        value = qkv_ref[ksrc, 2, krows, :]
        query = [head_lanes(h, query, query_rest) for h in range(heads)]
        grad = [head_lanes(h, grad, grad_rest) for h in range(heads)]
        scores = [dot(head_lanes(h, key, key_rest), query[h], NT) for h in range(heads)]
        slopes = [
            dot(head_lanes(h, value, jnp.ones_like(value)), grad[h], NT) for h in range(heads)
        ]
        dqt, dv, dk = [], None, None
        for h in range(heads):
            s = scores[h]
            if diagonal:
                s = jnp.where(causal(size), s, NEG)
            e = jnp.exp2(s)
            ds = (e * slopes[h]).astype(BF16)
            dvh = dot(e.astype(BF16), grad[h])
            dkh = dot(ds, query[h])
            dv = dvh if dv is None else head_lanes(h, dvh, dv)
            dk = dkh if dk is None else head_lanes(h, dkh, dk)
            dqt.append(dot(key[:, h * HEAD_DIM : (h + 1) * HEAD_DIM], ds, TN))
        dqt_sc[:, cols] += jnp.concatenate(dqt, 0)
        dv_sc[kcols, :] += dv
        dk_sc[kcols, :] += dk

    def out_copy(block, part):
        src, rows = rows_of(block, count, size)
        return remote(
            stage.at[src, part, rows], grad_sc.at[p, part, rows], out_s.at[block, part],
            out_r.at[p, part, lax.rem(block, count)], at.peer(src),
        )

    def give(block, part, value):
        src, rows = rows_of(block, count, size)

        @pl.when(src == p)
        def _():
            grad_sc[p, part, rows] = value

        @pl.when(src != p)
        def _():
            stage[src, part, rows] = value
            out_copy(block, part).start()

    def finish_query(q):
        give(q, 0, (dqt_sc[:, columns(q)] * scale).T.astype(BF16))

    def finish_key(k):
        give(k, 1, (dk_sc[columns(k), :] * (1.0 / LOG2E)).astype(BF16))
        give(k, 2, dv_sc[columns(k), :].astype(BF16))

    small = count * (count + 1) // 2
    far = 2 * small
    bulk = far + half * (half + 1) // 2
    cross = bulk + half * half
    end = cross + count * count

    @pl.loop(0, end)
    def _(step):
        second = step >= small
        row, col = triangle(step - pick(second, small, 0), count)
        base = pick(second, at.mate, p) * count
        q, k = base + row, base + col
        in_far = (step >= far) & (step < bulk)
        row, column = triangle_by_column(step - far, half)
        q = pick(in_far, at.far_block + row, q)
        k = pick(in_far, at.far_block + column, k)
        c = step - bulk
        in_bulk = (step >= bulk) & (step < cross)
        outer, inner = c // half, lax.rem(c, half)
        q = pick(in_bulk, half + pick(side == 0, outer, inner), q)
        k = pick(in_bulk, pick(side == 0, inner, outer), k)
        c = step - cross
        in_cross = step >= cross
        q = pick(in_cross, at.near_block + count + c // count, q)
        k = pick(in_cross, at.near_block + lax.rem(c, count), k)

        @pl.when(step == small)
        def _():
            near.wait_recv()

        @pl.when(in_far & (column == 0))
        def _():
            src, rows = rows_of(q, count, size)
            there = do_sc.at[src, rows]
            remote(there, there, far_s.at[0, 0], far_r.at[src, lax.rem(q, count)], at.peer(src)).wait_recv()

        @pl.when(((step < far) & (col == 0)) | (in_far & (column == 0)))
        def _():
            prepare(q)

        @pl.when(q == k)
        def _():
            block(q, k, True)

        @pl.when(q != k)
        def _():
            block(q, k, False)

        for n, fold in enumerate(folds):
            pl.when(step == end // 6 + n)(fold.pairs)
            pl.when(step == end // 2 + 1 + 3 * n)(fold.planes)
            pl.when(step == end - 2 + n)(fold.lines)

        column_done = in_far & (row == half - 1)
        outer_done = in_bulk & (inner == half - 1)
        done = step == end - 1
        near_low, near_high = at.near_block, at.near_block + half
        query = (column_done & (side == 1)) | (outer_done & (side == 0))
        block_id = at.far_block + pick(in_far, column, outer)
        pl.loop(
            pick(done, near_low, block_id),
            pick(done, near_high, pick(query, block_id + 1, block_id)),
        )(finish_query)
        key = (column_done & (side == 0)) | (outer_done & (side == 1))
        pl.loop(
            pick(done, near_low, block_id),
            pick(done, near_high, pick(key, block_id + 1, block_id)),
        )(finish_key)

    across = p + groups // 2 - side * groups
    cross = [
        remote(src, dst, xs.at[n], xr.at[n], at.peer(across))
        for n, (src, dst) in enumerate(((fa_sc, xa), (fp_sc, xp)))
    ]
    for copy in cross:
        copy.start()
    for q in at.others():
        for b in range(count):
            for part in range(3):
                there = grad_sc.at[q, part, pl.ds(b * size, size)]
                remote(there, there, out_s.at[0, 0], out_r.at[q, part, b], at.peer(q)).wait_recv()

    copies = []

    def go(copy):
        copy.start()
        copies.append(copy)

    shard = model // parts
    chunks, chunk = acc.shape[0], acc.shape[2] // 2

    def number(c, s, k):
        return (c * 2 + s) * chunks + k

    def lane(c, s, k):
        return pl.ds(pl.multiple_of(number(c, s, k) * chunk, 128), chunk)

    def product(c, k):
        pair = []
        for s in range(2):
            n = number(c, s, k)
            pair.append(grad_sc[lax.rem(n, groups), n // groups])
        return dot(act_sc[...], jnp.concatenate(pair, 1), TN)

    mate = at.peer(at.mate)
    for k in range(chunks):
        low[k] = product(1 - core, k).astype(BF16)
        if k:
            go(remote(low.at[k - 1], r1.at[k - 1], c1s.at[k - 1], c1r.at[k - 1], mate))
    acc[0] = product(core, 0)
    go(remote(low.at[chunks - 1], r1.at[chunks - 1], c1s.at[chunks - 1], c1r.at[chunks - 1], mate))
    for k in range(1, chunks):
        acc[k] = product(core, k)
    for g in range(groups):
        lanes = slice(g * width, (g + 1) * width)
        vec[2:3, lanes] = column_sum(grad_sc[g, 0].astype(F32))
        vec[3:4, lanes] = column_sum(grad_sc[g, 2].astype(F32))
    this = pl.ds(pl.multiple_of(side * chunk, 128), chunk)
    that = pl.ds(pl.multiple_of((1 - side) * chunk, 128), chunk)
    for k in range(chunks):
        remote(r1.at[k], r1.at[k], c1s.at[k], c1r.at[k], mate).wait_recv()
        s2[k] = (acc[k, :, that] + r1[k, :, that].astype(F32)).astype(BF16)
        go(remote(s2.at[k], r2.at[k], c2s.at[k], c2r.at[k], at.peer(across)))

    loads[1].wait()
    loads[2].wait()
    vec[0:2, :] = jnp.zeros_like(vec[0:2, :])
    weight = weight_rows(w_sc, w_sc.shape[1])

    def token_rows(i):
        rows = pl.ds(pl.multiple_of(i * tile, tile), tile)
        normed, inverse = normalize(x_sc[rows].astype(F32))
        grad = jnp.concatenate([grad_sc[g, part, rows] for part in range(3) for g in range(groups)], 1)
        grad_act = dot(grad, weight, NT)
        gt_ref[rows] = (
            resid_sc[rows] + normalize_back(grad_act * gain, normed, inverse)
        ).astype(BF16)
        vec[0:1, :] += column_sum(grad_act * normed)
        vec[1:2, :] += column_sum(grad_act)

    pl.loop(0, per // tile)(token_rows)

    vec[4:8, :] = sums_ref[1:5, 0:model]
    piece = model // parts
    fc = sums_ref.shape[1] // parts
    bits = min(128, fc)
    vsend[...] = jnp.zeros_like(vsend)
    for g in range(parts):
        vsend[g, 0:8, 0:piece] = vec[:, g * piece : (g + 1) * piece]
        for k in range(fc // bits):
            first = g * fc + k * bits
            vsend[g, 8 + k : 9 + k, 0:bits] = sums_ref[0:1, first : first + bits]

    for k in range(chunks):
        remote(s2.at[k], r2.at[k], c2s.at[k], c2r.at[k], at.peer(across)).wait_recv()
        total = acc[k, :, this] + r1[k, :, this].astype(F32) + r2[k].astype(F32)
        keep[k] = total
        s3[k] = total.astype(BF16)
        for n, g in enumerate(others(f, parts)):
            rows = pl.ds(pl.multiple_of(g * shard, shard), shard)
            go(remote(s3.at[k, rows], r3.at[k, f], c3s.at[k, n], c3r.at[k, f], peer(p, g)))
    for n, g in enumerate(others(f, parts)):
        go(remote(vsend.at[g], vpart.at[f], v1s.at[n], v1r.at[f], peer(p, g)))
    folded = []
    for n, (mine_ref, theirs, full) in enumerate(((fa_sc, xa, fulla), (fp_sc, xp, fullp))):
        cross[n].wait()
        wide = mine_ref.shape[1]
        here = full.at[:, pl.ds(pl.multiple_of(core * wide, 128), wide)]
        there = full.at[:, pl.ds(pl.multiple_of((1 - core) * wide, 128), wide)]
        here[...] = mine_ref[...].astype(F32) + theirs[...].astype(F32)
        go(remote(here, here, ys.at[n], yr.at[n], mate))
        folded.append(remote(there, there, ys.at[n], yr.at[n], mate))
    for g in others(f, parts):
        remote(vsend.at[g], vpart.at[g], v1s.at[0], v1r.at[g], peer(p, g)).wait_recv()
    total = vsend[f]
    for g in others(f, parts):
        total = total + vpart[g]
    mine[p] = total
    for k in range(chunks):
        for g in others(f, parts):
            remote(r3.at[k, g], r3.at[k, g], c3s.at[k, 0], c3r.at[k, g], peer(p, g)).wait_recv()
        total = keep[k, pl.ds(pl.multiple_of(f * shard, shard), shard)]
        for g in others(f, parts):
            total = total + r3[k, g].astype(F32)
        there = out.at[:, lane(core, side, k)]
        there[...] = total.astype(BF16)
        for n, q in enumerate(at.others()):
            go(remote(there, there, c4s.at[k, n], c4r.at[k, p], at.peer(q)))
        if k == 0:
            for n, q in enumerate(at.others()):
                go(remote(mine.at[p], mine.at[p], v2s.at[n], v2r.at[p], at.peer(q)))
    for copy in folded:
        copy.wait_recv()
    go_ref[...] = fulla[:, 0:model]
    gf_ref[...] = fulla[:, model:]
    gpo_ref[...] = fullp[...]
    for q in at.others():
        remote(mine.at[q], mine.at[q], v2s.at[0], v2r.at[q], at.peer(q)).wait_recv()
    total = mine[0]
    for q in range(1, groups):
        total = total + mine[q]
    gv_ref[...] = total
    for k in range(chunks):
        for q in at.others():
            there = out.at[:, lane(lax.rem(q, 2), q // 2, k)]
            remote(there, there, c4s.at[k, 0], c4r.at[k, q], at.peer(q)).wait_recv()
    gw_ref[...] = out[...].astype(F32)
    for copy in copies:
        copy.wait_send()
    for q in at.others():
        for b in range(count):
            for part in range(3):
                out_copy(q * count + b, part).wait_send()
    near.wait_send()
    for b in range(count):
        for d in range(2):
            far_copy(b, d).wait_send()


def back(qkv, grad, out, lse, code_q, code_k, g_a, g_p, x, resid, weight, small, sums, size=512, tile=256):
    groups, _, per, width = qkv.shape
    length = groups * per
    heads = width // HEAD_DIM
    count = per // size
    parts = g_a.shape[0]
    model = x.shape[1]
    triple = 3 * model
    shard = model // parts
    chunk = 128
    chunks = triple // 4 // chunk
    dma = pltpu.SemaphoreType.DMA
    vm = pltpu.VMEM
    vmem = pl.BlockSpec(memory_space=pltpu.VMEM)
    far = pl.BlockSpec(memory_space=pl.ANY)
    f_a = (g_a.shape[1], g_a.shape[2] // 2)
    f_p = (g_p.shape[1], g_p.shape[2] // 2)
    return pl.pallas_call(
        functools.partial(back_kernel, size, heads, parts, tile),
        out_shape=(
            jax.ShapeDtypeStruct((per, model), BF16),
            jax.ShapeDtypeStruct((shard, triple), F32),
            jax.ShapeDtypeStruct((16, 128), F32),
            jax.ShapeDtypeStruct((f_a[0], model), F32),
            jax.ShapeDtypeStruct((f_a[0], 2 * f_a[1] - model), F32),
            jax.ShapeDtypeStruct((f_p[0], 2 * f_p[1]), F32),
        ),
        in_specs=[vmem] * 6 + [far] * 5 + [vmem] * 2,
        out_specs=[vmem] * 6,
        scratch_shapes=[
            vm((groups, per, width), BF16), vm((length, width), BF16), vm((length, width), BF16),
            vm((width, length), F32), vm((length, width), F32),
            vm((length, width), F32), vm(qkv.shape, BF16), vm(qkv.shape, BF16),
            dma(()), dma(()), dma((2, count)), dma((groups, count)),
            dma((groups * count, 3)), dma((groups, 3, count)),
            vm(f_a, BF16), vm(f_p, BF16), vm(x.shape, BF16), vm(resid.shape, F32),
            vm(weight.shape, BF16), vm(x.shape, BF16), dma((3,)),
            vm(f_a, BF16), vm(f_p, BF16), vm((f_a[0], 2 * f_a[1]), F32),
            vm((f_p[0], 2 * f_p[1]), F32), dma((2,)), dma((2,)), dma((2,)), dma((2,)),
            vm((chunks, model, 2 * chunk), F32), vm((shard, triple), BF16), vm((8, model), F32),
            vm((groups, 16, 128), F32), vm((parts, 16, 128), F32), vm((parts, 16, 128), F32),
            vm((chunks, model, 2 * chunk), BF16), vm((chunks, model, 2 * chunk), BF16),
            vm((chunks, model, chunk), BF16), vm((chunks, model, chunk), BF16),
            vm((chunks, model, chunk), F32), vm((chunks, model, chunk), BF16),
            vm((chunks, parts, shard, chunk), BF16),
            dma((parts,)), dma((parts,)), dma((groups,)), dma((groups,)),
            dma((chunks,)), dma((chunks,)), dma((chunks,)), dma((chunks,)),
            dma((chunks, parts)), dma((chunks, parts)), dma((chunks, groups)), dma((chunks, groups)),
            *Fold.scratch(*g_a.shape), *Fold.scratch(*g_p.shape),
        ],
        compiler_params=pltpu.CompilerParams(
            vmem_limit_bytes=VMEM_LIMIT, collective_id=3, has_side_effects=True
        ),
        cost_estimate=cost(10 * length * length * width, 24 * length * width, length * length),
        name="back",
    )(qkv, grad, out, lse, code_q, code_k, g_a, g_p, x, resid, weight, small, sums)


def hand_out_kernel(piece, fc, *refs):
    ins, outs = refs[:6], refs[6:]
    for src, dst in zip(ins[:5], outs[:5]):
        dst[...] = src[...]
    vec = ins[5]
    for k in range(8):
        outs[5 + k][...] = vec[k : k + 1, 0:piece]
    bits = min(fc, 128)
    for k in range(fc // bits):
        outs[13][:, k * bits : (k + 1) * bits] = vec[8 + k : 9 + k, 0:bits]


def hand_out(arrays, vec, piece, fc):
    vmem = pl.BlockSpec(memory_space=pltpu.VMEM)
    return pl.pallas_call(
        functools.partial(hand_out_kernel, piece, fc),
        out_shape=tuple(
            [jax.ShapeDtypeStruct(v.shape, v.dtype) for v in arrays]
            + [jax.ShapeDtypeStruct((1, piece), F32)] * 8
            + [jax.ShapeDtypeStruct((1, fc), F32)]
        ),
        in_specs=[vmem] * 6,
        out_specs=tuple([vmem] * 14),
        compiler_params=params(),
        name="hand_out",
    )(*arrays, vec)


def middle_kernel(
    groups, x_ref, attn_ref, wo_ref, wf_ref, wp_ref, small_ref, fcb_ref, cot_ref,
    out_ref, resid_ref, ga_ref, gwa_ref, gwp_ref, gs_ref,
):
    model = x_ref.shape[-1]
    width = model // groups
    small = small_ref[...]
    w_out = weight_rows(wo_ref, wo_ref.shape[1])
    w_fc = weight_rows(wf_ref, wf_ref.shape[1])
    w_proj = weight_rows(wp_ref, wp_ref.shape[1])
    attn = jnp.concatenate([attn_ref[g] for g in range(groups)], 1)
    resid = x_ref[...].astype(F32) + dot(attn, w_out) + small[OUT_BIAS : OUT_BIAS + 1]
    normed, inverse = normalize(resid)
    gain = small[GAIN_TWO : GAIN_TWO + 1]
    act = (normed * gain + small[BIAS_TWO : BIAS_TWO + 1]).astype(BF16)
    hidden = dot(act, w_fc) + fcb_ref[...]
    sig = 1.0 / (1.0 + jnp.exp(-1.702 * hidden))
    gelu = hidden * sig
    slope = sig + 1.702 * gelu * (1.0 - sig)
    gelu = gelu.astype(BF16)
    out_ref[...] = (resid + dot(gelu, w_proj) + small[PROJ_BIAS : PROJ_BIAS + 1]).astype(BF16)
    up = cot_ref[...]
    gwp_ref[...] = dot(gelu, up, TN).astype(BF16)
    grad_hidden = dot(up, w_proj, NT) * slope
    low = grad_hidden.astype(BF16)
    gwa_ref[:, model:] = dot(act, low, TN).astype(BF16)
    grad_act = dot(low, w_fc, NT)
    up = up.astype(F32)
    grad_resid = up + normalize_back(grad_act * gain, normed, inverse)
    resid_ref[...] = grad_resid
    resid_low = grad_resid.astype(BF16)
    gwa_ref[:, 0:model] = dot(attn, resid_low, TN).astype(BF16)
    grad_attn = dot(resid_low, w_out, NT).astype(BF16)
    for g in range(groups):
        ga_ref[g] = grad_attn[:, g * width : (g + 1) * width]
    gs_ref[0:1, :] = column_sum(grad_hidden)
    gs_ref[1:2, 0:model] = column_sum(grad_resid)
    gs_ref[2:3, 0:model] = column_sum(grad_act * normed)
    gs_ref[3:4, 0:model] = column_sum(grad_act)
    gs_ref[4:5, 0:model] = column_sum(up)


def middle(x, attn, w_out, w_fc, w_proj, small, fc_bias, cotangent):
    length, model = x.shape
    tile = length
    groups = attn.shape[0]
    hid = w_fc.shape[2]
    rows = pl.BlockSpec((tile, model), lambda i: (i, 0))
    slabs = pl.BlockSpec((groups, tile, model // groups), lambda i: (0, i, 0))
    return pl.pallas_call(
        functools.partial(middle_kernel, groups),
        out_shape=(
            jax.ShapeDtypeStruct((length, model), BF16),
            jax.ShapeDtypeStruct((length, model), F32),
            jax.ShapeDtypeStruct(attn.shape, BF16),
            jax.ShapeDtypeStruct((model, model + hid), BF16),
            jax.ShapeDtypeStruct((hid, model), BF16),
            jax.ShapeDtypeStruct((8, hid), F32),
        ),
        grid=(length // tile,),
        in_specs=[rows, slabs, whole(w_out.shape), whole(w_fc.shape), whole(w_proj.shape), whole(small.shape),
                  whole(fc_bias.shape), rows],
        out_specs=[rows, rows, slabs, whole((model, model + hid)),
                   whole((hid, model)), whole((8, hid))],
        compiler_params=params(),
        cost_estimate=cost(12 * length * model * hid + 6 * length * model * model,
                           16 * model * hid, length * hid),
        name="middle",
    )(x, attn, w_out, w_fc, w_proj, small, fc_bias, cotangent)


def per_device(
    tokens, starts, norm1_gain, norm1_bias, w_qkv, q_bias, v_bias, w_out, out_bias, norm2_gain,
    norm2_bias, w_fc, fc_bias, w_proj, proj_bias, cotangent,
):
    groups = lax.axis_size("sp")
    parts = lax.axis_size("fsdp")
    rows, triple = w_qkv.shape
    piece = norm1_gain.shape[0]
    x = tokens[0]
    vectors = [
        norm1_gain, norm1_bias, q_bias, v_bias, out_bias, norm2_gain, norm2_bias, proj_bias, fc_bias
    ]
    qkv, out, lse, attn, code_q, code_k, small, fcb, packed, *wide = front(
        x, w_qkv, starts, vectors, (w_out, w_fc, w_proj), groups, parts
    )
    if rows % 16 == 0:
        weight, weight_count = packed, rows
    else:
        weight, weight_count = packed.reshape(1, parts * rows, triple), parts * rows
    wide = [w if w.shape[1] % 16 == 0 else w.reshape(1, -1, w.shape[2]) for w in wide]
    block_out, grad_resid, grad_attn, g_a, g_p, sums = middle(
        x, attn, *wide, small, fcb, cotangent[0]
    )
    grad_tokens, g_q, g_v, g_out, g_fc, g_p = back(
        qkv, grad_attn, out, lse, code_q, code_k,
        g_a.reshape(parts, -1, g_a.shape[1]), g_p.reshape(parts, -1, g_p.shape[1]),
        x, grad_resid, weight, small, sums,
    )
    grad_tokens, g_q, g_out, g_fc, g_p, *vec, g_fcb = hand_out(
        (grad_tokens, g_q, g_out, g_fc, g_p), g_v, piece, fc_bias.shape[0]
    )
    vec = [v.reshape(-1) for v in vec]
    return (
        block_out[None], grad_tokens[None], vec[0], vec[1], g_q, vec[2], vec[3],
        g_out, vec[4], vec[5], vec[6], g_fc, g_fcb.reshape(-1), g_p, vec[7],
    )


def solution(mesh):
    row, mat = P("fsdp"), P("fsdp", None)
    stream = P("fsdp", "sp", None)
    return jax.shard_map(
        per_device,
        mesh=mesh,
        in_specs=(stream, P("fsdp", "sp"), row, row, mat, row, row, mat, row, row, row, mat, row,
                  mat, row, stream),
        out_specs=(stream, stream, row, row, mat, row, row, mat, row, row, row, mat, row, mat, row),
        check_vma=False,
    )
```

```python
import functools

import jax
import jax.numpy as jnp
from jax import lax
from jax.experimental import pallas as pl
from jax.experimental.pallas import tpu as pltpu
from jax.sharding import PartitionSpec as P

HEAD_DIM = 64
EPSILON = 1e-05
NEG = -1e30
F32 = jnp.float32
BF16 = jnp.bfloat16
LOG2E = 1.4426950408889634
FAR = 2.0**60
SPARE = 60
RELAY_AT, RELAY_GAP, TWIN_AT = 12, 3, 20
NN = (((1,), (0,)), ((), ()))
NT = (((1,), (1,)), ((), ()))
TN = (((0,), (0,)), ((), ()))
VMEM_LIMIT = 60 << 20


def dot(left, right, dims=NN):
    return lax.dot_general(left, right, dims, preferred_element_type=F32)


def normalize(values):
    centered = values - jnp.mean(values, -1, keepdims=True)
    inverse = lax.rsqrt(jnp.mean(centered * centered, -1, keepdims=True) + EPSILON)
    return centered * inverse, inverse


def normalize_back(incoming, normed, inverse):
    return inverse * (
        incoming
        - jnp.mean(incoming, -1, keepdims=True)
        - normed * jnp.mean(incoming * normed, -1, keepdims=True)
    )


def whole(shape):
    return pl.BlockSpec(shape, lambda *_: (0,) * len(shape))


def params():
    return pltpu.CompilerParams(vmem_limit_bytes=VMEM_LIMIT)


def cost(flops, size, exps=0):
    return pl.CostEstimate(flops=flops, bytes_accessed=size, transcendentals=exps)


def weight_rows(w_ref, rows):
    parts = w_ref.shape[0]
    return w_ref[:, 0:rows, :].reshape(parts * rows, w_ref.shape[2])


def peer(sp, fsdp):
    return {"sp": sp, "fsdp": fsdp}


def remote(src, dst, send, recv, where):
    return pltpu.make_async_remote_copy(
        src_ref=src, dst_ref=dst, send_sem=send, recv_sem=recv,
        device_id=where, device_id_type=pl.DeviceIdType.MESH,
    )


def others(me, count):
    return [lax.rem(me + k, count) for k in range(1, count)]


def greet(groups, parts):
    p, f = lax.axis_index("sp"), lax.axis_index("fsdp")
    barrier = pltpu.get_barrier_semaphore()
    for q in others(p, groups):
        pl.semaphore_signal(barrier, inc=1, device_id=peer(q, f), device_id_type=pl.DeviceIdType.MESH)
    for g in others(f, parts):
        pl.semaphore_signal(barrier, inc=1, device_id=peer(p, g), device_id_type=pl.DeviceIdType.MESH)


def greeted(groups, parts):
    pl.semaphore_wait(pltpu.get_barrier_semaphore(), groups + parts - 2)


class Spread:
    def __init__(self, src, dst, parts, send, recv, own):
        self.src, self.dst, self.send, self.recv, self.own = src, dst, send, recv, own
        self.p, self.f = lax.axis_index("sp"), lax.axis_index("fsdp")
        core = lax.rem(self.p, 2)
        self.mate = self.p + 1 - 2 * core
        self.parts, self.major = parts, parts // 2
        self.a, self.b = self.f // 2, lax.rem(self.f, 2)
        self.twin = self.a * 2 + 1 - self.b
        half = src.shape[1] // 2
        self.lanes = pl.ds(pl.multiple_of(core * half, 128), half)
        self.mate_lanes = pl.ds(pl.multiple_of((1 - core) * half, 128), half)

    def back(self, k):
        return lax.rem(self.a + self.major - k, self.major)

    def block(self, g, lanes=None):
        return self.dst.at[g, :, self.lanes if lanes is None else lanes]

    def first(self, k):
        where = lax.rem(self.a + k, self.major) * 2 + self.b
        where = self.twin if k == 0 else where
        return remote(
            self.src.at[:, self.lanes], self.block(self.f), self.send.at[0, k],
            self.recv.at[0, self.f], peer(self.p, where),
        )

    def to_twin(self, k):
        g = self.back(k) * 2 + self.b
        return remote(
            self.block(g), self.block(g), self.send.at[1, k], self.recv.at[0, g],
            peer(self.p, self.twin),
        )

    def to_mate(self, k, b):
        g = self.back(k) * 2 + b
        slot = k if b is self.b else self.major + k
        return remote(
            self.block(g), self.block(g), self.send.at[2, slot], self.recv.at[1, g],
            peer(self.mate, self.f),
        )

    def keep(self):
        return pltpu.make_async_copy(self.src, self.dst.at[self.f], self.own)

    def start_lines(self):
        self.keep().start()
        for k in range(1, self.major):
            self.first(k).start()

    def start_twin(self):
        self.first(0).start()

    def start(self):
        self.start_lines()
        self.start_twin()

    def relay(self, k):
        self.to_twin(k).wait_recv()
        self.to_twin(k).start()
        self.to_mate(k, self.b).start()

    def relay_twin(self, k):
        other = 1 - self.b
        copy = self.to_mate(k, other)
        g = self.back(k) * 2 + other
        remote(
            self.block(g), self.block(g), self.send.at[1, 0], self.recv.at[0, g],
            peer(self.p, self.twin),
        ).wait_recv()
        copy.start()

    def finish(self):
        for g in others(self.f, self.parts):
            there = self.block(g, self.mate_lanes)
            remote(
                there, there, self.send.at[1, 0], self.recv.at[1, g], peer(self.mate, self.f)
            ).wait_recv()
        for k in range(self.major):
            self.first(k).wait_send()
            self.to_mate(k, 1 - self.b).wait_send()
        for k in range(1, self.major):
            self.to_twin(k).wait_send()
            self.to_mate(k, self.b).wait_send()
        self.keep().wait()

    @staticmethod
    def semaphores(parts):
        dma = pltpu.SemaphoreType.DMA
        return [dma((3, parts)), dma((2, parts)), dma(())]


class Fold:
    def __init__(self, src, out, parts, mine, r1, r2, s2, r3, own, send1, recv1, send2, recv2, send3, recv3):
        self.__dict__.update(
            src=src, out=out, mine=mine, r1=r1, r2=r2, s2=s2, r3=r3, own=own, send1=send1,
            recv1=recv1, send2=send2, recv2=recv2, send3=send3, recv3=recv3,
        )
        self.p, self.f = lax.axis_index("sp"), lax.axis_index("fsdp")
        core = lax.rem(self.p, 2)
        self.mate = self.p + 1 - 2 * core
        self.major = parts // 2
        self.a, self.b = self.f // 2, lax.rem(self.f, 2)
        self.twin = self.a * 2 + 1 - self.b
        half = src.shape[2] // 2
        self.lanes = pl.ds(pl.multiple_of(core * half, 128), half)
        self.mate_lanes = pl.ds(pl.multiple_of((1 - core) * half, 128), half)

    def keep(self):
        return pltpu.make_async_copy(self.src.at[:, :, self.lanes], self.mine, self.own)

    def to_mate(self):
        return remote(
            self.src.at[:, :, self.mate_lanes], self.r1, self.send1, self.recv1,
            peer(self.mate, self.f),
        )

    def to_twin(self, c):
        return remote(
            self.mine.at[c * 2 + 1 - self.b], self.r2.at[c], self.send2.at[c], self.recv2.at[c],
            peer(self.p, self.twin),
        )

    def along(self, k):
        c = lax.rem(self.a + k, self.major)
        return remote(
            self.s2.at[c], self.r3.at[self.a], self.send3.at[c], self.recv3.at[self.a],
            peer(self.p, c * 2 + self.b),
        )

    def start(self):
        self.to_mate().start()
        self.keep().start()

    def pairs(self):
        self.keep().wait()
        self.to_mate().wait()
        self.mine[...] = (self.mine[...].astype(F32) + self.r1[...].astype(F32)).astype(BF16)
        for c in range(self.major):
            self.to_twin(c).start()

    def planes(self):
        for c in range(self.major):
            self.to_twin(c).wait()
            self.s2[c] = (
                self.mine[c * 2 + self.b].astype(F32) + self.r2[c].astype(F32)
            ).astype(BF16)
        for k in range(1, self.major):
            self.along(k).start()

    def lines(self):
        total = self.mine[self.f].astype(F32) + self.r2[self.a].astype(F32)
        for k in range(1, self.major):
            c = lax.rem(self.a + k, self.major)
            remote(
                self.r3.at[c], self.r3.at[c], self.send3.at[0], self.recv3.at[c],
                peer(self.p, self.twin),
            ).wait_recv()
            total = total + self.r3[c].astype(F32)
        self.out[...] = total.astype(BF16)
        for k in range(1, self.major):
            self.along(k).wait_send()

    @staticmethod
    def scratch(parts, rows, lanes):
        dma = pltpu.SemaphoreType.DMA
        major, half = parts // 2, lanes // 2
        return [
            pltpu.VMEM((parts, rows, half), BF16), pltpu.VMEM((parts, rows, half), BF16),
            pltpu.VMEM((major, rows, half), BF16), pltpu.VMEM((major, rows, half), BF16),
            pltpu.VMEM((major, rows, half), BF16), dma(()), dma(()), dma(()),
            dma((major,)), dma((major,)), dma((major,)), dma((major,)),
        ]


def column_sum(x):
    return jnp.sum(x, 0, keepdims=True)


GAIN_ONE, BIAS_ONE, Q_BIAS, V_BIAS, OUT_BIAS, GAIN_TWO, BIAS_TWO, PROJ_BIAS = range(8)


def triangle(index, size):
    row = sum((index >= m * (m + 1) // 2).astype(jnp.int32) for m in range(1, size))
    return row, index - row * (row + 1) // 2


def triangle_by_column(index, size):
    starts = [c * (2 * size + 1 - c) // 2 for c in range(size)]
    col = sum((index >= at).astype(jnp.int32) for at in starts[1:])
    return col + index - col * (2 * size + 1 - col) // 2, col


def pick(cond, this, other):
    return jnp.where(cond, this, other)


class Place:
    def __init__(self, groups, count):
        self.p, self.f = lax.axis_index("sp"), lax.axis_index("fsdp")
        self.side = self.p // 2
        self.core = lax.rem(self.p, 2)
        self.mate = self.p + 1 - 2 * self.core
        far = (1 - self.side) * 2
        self.far = (far + self.core, far + 1 - self.core)
        self.groups = groups
        self.count = count
        self.half = 2 * count
        self.near_block = self.side * self.half
        self.far_block = (1 - self.side) * self.half

    def peer(self, q):
        return peer(q, self.f)

    def others(self):
        return others(self.p, self.groups)

    def meet(self):
        barrier = pltpu.get_barrier_semaphore()
        for q in self.others():
            pl.semaphore_signal(
                barrier, inc=1, device_id=self.peer(q), device_id_type=pl.DeviceIdType.MESH
            )
        pl.semaphore_wait(barrier, self.groups - 1)


def rows_of(block, count, size):
    return block // count, pl.ds(pl.multiple_of(lax.rem(block, count) * size, size), size)


def head_lanes(h, x, rest):
    lane = lax.broadcasted_iota(jnp.int32, x.shape, 1)
    return jnp.where(lane // HEAD_DIM == h, x, rest)


def causal(size):
    rows = lax.broadcasted_iota(jnp.int32, (size, size), 0)
    return rows <= lax.broadcasted_iota(jnp.int32, (size, size), 1)


def document_codes(starts, length):
    shape = (2 * HEAD_DIM, starts.shape[1])
    row = lax.rem(lax.broadcasted_iota(jnp.int32, shape, 0), HEAD_DIM)
    bits = max(1, (length - 1).bit_length())
    bit = lax.shift_right_logical(jnp.broadcast_to(starts, shape), row // 2) & 1
    code = jnp.where(lax.rem(row, 2) == 0, bit, 1 - bit).astype(F32)
    used = row < 2 * bits
    query = jnp.where(used, code, 0.0)
    key = jnp.where(used, (code - 1.0) * FAR, 1.0)
    return query.T.astype(BF16), key.T.astype(BF16)


def value_lanes(values, size):
    shape = (2 * HEAD_DIM, size)
    row = lax.broadcasted_iota(jnp.int32, shape, 0)
    out = jnp.zeros(shape, F32)
    for h, value in enumerate(values):
        rest = -value
        for n in range(3):
            piece = rest.astype(BF16).astype(F32)
            rest = rest - piece
            out = jnp.where(row == (1 - h) * HEAD_DIM + SPARE + n, piece, out)
    return out.T.astype(BF16)


def front_kernel(size, heads, groups, parts, tile, x_ref, wq_ref, st_in, *refs):
    vec_refs, shards, refs = refs[:9], refs[9:12], refs[12:]
    qkv_ref, o_ref, lse_ref, attn_ref, eq_ref, ek_ref, small_ref, fcb_ref, wq_all = refs[:9]
    wide, refs = refs[9:12], refs[12:]
    own_ref, sg, own_vec, vg, m_sc, l_sc, acc_sc = refs[:7]
    v_send, v_recv, s_send, s_recv, near_s, near_r, far_s, far_r, out_s, out_r = refs[7:17]
    first_spread, *spreads = [
        Spread(src, dst, parts, *refs[17 + 3 * n : 20 + 3 * n])
        for n, (src, dst) in enumerate(zip((wq_ref,) + shards, (wq_all,) + wide))
    ]
    per, model = x_ref.shape
    width = model // groups
    count = per // size
    major = parts // 2
    at = Place(groups, count)
    p, f, side, half = at.p, at.f, at.side, at.half

    greet(groups, parts)
    piece = vec_refs[0].shape[1]
    runs, bits = vec_refs[8].shape
    own_vec[...] = jnp.zeros_like(own_vec)
    for k in range(8):
        own_vec[k : k + 1, 0:piece] = vec_refs[k][...].astype(F32)
    own_vec[8 : 8 + runs, 0:bits] = vec_refs[8][...].astype(F32)
    vg[f] = own_vec[...]
    sg[p] = st_in[...]
    m_sc[...] = jnp.full_like(m_sc, NEG)
    l_sc[...] = jnp.zeros_like(l_sc)
    acc_sc[...] = jnp.zeros_like(acc_sc)
    greeted(groups, parts)

    copies = []

    def go(copy):
        copy.start()
        copies.append(copy)

    first_spread.start()
    for k, q in enumerate(at.others()):
        go(remote(st_in, sg.at[p], s_send.at[k], s_recv.at[p], at.peer(q)))
    for k, g in enumerate(others(f, parts)):
        go(remote(own_vec, vg.at[f], v_send.at[k], v_recv.at[f], peer(p, g)))
    for q in at.others():
        remote(st_in, sg.at[q], s_send.at[0], s_recv.at[q], at.peer(q)).wait_recv()

    @pl.loop(0, groups)
    def _(q):
        starts = jnp.concatenate([sg[q, k : k + 1] for k in range(per // 128)], 1)
        rows = pl.ds(pl.multiple_of(q * per, per), per)
        eq_ref[rows], ek_ref[rows] = document_codes(starts, groups * per)

    for k in range(1, major):
        first_spread.relay(k)
    for k in range(major):
        first_spread.relay_twin(k)
    for g in others(f, parts):
        remote(own_vec, vg.at[g], v_send.at[0], v_recv.at[g], peer(p, g)).wait_recv()
    for g in range(parts):
        small_ref[:, g * piece : (g + 1) * piece] = vg[g, 0:8, 0:piece]
        for k in range(runs):
            lane = (g * runs + k) * bits
            fcb_ref[:, lane : lane + bits] = vg[g, 8 + k : 9 + k, 0:bits]
    first_spread.finish()
    for spread in spreads:
        spread.start_lines()

    def far_copy(b, t, d):
        rows = pl.ds(pl.multiple_of(b * size, size), size)
        return remote(
            own_ref.at[at.far[d], t, rows], qkv_ref.at[p, t, rows], far_s.at[d, b, t],
            far_r.at[p, t, b], at.peer(at.far[d]),
        )

    near = remote(own_ref.at[at.mate], qkv_ref.at[p], near_s, near_r, at.peer(at.mate))

    @pl.loop(0, per // tile)
    def _(i):
        rows = pl.ds(pl.multiple_of(i * tile, tile), tile)
        normed, _ = normalize(x_ref[rows].astype(F32))
        small = small_ref[...]
        act = (normed * small[GAIN_ONE : GAIN_ONE + 1] + small[BIAS_ONE : BIAS_ONE + 1]).astype(BF16)
        weight = weight_rows(wq_all, wq_all.shape[1])
        for part, row in ((0, Q_BIAS), (1, None), (2, V_BIAS)):
            out = dot(act, weight[:, part * model : (part + 1) * model])
            if row is not None:
                out = out + small[row : row + 1]
            out = out.astype(BF16)
            if part == 0:
                out = (out.astype(F32) * (HEAD_DIM ** (-0.5) * LOG2E)).astype(BF16)
            for g in range(groups):
                own_ref[g, part, rows] = out[:, g * width : (g + 1) * width]

        @pl.when(lax.rem(i + 1, size // tile) == 0)
        def _():
            for n in range(3):
                for d in range(2):
                    far_copy((i + 1) // (size // tile) - 1, lax.rem(n + pick(side == 1, 0, 1), 3), d).start()

    near.start()
    for spread in spreads:
        spread.start_twin()
    qkv_ref[p] = own_ref[p]

    def far_wait(t, block):
        src, rows = rows_of(block, count, size)
        there = qkv_ref.at[src, t, rows]
        remote(there, there, far_s.at[0, 0, 0], far_r.at[src, t, lax.rem(block, count)], at.peer(src)).wait_recv()

    def block(q, k, diagonal):
        src, rows = rows_of(q, count, size)
        cols = pl.ds(pl.multiple_of(q * size, size), size)
        ksrc, krows = rows_of(k, count, size)
        query = qkv_ref[src, 0, rows, :]
        key = qkv_ref[ksrc, 1, krows, :]
        value = qkv_ref[ksrc, 2, krows, :]
        code_q = eq_ref[cols, :]
        code_k = ek_ref[pl.ds(pl.multiple_of(k * size, size), size), :]
        old = [(m_sc[h : h + 1, cols], l_sc[h : h + 1, cols]) for h in range(heads)]
        acc = acc_sc[:, cols]
        scores = [
            dot(head_lanes(h, key, code_k), head_lanes(h, query, code_q), NT) for h in range(heads)
        ]
        new, parts = [], []
        for h in range(heads):
            s = scores[h]
            if diagonal:
                s = jnp.where(causal(size), s, NEG)
            m_old, l_old = old[h]
            m_new = jnp.maximum(m_old, jnp.max(s, 0, keepdims=True))
            e = jnp.exp2(s - m_new).astype(BF16)
            alpha = jnp.exp2(m_old - m_new)
            mixed = dot(head_lanes(h, value, jnp.ones_like(value)), e, TN)
            low, other = h * HEAD_DIM, (1 - h) * HEAD_DIM
            new.append((m_new, l_old * alpha + mixed[other : other + 1]))
            parts.append(acc[low : low + HEAD_DIM] * alpha + mixed[low : low + HEAD_DIM])
        acc_sc[:, cols] = jnp.concatenate(parts, 0)
        for h in range(heads):
            m_sc[h : h + 1, cols], l_sc[h : h + 1, cols] = new[h]

    def out_copy(q):
        src, rows = rows_of(q, count, size)
        return remote(
            o_ref.at[src, rows], attn_ref.at[p, rows], out_s.at[q], out_r.at[p, lax.rem(q, count)],
            at.peer(src),
        )

    def finish(q):
        src, rows = rows_of(q, count, size)
        cols = pl.ds(pl.multiple_of(q * size, size), size)
        parts = []
        for h in range(heads):
            sl = slice(h * HEAD_DIM, (h + 1) * HEAD_DIM)
            total = l_sc[h : h + 1, cols]
            parts.append(acc_sc[sl, cols] * (1.0 / total))
            lse_ref[h : h + 1, cols] = m_sc[h : h + 1, cols] + jnp.log2(total)
        out = jnp.concatenate(parts, 0).T.astype(BF16)
        o_ref[src, rows] = out

        @pl.when(src == p)
        def _():
            attn_ref[p, rows] = out

        @pl.when(src != p)
        def _():
            out_copy(q).start()

    small = count * (count + 1) // 2
    cross = 2 * small + count * count
    bulk = cross + half * half
    end = bulk + half * (half + 1) // 2

    @pl.loop(0, end)
    def _(step):
        second = step >= small
        row, col = triangle(step - pick(second, small, 0), count)
        base = pick(second, at.mate, p) * count
        q, k = base + row, base + col
        c = step - 2 * small
        in_cross = (step >= 2 * small) & (step < cross)
        q = pick(in_cross, at.near_block + count + c // count, q)
        k = pick(in_cross, at.near_block + lax.rem(c, count), k)
        c = step - cross
        in_bulk = (step >= cross) & (step < bulk)
        outer, inner = c // half, lax.rem(c, half)
        outer = lax.rem(outer, 2) * count + outer // 2
        q = pick(in_bulk, half + pick(side == 0, outer, inner), q)
        k = pick(in_bulk, pick(side == 0, inner, outer), k)
        in_last = step >= bulk
        row, col = triangle(step - bulk, half)
        q = pick(in_last, at.far_block + row, q)
        k = pick(in_last, at.far_block + col, k)

        @pl.when(step == small)
        def _():
            near.wait_recv()

        starts_outer = in_bulk & (inner == 0)
        starts_row = in_last & (col == 0)

        @pl.when((starts_outer & (side == 0)) | (starts_row & (side == 1)))
        def _():
            far_wait(0, q)

        @pl.when((starts_outer & (side == 1)) | (starts_row & (side == 0)))
        def _():
            far_block = pick(in_bulk, k, q)
            far_wait(1, far_block)
            far_wait(2, far_block)

        @pl.when(q == k)
        def _():
            block(q, k, True)

        @pl.when(q != k)
        def _():
            block(q, k, False)

        for n in range(1, major):
            @pl.when(step == RELAY_AT + (n - 1) * RELAY_GAP * 2 // (major - 1))
            def _(n=n):
                for spread in spreads:
                    spread.relay(n)
        for n in range(major):
            @pl.when(step == TWIN_AT + n * (end - 1 - TWIN_AT) // (major - 1))
            def _(n=n):
                for spread in spreads:
                    spread.relay_twin(n)

        near_done = step == pick(side == 0, cross, bulk) - 1
        low = pick(near_done, at.near_block, q)
        high = pick(near_done, at.near_block + half, pick(in_last & (q == k), q + 1, q))
        pl.loop(low, high)(finish)

    for q in at.others():
        for b in range(count):
            rows = pl.ds(b * size, size)
            there = attn_ref.at[q, rows]
            remote(there, there, out_s.at[0], out_r.at[q, b], at.peer(q)).wait_recv()
            out_copy(q * count + b).wait_send()
    near.wait_send()
    for b in range(count):
        for t in range(3):
            for d in range(2):
                far_copy(b, t, d).wait_send()
    for copy in copies:
        copy.wait_send()
    for spread in spreads:
        spread.finish()


def front(x, w_qkv, starts, vectors, shards, groups, parts, size=512, tile=256):
    per, model = x.shape
    length = groups * per
    width = model // groups
    heads = width // HEAD_DIM
    count = per // size
    starts = starts.reshape(-1, 128)
    fc = vectors[8].shape[0]
    piece = vectors[0].shape[0]
    vectors = [v.reshape(1, -1) for v in vectors[:8]] + [vectors[8].reshape(-1, min(fc, 128))]
    dma = pltpu.SemaphoreType.DMA
    vmem = pl.BlockSpec(memory_space=pltpu.VMEM)
    slabs = (groups, 3, per, width)
    return pl.pallas_call(
        functools.partial(front_kernel, size, heads, groups, parts, tile),
        out_shape=(
            jax.ShapeDtypeStruct(slabs, BF16),
            jax.ShapeDtypeStruct((groups, per, width), BF16),
            jax.ShapeDtypeStruct((8, length), F32),
            jax.ShapeDtypeStruct((groups, per, width), BF16),
            jax.ShapeDtypeStruct((length, width), BF16),
            jax.ShapeDtypeStruct((length, width), BF16),
            jax.ShapeDtypeStruct((8, parts * piece), F32),
            jax.ShapeDtypeStruct((1, parts * fc), F32),
            jax.ShapeDtypeStruct((parts,) + w_qkv.shape, BF16),
            *[jax.ShapeDtypeStruct((parts,) + shard.shape, BF16) for shard in shards],
        ),
        in_specs=[vmem] * 15,
        out_specs=[vmem] * 9 + [pl.BlockSpec(memory_space=pl.ANY)] * 3,
        scratch_shapes=[
            pltpu.VMEM(slabs, BF16), pltpu.VMEM((groups,) + starts.shape, jnp.int32),
            pltpu.VMEM((16, 128), F32), pltpu.VMEM((parts, 16, 128), F32),
            pltpu.VMEM((8, length), F32), pltpu.VMEM((8, length), F32),
            pltpu.VMEM((width, length), F32),
            dma((parts,)), dma((parts,)), dma((groups,)), dma((groups,)), dma(()), dma(()),
            dma((2, count, 3)), dma((groups, 3, count)), dma((groups * count,)), dma((groups, count)),
        ] + Spread.semaphores(parts) * 4,
        compiler_params=pltpu.CompilerParams(
            vmem_limit_bytes=VMEM_LIMIT, collective_id=2, has_side_effects=True
        ),
        cost_estimate=cost(4 * length * length * width, 16 * length * width, length * length),
        name="front",
    )(x, w_qkv, starts, *vectors, *shards)


def back_kernel(
    size, heads, parts, tile, qkv_any, own_ref, o_any, lse_any, eq_any, ek_any, ga_ref, gp_ref,
    x_any, resid_any, w_any, small_ref, sums_ref,
    gt_ref, gw_ref, gv_ref, go_ref, gf_ref, gpo_ref, *refs
):
    (do_sc, qa_sc, da_sc, dqt_sc, dk_sc, dv_sc, stage, grad_sc,
     near_s, near_r, far_s, far_r, out_s, out_r) = refs[:14]
    fa_sc, fp_sc, x_sc, resid_sc, w_sc, act_sc, load = refs[14:21]
    (xa, xp, fulla, fullp, xs, xr, ys, yr) = refs[21:29]
    (acc, out, vec, mine, vsend, vpart, low, r1, s2, r2, keep, s3, r3) = refs[29:42]
    (v1s, v1r, v2s, v2r, c1s, c1r, c2s, c2r, c3s, c3r, c4s, c4r) = refs[42:54]
    folds = [Fold(ga_ref, fa_sc, parts, *refs[54:66]), Fold(gp_ref, fp_sc, parts, *refs[66:78])]
    qkv_ref, o_ref, lse_ref, eq_ref, ek_ref, more = refs[78:]
    groups, _, per, width = qkv_ref.shape
    model = x_sc.shape[1]
    count = per // size
    at = Place(groups, count)
    p, f, side, core, half = at.p, at.f, at.side, at.core, at.half
    scale = HEAD_DIM ** (-0.5)
    loads = [
        pltpu.make_async_copy(src, dst, load.at[n])
        for n, (src, dst) in enumerate(((x_any, x_sc), (w_any, w_sc), (resid_any, resid_sc)))
    ]
    early = [
        pltpu.make_async_copy(src, dst, more.at[n])
        for n, (src, dst) in enumerate((
            (own_ref.at[p], do_sc.at[p]), (qkv_any, qkv_ref), (o_any, o_ref),
            (lse_any, lse_ref), (eq_any, eq_ref), (ek_any, ek_ref),
        ))
    ]
    greet(groups, parts)
    for copy in loads[:1] + early + loads[1:]:
        copy.start()
    dqt_sc[...] = jnp.zeros_like(dqt_sc)
    dk_sc[...] = jnp.zeros_like(dk_sc)
    dv_sc[...] = jnp.zeros_like(dv_sc)
    greeted(groups, parts)

    near = remote(own_ref.at[at.mate], do_sc.at[p], near_s, near_r, at.peer(at.mate))
    near.start()

    def far_copy(b, d):
        rows = pl.ds(b * size, size)
        return remote(
            own_ref.at[at.far[d], rows], do_sc.at[p, rows], far_s.at[d, b], far_r.at[p, b],
            at.peer(at.far[d]),
        )

    for b in range(count):
        for d in range(2):
            far_copy(b, d).start()
    for fold in folds:
        fold.start()

    small = small_ref[...]
    gain = small[GAIN_ONE : GAIN_ONE + 1]
    bias = small[BIAS_ONE : BIAS_ONE + 1]
    loads[0].wait()

    @pl.loop(0, per // tile)
    def _(i):
        rows = pl.ds(pl.multiple_of(i * tile, tile), tile)
        normed, _ = normalize(x_sc[rows].astype(F32))
        act_sc[rows] = (normed * gain + bias).astype(BF16)

    for copy in early:
        copy.wait()

    def columns(block):
        return pl.ds(pl.multiple_of(block * size, size), size)

    def prepare(q):
        src, rows = rows_of(q, count, size)
        cols = columns(q)
        prod = (do_sc[src, rows].astype(F32) * o_ref[src, rows].astype(F32)).T
        delta = [
            jnp.sum(prod[h * HEAD_DIM : (h + 1) * HEAD_DIM], 0, keepdims=True) for h in range(heads)
        ]
        da_sc[cols, :] = value_lanes(delta, size)
        lse = [lse_ref[h : h + 1, cols] for h in range(heads)]
        qa_sc[cols, :] = eq_ref[cols, :] + value_lanes(lse, size)

    def block(q, k, diagonal):
        src, rows = rows_of(q, count, size)
        cols, kcols = columns(q), columns(k)
        ksrc, krows = rows_of(k, count, size)
        query, query_rest = qkv_ref[src, 0, rows, :], qa_sc[cols, :]
        grad, grad_rest = do_sc[src, rows], da_sc[cols, :]
        key, key_rest = qkv_ref[ksrc, 1, krows, :], ek_ref[kcols, :]
        value = qkv_ref[ksrc, 2, krows, :]
        query = [head_lanes(h, query, query_rest) for h in range(heads)]
        grad = [head_lanes(h, grad, grad_rest) for h in range(heads)]
        scores = [dot(head_lanes(h, key, key_rest), query[h], NT) for h in range(heads)]
        slopes = [
            dot(head_lanes(h, value, jnp.ones_like(value)), grad[h], NT) for h in range(heads)
        ]
        dqt, dv, dk = [], None, None
        for h in range(heads):
            s = scores[h]
            if diagonal:
                s = jnp.where(causal(size), s, NEG)
            e = jnp.exp2(s)
            ds = (e * slopes[h]).astype(BF16)
            dvh = dot(e.astype(BF16), grad[h])
            dkh = dot(ds, query[h])
            dv = dvh if dv is None else head_lanes(h, dvh, dv)
            dk = dkh if dk is None else head_lanes(h, dkh, dk)
            dqt.append(dot(key[:, h * HEAD_DIM : (h + 1) * HEAD_DIM], ds, TN))
        dqt_sc[:, cols] += jnp.concatenate(dqt, 0)
        dv_sc[kcols, :] += dv
        dk_sc[kcols, :] += dk

    def out_copy(block, part):
        src, rows = rows_of(block, count, size)
        return remote(
            stage.at[src, part, rows], grad_sc.at[p, part, rows], out_s.at[block, part],
            out_r.at[p, part, lax.rem(block, count)], at.peer(src),
        )

    def give(block, part, value):
        src, rows = rows_of(block, count, size)

        @pl.when(src == p)
        def _():
            grad_sc[p, part, rows] = value

        @pl.when(src != p)
        def _():
            stage[src, part, rows] = value
            out_copy(block, part).start()

    def finish_query(q):
        give(q, 0, (dqt_sc[:, columns(q)] * scale).T.astype(BF16))

    def finish_key(k):
        give(k, 1, (dk_sc[columns(k), :] * (1.0 / LOG2E)).astype(BF16))
        give(k, 2, dv_sc[columns(k), :].astype(BF16))

    small = count * (count + 1) // 2
    far = 2 * small
    bulk = far + half * (half + 1) // 2
    cross = bulk + half * half
    end = cross + count * count

    @pl.loop(0, end)
    def _(step):
        second = step >= small
        row, col = triangle(step - pick(second, small, 0), count)
        base = pick(second, at.mate, p) * count
        q, k = base + row, base + col
        in_far = (step >= far) & (step < bulk)
        row, column = triangle_by_column(step - far, half)
        q = pick(in_far, at.far_block + row, q)
        k = pick(in_far, at.far_block + column, k)
        c = step - bulk
        in_bulk = (step >= bulk) & (step < cross)
        outer, inner = c // half, lax.rem(c, half)
        q = pick(in_bulk, half + pick(side == 0, outer, inner), q)
        k = pick(in_bulk, pick(side == 0, inner, outer), k)
        c = step - cross
        in_cross = step >= cross
        q = pick(in_cross, at.near_block + count + c // count, q)
        k = pick(in_cross, at.near_block + lax.rem(c, count), k)

        @pl.when(step == small)
        def _():
            near.wait_recv()

        @pl.when(in_far & (column == 0))
        def _():
            src, rows = rows_of(q, count, size)
            there = do_sc.at[src, rows]
            remote(there, there, far_s.at[0, 0], far_r.at[src, lax.rem(q, count)], at.peer(src)).wait_recv()

        @pl.when(((step < far) & (col == 0)) | (in_far & (column == 0)))
        def _():
            prepare(q)

        @pl.when(q == k)
        def _():
            block(q, k, True)

        @pl.when(q != k)
        def _():
            block(q, k, False)

        for n, fold in enumerate(folds):
            pl.when(step == end // 6 + n)(fold.pairs)
            pl.when(step == end // 2 + 1 + 3 * n)(fold.planes)
            pl.when(step == end - 2 + n)(fold.lines)

        column_done = in_far & (row == half - 1)
        outer_done = in_bulk & (inner == half - 1)
        done = step == end - 1
        near_low, near_high = at.near_block, at.near_block + half
        query = (column_done & (side == 1)) | (outer_done & (side == 0))
        block_id = at.far_block + pick(in_far, column, outer)
        pl.loop(
            pick(done, near_low, block_id),
            pick(done, near_high, pick(query, block_id + 1, block_id)),
        )(finish_query)
        key = (column_done & (side == 0)) | (outer_done & (side == 1))
        pl.loop(
            pick(done, near_low, block_id),
            pick(done, near_high, pick(key, block_id + 1, block_id)),
        )(finish_key)

    across = p + groups // 2 - side * groups
    cross = [
        remote(src, dst, xs.at[n], xr.at[n], at.peer(across))
        for n, (src, dst) in enumerate(((fa_sc, xa), (fp_sc, xp)))
    ]
    for copy in cross:
        copy.start()
    for q in at.others():
        for b in range(count):
            for part in range(3):
                there = grad_sc.at[q, part, pl.ds(b * size, size)]
                remote(there, there, out_s.at[0, 0], out_r.at[q, part, b], at.peer(q)).wait_recv()

    copies = []

    def go(copy):
        copy.start()
        copies.append(copy)

    shard = model // parts
    chunks, chunk = acc.shape[0], acc.shape[2] // 2

    def number(c, s, k):
        return (c * 2 + s) * chunks + k

    def lane(c, s, k):
        return pl.ds(pl.multiple_of(number(c, s, k) * chunk, 128), chunk)

    def product(c, k):
        pair = []
        for s in range(2):
            n = number(c, s, k)
            pair.append(grad_sc[lax.rem(n, groups), n // groups])
        return dot(act_sc[...], jnp.concatenate(pair, 1), TN)

    mate = at.peer(at.mate)
    for k in range(chunks):
        low[k] = product(1 - core, k).astype(BF16)
        if k:
            go(remote(low.at[k - 1], r1.at[k - 1], c1s.at[k - 1], c1r.at[k - 1], mate))
    acc[0] = product(core, 0)
    go(remote(low.at[chunks - 1], r1.at[chunks - 1], c1s.at[chunks - 1], c1r.at[chunks - 1], mate))
    for k in range(1, chunks):
        acc[k] = product(core, k)
    for g in range(groups):
        lanes = slice(g * width, (g + 1) * width)
        vec[2:3, lanes] = column_sum(grad_sc[g, 0].astype(F32))
        vec[3:4, lanes] = column_sum(grad_sc[g, 2].astype(F32))
    this = pl.ds(pl.multiple_of(side * chunk, 128), chunk)
    that = pl.ds(pl.multiple_of((1 - side) * chunk, 128), chunk)
    for k in range(chunks):
        remote(r1.at[k], r1.at[k], c1s.at[k], c1r.at[k], mate).wait_recv()
        s2[k] = (acc[k, :, that] + r1[k, :, that].astype(F32)).astype(BF16)
        go(remote(s2.at[k], r2.at[k], c2s.at[k], c2r.at[k], at.peer(across)))

    loads[1].wait()
    loads[2].wait()
    vec[0:2, :] = jnp.zeros_like(vec[0:2, :])
    weight = weight_rows(w_sc, w_sc.shape[1])

    def token_rows(i):
        rows = pl.ds(pl.multiple_of(i * tile, tile), tile)
        normed, inverse = normalize(x_sc[rows].astype(F32))
        grad = jnp.concatenate([grad_sc[g, part, rows] for part in range(3) for g in range(groups)], 1)
        grad_act = dot(grad, weight, NT)
        gt_ref[rows] = (
            resid_sc[rows] + normalize_back(grad_act * gain, normed, inverse)
        ).astype(BF16)
        vec[0:1, :] += column_sum(grad_act * normed)
        vec[1:2, :] += column_sum(grad_act)

    pl.loop(0, per // tile)(token_rows)

    vec[4:8, :] = sums_ref[1:5, 0:model]
    piece = model // parts
    fc = sums_ref.shape[1] // parts
    bits = min(128, fc)
    vsend[...] = jnp.zeros_like(vsend)
    for g in range(parts):
        vsend[g, 0:8, 0:piece] = vec[:, g * piece : (g + 1) * piece]
        for k in range(fc // bits):
            first = g * fc + k * bits
            vsend[g, 8 + k : 9 + k, 0:bits] = sums_ref[0:1, first : first + bits]

    for k in range(chunks):
        remote(s2.at[k], r2.at[k], c2s.at[k], c2r.at[k], at.peer(across)).wait_recv()
        total = acc[k, :, this] + r1[k, :, this].astype(F32) + r2[k].astype(F32)
        keep[k] = total
        s3[k] = total.astype(BF16)
        for n, g in enumerate(others(f, parts)):
            rows = pl.ds(pl.multiple_of(g * shard, shard), shard)
            go(remote(s3.at[k, rows], r3.at[k, f], c3s.at[k, n], c3r.at[k, f], peer(p, g)))
    for n, g in enumerate(others(f, parts)):
        go(remote(vsend.at[g], vpart.at[f], v1s.at[n], v1r.at[f], peer(p, g)))
    folded = []
    for n, (mine_ref, theirs, full) in enumerate(((fa_sc, xa, fulla), (fp_sc, xp, fullp))):
        cross[n].wait()
        wide = mine_ref.shape[1]
        here = full.at[:, pl.ds(pl.multiple_of(core * wide, 128), wide)]
        there = full.at[:, pl.ds(pl.multiple_of((1 - core) * wide, 128), wide)]
        here[...] = mine_ref[...].astype(F32) + theirs[...].astype(F32)
        go(remote(here, here, ys.at[n], yr.at[n], mate))
        folded.append(remote(there, there, ys.at[n], yr.at[n], mate))
    for g in others(f, parts):
        remote(vsend.at[g], vpart.at[g], v1s.at[0], v1r.at[g], peer(p, g)).wait_recv()
    total = vsend[f]
    for g in others(f, parts):
        total = total + vpart[g]
    mine[p] = total
    for k in range(chunks):
        for g in others(f, parts):
            remote(r3.at[k, g], r3.at[k, g], c3s.at[k, 0], c3r.at[k, g], peer(p, g)).wait_recv()
        total = keep[k, pl.ds(pl.multiple_of(f * shard, shard), shard)]
        for g in others(f, parts):
            total = total + r3[k, g].astype(F32)
        there = out.at[:, lane(core, side, k)]
        there[...] = total.astype(BF16)
        for n, q in enumerate(at.others()):
            go(remote(there, there, c4s.at[k, n], c4r.at[k, p], at.peer(q)))
        if k == 0:
            for n, q in enumerate(at.others()):
                go(remote(mine.at[p], mine.at[p], v2s.at[n], v2r.at[p], at.peer(q)))
    for copy in folded:
        copy.wait_recv()
    go_ref[...] = fulla[:, 0:model]
    gf_ref[...] = fulla[:, model:]
    gpo_ref[...] = fullp[...]
    for q in at.others():
        remote(mine.at[q], mine.at[q], v2s.at[0], v2r.at[q], at.peer(q)).wait_recv()
    total = mine[0]
    for q in range(1, groups):
        total = total + mine[q]
    gv_ref[...] = total
    for k in range(chunks):
        for q in at.others():
            there = out.at[:, lane(lax.rem(q, 2), q // 2, k)]
            remote(there, there, c4s.at[k, 0], c4r.at[k, q], at.peer(q)).wait_recv()
    gw_ref[...] = out[...].astype(F32)
    for copy in copies:
        copy.wait_send()
    for q in at.others():
        for b in range(count):
            for part in range(3):
                out_copy(q * count + b, part).wait_send()
    near.wait_send()
    for b in range(count):
        for d in range(2):
            far_copy(b, d).wait_send()


def back(qkv, grad, out, lse, code_q, code_k, g_a, g_p, x, resid, weight, small, sums, size=512, tile=256):
    groups, _, per, width = qkv.shape
    length = groups * per
    heads = width // HEAD_DIM
    count = per // size
    parts = g_a.shape[0]
    model = x.shape[1]
    triple = 3 * model
    shard = model // parts
    chunk = 128
    chunks = triple // 4 // chunk
    dma = pltpu.SemaphoreType.DMA
    vm = pltpu.VMEM
    vmem = pl.BlockSpec(memory_space=pltpu.VMEM)
    far = pl.BlockSpec(memory_space=pl.ANY)
    f_a = (g_a.shape[1], g_a.shape[2] // 2)
    f_p = (g_p.shape[1], g_p.shape[2] // 2)
    return pl.pallas_call(
        functools.partial(back_kernel, size, heads, parts, tile),
        out_shape=(
            jax.ShapeDtypeStruct((per, model), BF16),
            jax.ShapeDtypeStruct((shard, triple), F32),
            jax.ShapeDtypeStruct((16, 128), F32),
            jax.ShapeDtypeStruct((f_a[0], model), F32),
            jax.ShapeDtypeStruct((f_a[0], 2 * f_a[1] - model), F32),
            jax.ShapeDtypeStruct((f_p[0], 2 * f_p[1]), F32),
        ),
        in_specs=[far] * 11 + [vmem] * 2,
        out_specs=[vmem] * 6,
        scratch_shapes=[
            vm((groups, per, width), BF16), vm((length, width), BF16), vm((length, width), BF16),
            vm((width, length), F32), vm((length, width), F32),
            vm((length, width), F32), vm(qkv.shape, BF16), vm(qkv.shape, BF16),
            dma(()), dma(()), dma((2, count)), dma((groups, count)),
            dma((groups * count, 3)), dma((groups, 3, count)),
            vm(f_a, BF16), vm(f_p, BF16), vm(x.shape, BF16), vm(resid.shape, F32),
            vm(weight.shape, BF16), vm(x.shape, BF16), dma((3,)),
            vm(f_a, BF16), vm(f_p, BF16), vm((f_a[0], 2 * f_a[1]), F32),
            vm((f_p[0], 2 * f_p[1]), F32), dma((2,)), dma((2,)), dma((2,)), dma((2,)),
            vm((chunks, model, 2 * chunk), F32), vm((shard, triple), BF16), vm((8, model), F32),
            vm((groups, 16, 128), F32), vm((parts, 16, 128), F32), vm((parts, 16, 128), F32),
            vm((chunks, model, 2 * chunk), BF16), vm((chunks, model, 2 * chunk), BF16),
            vm((chunks, model, chunk), BF16), vm((chunks, model, chunk), BF16),
            vm((chunks, model, chunk), F32), vm((chunks, model, chunk), BF16),
            vm((chunks, parts, shard, chunk), BF16),
            dma((parts,)), dma((parts,)), dma((groups,)), dma((groups,)),
            dma((chunks,)), dma((chunks,)), dma((chunks,)), dma((chunks,)),
            dma((chunks, parts)), dma((chunks, parts)), dma((chunks, groups)), dma((chunks, groups)),
            *Fold.scratch(*g_a.shape), *Fold.scratch(*g_p.shape),
            vm(qkv.shape, BF16), vm(out.shape, BF16), vm(lse.shape, F32),
            vm(code_q.shape, BF16), vm(code_k.shape, BF16), dma((6,)),
        ],
        compiler_params=pltpu.CompilerParams(
            vmem_limit_bytes=VMEM_LIMIT, collective_id=3, has_side_effects=True
        ),
        cost_estimate=cost(10 * length * length * width, 24 * length * width, length * length),
        name="back",
    )(qkv, grad, out, lse, code_q, code_k, g_a, g_p, x, resid, weight, small, sums)


def hand_out_kernel(piece, fc, *refs):
    ins, outs = refs[:6], refs[6:]
    for src, dst in zip(ins[:5], outs[:5]):
        dst[...] = src[...]
    vec = ins[5]
    for k in range(8):
        outs[5 + k][...] = vec[k : k + 1, 0:piece]
    bits = min(fc, 128)
    for k in range(fc // bits):
        outs[13][:, k * bits : (k + 1) * bits] = vec[8 + k : 9 + k, 0:bits]


def hand_out(arrays, vec, piece, fc):
    vmem = pl.BlockSpec(memory_space=pltpu.VMEM)
    return pl.pallas_call(
        functools.partial(hand_out_kernel, piece, fc),
        out_shape=tuple(
            [jax.ShapeDtypeStruct(v.shape, v.dtype) for v in arrays]
            + [jax.ShapeDtypeStruct((1, piece), F32)] * 8
            + [jax.ShapeDtypeStruct((1, fc), F32)]
        ),
        in_specs=[vmem] * 6,
        out_specs=tuple([vmem] * 14),
        compiler_params=params(),
        name="hand_out",
    )(*arrays, vec)


def middle_kernel(
    groups, x_ref, attn_ref, wo_ref, small_ref, fcb_ref, wf_any, wp_any, cot_any,
    out_any, resid_any, ga_any, gwa_any, gwp_any, gs_ref,
    wf_ref, wp_ref, cot_ref, out_ref, resid_ref, ga_ref, gwo_ref, gwf_ref, gwp_ref, load, store,
):
    loads = [
        pltpu.make_async_copy(src, dst, load.at[n])
        for n, (src, dst) in enumerate(((wf_any, wf_ref), (wp_any, wp_ref), (cot_any, cot_ref)))
    ]
    for copy in loads:
        copy.start()
    stores = []

    def save(src, dst):
        copy = pltpu.make_async_copy(src, dst, store.at[len(stores)])
        copy.start()
        stores.append(copy)

    model = x_ref.shape[-1]
    width = model // groups
    small = small_ref[...]
    w_out = weight_rows(wo_ref, wo_ref.shape[1])
    attn = jnp.concatenate([attn_ref[g] for g in range(groups)], 1)
    resid = x_ref[...].astype(F32) + dot(attn, w_out) + small[OUT_BIAS : OUT_BIAS + 1]
    normed, inverse = normalize(resid)
    gain = small[GAIN_TWO : GAIN_TWO + 1]
    act = (normed * gain + small[BIAS_TWO : BIAS_TWO + 1]).astype(BF16)
    loads[0].wait()
    w_fc = weight_rows(wf_ref, wf_ref.shape[1])
    hidden = dot(act, w_fc) + fcb_ref[...]
    sig = 1.0 / (1.0 + jnp.exp(-1.702 * hidden))
    gelu = hidden * sig
    slope = sig + 1.702 * gelu * (1.0 - sig)
    gelu = gelu.astype(BF16)
    loads[1].wait()
    w_proj = weight_rows(wp_ref, wp_ref.shape[1])
    out_ref[...] = (resid + dot(gelu, w_proj) + small[PROJ_BIAS : PROJ_BIAS + 1]).astype(BF16)
    save(out_ref, out_any)
    loads[2].wait()
    up = cot_ref[...]
    gwp_ref[...] = dot(gelu, up, TN).astype(BF16)
    save(gwp_ref, gwp_any)
    grad_hidden = dot(up, w_proj, NT) * slope
    low = grad_hidden.astype(BF16)
    gs_ref[0:1, :] = column_sum(grad_hidden)
    gwf_ref[...] = dot(act, low, TN).astype(BF16)
    save(gwf_ref, gwa_any.at[:, model:])
    grad_act = dot(low, w_fc, NT)
    up = up.astype(F32)
    grad_resid = up + normalize_back(grad_act * gain, normed, inverse)
    resid_ref[...] = grad_resid
    save(resid_ref, resid_any)
    resid_low = grad_resid.astype(BF16)
    grad_attn = dot(resid_low, w_out, NT).astype(BF16)
    for g in range(groups):
        ga_ref[g] = grad_attn[:, g * width : (g + 1) * width]
    save(ga_ref, ga_any)
    gwo_ref[...] = dot(attn, resid_low, TN).astype(BF16)
    save(gwo_ref, gwa_any.at[:, 0:model])
    gs_ref[1:2, 0:model] = column_sum(grad_resid)
    gs_ref[2:3, 0:model] = column_sum(grad_act * normed)
    gs_ref[3:4, 0:model] = column_sum(grad_act)
    gs_ref[4:5, 0:model] = column_sum(up)
    for copy in stores:
        copy.wait()


def middle(x, attn, w_out, w_fc, w_proj, small, fc_bias, cotangent):
    length, model = x.shape
    groups = attn.shape[0]
    hid = w_fc.shape[2]
    vm = pltpu.VMEM
    vmem, far = pl.BlockSpec(memory_space=pltpu.VMEM), pl.BlockSpec(memory_space=pl.ANY)
    return pl.pallas_call(
        functools.partial(middle_kernel, groups),
        out_shape=(
            jax.ShapeDtypeStruct((length, model), BF16),
            jax.ShapeDtypeStruct((length, model), F32),
            jax.ShapeDtypeStruct(attn.shape, BF16),
            jax.ShapeDtypeStruct((model, model + hid), BF16),
            jax.ShapeDtypeStruct((hid, model), BF16),
            jax.ShapeDtypeStruct((8, hid), F32),
        ),
        in_specs=[vmem] * 5 + [far] * 3,
        out_specs=[far] * 5 + [vmem],
        scratch_shapes=[
            vm(w_fc.shape, BF16), vm(w_proj.shape, BF16), vm(cotangent.shape, BF16),
            vm((length, model), BF16), vm((length, model), F32), vm(attn.shape, BF16),
            vm((model, model), BF16), vm((model, hid), BF16), vm((hid, model), BF16),
            pltpu.SemaphoreType.DMA((3,)), pltpu.SemaphoreType.DMA((6,)),
        ],
        compiler_params=params(),
        cost_estimate=cost(12 * length * model * hid + 6 * length * model * model,
                           16 * model * hid, length * hid),
        name="middle",
    )(x, attn, w_out, small, fc_bias, w_fc, w_proj, cotangent)


def per_device(
    tokens, starts, norm1_gain, norm1_bias, w_qkv, q_bias, v_bias, w_out, out_bias, norm2_gain,
    norm2_bias, w_fc, fc_bias, w_proj, proj_bias, cotangent,
):
    groups = lax.axis_size("sp")
    parts = lax.axis_size("fsdp")
    rows, triple = w_qkv.shape
    piece = norm1_gain.shape[0]
    x = tokens[0]
    vectors = [
        norm1_gain, norm1_bias, q_bias, v_bias, out_bias, norm2_gain, norm2_bias, proj_bias, fc_bias
    ]
    qkv, out, lse, attn, code_q, code_k, small, fcb, packed, *wide = front(
        x, w_qkv, starts, vectors, (w_out, w_fc, w_proj), groups, parts
    )
    if rows % 16 == 0:
        weight, weight_count = packed, rows
    else:
        weight, weight_count = packed.reshape(1, parts * rows, triple), parts * rows
    wide = [w if w.shape[1] % 16 == 0 else w.reshape(1, -1, w.shape[2]) for w in wide]
    block_out, grad_resid, grad_attn, g_a, g_p, sums = middle(
        x, attn, *wide, small, fcb, cotangent[0]
    )
    grad_tokens, g_q, g_v, g_out, g_fc, g_p = back(
        qkv, grad_attn, out, lse, code_q, code_k,
        g_a.reshape(parts, -1, g_a.shape[1]), g_p.reshape(parts, -1, g_p.shape[1]),
        x, grad_resid, weight, small, sums,
    )
    grad_tokens, g_q, g_out, g_fc, g_p, *vec, g_fcb = hand_out(
        (grad_tokens, g_q, g_out, g_fc, g_p), g_v, piece, fc_bias.shape[0]
    )
    vec = [v.reshape(-1) for v in vec]
    return (
        block_out[None], grad_tokens[None], vec[0], vec[1], g_q, vec[2], vec[3],
        g_out, vec[4], vec[5], vec[6], g_fc, g_fcb.reshape(-1), g_p, vec[7],
    )


def solution(mesh):
    row, mat = P("fsdp"), P("fsdp", None)
    stream = P("fsdp", "sp", None)
    return jax.shard_map(
        per_device,
        mesh=mesh,
        in_specs=(stream, P("fsdp", "sp"), row, row, mat, row, row, mat, row, row, row, mat, row,
                  mat, row, stream),
        out_specs=(stream, stream, row, row, mat, row, row, mat, row, row, row, mat, row, mat, row),
        check_vma=False,
    )
```

```python
import functools

import jax
import jax.numpy as jnp
from jax import lax
from jax.experimental import pallas as pl
from jax.experimental.pallas import tpu as pltpu
from jax.sharding import PartitionSpec as P

HEAD_DIM = 64
EPSILON = 1e-05
NEG = -1e30
F32 = jnp.float32
BF16 = jnp.bfloat16
LOG2E = 1.4426950408889634
FAR = 2.0**60
SPARE = 60
RELAY_AT, RELAY_GAP, TWIN_AT = 12, 3, 20
NN = (((1,), (0,)), ((), ()))
NT = (((1,), (1,)), ((), ()))
TN = (((0,), (0,)), ((), ()))
VMEM_LIMIT = 60 << 20


def dot(left, right, dims=NN):
    return lax.dot_general(left, right, dims, preferred_element_type=F32)


def normalize(values):
    centered = values - jnp.mean(values, -1, keepdims=True)
    inverse = lax.rsqrt(jnp.mean(centered * centered, -1, keepdims=True) + EPSILON)
    return centered * inverse, inverse


def normalize_back(incoming, normed, inverse):
    return inverse * (
        incoming
        - jnp.mean(incoming, -1, keepdims=True)
        - normed * jnp.mean(incoming * normed, -1, keepdims=True)
    )


def whole(shape):
    return pl.BlockSpec(shape, lambda *_: (0,) * len(shape))


def params():
    return pltpu.CompilerParams(vmem_limit_bytes=VMEM_LIMIT)


def cost(flops, size, exps=0):
    return pl.CostEstimate(flops=flops, bytes_accessed=size, transcendentals=exps)


def weight_rows(w_ref, rows):
    parts = w_ref.shape[0]
    return w_ref[:, 0:rows, :].reshape(parts * rows, w_ref.shape[2])


def peer(sp, fsdp):
    return {"sp": sp, "fsdp": fsdp}


def remote(src, dst, send, recv, where):
    return pltpu.make_async_remote_copy(
        src_ref=src, dst_ref=dst, send_sem=send, recv_sem=recv,
        device_id=where, device_id_type=pl.DeviceIdType.MESH,
    )


def others(me, count):
    return [lax.rem(me + k, count) for k in range(1, count)]


def greet(groups, parts):
    p, f = lax.axis_index("sp"), lax.axis_index("fsdp")
    barrier = pltpu.get_barrier_semaphore()
    for q in others(p, groups):
        pl.semaphore_signal(barrier, inc=1, device_id=peer(q, f), device_id_type=pl.DeviceIdType.MESH)
    for g in others(f, parts):
        pl.semaphore_signal(barrier, inc=1, device_id=peer(p, g), device_id_type=pl.DeviceIdType.MESH)


def greeted(groups, parts):
    pl.semaphore_wait(pltpu.get_barrier_semaphore(), groups + parts - 2)


class Spread:
    def __init__(self, src, dst, parts, send, recv, own):
        self.src, self.dst, self.send, self.recv, self.own = src, dst, send, recv, own
        self.p, self.f = lax.axis_index("sp"), lax.axis_index("fsdp")
        core = lax.rem(self.p, 2)
        self.mate = self.p + 1 - 2 * core
        self.parts, self.major = parts, parts // 2
        self.a, self.b = self.f // 2, lax.rem(self.f, 2)
        self.twin = self.a * 2 + 1 - self.b
        half = src.shape[1] // 2
        self.lanes = pl.ds(pl.multiple_of(core * half, 128), half)
        self.mate_lanes = pl.ds(pl.multiple_of((1 - core) * half, 128), half)

    def back(self, k):
        return lax.rem(self.a + self.major - k, self.major)

    def block(self, g, lanes=None):
        return self.dst.at[g, :, self.lanes if lanes is None else lanes]

    def first(self, k):
        where = lax.rem(self.a + k, self.major) * 2 + self.b
        where = self.twin if k == 0 else where
        return remote(
            self.src.at[:, self.lanes], self.block(self.f), self.send.at[0, k],
            self.recv.at[0, self.f], peer(self.p, where),
        )

    def to_twin(self, k):
        g = self.back(k) * 2 + self.b
        return remote(
            self.block(g), self.block(g), self.send.at[1, k], self.recv.at[0, g],
            peer(self.p, self.twin),
        )

    def to_mate(self, k, b):
        g = self.back(k) * 2 + b
        slot = k if b is self.b else self.major + k
        return remote(
            self.block(g), self.block(g), self.send.at[2, slot], self.recv.at[1, g],
            peer(self.mate, self.f),
        )

    def keep(self):
        return pltpu.make_async_copy(self.src, self.dst.at[self.f], self.own)

    def start_lines(self):
        self.keep().start()
        for k in range(1, self.major):
            self.first(k).start()

    def start_twin(self):
        self.first(0).start()

    def start(self):
        self.start_lines()
        self.start_twin()

    def relay(self, k):
        self.to_twin(k).wait_recv()
        self.to_twin(k).start()
        self.to_mate(k, self.b).start()

    def relay_twin(self, k):
        other = 1 - self.b
        copy = self.to_mate(k, other)
        g = self.back(k) * 2 + other
        remote(
            self.block(g), self.block(g), self.send.at[1, 0], self.recv.at[0, g],
            peer(self.p, self.twin),
        ).wait_recv()
        copy.start()

    def finish(self):
        for g in others(self.f, self.parts):
            there = self.block(g, self.mate_lanes)
            remote(
                there, there, self.send.at[1, 0], self.recv.at[1, g], peer(self.mate, self.f)
            ).wait_recv()
        for k in range(self.major):
            self.first(k).wait_send()
            self.to_mate(k, 1 - self.b).wait_send()
        for k in range(1, self.major):
            self.to_twin(k).wait_send()
            self.to_mate(k, self.b).wait_send()
        self.keep().wait()

    @staticmethod
    def semaphores(parts):
        dma = pltpu.SemaphoreType.DMA
        return [dma((3, parts)), dma((2, parts)), dma(())]


class Fold:
    def __init__(self, src, out, parts, mine, r1, r2, s2, r3, own, send1, recv1, send2, recv2, send3, recv3):
        self.__dict__.update(
            src=src, out=out, mine=mine, r1=r1, r2=r2, s2=s2, r3=r3, own=own, send1=send1,
            recv1=recv1, send2=send2, recv2=recv2, send3=send3, recv3=recv3,
        )
        self.p, self.f = lax.axis_index("sp"), lax.axis_index("fsdp")
        core = lax.rem(self.p, 2)
        self.mate = self.p + 1 - 2 * core
        self.major = parts // 2
        self.a, self.b = self.f // 2, lax.rem(self.f, 2)
        self.twin = self.a * 2 + 1 - self.b
        half = src.shape[2] // 2
        self.lanes = pl.ds(pl.multiple_of(core * half, 128), half)
        self.mate_lanes = pl.ds(pl.multiple_of((1 - core) * half, 128), half)

    def keep(self):
        return pltpu.make_async_copy(self.src.at[:, :, self.lanes], self.mine, self.own)

    def to_mate(self):
        return remote(
            self.src.at[:, :, self.mate_lanes], self.r1, self.send1, self.recv1,
            peer(self.mate, self.f),
        )

    def to_twin(self, c):
        return remote(
            self.mine.at[c * 2 + 1 - self.b], self.r2.at[c], self.send2.at[c], self.recv2.at[c],
            peer(self.p, self.twin),
        )

    def along(self, k):
        c = lax.rem(self.a + k, self.major)
        return remote(
            self.s2.at[c], self.r3.at[self.a], self.send3.at[c], self.recv3.at[self.a],
            peer(self.p, c * 2 + self.b),
        )

    def start(self):
        self.to_mate().start()
        self.keep().start()

    def pairs(self):
        self.keep().wait()
        self.to_mate().wait()
        self.mine[...] = (self.mine[...].astype(F32) + self.r1[...].astype(F32)).astype(BF16)
        for c in range(self.major):
            self.to_twin(c).start()

    def planes(self):
        for c in range(self.major):
            self.to_twin(c).wait()
            self.s2[c] = (
                self.mine[c * 2 + self.b].astype(F32) + self.r2[c].astype(F32)
            ).astype(BF16)
        for k in range(1, self.major):
            self.along(k).start()

    def lines(self):
        total = self.mine[self.f].astype(F32) + self.r2[self.a].astype(F32)
        for k in range(1, self.major):
            c = lax.rem(self.a + k, self.major)
            remote(
                self.r3.at[c], self.r3.at[c], self.send3.at[0], self.recv3.at[c],
                peer(self.p, self.twin),
            ).wait_recv()
            total = total + self.r3[c].astype(F32)
        self.out[...] = total.astype(BF16)
        for k in range(1, self.major):
            self.along(k).wait_send()

    @staticmethod
    def scratch(parts, rows, lanes):
        dma = pltpu.SemaphoreType.DMA
        major, half = parts // 2, lanes // 2
        return [
            pltpu.VMEM((parts, rows, half), BF16), pltpu.VMEM((parts, rows, half), BF16),
            pltpu.VMEM((major, rows, half), BF16), pltpu.VMEM((major, rows, half), BF16),
            pltpu.VMEM((major, rows, half), BF16), dma(()), dma(()), dma(()),
            dma((major,)), dma((major,)), dma((major,)), dma((major,)),
        ]


def column_sum(x):
    return jnp.sum(x, 0, keepdims=True)


GAIN_ONE, BIAS_ONE, Q_BIAS, V_BIAS, OUT_BIAS, GAIN_TWO, BIAS_TWO, PROJ_BIAS = range(8)


def triangle(index, size):
    row = sum((index >= m * (m + 1) // 2).astype(jnp.int32) for m in range(1, size))
    return row, index - row * (row + 1) // 2


def triangle_by_column(index, size):
    starts = [c * (2 * size + 1 - c) // 2 for c in range(size)]
    col = sum((index >= at).astype(jnp.int32) for at in starts[1:])
    return col + index - col * (2 * size + 1 - col) // 2, col


def pick(cond, this, other):
    return jnp.where(cond, this, other)


class Place:
    def __init__(self, groups, count):
        self.p, self.f = lax.axis_index("sp"), lax.axis_index("fsdp")
        self.side = self.p // 2
        self.core = lax.rem(self.p, 2)
        self.mate = self.p + 1 - 2 * self.core
        far = (1 - self.side) * 2
        self.far = (far + self.core, far + 1 - self.core)
        self.groups = groups
        self.count = count
        self.half = 2 * count
        self.near_block = self.side * self.half
        self.far_block = (1 - self.side) * self.half

    def peer(self, q):
        return peer(q, self.f)

    def others(self):
        return others(self.p, self.groups)

    def meet(self):
        barrier = pltpu.get_barrier_semaphore()
        for q in self.others():
            pl.semaphore_signal(
                barrier, inc=1, device_id=self.peer(q), device_id_type=pl.DeviceIdType.MESH
            )
        pl.semaphore_wait(barrier, self.groups - 1)


def rows_of(block, count, size):
    return block // count, pl.ds(pl.multiple_of(lax.rem(block, count) * size, size), size)


def head_lanes(h, x, rest):
    lane = lax.broadcasted_iota(jnp.int32, x.shape, 1)
    return jnp.where(lane // HEAD_DIM == h, x, rest)


def causal(size):
    rows = lax.broadcasted_iota(jnp.int32, (size, size), 0)
    return rows <= lax.broadcasted_iota(jnp.int32, (size, size), 1)


def document_codes(starts, length):
    shape = (2 * HEAD_DIM, starts.shape[1])
    row = lax.rem(lax.broadcasted_iota(jnp.int32, shape, 0), HEAD_DIM)
    bits = max(1, (length - 1).bit_length())
    bit = lax.shift_right_logical(jnp.broadcast_to(starts, shape), row // 2) & 1
    code = jnp.where(lax.rem(row, 2) == 0, bit, 1 - bit).astype(F32)
    used = row < 2 * bits
    query = jnp.where(used, code, 0.0)
    key = jnp.where(used, (code - 1.0) * FAR, 1.0)
    return query.T.astype(BF16), key.T.astype(BF16)


def value_lanes(values, size):
    shape = (2 * HEAD_DIM, size)
    row = lax.broadcasted_iota(jnp.int32, shape, 0)
    out = jnp.zeros(shape, F32)
    for h, value in enumerate(values):
        rest = -value
        for n in range(3):
            piece = rest.astype(BF16).astype(F32)
            rest = rest - piece
            out = jnp.where(row == (1 - h) * HEAD_DIM + SPARE + n, piece, out)
    return out.T.astype(BF16)


def front_kernel(size, heads, groups, parts, tile, x_ref, wq_ref, st_in, *refs):
    vec_refs, shards, refs = refs[:9], refs[9:12], refs[12:]
    qkv_any, o_ref, lse_ref, attn_ref, eq_any, ek_any, small_ref, fcb_ref, wq_all = refs[:9]
    qkv_ref, eq_ref, ek_ref, store = refs[-4:]
    wide, refs = refs[9:12], refs[12:]
    own_ref, sg, own_vec, vg, m_sc, l_sc, acc_sc = refs[:7]
    v_send, v_recv, s_send, s_recv, near_s, near_r, far_s, far_r, out_s, out_r = refs[7:17]
    first_spread, *spreads = [
        Spread(src, dst, parts, *refs[17 + 3 * n : 20 + 3 * n])
        for n, (src, dst) in enumerate(zip((wq_ref,) + shards, (wq_all,) + wide))
    ]
    per, model = x_ref.shape
    width = model // groups
    count = per // size
    major = parts // 2
    at = Place(groups, count)
    p, f, side, half = at.p, at.f, at.side, at.half

    greet(groups, parts)
    piece = vec_refs[0].shape[1]
    runs, bits = vec_refs[8].shape
    own_vec[...] = jnp.zeros_like(own_vec)
    for k in range(8):
        own_vec[k : k + 1, 0:piece] = vec_refs[k][...].astype(F32)
    own_vec[8 : 8 + runs, 0:bits] = vec_refs[8][...].astype(F32)
    vg[f] = own_vec[...]
    sg[p] = st_in[...]
    m_sc[...] = jnp.full_like(m_sc, NEG)
    l_sc[...] = jnp.zeros_like(l_sc)
    acc_sc[...] = jnp.zeros_like(acc_sc)
    greeted(groups, parts)

    copies = []

    def go(copy):
        copy.start()
        copies.append(copy)

    first_spread.start()
    for k, q in enumerate(at.others()):
        go(remote(st_in, sg.at[p], s_send.at[k], s_recv.at[p], at.peer(q)))
    for k, g in enumerate(others(f, parts)):
        go(remote(own_vec, vg.at[f], v_send.at[k], v_recv.at[f], peer(p, g)))
    for q in at.others():
        remote(st_in, sg.at[q], s_send.at[0], s_recv.at[q], at.peer(q)).wait_recv()

    @pl.loop(0, groups)
    def _(q):
        starts = jnp.concatenate([sg[q, k : k + 1] for k in range(per // 128)], 1)
        rows = pl.ds(pl.multiple_of(q * per, per), per)
        eq_ref[rows], ek_ref[rows] = document_codes(starts, groups * per)

    stores = [
        pltpu.make_async_copy(src, dst, store.at[n])
        for n, (src, dst) in enumerate(
            [(eq_ref, eq_any), (ek_ref, ek_any)]
            + [(qkv_ref.at[q], qkv_any.at[q]) for q in (p, at.mate, *at.far)]
        )
    ]
    for copy in stores[:2]:
        copy.start()

    for k in range(1, major):
        first_spread.relay(k)
    for k in range(major):
        first_spread.relay_twin(k)
    for g in others(f, parts):
        remote(own_vec, vg.at[g], v_send.at[0], v_recv.at[g], peer(p, g)).wait_recv()
    for g in range(parts):
        small_ref[:, g * piece : (g + 1) * piece] = vg[g, 0:8, 0:piece]
        for k in range(runs):
            lane = (g * runs + k) * bits
            fcb_ref[:, lane : lane + bits] = vg[g, 8 + k : 9 + k, 0:bits]
    first_spread.finish()
    for spread in spreads:
        spread.start_lines()

    def far_copy(b, t, d):
        rows = pl.ds(pl.multiple_of(b * size, size), size)
        return remote(
            own_ref.at[at.far[d], t, rows], qkv_ref.at[p, t, rows], far_s.at[d, b, t],
            far_r.at[p, t, b], at.peer(at.far[d]),
        )

    near = remote(own_ref.at[at.mate], qkv_ref.at[p], near_s, near_r, at.peer(at.mate))

    @pl.loop(0, per // tile)
    def _(i):
        rows = pl.ds(pl.multiple_of(i * tile, tile), tile)
        normed, _ = normalize(x_ref[rows].astype(F32))
        small = small_ref[...]
        act = (normed * small[GAIN_ONE : GAIN_ONE + 1] + small[BIAS_ONE : BIAS_ONE + 1]).astype(BF16)
        weight = weight_rows(wq_all, wq_all.shape[1])
        for part, row in ((0, Q_BIAS), (1, None), (2, V_BIAS)):
            out = dot(act, weight[:, part * model : (part + 1) * model])
            if row is not None:
                out = out + small[row : row + 1]
            out = out.astype(BF16)
            if part == 0:
                out = (out.astype(F32) * (HEAD_DIM ** (-0.5) * LOG2E)).astype(BF16)
            for g in range(groups):
                own_ref[g, part, rows] = out[:, g * width : (g + 1) * width]

        @pl.when(lax.rem(i + 1, size // tile) == 0)
        def _():
            for n in range(3):
                for d in range(2):
                    far_copy((i + 1) // (size // tile) - 1, lax.rem(n + pick(side == 1, 0, 1), 3), d).start()

    near.start()
    for spread in spreads:
        spread.start_twin()
    qkv_ref[p] = own_ref[p]

    def far_wait(t, block):
        src, rows = rows_of(block, count, size)
        there = qkv_ref.at[src, t, rows]
        remote(there, there, far_s.at[0, 0, 0], far_r.at[src, t, lax.rem(block, count)], at.peer(src)).wait_recv()

    def block(q, k, diagonal):
        src, rows = rows_of(q, count, size)
        cols = pl.ds(pl.multiple_of(q * size, size), size)
        ksrc, krows = rows_of(k, count, size)
        query = qkv_ref[src, 0, rows, :]
        key = qkv_ref[ksrc, 1, krows, :]
        value = qkv_ref[ksrc, 2, krows, :]
        code_q = eq_ref[cols, :]
        code_k = ek_ref[pl.ds(pl.multiple_of(k * size, size), size), :]
        old = [(m_sc[h : h + 1, cols], l_sc[h : h + 1, cols]) for h in range(heads)]
        acc = acc_sc[:, cols]
        scores = [
            dot(head_lanes(h, key, code_k), head_lanes(h, query, code_q), NT) for h in range(heads)
        ]
        new, parts = [], []
        for h in range(heads):
            s = scores[h]
            if diagonal:
                s = jnp.where(causal(size), s, NEG)
            m_old, l_old = old[h]
            m_new = jnp.maximum(m_old, jnp.max(s, 0, keepdims=True))
            e = jnp.exp2(s - m_new).astype(BF16)
            alpha = jnp.exp2(m_old - m_new)
            mixed = dot(head_lanes(h, value, jnp.ones_like(value)), e, TN)
            low, other = h * HEAD_DIM, (1 - h) * HEAD_DIM
            new.append((m_new, l_old * alpha + mixed[other : other + 1]))
            parts.append(acc[low : low + HEAD_DIM] * alpha + mixed[low : low + HEAD_DIM])
        acc_sc[:, cols] = jnp.concatenate(parts, 0)
        for h in range(heads):
            m_sc[h : h + 1, cols], l_sc[h : h + 1, cols] = new[h]

    def out_copy(q):
        src, rows = rows_of(q, count, size)
        return remote(
            o_ref.at[src, rows], attn_ref.at[p, rows], out_s.at[q], out_r.at[p, lax.rem(q, count)],
            at.peer(src),
        )

    def finish(q):
        src, rows = rows_of(q, count, size)
        cols = pl.ds(pl.multiple_of(q * size, size), size)
        parts = []
        for h in range(heads):
            sl = slice(h * HEAD_DIM, (h + 1) * HEAD_DIM)
            total = l_sc[h : h + 1, cols]
            parts.append(acc_sc[sl, cols] * (1.0 / total))
            lse_ref[h : h + 1, cols] = m_sc[h : h + 1, cols] + jnp.log2(total)
        out = jnp.concatenate(parts, 0).T.astype(BF16)
        o_ref[src, rows] = out

        @pl.when(src == p)
        def _():
            attn_ref[p, rows] = out

        @pl.when(src != p)
        def _():
            out_copy(q).start()

    small = count * (count + 1) // 2
    cross = 2 * small + count * count
    bulk = cross + half * half
    end = bulk + half * (half + 1) // 2

    @pl.loop(0, end)
    def _(step):
        second = step >= small
        row, col = triangle(step - pick(second, small, 0), count)
        base = pick(second, at.mate, p) * count
        q, k = base + row, base + col
        c = step - 2 * small
        in_cross = (step >= 2 * small) & (step < cross)
        q = pick(in_cross, at.near_block + count + c // count, q)
        k = pick(in_cross, at.near_block + lax.rem(c, count), k)
        c = step - cross
        in_bulk = (step >= cross) & (step < bulk)
        outer, inner = c // half, lax.rem(c, half)
        outer = lax.rem(outer, 2) * count + outer // 2
        q = pick(in_bulk, half + pick(side == 0, outer, inner), q)
        k = pick(in_bulk, pick(side == 0, inner, outer), k)
        in_last = step >= bulk
        row, col = triangle(step - bulk, half)
        q = pick(in_last, at.far_block + row, q)
        k = pick(in_last, at.far_block + col, k)

        @pl.when(step == small)
        def _():
            near.wait_recv()

        starts_outer = in_bulk & (inner == 0)
        starts_row = in_last & (col == 0)

        @pl.when((starts_outer & (side == 0)) | (starts_row & (side == 1)))
        def _():
            far_wait(0, q)

        @pl.when((starts_outer & (side == 1)) | (starts_row & (side == 0)))
        def _():
            far_block = pick(in_bulk, k, q)
            far_wait(1, far_block)
            far_wait(2, far_block)

        @pl.when(q == k)
        def _():
            block(q, k, True)

        @pl.when(q != k)
        def _():
            block(q, k, False)

        for n in range(1, major):
            @pl.when(step == RELAY_AT + (n - 1) * RELAY_GAP * 2 // (major - 1))
            def _(n=n):
                for spread in spreads:
                    spread.relay(n)
        for n in range(major):
            @pl.when(step == TWIN_AT + n * (end - 1 - TWIN_AT) // (major - 1))
            def _(n=n):
                for spread in spreads:
                    spread.relay_twin(n)

        @pl.when(step == cross)
        def _():
            for copy in stores[2:4]:
                copy.start()

        near_done = step == pick(side == 0, cross, bulk) - 1
        low = pick(near_done, at.near_block, q)
        high = pick(near_done, at.near_block + half, pick(in_last & (q == k), q + 1, q))
        pl.loop(low, high)(finish)

    for copy in stores[4:]:
        copy.start()
    for q in at.others():
        for b in range(count):
            rows = pl.ds(b * size, size)
            there = attn_ref.at[q, rows]
            remote(there, there, out_s.at[0], out_r.at[q, b], at.peer(q)).wait_recv()
            out_copy(q * count + b).wait_send()
    near.wait_send()
    for b in range(count):
        for t in range(3):
            for d in range(2):
                far_copy(b, t, d).wait_send()
    for copy in copies:
        copy.wait_send()
    for spread in spreads:
        spread.finish()
    for copy in stores:
        copy.wait()


def front(x, w_qkv, starts, vectors, shards, groups, parts, size=512, tile=256):
    per, model = x.shape
    length = groups * per
    width = model // groups
    heads = width // HEAD_DIM
    count = per // size
    starts = starts.reshape(-1, 128)
    fc = vectors[8].shape[0]
    piece = vectors[0].shape[0]
    vectors = [v.reshape(1, -1) for v in vectors[:8]] + [vectors[8].reshape(-1, min(fc, 128))]
    dma = pltpu.SemaphoreType.DMA
    vmem = pl.BlockSpec(memory_space=pltpu.VMEM)
    slabs = (groups, 3, per, width)
    far = pl.BlockSpec(memory_space=pl.ANY)
    return pl.pallas_call(
        functools.partial(front_kernel, size, heads, groups, parts, tile),
        out_shape=(
            jax.ShapeDtypeStruct(slabs, BF16),
            jax.ShapeDtypeStruct((groups, per, width), BF16),
            jax.ShapeDtypeStruct((8, length), F32),
            jax.ShapeDtypeStruct((groups, per, width), BF16),
            jax.ShapeDtypeStruct((length, width), BF16),
            jax.ShapeDtypeStruct((length, width), BF16),
            jax.ShapeDtypeStruct((8, parts * piece), F32),
            jax.ShapeDtypeStruct((1, parts * fc), F32),
            jax.ShapeDtypeStruct((parts,) + w_qkv.shape, BF16),
            *[jax.ShapeDtypeStruct((parts,) + shard.shape, BF16) for shard in shards],
        ),
        in_specs=[vmem] * 15,
        out_specs=[far] + [vmem] * 3 + [far] * 2 + [vmem] * 3 + [far] * 3,
        scratch_shapes=[
            pltpu.VMEM(slabs, BF16), pltpu.VMEM((groups,) + starts.shape, jnp.int32),
            pltpu.VMEM((16, 128), F32), pltpu.VMEM((parts, 16, 128), F32),
            pltpu.VMEM((8, length), F32), pltpu.VMEM((8, length), F32),
            pltpu.VMEM((width, length), F32),
            dma((parts,)), dma((parts,)), dma((groups,)), dma((groups,)), dma(()), dma(()),
            dma((2, count, 3)), dma((groups, 3, count)), dma((groups * count,)), dma((groups, count)),
        ] + Spread.semaphores(parts) * 4 + [
            pltpu.VMEM(slabs, BF16), pltpu.VMEM((length, width), BF16),
            pltpu.VMEM((length, width), BF16), dma((6,)),
        ],
        compiler_params=pltpu.CompilerParams(
            vmem_limit_bytes=VMEM_LIMIT, collective_id=2, has_side_effects=True
        ),
        cost_estimate=cost(4 * length * length * width, 16 * length * width, length * length),
        name="front",
    )(x, w_qkv, starts, *vectors, *shards)


def back_kernel(
    size, heads, parts, tile, qkv_any, own_ref, o_any, lse_any, eq_any, ek_any, ga_ref, gp_ref,
    x_any, resid_any, w_any, small_ref, sums_ref,
    gt_ref, gw_ref, gv_ref, go_ref, gf_ref, gpo_ref, *refs
):
    (do_sc, qa_sc, da_sc, dqt_sc, dk_sc, dv_sc, stage, grad_sc,
     near_s, near_r, far_s, far_r, out_s, out_r) = refs[:14]
    fa_sc, fp_sc, x_sc, resid_sc, w_sc, act_sc, load = refs[14:21]
    (xa, xp, fulla, fullp, xs, xr, ys, yr) = refs[21:29]
    (acc, out, vec, mine, vsend, vpart, low, r1, s2, r2, keep, s3, r3) = refs[29:42]
    (v1s, v1r, v2s, v2r, c1s, c1r, c2s, c2r, c3s, c3r, c4s, c4r) = refs[42:54]
    folds = [Fold(ga_ref, fa_sc, parts, *refs[54:66]), Fold(gp_ref, fp_sc, parts, *refs[66:78])]
    qkv_ref, o_ref, lse_ref, eq_ref, ek_ref, more = refs[78:]
    groups, _, per, width = qkv_ref.shape
    model = x_sc.shape[1]
    count = per // size
    at = Place(groups, count)
    p, f, side, core, half = at.p, at.f, at.side, at.core, at.half
    scale = HEAD_DIM ** (-0.5)
    loads = [
        pltpu.make_async_copy(src, dst, load.at[n])
        for n, (src, dst) in enumerate(((x_any, x_sc), (w_any, w_sc), (resid_any, resid_sc)))
    ]
    early = [
        pltpu.make_async_copy(src, dst, more.at[n])
        for n, (src, dst) in enumerate((
            (own_ref.at[p], do_sc.at[p]), (qkv_any, qkv_ref), (o_any, o_ref),
            (lse_any, lse_ref), (eq_any, eq_ref), (ek_any, ek_ref),
        ))
    ]
    greet(groups, parts)
    for copy in loads[:1] + early + loads[1:]:
        copy.start()
    dqt_sc[...] = jnp.zeros_like(dqt_sc)
    dk_sc[...] = jnp.zeros_like(dk_sc)
    dv_sc[...] = jnp.zeros_like(dv_sc)
    greeted(groups, parts)

    near = remote(own_ref.at[at.mate], do_sc.at[p], near_s, near_r, at.peer(at.mate))
    near.start()

    def far_copy(b, d):
        rows = pl.ds(b * size, size)
        return remote(
            own_ref.at[at.far[d], rows], do_sc.at[p, rows], far_s.at[d, b], far_r.at[p, b],
            at.peer(at.far[d]),
        )

    for b in range(count):
        for d in range(2):
            far_copy(b, d).start()
    for fold in folds:
        fold.start()

    small = small_ref[...]
    gain = small[GAIN_ONE : GAIN_ONE + 1]
    bias = small[BIAS_ONE : BIAS_ONE + 1]
    loads[0].wait()

    @pl.loop(0, per // tile)
    def _(i):
        rows = pl.ds(pl.multiple_of(i * tile, tile), tile)
        normed, _ = normalize(x_sc[rows].astype(F32))
        act_sc[rows] = (normed * gain + bias).astype(BF16)

    for copy in early:
        copy.wait()

    def columns(block):
        return pl.ds(pl.multiple_of(block * size, size), size)

    def prepare(q):
        src, rows = rows_of(q, count, size)
        cols = columns(q)
        prod = (do_sc[src, rows].astype(F32) * o_ref[src, rows].astype(F32)).T
        delta = [
            jnp.sum(prod[h * HEAD_DIM : (h + 1) * HEAD_DIM], 0, keepdims=True) for h in range(heads)
        ]
        da_sc[cols, :] = value_lanes(delta, size)
        lse = [lse_ref[h : h + 1, cols] for h in range(heads)]
        qa_sc[cols, :] = eq_ref[cols, :] + value_lanes(lse, size)

    def block(q, k, diagonal):
        src, rows = rows_of(q, count, size)
        cols, kcols = columns(q), columns(k)
        ksrc, krows = rows_of(k, count, size)
        query, query_rest = qkv_ref[src, 0, rows, :], qa_sc[cols, :]
        grad, grad_rest = do_sc[src, rows], da_sc[cols, :]
        key, key_rest = qkv_ref[ksrc, 1, krows, :], ek_ref[kcols, :]
        value = qkv_ref[ksrc, 2, krows, :]
        query = [head_lanes(h, query, query_rest) for h in range(heads)]
        grad = [head_lanes(h, grad, grad_rest) for h in range(heads)]
        scores = [dot(head_lanes(h, key, key_rest), query[h], NT) for h in range(heads)]
        slopes = [
            dot(head_lanes(h, value, jnp.ones_like(value)), grad[h], NT) for h in range(heads)
        ]
        dqt, dv, dk = [], None, None
        for h in range(heads):
            s = scores[h]
            if diagonal:
                s = jnp.where(causal(size), s, NEG)
            e = jnp.exp2(s)
            ds = (e * slopes[h]).astype(BF16)
            dvh = dot(e.astype(BF16), grad[h])
            dkh = dot(ds, query[h])
            dv = dvh if dv is None else head_lanes(h, dvh, dv)
            dk = dkh if dk is None else head_lanes(h, dkh, dk)
            dqt.append(dot(key[:, h * HEAD_DIM : (h + 1) * HEAD_DIM], ds, TN))
        dqt_sc[:, cols] += jnp.concatenate(dqt, 0)
        dv_sc[kcols, :] += dv
        dk_sc[kcols, :] += dk

    def out_copy(block, part):
        src, rows = rows_of(block, count, size)
        return remote(
            stage.at[src, part, rows], grad_sc.at[p, part, rows], out_s.at[block, part],
            out_r.at[p, part, lax.rem(block, count)], at.peer(src),
        )

    def give(block, part, value):
        src, rows = rows_of(block, count, size)

        @pl.when(src == p)
        def _():
            grad_sc[p, part, rows] = value

        @pl.when(src != p)
        def _():
            stage[src, part, rows] = value
            out_copy(block, part).start()

    def finish_query(q):
        give(q, 0, (dqt_sc[:, columns(q)] * scale).T.astype(BF16))

    def finish_key(k):
        give(k, 1, (dk_sc[columns(k), :] * (1.0 / LOG2E)).astype(BF16))
        give(k, 2, dv_sc[columns(k), :].astype(BF16))

    small = count * (count + 1) // 2
    far = 2 * small
    bulk = far + half * (half + 1) // 2
    cross = bulk + half * half
    end = cross + count * count

    @pl.loop(0, end)
    def _(step):
        second = step >= small
        row, col = triangle(step - pick(second, small, 0), count)
        base = pick(second, at.mate, p) * count
        q, k = base + row, base + col
        in_far = (step >= far) & (step < bulk)
        row, column = triangle_by_column(step - far, half)
        q = pick(in_far, at.far_block + row, q)
        k = pick(in_far, at.far_block + column, k)
        c = step - bulk
        in_bulk = (step >= bulk) & (step < cross)
        outer, inner = c // half, lax.rem(c, half)
        q = pick(in_bulk, half + pick(side == 0, outer, inner), q)
        k = pick(in_bulk, pick(side == 0, inner, outer), k)
        c = step - cross
        in_cross = step >= cross
        q = pick(in_cross, at.near_block + count + c // count, q)
        k = pick(in_cross, at.near_block + lax.rem(c, count), k)

        @pl.when(step == small)
        def _():
            near.wait_recv()

        @pl.when(in_far & (column == 0))
        def _():
            src, rows = rows_of(q, count, size)
            there = do_sc.at[src, rows]
            remote(there, there, far_s.at[0, 0], far_r.at[src, lax.rem(q, count)], at.peer(src)).wait_recv()

        @pl.when(((step < far) & (col == 0)) | (in_far & (column == 0)))
        def _():
            prepare(q)

        @pl.when(q == k)
        def _():
            block(q, k, True)

        @pl.when(q != k)
        def _():
            block(q, k, False)

        for n, fold in enumerate(folds):
            pl.when(step == end // 9 + n)(fold.pairs)
            pl.when(step == end // 2 - 1 + 3 * n)(fold.planes)

        column_done = in_far & (row == half - 1)
        outer_done = in_bulk & (inner == half - 1)
        done = step == end - 1
        near_low, near_high = at.near_block, at.near_block + half
        query = (column_done & (side == 1)) | (outer_done & (side == 0))
        block_id = at.far_block + pick(in_far, column, outer)
        pl.loop(
            pick(done, near_low, block_id),
            pick(done, near_high, pick(query, block_id + 1, block_id)),
        )(finish_query)
        key = (column_done & (side == 0)) | (outer_done & (side == 1))
        pl.loop(
            pick(done, near_low, block_id),
            pick(done, near_high, pick(key, block_id + 1, block_id)),
        )(finish_key)

    across = p + groups // 2 - side * groups
    cross = [
        remote(src, dst, xs.at[n], xr.at[n], at.peer(across))
        for n, (src, dst) in enumerate(((fa_sc, xa), (fp_sc, xp)))
    ]
    for q in at.others():
        for b in range(count):
            for part in range(3):
                there = grad_sc.at[q, part, pl.ds(b * size, size)]
                remote(there, there, out_s.at[0, 0], out_r.at[q, part, b], at.peer(q)).wait_recv()

    copies = []

    def go(copy):
        copy.start()
        copies.append(copy)

    shard = model // parts
    chunks, chunk = acc.shape[0], acc.shape[2] // 2

    def number(c, s, k):
        return (c * 2 + s) * chunks + k

    def lane(c, s, k):
        return pl.ds(pl.multiple_of(number(c, s, k) * chunk, 128), chunk)

    def product(c, k):
        pair = []
        for s in range(2):
            n = number(c, s, k)
            pair.append(grad_sc[lax.rem(n, groups), n // groups])
        return dot(act_sc[...], jnp.concatenate(pair, 1), TN)

    mate = at.peer(at.mate)
    for k in range(chunks):
        low[k] = product(1 - core, k).astype(BF16)
        if k:
            go(remote(low.at[k - 1], r1.at[k - 1], c1s.at[k - 1], c1r.at[k - 1], mate))
    acc[0] = product(core, 0)
    go(remote(low.at[chunks - 1], r1.at[chunks - 1], c1s.at[chunks - 1], c1r.at[chunks - 1], mate))
    for k in range(1, chunks):
        acc[k] = product(core, k)
    for g in range(groups):
        lanes = slice(g * width, (g + 1) * width)
        vec[2:3, lanes] = column_sum(grad_sc[g, 0].astype(F32))
        vec[3:4, lanes] = column_sum(grad_sc[g, 2].astype(F32))
    this = pl.ds(pl.multiple_of(side * chunk, 128), chunk)
    that = pl.ds(pl.multiple_of((1 - side) * chunk, 128), chunk)
    for k in range(chunks):
        remote(r1.at[k], r1.at[k], c1s.at[k], c1r.at[k], mate).wait_recv()
        s2[k] = (acc[k, :, that] + r1[k, :, that].astype(F32)).astype(BF16)
        go(remote(s2.at[k], r2.at[k], c2s.at[k], c2r.at[k], at.peer(across)))
    for fold in folds:
        fold.lines()
    for copy in cross:
        copy.start()

    loads[1].wait()
    loads[2].wait()
    vec[0:2, :] = jnp.zeros_like(vec[0:2, :])
    weight = weight_rows(w_sc, w_sc.shape[1])

    def token_rows(i):
        rows = pl.ds(pl.multiple_of(i * tile, tile), tile)
        normed, inverse = normalize(x_sc[rows].astype(F32))
        grad = jnp.concatenate([grad_sc[g, part, rows] for part in range(3) for g in range(groups)], 1)
        grad_act = dot(grad, weight, NT)
        gt_ref[rows] = (
            resid_sc[rows] + normalize_back(grad_act * gain, normed, inverse)
        ).astype(BF16)
        vec[0:1, :] += column_sum(grad_act * normed)
        vec[1:2, :] += column_sum(grad_act)

    pl.loop(0, per // tile)(token_rows)

    vec[4:8, :] = sums_ref[1:5, 0:model]
    piece = model // parts
    fc = sums_ref.shape[1] // parts
    bits = min(128, fc)
    vsend[...] = jnp.zeros_like(vsend)
    for g in range(parts):
        vsend[g, 0:8, 0:piece] = vec[:, g * piece : (g + 1) * piece]
        for k in range(fc // bits):
            first = g * fc + k * bits
            vsend[g, 8 + k : 9 + k, 0:bits] = sums_ref[0:1, first : first + bits]

    for k in range(chunks):
        remote(s2.at[k], r2.at[k], c2s.at[k], c2r.at[k], at.peer(across)).wait_recv()
        total = acc[k, :, this] + r1[k, :, this].astype(F32) + r2[k].astype(F32)
        keep[k] = total
        s3[k] = total.astype(BF16)
        for n, g in enumerate(others(f, parts)):
            rows = pl.ds(pl.multiple_of(g * shard, shard), shard)
            go(remote(s3.at[k, rows], r3.at[k, f], c3s.at[k, n], c3r.at[k, f], peer(p, g)))
    for n, g in enumerate(others(f, parts)):
        go(remote(vsend.at[g], vpart.at[f], v1s.at[n], v1r.at[f], peer(p, g)))
    folded = []
    for n, (mine_ref, theirs, full) in enumerate(((fa_sc, xa, fulla), (fp_sc, xp, fullp))):
        cross[n].wait()
        wide = mine_ref.shape[1]
        here = full.at[:, pl.ds(pl.multiple_of(core * wide, 128), wide)]
        there = full.at[:, pl.ds(pl.multiple_of((1 - core) * wide, 128), wide)]
        here[...] = mine_ref[...].astype(F32) + theirs[...].astype(F32)
        go(remote(here, here, ys.at[n], yr.at[n], mate))
        folded.append(remote(there, there, ys.at[n], yr.at[n], mate))
    for g in others(f, parts):
        remote(vsend.at[g], vpart.at[g], v1s.at[0], v1r.at[g], peer(p, g)).wait_recv()
    total = vsend[f]
    for g in others(f, parts):
        total = total + vpart[g]
    mine[p] = total
    for k in range(chunks):
        for g in others(f, parts):
            remote(r3.at[k, g], r3.at[k, g], c3s.at[k, 0], c3r.at[k, g], peer(p, g)).wait_recv()
        total = keep[k, pl.ds(pl.multiple_of(f * shard, shard), shard)]
        for g in others(f, parts):
            total = total + r3[k, g].astype(F32)
        there = out.at[:, lane(core, side, k)]
        there[...] = total.astype(BF16)
        for n, q in enumerate(at.others()):
            go(remote(there, there, c4s.at[k, n], c4r.at[k, p], at.peer(q)))
        if k == 0:
            for n, q in enumerate(at.others()):
                go(remote(mine.at[p], mine.at[p], v2s.at[n], v2r.at[p], at.peer(q)))
    for copy in folded:
        copy.wait_recv()
    go_ref[...] = fulla[:, 0:model]
    gf_ref[...] = fulla[:, model:]
    gpo_ref[...] = fullp[...]
    for q in at.others():
        remote(mine.at[q], mine.at[q], v2s.at[0], v2r.at[q], at.peer(q)).wait_recv()
    total = mine[0]
    for q in range(1, groups):
        total = total + mine[q]
    gv_ref[...] = total
    for k in range(chunks):
        for q in at.others():
            there = out.at[:, lane(lax.rem(q, 2), q // 2, k)]
            remote(there, there, c4s.at[k, 0], c4r.at[k, q], at.peer(q)).wait_recv()
    gw_ref[...] = out[...].astype(F32)
    for copy in copies:
        copy.wait_send()
    for q in at.others():
        for b in range(count):
            for part in range(3):
                out_copy(q * count + b, part).wait_send()
    near.wait_send()
    for b in range(count):
        for d in range(2):
            far_copy(b, d).wait_send()


def back(qkv, grad, out, lse, code_q, code_k, g_a, g_p, x, resid, weight, small, sums, size=512, tile=256):
    groups, _, per, width = qkv.shape
    length = groups * per
    heads = width // HEAD_DIM
    count = per // size
    parts = g_a.shape[0]
    model = x.shape[1]
    triple = 3 * model
    shard = model // parts
    chunk = 128
    chunks = triple // 4 // chunk
    dma = pltpu.SemaphoreType.DMA
    vm = pltpu.VMEM
    vmem = pl.BlockSpec(memory_space=pltpu.VMEM)
    far = pl.BlockSpec(memory_space=pl.ANY)
    f_a = (g_a.shape[1], g_a.shape[2] // 2)
    f_p = (g_p.shape[1], g_p.shape[2] // 2)
    return pl.pallas_call(
        functools.partial(back_kernel, size, heads, parts, tile),
        out_shape=(
            jax.ShapeDtypeStruct((per, model), BF16),
            jax.ShapeDtypeStruct((shard, triple), F32),
            jax.ShapeDtypeStruct((16, 128), F32),
            jax.ShapeDtypeStruct((f_a[0], model), F32),
            jax.ShapeDtypeStruct((f_a[0], 2 * f_a[1] - model), F32),
            jax.ShapeDtypeStruct((f_p[0], 2 * f_p[1]), F32),
        ),
        in_specs=[far] * 11 + [vmem] * 2,
        out_specs=[vmem] * 6,
        scratch_shapes=[
            vm((groups, per, width), BF16), vm((length, width), BF16), vm((length, width), BF16),
            vm((width, length), F32), vm((length, width), F32),
            vm((length, width), F32), vm(qkv.shape, BF16), vm(qkv.shape, BF16),
            dma(()), dma(()), dma((2, count)), dma((groups, count)),
            dma((groups * count, 3)), dma((groups, 3, count)),
            vm(f_a, BF16), vm(f_p, BF16), vm(x.shape, BF16), vm(resid.shape, F32),
            vm(weight.shape, BF16), vm(x.shape, BF16), dma((3,)),
            vm(f_a, BF16), vm(f_p, BF16), vm((f_a[0], 2 * f_a[1]), F32),
            vm((f_p[0], 2 * f_p[1]), F32), dma((2,)), dma((2,)), dma((2,)), dma((2,)),
            vm((chunks, model, 2 * chunk), F32), vm((shard, triple), BF16), vm((8, model), F32),
            vm((groups, 16, 128), F32), vm((parts, 16, 128), F32), vm((parts, 16, 128), F32),
            vm((chunks, model, 2 * chunk), BF16), vm((chunks, model, 2 * chunk), BF16),
            vm((chunks, model, chunk), BF16), vm((chunks, model, chunk), BF16),
            vm((chunks, model, chunk), F32), vm((chunks, model, chunk), BF16),
            vm((chunks, parts, shard, chunk), BF16),
            dma((parts,)), dma((parts,)), dma((groups,)), dma((groups,)),
            dma((chunks,)), dma((chunks,)), dma((chunks,)), dma((chunks,)),
            dma((chunks, parts)), dma((chunks, parts)), dma((chunks, groups)), dma((chunks, groups)),
            *Fold.scratch(*g_a.shape), *Fold.scratch(*g_p.shape),
            vm(qkv.shape, BF16), vm(out.shape, BF16), vm(lse.shape, F32),
            vm(code_q.shape, BF16), vm(code_k.shape, BF16), dma((6,)),
        ],
        compiler_params=pltpu.CompilerParams(
            vmem_limit_bytes=VMEM_LIMIT, collective_id=3, has_side_effects=True
        ),
        cost_estimate=cost(10 * length * length * width, 24 * length * width, length * length),
        name="back",
    )(qkv, grad, out, lse, code_q, code_k, g_a, g_p, x, resid, weight, small, sums)


def hand_out_kernel(piece, fc, *refs):
    ins, outs = refs[:6], refs[6:]
    for src, dst in zip(ins[:5], outs[:5]):
        dst[...] = src[...]
    vec = ins[5]
    for k in range(8):
        outs[5 + k][...] = vec[k : k + 1, 0:piece]
    bits = min(fc, 128)
    for k in range(fc // bits):
        outs[13][:, k * bits : (k + 1) * bits] = vec[8 + k : 9 + k, 0:bits]


def hand_out(arrays, vec, piece, fc):
    vmem = pl.BlockSpec(memory_space=pltpu.VMEM)
    return pl.pallas_call(
        functools.partial(hand_out_kernel, piece, fc),
        out_shape=tuple(
            [jax.ShapeDtypeStruct(v.shape, v.dtype) for v in arrays]
            + [jax.ShapeDtypeStruct((1, piece), F32)] * 8
            + [jax.ShapeDtypeStruct((1, fc), F32)]
        ),
        in_specs=[vmem] * 6,
        out_specs=tuple([vmem] * 14),
        compiler_params=params(),
        name="hand_out",
    )(*arrays, vec)


def middle_kernel(
    groups, x_ref, attn_ref, wo_ref, small_ref, fcb_ref, wf_any, wp_any, cot_any,
    out_any, resid_any, ga_any, gwa_any, gwp_any, gs_ref,
    wf_ref, wp_ref, cot_ref, out_ref, resid_ref, ga_ref, gwo_ref, gwf_ref, gwp_ref, load, store,
):
    loads = [
        pltpu.make_async_copy(src, dst, load.at[n])
        for n, (src, dst) in enumerate(((wf_any, wf_ref), (wp_any, wp_ref), (cot_any, cot_ref)))
    ]
    for copy in loads:
        copy.start()
    stores = []

    def save(src, dst):
        copy = pltpu.make_async_copy(src, dst, store.at[len(stores)])
        copy.start()
        stores.append(copy)

    model = x_ref.shape[-1]
    width = model // groups
    small = small_ref[...]
    w_out = weight_rows(wo_ref, wo_ref.shape[1])
    attn = jnp.concatenate([attn_ref[g] for g in range(groups)], 1)
    resid = x_ref[...].astype(F32) + dot(attn, w_out) + small[OUT_BIAS : OUT_BIAS + 1]
    normed, inverse = normalize(resid)
    gain = small[GAIN_TWO : GAIN_TWO + 1]
    act = (normed * gain + small[BIAS_TWO : BIAS_TWO + 1]).astype(BF16)
    loads[0].wait()
    w_fc = weight_rows(wf_ref, wf_ref.shape[1])
    hidden = dot(act, w_fc) + fcb_ref[...]
    sig = 1.0 / (1.0 + jnp.exp(-1.702 * hidden))
    gelu = hidden * sig
    slope = sig + 1.702 * gelu * (1.0 - sig)
    gelu = gelu.astype(BF16)
    loads[1].wait()
    w_proj = weight_rows(wp_ref, wp_ref.shape[1])
    out_ref[...] = (resid + dot(gelu, w_proj) + small[PROJ_BIAS : PROJ_BIAS + 1]).astype(BF16)
    save(out_ref, out_any)
    loads[2].wait()
    up = cot_ref[...]
    gwp_ref[...] = dot(gelu, up, TN).astype(BF16)
    save(gwp_ref, gwp_any)
    grad_hidden = dot(up, w_proj, NT) * slope
    low = grad_hidden.astype(BF16)
    gs_ref[0:1, :] = column_sum(grad_hidden)
    gwf_ref[...] = dot(act, low, TN).astype(BF16)
    save(gwf_ref, gwa_any.at[:, model:])
    grad_act = dot(low, w_fc, NT)
    up = up.astype(F32)
    grad_resid = up + normalize_back(grad_act * gain, normed, inverse)
    resid_ref[...] = grad_resid
    save(resid_ref, resid_any)
    resid_low = grad_resid.astype(BF16)
    grad_attn = dot(resid_low, w_out, NT).astype(BF16)
    for g in range(groups):
        ga_ref[g] = grad_attn[:, g * width : (g + 1) * width]
    save(ga_ref, ga_any)
    gwo_ref[...] = dot(attn, resid_low, TN).astype(BF16)
    save(gwo_ref, gwa_any.at[:, 0:model])
    gs_ref[1:2, 0:model] = column_sum(grad_resid)
    gs_ref[2:3, 0:model] = column_sum(grad_act * normed)
    gs_ref[3:4, 0:model] = column_sum(grad_act)
    gs_ref[4:5, 0:model] = column_sum(up)
    for copy in stores:
        copy.wait()


def middle(x, attn, w_out, w_fc, w_proj, small, fc_bias, cotangent):
    length, model = x.shape
    groups = attn.shape[0]
    hid = w_fc.shape[2]
    vm = pltpu.VMEM
    vmem, far = pl.BlockSpec(memory_space=pltpu.VMEM), pl.BlockSpec(memory_space=pl.ANY)
    return pl.pallas_call(
        functools.partial(middle_kernel, groups),
        out_shape=(
            jax.ShapeDtypeStruct((length, model), BF16),
            jax.ShapeDtypeStruct((length, model), F32),
            jax.ShapeDtypeStruct(attn.shape, BF16),
            jax.ShapeDtypeStruct((model, model + hid), BF16),
            jax.ShapeDtypeStruct((hid, model), BF16),
            jax.ShapeDtypeStruct((8, hid), F32),
        ),
        in_specs=[vmem] * 5 + [far] * 3,
        out_specs=[far] * 5 + [vmem],
        scratch_shapes=[
            vm(w_fc.shape, BF16), vm(w_proj.shape, BF16), vm(cotangent.shape, BF16),
            vm((length, model), BF16), vm((length, model), F32), vm(attn.shape, BF16),
            vm((model, model), BF16), vm((model, hid), BF16), vm((hid, model), BF16),
            pltpu.SemaphoreType.DMA((3,)), pltpu.SemaphoreType.DMA((6,)),
        ],
        compiler_params=params(),
        cost_estimate=cost(12 * length * model * hid + 6 * length * model * model,
                           16 * model * hid, length * hid),
        name="middle",
    )(x, attn, w_out, small, fc_bias, w_fc, w_proj, cotangent)


def per_device(
    tokens, starts, norm1_gain, norm1_bias, w_qkv, q_bias, v_bias, w_out, out_bias, norm2_gain,
    norm2_bias, w_fc, fc_bias, w_proj, proj_bias, cotangent,
):
    groups = lax.axis_size("sp")
    parts = lax.axis_size("fsdp")
    rows, triple = w_qkv.shape
    piece = norm1_gain.shape[0]
    x = tokens[0]
    vectors = [
        norm1_gain, norm1_bias, q_bias, v_bias, out_bias, norm2_gain, norm2_bias, proj_bias, fc_bias
    ]
    qkv, out, lse, attn, code_q, code_k, small, fcb, packed, *wide = front(
        x, w_qkv, starts, vectors, (w_out, w_fc, w_proj), groups, parts
    )
    if rows % 16 == 0:
        weight, weight_count = packed, rows
    else:
        weight, weight_count = packed.reshape(1, parts * rows, triple), parts * rows
    wide = [w if w.shape[1] % 16 == 0 else w.reshape(1, -1, w.shape[2]) for w in wide]
    block_out, grad_resid, grad_attn, g_a, g_p, sums = middle(
        x, attn, *wide, small, fcb, cotangent[0]
    )
    grad_tokens, g_q, g_v, g_out, g_fc, g_p = back(
        qkv, grad_attn, out, lse, code_q, code_k,
        g_a.reshape(parts, -1, g_a.shape[1]), g_p.reshape(parts, -1, g_p.shape[1]),
        x, grad_resid, weight, small, sums,
    )
    grad_tokens, g_q, g_out, g_fc, g_p, *vec, g_fcb = hand_out(
        (grad_tokens, g_q, g_out, g_fc, g_p), g_v, piece, fc_bias.shape[0]
    )
    vec = [v.reshape(-1) for v in vec]
    return (
        block_out[None], grad_tokens[None], vec[0], vec[1], g_q, vec[2], vec[3],
        g_out, vec[4], vec[5], vec[6], g_fc, g_fcb.reshape(-1), g_p, vec[7],
    )


def solution(mesh):
    row, mat = P("fsdp"), P("fsdp", None)
    stream = P("fsdp", "sp", None)
    return jax.shard_map(
        per_device,
        mesh=mesh,
        in_specs=(stream, P("fsdp", "sp"), row, row, mat, row, row, mat, row, row, row, mat, row,
                  mat, row, stream),
        out_specs=(stream, stream, row, row, mat, row, row, mat, row, row, row, mat, row, mat, row),
        check_vma=False,
    )
```
